32 devices in a mesh: fsdp: 4 (over y, x), ctx: 2 (over core), tp: 4 (over z).
Axes of the slice: x: 2, y: 2, z: 4, core: 2. Of those that a mesh axis runs over, the one named last changes fastest.
Arguments:
- inputs: bfloat16 [4, 2048, 2048], P('fsdp', 'ctx'), may hold values from -6 to 6
- lengths: int32 [4], P('fsdp'), may hold values from 512 to 2048, as said below
- w_query: bfloat16 [2048, 2048], P('fsdp', 'tp'), may hold values from -0.125 to 0.125
- w_forget: bfloat16 [2048, 2048], P('fsdp', 'tp'), may hold values from -0.125 to 0.125
- w_input: bfloat16 [2048, 2048], P('fsdp', 'tp'), may hold values from -0.125 to 0.125
- w_outgate: bfloat16 [2048, 2048], P('fsdp', 'tp'), may hold values from -0.125 to 0.125
- w_output: bfloat16 [2048, 2048], P('tp', 'fsdp'), may hold values from -0.125 to 0.125
- w_gate: bfloat16 [2048, 5632], P('fsdp', 'tp'), may hold values from -0.125 to 0.125
- w_up: bfloat16 [2048, 5632], P('fsdp', 'tp'), may hold values from -0.125 to 0.125
- w_down: bfloat16 [5632, 2048], P('tp', 'fsdp'), may hold values from -0.078125 to 0.078125
- norm_gain: float32 [2048], replicated, may hold values from 0.5 to 1.5
- ffn_gain: float32 [2048], replicated, may hold values from 0.5 to 1.5
- head_gain: float32 [128], replicated, may hold values from 0.5 to 1.5
- forget_gap: float32 [2048], P('tp'), may hold values from 0.0002 to 0.06
- cotangent: bfloat16 [4, 2048, 2048], P('fsdp', 'ctx'), may hold values from -6 to 6
Outputs:
- output: bfloat16 [4, 2048, 2048], P('fsdp', 'ctx')
- input_grad: bfloat16 [4, 2048, 2048], P('fsdp', 'ctx')
- grad_w_query: float32 [2048, 2048], P(('fsdp', 'ctx'), 'tp')
- grad_w_forget: float32 [2048, 2048], P(('fsdp', 'ctx'), 'tp')
- grad_w_input: float32 [2048, 2048], P(('fsdp', 'ctx'), 'tp')
- grad_w_outgate: float32 [2048, 2048], P(('fsdp', 'ctx'), 'tp')
- grad_w_output: float32 [2048, 2048], P('tp', ('fsdp', 'ctx'))
- grad_w_gate: float32 [2048, 5632], P(('fsdp', 'ctx'), 'tp')
- grad_w_up: float32 [2048, 5632], P(('fsdp', 'ctx'), 'tp')
- grad_w_down: float32 [5632, 2048], P('tp', ('fsdp', 'ctx'))
- grad_norm_gain: float32 [2048], replicated
- grad_ffn_gain: float32 [2048], replicated
- grad_head_gain: float32 [128], replicated
- grad_forget_gap: float32 [2048], P('tp')
The draws below stay inside these ranges and needn't reach their ends.
Inputs may be any that keep to these rules, and one draw needn't show every extreme that they name: `lengths`: valid slots of each sequence; slots from that length on are padding. Some sequence is full and some has 512 slots.
All inputs are finite; a program needn't handle non-finite values.
Results may differ from the reference program's by a relative error of at most 0.0095.
Values may be sent and summed in bfloat16 or wider, within the bound.
A program may use at most 320 MiB of HBM per device.

```python
import math
import jax
import jax.numpy as jnp
from jax import lax

D = 2048
HEADS = 16
HEAD_DIM = 128
FF = 5632
SEQ_LEN = 2048
SEQS = 4


def draw_lengths(key, part):
    values = jax.random.randint(key, (SEQS,), SEQ_LEN // 4, SEQ_LEN + 1, dtype=jnp.int32)
    values = values.at[0].set(SEQ_LEN).at[SEQS - 1].set(SEQ_LEN // 4)
    return values.astype(jnp.int32)


def steps_of(rng, extent, pieces, least, high):
    def one(axis_at, shards_of):
        draws = jax.random.uniform(jax.random.fold_in(jax.random.fold_in(rng, 6), axis_at), (shards_of,), jnp.float32, least / len(pieces), high / len(pieces))
        return jnp.repeat(jnp.exp(draws), extent[axis_at] // shards_of).reshape((-1,) + (1,) * (len(extent) - axis_at - 1))

    loudness = one(*pieces[0])
    for cut in pieces[1:]:
        loudness = loudness * one(*cut)
    return loudness


def scatter_about(own_key, extent, spread, bound, split=(), kind=jnp.bfloat16):
    drawn = spread * jax.random.normal(own_key, extent, jnp.float32)
    if split:
        drawn = drawn * steps_of(own_key, extent, split, -0.22, 0.18)
    return jnp.clip(drawn, -bound, bound).astype(kind)


def setup_inputs(seed: int = 0) -> dict:
    arg_keys = jax.random.split(jax.random.key(seed), 16)
    inputs = scatter_about(arg_keys[0], (SEQS, SEQ_LEN, D), 1.0, 6.0, ((0, 4), (1, 2)))
    lengths = draw_lengths(jax.random.fold_in(arg_keys[15], 71), 0)
    w_query = scatter_about(arg_keys[2], (D, D), D ** -0.5, 0.125, ((0, 4), (1, 4)))
    w_forget = scatter_about(arg_keys[3], (D, D), D ** -0.5, 0.125, ((0, 4), (1, 4)))
    w_input = scatter_about(arg_keys[4], (D, D), D ** -0.5, 0.125, ((0, 4), (1, 4)))
    w_outgate = scatter_about(arg_keys[5], (D, D), D ** -0.5, 0.125, ((0, 4), (1, 4)))
    w_output = scatter_about(arg_keys[6], (D, D), D ** -0.5, 0.125, ((0, 4), (1, 4)))
    w_gate = scatter_about(arg_keys[7], (D, FF), D ** -0.5, 0.125, ((0, 4), (1, 4)))
    w_up = scatter_about(arg_keys[8], (D, FF), D ** -0.5, 0.125, ((0, 4), (1, 4)))
    w_down = scatter_about(arg_keys[9], (FF, D), FF ** -0.5, 0.078125, ((0, 4), (1, 4)))
    norm_gain = jnp.clip(1.0 + 0.1 * jax.random.normal(arg_keys[10], (D,), jnp.float32), 0.5, 1.5)
    ffn_gain = jnp.clip(1.0 + 0.1 * jax.random.normal(arg_keys[11], (D,), jnp.float32), 0.5, 1.5)
    head_gain = jnp.clip(1.0 + 0.1 * jax.random.normal(arg_keys[12], (HEAD_DIM,), jnp.float32), 0.5, 1.5)
    forget_gap = jnp.clip(jnp.exp(math.log(0.06) - 5.7037825 * jax.random.uniform(arg_keys[13], (D,), jnp.float32) ** steps_of(arg_keys[13], (D,), ((0, 4),), -0.2, 0.2)), 0.0002, 0.06)
    cotangent = scatter_about(arg_keys[14], (SEQS, SEQ_LEN, D), 1.0, 6.0, ((0, 4), (1, 2)))
    return dict(inputs=inputs, lengths=lengths, w_query=w_query, w_forget=w_forget, w_input=w_input, w_outgate=w_outgate, w_output=w_output, w_gate=w_gate, w_up=w_up, w_down=w_down, norm_gain=norm_gain, ffn_gain=ffn_gain, head_gain=head_gain, forget_gap=forget_gap, cotangent=cotangent)


EPSILON = 1e-05
HIGHEST = lax.Precision.HIGHEST

@jax.custom_vjp
def low(v):
    return lax.optimization_barrier(v.astype(jnp.bfloat16)).astype(jnp.float32)

@jax.custom_vjp
def low_back(v):
    return v

def low_keep(v):
    return (low(v), None)

def low_pass(kept, grad):
    return (grad,)

def back_keep(v):
    return (v, None)

def back_low(kept, grad):
    return (low(grad),)
low.defvjp(low_keep, low_pass)
low_back.defvjp(back_keep, back_low)

def matmul_high(left_side, right_side):
    return jnp.matmul(left_side, right_side, precision=HIGHEST)

def rms_scale(tensor, gain_vec):
    return tensor * lax.rsqrt(lax.optimization_barrier(jnp.mean(tensor * tensor, axis=-1, keepdims=True)) + EPSILON) * gain_vec

def recurrence(queries, keys_all, values, decays):
    seq_count = queries.shape[0]
    block_len = min(128, SEQ_LEN)
    block_count = SEQ_LEN // block_len

    def arrange(tensor):
        return tensor.reshape(seq_count, block_count, block_len, HEADS, HEAD_DIM).transpose(1, 0, 3, 2, 4)
    lower_mask = jnp.tril(jnp.ones((block_len, block_len), jnp.float32))

    @jax.checkpoint
    def advance(carried, block_data):
        query_block, key_block, value_block, decay_block = block_data
        cumulative = jnp.cumsum(decay_block, axis=2)
        growth = jnp.exp(cumulative)
        query_scaled = query_block * growth
        key_scaled = key_block * jnp.exp(-cumulative)
        scores = jnp.einsum('nhtd,nhsd->nhts', query_scaled, key_scaled, precision=HIGHEST) * lower_mask
        outputs = jnp.einsum('nhts,nhse->nhte', scores, value_block, precision=HIGHEST)
        outputs = outputs + jnp.einsum('nhtd,nhde->nhte', query_scaled, carried, precision=HIGHEST)
        final_growth = growth[:, :, -1, :]
        updated = final_growth[:, :, :, None] * carried + jnp.einsum('nhsd,nhse->nhde', key_scaled * final_growth[:, :, None, :], value_block, precision=HIGHEST)
        return (updated, outputs)
    start_state = jnp.zeros((seq_count, HEADS, HEAD_DIM, HEAD_DIM), jnp.float32)
    _, outputs = lax.scan(advance, start_state, (arrange(queries), arrange(keys_all), arrange(values), arrange(decays)))
    return outputs.transpose(1, 0, 3, 2, 4).reshape(seq_count, SEQ_LEN, HEADS * HEAD_DIM)

def block_forward(inputs, w_query, w_forget, w_input, w_outgate, w_output, w_gate, w_up, w_down, norm_gain, ffn_gain, head_gain, forget_gap, keep_rows):
    normed = low(rms_scale(inputs, norm_gain))
    query_pre = low_back(matmul_high(normed, w_query))
    forget_pre = low_back(matmul_high(normed, w_forget))
    value_pre = low_back(matmul_high(normed, w_input))
    gate_pre = low_back(matmul_high(normed, w_outgate))
    queries = jax.nn.silu(query_pre)
    closing = jax.nn.sigmoid(-forget_pre)
    keys_all = forget_gap * closing * keep_rows
    decays = jnp.log(1.0 - forget_gap * closing) * keep_rows
    mixed_out = recurrence(queries, keys_all, value_pre, decays)
    seq_count = inputs.shape[0]
    heads_view = mixed_out.reshape(seq_count, SEQ_LEN, HEADS, HEAD_DIM)
    normed_heads = rms_scale(heads_view, head_gain).reshape(seq_count, SEQ_LEN, D)
    gated = low(normed_heads * jax.nn.silu(gate_pre))
    branch = low_back(matmul_high(gated, w_output))
    middle = inputs + branch
    normed_two = low(rms_scale(middle, ffn_gain))
    gate_hidden = low_back(matmul_high(normed_two, w_gate))
    up_hidden = low_back(matmul_high(normed_two, w_up))
    hidden = low(jax.nn.silu(gate_hidden) * up_hidden)
    feed = low_back(matmul_high(hidden, w_down))
    return middle + feed

def reference(inputs, lengths, w_query, w_forget, w_input, w_outgate, w_output, w_gate, w_up, w_down, norm_gain, ffn_gain, head_gain, forget_gap, cotangent):
    weights = tuple((tensor.astype(jnp.float32) for tensor in (w_query, w_forget, w_input, w_outgate, w_output, w_gate, w_up, w_down)))
    gains = (norm_gain, ffn_gain, head_gain, forget_gap)
    positions = jnp.arange(SEQ_LEN, dtype=jnp.int32)
    keep_all = (positions[None, :] < lengths[:, None]).astype(jnp.float32)[:, :, None]
    pair_count = SEQS // 2

    def regroup(tensor):
        return tensor.reshape((pair_count, 2) + tensor.shape[1:])

    def one_pair(running, element):
        pair_inputs, pair_cotangent, pair_keep = element

        def forward(pair_source, *params):
            return block_forward(pair_source, *params, pair_keep)
        result, pullback = jax.vjp(forward, pair_inputs.astype(jnp.float32), *weights, *gains)
        gradients = pullback(pair_cotangent.astype(jnp.float32) * pair_keep)
        running = tuple((total_now + grad_now for total_now, grad_now in zip(running, gradients[1:])))
        return (running, (result.astype(jnp.bfloat16), gradients[0].astype(jnp.bfloat16)))
    initial = tuple((jnp.zeros_like(tensor) for tensor in weights + gains))
    totals, (outputs, input_grads) = lax.scan(one_pair, initial, (regroup(inputs), regroup(cotangent), regroup(keep_all)))
    return (outputs.reshape(SEQS, SEQ_LEN, D), input_grads.reshape(SEQS, SEQ_LEN, D), totals[0], totals[1], totals[2], totals[3], totals[4], totals[5], totals[6], totals[7], totals[8], totals[9], totals[10], totals[11])
```

```python
import functools

import jax
import jax.numpy as jnp
from jax import lax
from jax.experimental import pallas as pl
from jax.experimental.pallas import tpu as pltpu
from jax.sharding import PartitionSpec as P

HEAD_DIM = 128
EPSILON = 1e-05
F32 = jnp.float32
BF16 = jnp.bfloat16
BY_AXIS = pl.DeviceIdType.MESH
VMEM_BYTES = 62 * 1024 * 1024
ANY = pl.BlockSpec(memory_space=pl.ANY)
WHOLE = pl.BlockSpec(memory_space=pltpu.VMEM)


def dot(left, right, dims=((1,), (0,))):
    return lax.dot_general(left, right, (dims, ((), ())), preferred_element_type=F32)


NT = ((1,), (1,))
TN = ((0,), (0,))


def sigmoid(value):
    return 1.0 / (1.0 + jnp.exp(-value))


def slope(pre, sig):
    return sig * (1.0 + pre * (1.0 - sig))


def ones_times(ones, value):
    high = value.astype(BF16)
    rest = (value - high.astype(F32)).astype(BF16)
    return dot(ones, high) + dot(ones, rest)


def ring_place(index, size, folded):
    if folded:
        return index + (index // 2) * (1 - 2 * (index % 2))
    return index


class RingGather:
    def __init__(self, shards, outs, where, sems, size, folded):
        self.shards, self.outs, self.where, self.size = shards, outs, where, size
        self.ring_send, self.ring_recv, self.pair_send, self.pair_recv, self.local = sems
        self.place = ring_place(lax.axis_index("fsdp"), size, folded)
        self.folded = folded
        self.core = lax.axis_index("ctx") % 2
        self.pair = lax.axis_index("ctx") + 1 - 2 * self.core

    def device(self, place):
        return ring_place(lax.rem(place + 2 * self.size, self.size), self.size, self.folded)

    def peers(self):
        return [
            {"fsdp": self.device(self.place + 1)},
            {"fsdp": self.device(self.place - 1)},
            {"ctx": self.pair},
        ]

    def rows(self, i, core, way):
        quarter = self.shards[i].shape[0] // 4
        return pl.multiple_of((2 * core + way) * quarter, 16), quarter

    def in_shard(self, i, core, way):
        at, length = self.rows(i, core, way)
        return self.shards[i].at[pl.ds(at, length), :]

    def in_out(self, i, block, core, way):
        out, dim, column = self.where[i]
        at, length = self.rows(i, core, way)
        deep, wide = self.shards[i].shape
        if dim == 0:
            start = pl.multiple_of(block * deep + at, 16)
            return self.outs[out].at[pl.ds(start, length), pl.ds(column, wide)]
        start = pl.multiple_of(block * wide, 128)
        return self.outs[out].at[pl.ds(at, length), pl.ds(start, wide)]

    def own_block(self, i):
        out, dim, column = self.where[i]
        deep, wide = self.shards[i].shape
        block = self.device(self.place)
        if dim == 0:
            start = pl.multiple_of(block * deep, 16)
            return self.outs[out].at[pl.ds(start, deep), pl.ds(column, wide)]
        return self.outs[out].at[:, pl.ds(pl.multiple_of(block * wide, 128), wide)]

    def local_copy(self, i):
        return pltpu.make_async_copy(self.shards[i], self.own_block(i), self.local.at[i])

    def ring(self, i, way, step):
        sign = 1 - 2 * way
        block = self.device(self.place - sign * step)
        there = self.in_out(i, block, self.core, way)
        here = self.in_shard(i, self.core, way) if step == 0 else there
        at = (i * 2 + way) * (self.size - 1) + step
        return pltpu.make_async_remote_copy(
            src_ref=here,
            dst_ref=there,
            send_sem=self.ring_send.at[at],
            recv_sem=self.ring_recv.at[at],
            device_id={"fsdp": self.device(self.place + sign)},
            device_id_type=BY_AXIS,
        )

    def across(self, i, way, step, core):
        sign = 1 - 2 * way
        block = self.device(self.place - sign * (step + 1))
        piece = self.in_out(i, block, core, way)
        at = (i * 2 + way) * (self.size - 1) + step
        return pltpu.make_async_remote_copy(
            src_ref=piece,
            dst_ref=piece,
            send_sem=self.pair_send.at[at],
            recv_sem=self.pair_recv.at[at],
            device_id={"ctx": self.pair},
            device_id_type=BY_AXIS,
        )

    def each(self):
        return [(i, way) for i in range(len(self.shards)) for way in range(2)]

    def start(self):
        for i, way in self.each():
            self.ring(i, way, 0).start()
        for i in range(len(self.shards)):
            self.local_copy(i).start()

    def advance(self, step):
        for i, way in self.each():
            arrived = self.ring(i, way, step)
            arrived.wait_recv()
            if step + 1 < self.size - 1:
                self.ring(i, way, step + 1).start()
            self.across(i, way, step, self.core).start()

    def finish(self):
        for i, way in self.each():
            for step in range(self.size - 1):
                self.ring(i, way, step).wait_send()
                self.across(i, way, step, self.core).wait_send()
                self.across(i, way, step, 1 - self.core).wait_recv()
        for i in range(len(self.shards)):
            self.local_copy(i).wait()

    @staticmethod
    def scratch(count, size):
        copies = count * 2 * (size - 1)
        return [pltpu.SemaphoreType.DMA((copies,)) for _ in range(4)] + [
            pltpu.SemaphoreType.DMA((count,))
        ]


def meet(peers):
    barrier = pltpu.get_barrier_semaphore()
    total = 0
    for condition, peer in peers:
        if condition is None:
            pl.semaphore_signal(barrier, inc=1, device_id=peer, device_id_type=BY_AXIS)
            total = total + 1
        else:

            @pl.when(condition)
            def _():
                pl.semaphore_signal(barrier, inc=1, device_id=peer, device_id_type=BY_AXIS)

            total = total + condition.astype(jnp.int32)
    pl.semaphore_wait(barrier, total)


def gather_weights(shards, out_shapes, where, collective_id):
    size = lax.axis_size("fsdp")
    folded = size == 4
    count = len(shards)

    def kernel(*refs):
        ins, outs, sems = refs[:count], refs[count : count + len(out_shapes)], refs[-5:]
        job = RingGather(ins, outs, where, sems, size, folded)
        meet([(None, peer) for peer in job.peers()])
        job.start()
        for step in range(size - 1):
            job.advance(step)
        job.finish()

    return pl.pallas_call(
        kernel,
        out_shape=[jax.ShapeDtypeStruct(s, BF16) for s in out_shapes],
        in_specs=[WHOLE] * count,
        out_specs=[ANY] * len(out_shapes),
        scratch_shapes=RingGather.scratch(count, size),
        compiler_params=pltpu.CompilerParams(
            collective_id=collective_id, has_side_effects=True, vmem_limit_bytes=VMEM_BYTES
        ),
        name="gather_weights",
    )(*shards)


def line_sum(name, part, extras, extra_outs, epilogue, collective_id, chunk=32, gather=None):
    size = lax.axis_size("tp")
    rows, width = part.shape
    half = rows // 2
    chunk = min(chunk, half)
    count = half // chunk
    n_extra, n_extra_out = len(extras), len(extra_outs)
    if gather is None:
        shards, gathered, where = [], [], []
    else:
        shards, gathered, where = gather
    n_shards, n_gathered = len(shards), len(gathered)
    fsdp_size = lax.axis_size("fsdp")

    def kernel(*refs):
        refs = list(refs)

        def take(n):
            taken = refs[:n]
            del refs[:n]
            return taken

        (part_ref,) = take(1)
        extra_refs = take(n_extra)
        shard_refs = take(n_shards)
        (out_ref,) = take(1)
        extra_out_refs = take(n_extra_out)
        gathered_refs = take(n_gathered)
        came, gone, sum_send, sum_recv, back_send, back_recv = take(6)
        place = lax.axis_index("tp")
        first, last = place == 0, place == size - 1
        peers = [(jnp.logical_not(first), {"tp": place - 1}), (jnp.logical_not(last), {"tp": place + 1})]
        job = None
        if n_shards:
            job = RingGather(shard_refs, gathered_refs, where, take(5), fsdp_size, fsdp_size == 4)
            peers += [(None, peer) for peer in job.peers()]
        meet(peers)

        source = (first, last)
        owner = (last, first)
        ahead = (place + 1, place - 1)
        behind = (place - 1, place + 1)

        def at(way, k):
            start = k * chunk + (half if way == 0 else 0)
            return pl.ds(pl.multiple_of(start, chunk), chunk)

        def onward(way, k, from_part):
            source_ref = part_ref.at[at(way, k), :] if from_part else gone.at[way, k]
            return pltpu.make_async_remote_copy(
                src_ref=source_ref,
                dst_ref=came.at[way, k],
                send_sem=sum_send.at[way, k],
                recv_sem=sum_recv.at[way, k],
                device_id={"tp": ahead[way]},
                device_id_type=BY_AXIS,
            )

        def back(way, k):
            piece = out_ref.at[at(way, k), :]
            return pltpu.make_async_remote_copy(
                src_ref=piece,
                dst_ref=piece,
                send_sem=back_send.at[way, k],
                recv_sem=back_recv.at[way, k],
                device_id={"tp": behind[way]},
                device_id_type=BY_AXIS,
            )

        for way in range(2):

            @pl.when(source[way])
            def _():
                @pl.loop(0, count)
                def _(k):
                    onward(way, k, True).start()

        if job is not None:
            job.start()

        def add(k):
            for way in range(2):

                @pl.when(jnp.logical_not(source[way]))
                def _():
                    onward(way, k, False).wait_recv()
                    total = came[way, k].astype(F32) + part_ref[at(way, k), :].astype(F32)

                    @pl.when(owner[way])
                    def _():
                        start = pl.multiple_of(k * chunk, chunk)
                        out_ref[at(way, k), :] = epilogue(
                            extra_refs, extra_out_refs, at(way, k), pl.ds(start, chunk), total
                        )
                        back(way, k).start()

                    @pl.when(jnp.logical_not(owner[way]))
                    def _():
                        gone[way, k] = total.astype(BF16)
                        onward(way, k, False).start()

        def spread(k):
            for way in range(2):

                @pl.when(jnp.logical_not(owner[way]))
                def _():
                    back(way, k).wait_recv()

                    @pl.when(jnp.logical_not(source[way]))
                    def _():
                        back(way, k).start()

        steps = [add, spread]
        cuts = []
        if job is not None:
            cuts = [((2 * count - 2) * (i + 1)) // fsdp_size for i in range(fsdp_size - 1)]
        for number, step in enumerate(steps):
            low, high = number * count, (number + 1) * count
            edges = [low] + [c for c in cuts if low < c < high] + [high]
            for left, right in zip(edges[:-1], edges[1:]):
                if left in cuts:
                    job.advance(cuts.index(left))

                @pl.loop(left - low, right - low)
                def _(k):
                    step(k)

        if job is not None:
            job.finish()

        for way in range(2):

            @pl.when(jnp.logical_not(owner[way]))
            def _():
                @pl.loop(0, count)
                def _(k):
                    onward(way, k, False).wait_send()

            @pl.when(jnp.logical_not(source[way]))
            def _():
                @pl.loop(0, count)
                def _(k):
                    back(way, k).wait_send()

    scratch = [
        pltpu.VMEM((2, count, chunk, width), BF16),
        pltpu.VMEM((2, count, chunk, width), BF16),
    ] + [pltpu.SemaphoreType.DMA((2, count)) for _ in range(4)]
    if n_shards:
        scratch += RingGather.scratch(n_shards, fsdp_size)
    return pl.pallas_call(
        kernel,
        out_shape=[jax.ShapeDtypeStruct((rows, width), BF16)]
        + [jax.ShapeDtypeStruct(s, d) for s, d in extra_outs]
        + [jax.ShapeDtypeStruct(s, BF16) for s in gathered],
        in_specs=[WHOLE] * (1 + n_extra + n_shards),
        out_specs=[WHOLE] * (1 + n_extra_out) + [ANY] * n_gathered,
        scratch_shapes=scratch,
        compiler_params=pltpu.CompilerParams(
            collective_id=collective_id, has_side_effects=True, vmem_limit_bytes=VMEM_BYTES
        ),
        name=name,
    )(part, *extras, *shards)


def rms(value):
    return lax.rsqrt(jnp.mean(value * value, axis=-1, keepdims=True) + EPSILON)


def middle_rows(extra, extra_out, rows, own, total):
    x_ref, gain_ref = extra
    middle = x_ref[rows, :].astype(F32) + total
    extra_out[0][own, :] = middle
    return (middle * rms(middle) * gain_ref[...]).astype(BF16)


def norm_back(grad, value, gain):
    inverse = rms(value)
    scaled = value * inverse
    weighted = grad * gain
    back = inverse * (weighted - scaled * jnp.mean(weighted * scaled, axis=-1, keepdims=True))
    return back, jnp.sum(grad * scaled, axis=0, keepdims=True)


def grad_middle_rows(extra, extra_out, rows, own, total):
    middle_ref, grad_out_ref, gain_ref = extra
    back, gain_part = norm_back(total, middle_ref[own, :], gain_ref[...])
    grad_middle = grad_out_ref[rows, :].astype(F32) + back
    extra_out[0][own, :] = grad_middle
    add_rows(extra_out[1], own, gain_part)
    return grad_middle.astype(BF16)


def input_grad_rows(extra, extra_out, rows, own, total):
    x_ref, grad_middle_ref, gain_ref = extra
    back, gain_part = norm_back(total, x_ref[rows, :].astype(F32), gain_ref[...])
    add_rows(extra_out[0], own, gain_part)
    return (grad_middle_ref[own, :] + back).astype(BF16)


def add_rows(sum_ref, own, term):
    sum_ref[pl.ds(own.start // own.size, 1), :] = term


def lower_ones(length):
    at = lax.broadcasted_iota(jnp.int32, (length, length), 0)
    before = lax.broadcasted_iota(jnp.int32, (length, length), 1)
    return at >= before


def chunk_decay(forget, gap, live, lower):
    closing = sigmoid(-forget)
    opened = gap * closing
    remain = 1.0 - opened
    decay = jnp.where(live, jnp.log(remain), 0.0)
    keys = jnp.where(live, opened, 0.0)
    return closing, remain, keys, ones_times(lower, decay)


def rows_live(valid_ref, chunk_index, length):
    at = lax.broadcasted_iota(jnp.int32, (length, HEAD_DIM), 0) + chunk_index * length
    return at < valid_ref[0]


def span_end_kernel(heads, length, valid_ref, forget_ref, value_ref, gap_ref, end_ref):
    index = pl.program_id(0)

    @pl.when(index == 0)
    def _():
        end_ref[...] = jnp.zeros_like(end_ref)

    live = rows_live(valid_ref, index, length)
    lower = lower_ones(length).astype(BF16)
    for h in range(heads):
        cols = slice(h * HEAD_DIM, (h + 1) * HEAD_DIM)
        _, _, keys, cumulative = chunk_decay(forget_ref[:, cols], gap_ref[:, cols], live, lower)
        total = cumulative[length - 1 :, :]
        tail = (keys * jnp.exp(total - cumulative)).astype(BF16)
        end_ref[h] = jnp.exp(total) * end_ref[h] + dot(value_ref[:, cols].astype(BF16), tail, TN)


def mix_kernel(
    heads, length, valid_ref, query_ref, forget_ref, value_ref, gate_ref, gap_ref, gain_ref, start_ref,
    gated_ref, mixed_ref, states_ref, state_ref,
):
    index = pl.program_id(0)

    @pl.when(index == 0)
    def _():
        state_ref[...] = start_ref[...]

    live = rows_live(valid_ref, index, length)
    mask = lower_ones(length)
    lower = mask.astype(BF16)
    for h in range(heads):
        cols = slice(h * HEAD_DIM, (h + 1) * HEAD_DIM)
        _, _, keys, cumulative = chunk_decay(forget_ref[:, cols], gap_ref[:, cols], live, lower)
        pre = query_ref[:, cols]
        queries = (pre * sigmoid(pre) * jnp.exp(cumulative)).astype(BF16)
        shrunk = keys * jnp.exp(-cumulative)
        values = value_ref[:, cols].astype(BF16)
        state = state_ref[h]
        states_ref[0, h] = state
        scores = jnp.where(mask, dot(queries, shrunk.astype(BF16), NT), 0.0).astype(BF16)
        mixed = dot(scores, values) + dot(queries, state.astype(BF16), NT)
        mixed_ref[:, cols] = mixed
        growth = jnp.exp(cumulative[length - 1 :, :])
        state_ref[h] = growth * state + dot(values, (shrunk * growth).astype(BF16), TN)
        gate = gate_ref[:, cols]
        gated_ref[:, cols] = (mixed * rms(mixed) * gain_ref[...] * (gate * sigmoid(gate))).astype(BF16)


def span_begin_kernel(
    heads, length, valid_ref, grad_ref, mixed_ref, query_ref, forget_ref, gate_ref, gap_ref, gain_ref,
    grad_gate_ref, grad_mixed_ref, gain_part_ref, begin_ref,
):
    step = pl.program_id(0)
    index = pl.num_programs(0) - 1 - step

    @pl.when(step == 0)
    def _():
        begin_ref[...] = jnp.zeros_like(begin_ref)
        gain_part_ref[...] = jnp.zeros_like(gain_part_ref)

    live = rows_live(valid_ref, index, length)
    lower = lower_ones(length).astype(BF16)
    gain = gain_ref[...]
    for h in range(heads):
        cols = slice(h * HEAD_DIM, (h + 1) * HEAD_DIM)
        mixed = mixed_ref[:, cols]
        inverse = rms(mixed)
        scaled = mixed * inverse
        gate = gate_ref[:, cols]
        sig = sigmoid(gate)
        grad = grad_ref[:, cols].astype(F32)
        grad_gate_ref[:, cols] = (grad * scaled * gain * slope(gate, sig)).astype(BF16)
        grad_scaled = grad * (gate * sig)
        gain_part_ref[...] += jnp.sum(grad_scaled * scaled, axis=0, keepdims=True)
        weighted = grad_scaled * gain
        grad_mixed = inverse * (weighted - scaled * jnp.mean(weighted * scaled, axis=-1, keepdims=True))
        grad_mixed = grad_mixed.astype(BF16)
        grad_mixed_ref[:, cols] = grad_mixed
        _, _, _, cumulative = chunk_decay(forget_ref[:, cols], gap_ref[:, cols], live, lower)
        pre = query_ref[:, cols]
        queries = (pre * sigmoid(pre) * jnp.exp(cumulative)).astype(BF16)
        growth = jnp.exp(cumulative[length - 1 :, :])
        begin_ref[h] = growth * begin_ref[h] + dot(grad_mixed, queries, TN)


def mix_back_kernel(
    heads, length, valid_ref, grad_ref, query_ref, forget_ref, value_ref, gap_ref, states_ref, last_ref, end_ref,
    grad_query_ref, grad_forget_ref, grad_value_ref, gap_part_ref, flow_ref, after_ref,
):
    step = pl.program_id(0)
    index = pl.num_programs(0) - 1 - step

    @pl.when(step == 0)
    def _():
        flow_ref[...] = end_ref[...]
        after_ref[...] = last_ref[...]
        gap_part_ref[...] = jnp.zeros_like(gap_part_ref)

    live = rows_live(valid_ref, index, length)
    mask = lower_ones(length)
    lower = mask.astype(BF16)
    for h in range(heads):
        cols = slice(h * HEAD_DIM, (h + 1) * HEAD_DIM)
        gap = gap_ref[:, cols]
        closing, remain, keys, cumulative = chunk_decay(forget_ref[:, cols], gap, live, lower)
        pre = query_ref[:, cols]
        sig = sigmoid(pre)
        growth = jnp.exp(cumulative)
        shrink = jnp.exp(-cumulative)
        end_growth = growth[length - 1 :, :]
        queries = (pre * sig * growth).astype(BF16)
        shrunk_wide = keys * shrink
        shrunk = shrunk_wide.astype(BF16)
        tail = (shrunk_wide * end_growth).astype(BF16)
        values = value_ref[:, cols].astype(BF16)
        grad = grad_ref[:, cols]
        state = states_ref[0, h]
        flow = flow_ref[h]
        low_flow = flow.astype(BF16)
        scores = jnp.where(mask, dot(queries, shrunk, NT), 0.0).astype(BF16)
        grad_scores = jnp.where(mask, dot(grad, values, NT), 0.0).astype(BF16)
        to_queries = dot(grad, state.astype(BF16)) + dot(grad_scores, shrunk)
        to_keys = dot(grad_scores, queries, TN) + end_growth * dot(values, low_flow)
        grad_value_ref[:, cols] = (dot(scores, grad, TN) + dot(tail, low_flow, NT)).astype(BF16)
        grad_query_ref[:, cols] = (to_queries * growth * slope(pre, sig)).astype(BF16)
        terms = queries.astype(F32) * to_queries - shrunk.astype(F32) * to_keys
        high = terms.astype(BF16)
        rest = (terms - high.astype(F32)).astype(BF16)
        suffix = dot(lower, high, TN) + dot(lower, rest, TN)
        crossing = jnp.sum(flow * after_ref[h], axis=0, keepdims=True)
        pressure = jnp.where(live, to_keys * shrink - (suffix + crossing) / remain, 0.0)
        gap_part_ref[:, cols] += jnp.sum(closing * pressure, axis=0, keepdims=True)
        grad_forget_ref[:, cols] = (-closing * (1.0 - closing) * gap * pressure).astype(BF16)
        flow_ref[h] = end_growth * flow + dot(grad, queries, TN)
        after_ref[h] = state


def plain_call(kernel, name, grid, in_specs, out_specs, out_shape, scratch, flops, moved):
    return pl.pallas_call(
        kernel,
        grid_spec=pltpu.PrefetchScalarGridSpec(
            num_scalar_prefetch=1, grid=grid, in_specs=in_specs, out_specs=out_specs, scratch_shapes=scratch
        ),
        out_shape=out_shape,
        compiler_params=pltpu.CompilerParams(
            dimension_semantics=("arbitrary",), vmem_limit_bytes=VMEM_BYTES
        ),
        cost_estimate=pl.CostEstimate(flops=flops, bytes_accessed=moved, transcendentals=flops // 64),
        name=name,
    )


def combine(earlier, later):
    return (earlier[0] * later[0], later[0][:, None, :] * earlier[1] + later[1])


def from_earlier(state, decay, axis):
    size = lax.axis_size(axis)
    if size == 2:
        return lax.ppermute(state, axis, [(0, 1)])
    mine = lax.axis_index(axis)
    states, decays = lax.all_gather(state, axis), lax.all_gather(decay, axis)
    total = jnp.zeros_like(state)
    for k in range(size):
        new = decays[k][:, None, :] * total + states[k]
        total = jnp.where(k < mine, new, total)
    return total


def from_later(state, decay, axis):
    size = lax.axis_size(axis)
    if size == 2:
        return lax.ppermute(state, axis, [(1, 0)])
    mine = lax.axis_index(axis)
    states, decays = lax.all_gather(state, axis), lax.all_gather(decay, axis)
    total = jnp.zeros_like(state)
    for k in reversed(range(size)):
        new = decays[k][:, None, :] * total + states[k]
        total = jnp.where(k > mine, new, total)
    return total


def per_device(
    inputs, lengths, w_query, w_forget, w_input, w_outgate, w_output, w_gate, w_up, w_down,
    norm_gain, ffn_gain, head_gain, forget_gap, cotangent,
):
    groups, span, width = inputs.shape
    rows = groups * span
    fsdp, ctx, tp = lax.axis_size("fsdp"), lax.axis_size("ctx"), lax.axis_size("tp")
    local = forget_gap.shape[0]
    heads = local // HEAD_DIM
    ff = w_gate.shape[1]
    length = min(128, span)
    chunks = span // length
    place = lax.axis_index("tp")
    half = rows // 2

    valid = jnp.clip(lengths - lax.axis_index("ctx") * span, 0, span).astype(jnp.int32)
    keep = (jnp.arange(rows, dtype=jnp.int32) < valid[0])[:, None]
    x = inputs.reshape(rows, width)
    grad_low = jnp.where(keep, cotangent.reshape(rows, width), jnp.zeros((), BF16))
    gap = forget_gap.reshape(1, local)
    head_row = head_gain.reshape(1, HEAD_DIM)

    w_four, w_out = gather_weights(
        [w_query, w_forget, w_input, w_outgate, w_output],
        [(fsdp * w_query.shape[0], 4 * local), (local, width)],
        [(0, 0, 0), (0, 0, local), (0, 0, 2 * local), (0, 0, 3 * local), (1, 1, 0)],
        1,
    )

    wide = x.astype(F32)
    normed = (wide * rms(wide) * norm_gain).astype(BF16)
    pre = dot(normed, w_four)

    def column(j):
        return pl.BlockSpec((length, local), lambda i, *_: (i, j))

    def column_back(j):
        return pl.BlockSpec((length, local), lambda i, *_: (chunks - 1 - i, j))

    fixed = lambda shape: pl.BlockSpec(shape, lambda i, *_: (0,) * len(shape))
    state_shape = (heads, HEAD_DIM, HEAD_DIM)
    work = 2 * rows * local * HEAD_DIM
    moved = rows * local * 4

    local_end = plain_call(
        functools.partial(span_end_kernel, heads, length), "span_end", (chunks,),
        [column(1), column(2), fixed((1, local))], fixed(state_shape),
        jax.ShapeDtypeStruct(state_shape, F32), [], 3 * work, 2 * moved,
    )(valid, pre, pre, gap)
    span_decay = None
    if ctx > 2:
        keep_rows = keep.astype(F32)
        closing = jax.nn.sigmoid(-pre[:, local : 2 * local])
        logs = jnp.log(1.0 - gap * closing) * keep_rows
        span_decay = jnp.exp(jnp.sum(logs, axis=0)).reshape(heads, HEAD_DIM)
    start = from_earlier(local_end, span_decay, "ctx")
    gated, mixed, states = plain_call(
        functools.partial(mix_kernel, heads, length), "mix", (chunks,),
        [column(0), column(1), column(2), column(3), fixed((1, local)), fixed((1, HEAD_DIM)), fixed(state_shape)],
        [column(0), column(0), pl.BlockSpec((1,) + state_shape, lambda i, *_: (i, 0, 0, 0))],
        [
            jax.ShapeDtypeStruct((rows, local), BF16),
            jax.ShapeDtypeStruct((rows, local), F32),
            jax.ShapeDtypeStruct((chunks,) + state_shape, F32),
        ],
        [pltpu.VMEM(state_shape, F32)], 6 * work, 6 * moved,
    )(valid, pre, pre, pre, pre, gap, head_row, start)
    if ctx == 2:
        keep_rows = keep.astype(F32)
        closing = jax.nn.sigmoid(-pre[:, local : 2 * local])
        logs = jnp.log(1.0 - gap * closing) * keep_rows
        span_decay = jnp.exp(jnp.sum(logs, axis=0)).reshape(heads, HEAD_DIM)
    state_end = local_end + span_decay[:, None, :] * start

    branch = dot(gated, w_out).astype(BF16)
    normed_two, middle, w_both, w_back = line_sum(
        "sum_branch", branch, [x, ffn_gain.reshape(1, width)], [((half, width), F32)], middle_rows, 2,
        gather=(
            [w_gate, w_up, w_down],
            [(fsdp * w_gate.shape[0], 2 * ff), (ff, width)],
            [(0, 0, 0), (0, 0, ff), (1, 1, 0)],
        ),
    )

    both = dot(normed_two, w_both)
    gate_hidden, up_hidden = both[:, :ff], both[:, ff:]
    sig = jax.nn.sigmoid(gate_hidden)
    act = gate_hidden * sig
    hidden = (act * up_hidden).astype(BF16)
    mine = jnp.concatenate(
        [jnp.where(place == 0, middle, 0.0), jnp.where(place == tp - 1, middle, 0.0)], axis=0
    )
    feed = (dot(hidden, w_back) + mine).astype(BF16)
    result = lax.psum(feed, "tp").reshape(groups, span, width)

    grad_hidden = dot(grad_low, w_back, NT)
    grad_gate = (grad_hidden * up_hidden * slope(gate_hidden, sig)).astype(BF16)
    grad_up = (grad_hidden * act).astype(BF16)
    grad_both = jnp.concatenate([grad_gate, grad_up], axis=1)
    part_two = dot(grad_both, w_both, NT).astype(BF16)
    grad_branch, grad_middle, ffn_gain_part = line_sum(
        "sum_norm_two", part_two, [middle, grad_low, ffn_gain.reshape(1, width)],
        [((half, width), F32), ((half // min(32, half), width), F32)], grad_middle_rows, 3,
    )
    grad_w_down = dot(hidden, grad_low, TN).astype(BF16)
    grad_w_both = dot(normed_two, grad_both, TN).astype(BF16)

    grad_gated = dot(grad_branch, w_out, NT)
    grad_outgate, grad_mixed, head_part, local_begin = plain_call(
        functools.partial(span_begin_kernel, heads, length), "span_begin", (chunks,),
        [column_back(0), column_back(0), column_back(0), column_back(1), column_back(3), fixed((1, local)),
         fixed((1, HEAD_DIM))],
        [column_back(0), column_back(0), fixed((1, HEAD_DIM)), fixed(state_shape)],
        [
            jax.ShapeDtypeStruct((rows, local), BF16),
            jax.ShapeDtypeStruct((rows, local), BF16),
            jax.ShapeDtypeStruct((1, HEAD_DIM), F32),
            jax.ShapeDtypeStruct(state_shape, F32),
        ],
        [], 3 * work, 6 * moved,
    )(valid, grad_gated, mixed, pre, pre, pre, gap, head_row)
    grad_end = from_later(local_begin, span_decay, "ctx")
    grad_query, grad_forget, grad_value, gap_part = plain_call(
        functools.partial(mix_back_kernel, heads, length), "mix_back", (chunks,),
        [column_back(0), column_back(0), column_back(1), column_back(2), fixed((1, local)),
         pl.BlockSpec((1,) + state_shape, lambda i, *_: (chunks - 1 - i, 0, 0, 0)), fixed(state_shape),
         fixed(state_shape)],
        [column_back(0), column_back(0), column_back(0), fixed((1, local))],
        [jax.ShapeDtypeStruct((rows, local), BF16)] * 3 + [jax.ShapeDtypeStruct((1, local), F32)],
        [pltpu.VMEM(state_shape, F32), pltpu.VMEM(state_shape, F32)], 12 * work, 6 * moved,
    )(valid, grad_mixed, pre, pre, pre, gap, states, state_end, grad_end)

    grad_four = jnp.concatenate([grad_query, grad_forget, grad_value, grad_outgate], axis=1)
    part_one = dot(grad_four, w_four, NT).astype(BF16)
    input_grad, norm_gain_part = line_sum(
        "sum_norm_one", part_one, [x, grad_middle, norm_gain.reshape(1, width)],
        [((half // min(32, half), width), F32)], input_grad_rows, 4,
    )
    input_grad = input_grad.reshape(groups, span, width)
    grad_w_output = dot(gated, grad_branch, TN).astype(BF16)
    grad_w_four = dot(normed, grad_four, TN).astype(BF16)

    both_axes = ("fsdp", "ctx")

    def scatter(grad, dim):
        return lax.psum_scatter(grad, both_axes, scatter_dimension=dim, tiled=True).astype(F32)

    out_down = scatter(grad_w_down, 1)
    out_both = scatter(grad_w_both, 0)
    out_output = scatter(grad_w_output, 1)
    out_four = scatter(grad_w_four, 0)

    owner = jnp.logical_or(place == 0, place == tp - 1)
    sums = jnp.concatenate(
        [
            jnp.where(owner, jnp.sum(norm_gain_part, axis=0), 0.0),
            jnp.where(owner, jnp.sum(ffn_gain_part, axis=0), 0.0),
            head_part[0],
            lax.dynamic_update_slice(jnp.zeros((tp * local,), F32), gap_part[0], (place * local,)),
        ]
    )
    sums = lax.psum(sums, ("fsdp", "ctx", "tp"))
    grad_norm_gain, grad_ffn_gain = sums[:width], sums[width : 2 * width]
    grad_head_gain = sums[2 * width : 2 * width + HEAD_DIM]
    grad_gap = lax.dynamic_slice(sums, (2 * width + HEAD_DIM + place * local,), (local,))
    return (
        result,
        input_grad,
        out_four[:, :local],
        out_four[:, local : 2 * local],
        out_four[:, 2 * local : 3 * local],
        out_four[:, 3 * local :],
        out_output,
        out_both[:, :ff],
        out_both[:, ff:],
        out_down,
        grad_norm_gain,
        grad_ffn_gain,
        grad_head_gain,
        grad_gap,
    )


def solution(mesh):
    tokens = P("fsdp", "ctx", None)
    inward, outward = P("fsdp", "tp"), P("tp", "fsdp")
    grad_in, grad_back = P(("fsdp", "ctx"), "tp"), P("tp", ("fsdp", "ctx"))
    return jax.shard_map(
        per_device,
        mesh=mesh,
        in_specs=(tokens, P("fsdp")) + (inward,) * 4 + (outward, inward, inward, outward)
        + (P(), P(), P(), P("tp"), tokens),
        out_specs=(tokens, tokens) + (grad_in,) * 4 + (grad_back, grad_in, grad_in, grad_back)
        + (P(), P(), P(), P("tp")),
        check_vma=False,
    )
```

```python
import functools

import jax
import jax.numpy as jnp
from jax import lax
from jax.experimental import pallas as pl
from jax.experimental.pallas import tpu as pltpu
from jax.sharding import PartitionSpec as P

HEAD_DIM = 128
EPSILON = 1e-05
F32 = jnp.float32
BF16 = jnp.bfloat16
BY_AXIS = pl.DeviceIdType.MESH
VMEM_BYTES = 62 * 1024 * 1024
ANY = pl.BlockSpec(memory_space=pl.ANY)
WHOLE = pl.BlockSpec(memory_space=pltpu.VMEM)


def dot(left, right, dims=((1,), (0,))):
    return lax.dot_general(left, right, (dims, ((), ())), preferred_element_type=F32)


NT = ((1,), (1,))
TN = ((0,), (0,))


def sigmoid(value):
    return 1.0 / (1.0 + jnp.exp(-value))


def slope(pre, sig):
    return sig * (1.0 + pre * (1.0 - sig))


def ones_times(ones, value):
    high = value.astype(BF16)
    rest = (value - high.astype(F32)).astype(BF16)
    return dot(ones, high) + dot(ones, rest)


def ring_place(index, size, folded):
    if folded:
        return index + (index // 2) * (1 - 2 * (index % 2))
    return index


class RingGather:
    def __init__(self, shards, outs, where, sems, size, folded):
        self.shards, self.outs, self.where, self.size = shards, outs, where, size
        self.ring_send, self.ring_recv, self.pair_send, self.pair_recv, self.local = sems
        self.place = ring_place(lax.axis_index("fsdp"), size, folded)
        self.folded = folded
        self.core = lax.axis_index("ctx") % 2
        self.pair = lax.axis_index("ctx") + 1 - 2 * self.core

    def device(self, place):
        return ring_place(lax.rem(place + 2 * self.size, self.size), self.size, self.folded)

    def peers(self):
        return [
            {"fsdp": self.device(self.place + 1)},
            {"fsdp": self.device(self.place - 1)},
            {"ctx": self.pair},
        ]

    def rows(self, i, core, way):
        quarter = self.shards[i].shape[0] // 4
        return pl.multiple_of((2 * core + way) * quarter, 16), quarter

    def in_shard(self, i, core, way):
        at, length = self.rows(i, core, way)
        return self.shards[i].at[pl.ds(at, length), :]

    def in_out(self, i, block, core, way):
        out, dim, column = self.where[i]
        at, length = self.rows(i, core, way)
        deep, wide = self.shards[i].shape
        if dim == 0:
            start = pl.multiple_of(block * deep + at, 16)
            return self.outs[out].at[pl.ds(start, length), pl.ds(column, wide)]
        start = pl.multiple_of(block * wide, 128)
        return self.outs[out].at[pl.ds(at, length), pl.ds(start, wide)]

    def own_block(self, i):
        out, dim, column = self.where[i]
        deep, wide = self.shards[i].shape
        block = self.device(self.place)
        if dim == 0:
            start = pl.multiple_of(block * deep, 16)
            return self.outs[out].at[pl.ds(start, deep), pl.ds(column, wide)]
        return self.outs[out].at[:, pl.ds(pl.multiple_of(block * wide, 128), wide)]

    def local_copy(self, i):
        return pltpu.make_async_copy(self.shards[i], self.own_block(i), self.local.at[i])

    def ring(self, i, way, step):
        sign = 1 - 2 * way
        block = self.device(self.place - sign * step)
        there = self.in_out(i, block, self.core, way)
        here = self.in_shard(i, self.core, way) if step == 0 else there
        at = (i * 2 + way) * (self.size - 1) + step
        return pltpu.make_async_remote_copy(
            src_ref=here,
            dst_ref=there,
            send_sem=self.ring_send.at[at],
            recv_sem=self.ring_recv.at[at],
            device_id={"fsdp": self.device(self.place + sign)},
            device_id_type=BY_AXIS,
        )

    def across(self, i, way, step, core):
        sign = 1 - 2 * way
        block = self.device(self.place - sign * (step + 1))
        piece = self.in_out(i, block, core, way)
        at = (i * 2 + way) * (self.size - 1) + step
        return pltpu.make_async_remote_copy(
            src_ref=piece,
            dst_ref=piece,
            send_sem=self.pair_send.at[at],
            recv_sem=self.pair_recv.at[at],
            device_id={"ctx": self.pair},
            device_id_type=BY_AXIS,
        )

    def each(self):
        return [(i, way) for i in range(len(self.shards)) for way in range(2)]

    def start(self):
        for i, way in self.each():
            self.ring(i, way, 0).start()
        for i in range(len(self.shards)):
            self.local_copy(i).start()

    def advance(self, step):
        for i, way in self.each():
            arrived = self.ring(i, way, step)
            arrived.wait_recv()
            if step + 1 < self.size - 1:
                self.ring(i, way, step + 1).start()
            self.across(i, way, step, self.core).start()

    def finish(self):
        for i, way in self.each():
            for step in range(self.size - 1):
                self.ring(i, way, step).wait_send()
                self.across(i, way, step, self.core).wait_send()
                self.across(i, way, step, 1 - self.core).wait_recv()
        for i in range(len(self.shards)):
            self.local_copy(i).wait()

    @staticmethod
    def scratch(count, size):
        copies = count * 2 * (size - 1)
        return [pltpu.SemaphoreType.DMA((copies,)) for _ in range(4)] + [
            pltpu.SemaphoreType.DMA((count,))
        ]


class RingScatter:
    def __init__(self, grads, outs, dims, scratch, sems, size, folded):
        self.grads, self.outs, self.dims, self.size, self.folded = grads, outs, dims, size, folded
        count = len(grads)
        self.own, self.came, self.passed = scratch[:count], scratch[count : 2 * count], scratch[2 * count :]
        self.pair_send, self.pair_recv, self.local, self.ring_send, self.ring_recv = sems
        self.place = ring_place(lax.axis_index("fsdp"), size, folded)
        self.core = lax.axis_index("ctx")

    device = RingGather.device

    def peers(self):
        return [
            {"fsdp": self.device(self.place + 1)},
            {"fsdp": self.device(self.place - 1)},
            {"ctx": 1 - self.core},
        ]

    def block(self, i, offset, core):
        index = self.device(self.place + offset) * 2 + core
        extent = self.outs[i].shape[self.dims[i]]
        start = pl.multiple_of(index * extent, extent)
        if self.dims[i] == 0:
            return self.grads[i].at[pl.ds(start, extent), :]
        return self.grads[i].at[:, pl.ds(start, extent)]

    def local_copy(self, i, offset):
        return pltpu.make_async_copy(
            self.block(i, offset, self.core), self.own[i].at[offset], self.local.at[i * self.size + offset]
        )

    def across(self, i, offset):
        at = i * self.size + offset
        return pltpu.make_async_remote_copy(
            src_ref=self.block(i, offset, 1 - self.core),
            dst_ref=self.came[i].at[offset],
            send_sem=self.pair_send.at[at],
            recv_sem=self.pair_recv.at[at],
            device_id={"ctx": 1 - self.core},
            device_id_type=BY_AXIS,
        )

    def offset(self, way, step):
        return (-(step + 1) if way == 0 else step + 1) % self.size

    def ring(self, i, way, step):
        half = self.outs[i].shape[0] // 2
        at = (i * 2 + way) * (self.size - 1) + step
        return pltpu.make_async_remote_copy(
            src_ref=self.came[i].at[self.offset(way, step), pl.ds(way * half, half), :],
            dst_ref=self.passed[i].at[way, step],
            send_sem=self.ring_send.at[at],
            recv_sem=self.ring_recv.at[at],
            device_id={"fsdp": self.device(self.place + 1 - 2 * way)},
            device_id_type=BY_AXIS,
        )

    def order(self):
        used = []
        for step in range(self.size):
            for way in range(2):
                if self.offset(way, step) not in used:
                    used.append(self.offset(way, step))
        return used

    def start(self):
        for offset in self.order():
            for i in range(len(self.grads)):
                self.across(i, offset).start()
                self.local_copy(i, offset).start()

    def advance(self, step):
        before = {self.offset(way, s) for s in range(step) for way in range(2)}
        fresh = {self.offset(way, step) for way in range(2)} - before
        for i in range(len(self.grads)):
            for offset in sorted(fresh):
                self.across(i, offset).wait_recv()
                self.local_copy(i, offset).wait()
            for way in range(2):
                if step > 0:
                    self.ring(i, way, step - 1).wait_recv()
                self.add(i, way, step)
                if step < self.size - 1:
                    self.ring(i, way, step).start()

    def add(self, i, way, step):
        half = self.outs[i].shape[0] // 2
        offset = self.offset(way, step)
        own, came, passed, out = self.own[i], self.came[i], self.passed[i], self.outs[i]

        @pl.loop(0, half // 16)
        def _(r):
            rows = pl.ds(pl.multiple_of(way * half + r * 16, 16), 16)
            total = own[offset, rows, :].astype(F32) + came[offset, rows, :].astype(F32)
            if step > 0:
                total += passed[way, step - 1, pl.ds(pl.multiple_of(r * 16, 16), 16), :].astype(F32)
            if step < self.size - 1:
                came[offset, rows, :] = total.astype(BF16)
            else:
                out[rows, :] = total

    def finish(self):
        for i in range(len(self.grads)):
            for offset in range(self.size):
                self.across(i, offset).wait_send()
            for way in range(2):
                for step in range(self.size - 1):
                    self.ring(i, way, step).wait_send()

    @staticmethod
    def out_shape(grad, dim, size):
        deep, wide = grad.shape
        return (deep // (2 * size), wide) if dim == 0 else (deep, wide // (2 * size))

    @staticmethod
    def buffers(shapes, size):
        full = [pltpu.VMEM((size,) + s, BF16) for s in shapes]
        return full + full + [pltpu.VMEM((2, size - 1, s[0] // 2, s[1]), BF16) for s in shapes]

    @staticmethod
    def scratch(count, size):
        return [pltpu.SemaphoreType.DMA((count * size,)) for _ in range(3)] + [
            pltpu.SemaphoreType.DMA((count * 2 * (size - 1),)) for _ in range(2)
        ]


def meet(peers):
    barrier = pltpu.get_barrier_semaphore()
    total = 0
    for condition, peer in peers:
        if condition is None:
            pl.semaphore_signal(barrier, inc=1, device_id=peer, device_id_type=BY_AXIS)
            total = total + 1
        else:

            @pl.when(condition)
            def _():
                pl.semaphore_signal(barrier, inc=1, device_id=peer, device_id_type=BY_AXIS)

            total = total + condition.astype(jnp.int32)
    pl.semaphore_wait(barrier, total)


def gather_weights(shards, out_shapes, where, collective_id):
    size = lax.axis_size("fsdp")
    folded = size == 4
    count = len(shards)

    def kernel(*refs):
        ins, outs, sems = refs[:count], refs[count : count + len(out_shapes)], refs[-5:]
        job = RingGather(ins, outs, where, sems, size, folded)
        meet([(None, peer) for peer in job.peers()])
        job.start()
        for step in range(size - 1):
            job.advance(step)
        job.finish()

    return pl.pallas_call(
        kernel,
        out_shape=[jax.ShapeDtypeStruct(s, BF16) for s in out_shapes],
        in_specs=[WHOLE] * count,
        out_specs=[ANY] * len(out_shapes),
        scratch_shapes=RingGather.scratch(count, size),
        compiler_params=pltpu.CompilerParams(
            collective_id=collective_id, has_side_effects=True, vmem_limit_bytes=VMEM_BYTES
        ),
        name="gather_weights",
    )(*shards)


def line_sum(name, part, extras, extra_outs, epilogue, collective_id, chunk=32, skew=2, gather=None, scatter=None):
    size = lax.axis_size("tp")
    rows, width = part.shape
    half = rows // 2
    chunk = min(chunk, half)
    count = half // chunk
    n_extra, n_extra_out = len(extras), len(extra_outs)
    if gather is None:
        shards, gathered, where = [], [], []
    else:
        shards, gathered, where = gather
    n_shards, n_gathered = len(shards), len(gathered)
    grads, dims = scatter or ([], [])
    n_grads = len(grads)
    fsdp_size = lax.axis_size("fsdp")
    scattered = [RingScatter.out_shape(g, d, fsdp_size) for g, d in zip(grads, dims)]

    def kernel(*refs):
        refs = list(refs)

        def take(n):
            taken = refs[:n]
            del refs[:n]
            return taken

        (part_ref,) = take(1)
        extra_refs = take(n_extra)
        shard_refs = take(n_shards)
        grad_refs = take(n_grads)
        (out_ref,) = take(1)
        extra_out_refs = take(n_extra_out)
        gathered_refs = take(n_gathered)
        scattered_refs = take(n_grads)
        came, gone, sum_send, sum_recv, back_send, back_recv = take(6)
        place = lax.axis_index("tp")
        first, last = place == 0, place == size - 1
        peers = [(jnp.logical_not(first), {"tp": place - 1}), (jnp.logical_not(last), {"tp": place + 1})]
        job = None
        if n_shards:
            job = RingGather(shard_refs, gathered_refs, where, take(5), fsdp_size, fsdp_size == 4)
            peers += [(None, peer) for peer in job.peers()]
        if n_grads:
            buffers = take(3 * n_grads)
            job = RingScatter(
                grad_refs, scattered_refs, dims, buffers, take(5), fsdp_size, fsdp_size == 4
            )
            peers += [(None, peer) for peer in job.peers()]
        meet(peers)

        source = (first, last)
        owner = (last, first)
        ahead = (place + 1, place - 1)
        behind = (place - 1, place + 1)

        def at(way, k):
            start = k * chunk + (half if way == 0 else 0)
            return pl.ds(pl.multiple_of(start, chunk), chunk)

        def onward(way, k, from_part):
            source_ref = part_ref.at[at(way, k), :] if from_part else gone.at[way, k]
            return pltpu.make_async_remote_copy(
                src_ref=source_ref,
                dst_ref=came.at[way, k],
                send_sem=sum_send.at[way, k],
                recv_sem=sum_recv.at[way, k],
                device_id={"tp": ahead[way]},
                device_id_type=BY_AXIS,
            )

        def back(way, k):
            piece = out_ref.at[at(way, k), :]
            return pltpu.make_async_remote_copy(
                src_ref=piece,
                dst_ref=piece,
                send_sem=back_send.at[way, k],
                recv_sem=back_recv.at[way, k],
                device_id={"tp": behind[way]},
                device_id_type=BY_AXIS,
            )

        for way in range(2):

            @pl.when(source[way])
            def _():
                @pl.loop(0, count)
                def _(k):
                    onward(way, k, True).start()

        if job is not None:
            job.start()

        away = (place - 1, size - 2 - place)

        def each_way(step, lead, act):
            for way in range(2):
                k = step - skew * lead[way]

                @pl.when(jnp.logical_and(k >= 0, k < count))
                def _():
                    act(way, k)

        def add(way, k):
            @pl.when(jnp.logical_not(source[way]))
            def _():
                onward(way, k, False).wait_recv()
                total = came[way, k].astype(F32) + part_ref[at(way, k), :].astype(F32)

                @pl.when(owner[way])
                def _():
                    start = pl.multiple_of(k * chunk, chunk)
                    out_ref[at(way, k), :] = epilogue(
                        extra_refs, extra_out_refs, at(way, k), pl.ds(start, chunk), total
                    )
                    back(way, k).start()

                @pl.when(jnp.logical_not(owner[way]))
                def _():
                    gone[way, k] = total.astype(BF16)
                    onward(way, k, False).start()

        def spread(way, k):
            @pl.when(jnp.logical_not(owner[way]))
            def _():
                back(way, k).wait_recv()

                @pl.when(jnp.logical_not(source[way]))
                def _():
                    back(way, k).start()

        steps = count + skew * (size - 2)
        phases = [(add, away), (spread, (away[1], away[0]))]
        cuts = []
        if n_shards:
            cuts = [((2 * steps - 2) * (i + 1)) // fsdp_size for i in range(fsdp_size - 1)]
        if n_grads:
            first_cut, last_cut = (2 * steps) // 5, 2 * steps - 2
            cuts = [first_cut + ((last_cut - first_cut) * i) // (fsdp_size - 1) for i in range(fsdp_size)]
        for number, (act, lead) in enumerate(phases):
            low, high = number * steps, (number + 1) * steps
            edges = [low] + [c for c in cuts if low < c < high] + [high]
            for left, right in zip(edges[:-1], edges[1:]):
                if left in cuts:
                    job.advance(cuts.index(left))

                @pl.loop(left - low, right - low)
                def _(step):
                    each_way(step, lead, act)

        if job is not None:
            job.finish()

        for way in range(2):

            @pl.when(jnp.logical_not(owner[way]))
            def _():
                @pl.loop(0, count)
                def _(k):
                    onward(way, k, False).wait_send()

            @pl.when(jnp.logical_not(source[way]))
            def _():
                @pl.loop(0, count)
                def _(k):
                    back(way, k).wait_send()

    scratch = [
        pltpu.VMEM((2, count, chunk, width), BF16),
        pltpu.VMEM((2, count, chunk, width), BF16),
    ] + [pltpu.SemaphoreType.DMA((2, count)) for _ in range(4)]
    if n_shards:
        scratch += RingGather.scratch(n_shards, fsdp_size)
    if n_grads:
        scratch += RingScatter.buffers(scattered, fsdp_size) + RingScatter.scratch(n_grads, fsdp_size)
    return pl.pallas_call(
        kernel,
        out_shape=[jax.ShapeDtypeStruct((rows, width), BF16)]
        + [jax.ShapeDtypeStruct(s, d) for s, d in extra_outs]
        + [jax.ShapeDtypeStruct(s, BF16) for s in gathered]
        + [jax.ShapeDtypeStruct(s, F32) for s in scattered],
        in_specs=[WHOLE] * (1 + n_extra + n_shards) + [ANY] * n_grads,
        out_specs=[WHOLE] * (1 + n_extra_out) + [ANY] * n_gathered + [WHOLE] * n_grads,
        scratch_shapes=scratch,
        compiler_params=pltpu.CompilerParams(
            collective_id=collective_id, has_side_effects=True, vmem_limit_bytes=VMEM_BYTES
        ),
        name=name,
    )(part, *extras, *shards, *grads)


def small_sum(vector, collective_id):
    length = vector.shape[0]
    rows = -(-length // 1024) * 8
    block = jnp.pad(vector, (0, rows * 128 - length)).reshape(rows, 128)
    axes = [(axis, lax.axis_size(axis)) for axis in ("ctx", "fsdp", "tp")]

    def kernel(in_ref, out_ref, *scratch):
        slots, sends, recvs = scratch[:3], scratch[3:6], scratch[6:9]
        meet(
            [
                (None, {axis: lax.rem(lax.axis_index(axis) + step, size)})
                for axis, size in axes
                for step in range(1, size)
            ]
        )
        total = in_ref[...]
        for number, (axis, size) in enumerate(axes):
            mine = lax.axis_index(axis)
            slot = slots[number]
            slot[mine] = total
            copies = [
                pltpu.make_async_remote_copy(
                    src_ref=slot.at[mine],
                    dst_ref=slot.at[mine],
                    send_sem=sends[number].at[step - 1],
                    recv_sem=recvs[number].at[step - 1],
                    device_id={axis: lax.rem(mine + step, size)},
                    device_id_type=BY_AXIS,
                )
                for step in range(1, size)
            ]
            for copy in copies:
                copy.start()
            for copy in copies:
                copy.wait_recv()
            total = slot[0]
            for k in range(1, size):
                total = total + slot[k]
            for copy in copies:
                copy.wait_send()
        out_ref[...] = total

    summed = pl.pallas_call(
        kernel,
        out_shape=jax.ShapeDtypeStruct((rows, 128), F32),
        in_specs=[WHOLE],
        out_specs=WHOLE,
        scratch_shapes=[pltpu.VMEM((size, rows, 128), F32) for _, size in axes]
        + [pltpu.SemaphoreType.DMA((size - 1,)) for _, size in axes] * 2,
        compiler_params=pltpu.CompilerParams(collective_id=collective_id, has_side_effects=True),
        name="small_sum",
    )(block)
    return summed.reshape(-1)[:length]


def rms(value):
    return lax.rsqrt(jnp.mean(value * value, axis=-1, keepdims=True) + EPSILON)


def middle_rows(extra, extra_out, rows, own, total):
    x_ref, gain_ref = extra
    middle = x_ref[rows, :].astype(F32) + total
    extra_out[0][own, :] = middle
    return (middle * rms(middle) * gain_ref[...]).astype(BF16)


def norm_back(grad, value, gain):
    inverse = rms(value)
    scaled = value * inverse
    weighted = grad * gain
    back = inverse * (weighted - scaled * jnp.mean(weighted * scaled, axis=-1, keepdims=True))
    return back, jnp.sum(grad * scaled, axis=0, keepdims=True)


def grad_middle_rows(extra, extra_out, rows, own, total):
    middle_ref, grad_out_ref, gain_ref = extra
    back, gain_part = norm_back(total, middle_ref[own, :], gain_ref[...])
    grad_middle = grad_out_ref[rows, :].astype(F32) + back
    extra_out[0][own, :] = grad_middle
    add_rows(extra_out[1], own, gain_part)
    return grad_middle.astype(BF16)


def input_grad_rows(extra, extra_out, rows, own, total):
    x_ref, grad_middle_ref, gain_ref = extra
    back, gain_part = norm_back(total, x_ref[rows, :].astype(F32), gain_ref[...])
    add_rows(extra_out[0], own, gain_part)
    return (grad_middle_ref[own, :] + back).astype(BF16)


def add_rows(sum_ref, own, term):
    sum_ref[pl.ds(own.start // own.size, 1), :] = term


def lower_ones(length):
    at = lax.broadcasted_iota(jnp.int32, (length, length), 0)
    before = lax.broadcasted_iota(jnp.int32, (length, length), 1)
    return at >= before


def chunk_decay(forget, gap, live, lower):
    closing = sigmoid(-forget)
    opened = gap * closing
    remain = 1.0 - opened
    decay = jnp.where(live, jnp.log(remain), 0.0)
    keys = jnp.where(live, opened, 0.0)
    return closing, remain, keys, ones_times(lower, decay)


def rows_live(valid_ref, chunk_index, length):
    at = lax.broadcasted_iota(jnp.int32, (length, HEAD_DIM), 0) + chunk_index * length
    return at < valid_ref[0]


def span_end_kernel(heads, length, valid_ref, forget_ref, value_ref, gap_ref, end_ref):
    index = pl.program_id(0)

    @pl.when(index == 0)
    def _():
        end_ref[...] = jnp.zeros_like(end_ref)

    live = rows_live(valid_ref, index, length)
    lower = lower_ones(length).astype(BF16)
    for h in range(heads):
        cols = slice(h * HEAD_DIM, (h + 1) * HEAD_DIM)
        _, _, keys, cumulative = chunk_decay(forget_ref[:, cols], gap_ref[:, cols], live, lower)
        total = cumulative[length - 1 :, :]
        tail = (keys * jnp.exp(total - cumulative)).astype(BF16)
        end_ref[h] = jnp.exp(total) * end_ref[h] + dot(value_ref[:, cols].astype(BF16), tail, TN)


def mix_kernel(
    heads, length, valid_ref, query_ref, forget_ref, value_ref, gate_ref, gap_ref, gain_ref, start_ref,
    gated_ref, mixed_ref, states_ref, state_ref,
):
    index = pl.program_id(0)

    @pl.when(index == 0)
    def _():
        state_ref[...] = start_ref[...]

    live = rows_live(valid_ref, index, length)
    mask = lower_ones(length)
    lower = mask.astype(BF16)
    for h in range(heads):
        cols = slice(h * HEAD_DIM, (h + 1) * HEAD_DIM)
        _, _, keys, cumulative = chunk_decay(forget_ref[:, cols], gap_ref[:, cols], live, lower)
        pre = query_ref[:, cols]
        queries = (pre * sigmoid(pre) * jnp.exp(cumulative)).astype(BF16)
        shrunk = keys * jnp.exp(-cumulative)
        values = value_ref[:, cols].astype(BF16)
        state = state_ref[h]
        states_ref[0, h] = state
        scores = jnp.where(mask, dot(queries, shrunk.astype(BF16), NT), 0.0).astype(BF16)
        mixed = dot(scores, values) + dot(queries, state.astype(BF16), NT)
        mixed_ref[:, cols] = mixed
        growth = jnp.exp(cumulative[length - 1 :, :])
        state_ref[h] = growth * state + dot(values, (shrunk * growth).astype(BF16), TN)
        gate = gate_ref[:, cols]
        gated_ref[:, cols] = (mixed * rms(mixed) * gain_ref[...] * (gate * sigmoid(gate))).astype(BF16)


def span_begin_kernel(
    heads, length, valid_ref, grad_ref, mixed_ref, query_ref, forget_ref, gate_ref, gap_ref, gain_ref,
    grad_gate_ref, grad_mixed_ref, gain_part_ref, begin_ref,
):
    step = pl.program_id(0)
    index = pl.num_programs(0) - 1 - step

    @pl.when(step == 0)
    def _():
        begin_ref[...] = jnp.zeros_like(begin_ref)
        gain_part_ref[...] = jnp.zeros_like(gain_part_ref)

    live = rows_live(valid_ref, index, length)
    lower = lower_ones(length).astype(BF16)
    gain = gain_ref[...]
    for h in range(heads):
        cols = slice(h * HEAD_DIM, (h + 1) * HEAD_DIM)
        mixed = mixed_ref[:, cols]
        inverse = rms(mixed)
        scaled = mixed * inverse
        gate = gate_ref[:, cols]
        sig = sigmoid(gate)
        grad = grad_ref[:, cols].astype(F32)
        grad_gate_ref[:, cols] = (grad * scaled * gain * slope(gate, sig)).astype(BF16)
        grad_scaled = grad * (gate * sig)
        gain_part_ref[...] += jnp.sum(grad_scaled * scaled, axis=0, keepdims=True)
        weighted = grad_scaled * gain
        grad_mixed = inverse * (weighted - scaled * jnp.mean(weighted * scaled, axis=-1, keepdims=True))
        grad_mixed = grad_mixed.astype(BF16)
        grad_mixed_ref[:, cols] = grad_mixed
        _, _, _, cumulative = chunk_decay(forget_ref[:, cols], gap_ref[:, cols], live, lower)
        pre = query_ref[:, cols]
        queries = (pre * sigmoid(pre) * jnp.exp(cumulative)).astype(BF16)
        growth = jnp.exp(cumulative[length - 1 :, :])
        begin_ref[h] = growth * begin_ref[h] + dot(grad_mixed, queries, TN)


def mix_back_kernel(
    heads, length, valid_ref, grad_ref, query_ref, forget_ref, value_ref, gap_ref, states_ref, last_ref, end_ref,
    grad_query_ref, grad_forget_ref, grad_value_ref, gap_part_ref, flow_ref, after_ref,
):
    step = pl.program_id(0)
    index = pl.num_programs(0) - 1 - step

    @pl.when(step == 0)
    def _():
        flow_ref[...] = end_ref[...]
        after_ref[...] = last_ref[...]
        gap_part_ref[...] = jnp.zeros_like(gap_part_ref)

    live = rows_live(valid_ref, index, length)
    mask = lower_ones(length)
    lower = mask.astype(BF16)
    for h in range(heads):
        cols = slice(h * HEAD_DIM, (h + 1) * HEAD_DIM)
        gap = gap_ref[:, cols]
        closing, remain, keys, cumulative = chunk_decay(forget_ref[:, cols], gap, live, lower)
        pre = query_ref[:, cols]
        sig = sigmoid(pre)
        growth = jnp.exp(cumulative)
        shrink = jnp.exp(-cumulative)
        end_growth = growth[length - 1 :, :]
        queries = (pre * sig * growth).astype(BF16)
        shrunk_wide = keys * shrink
        shrunk = shrunk_wide.astype(BF16)
        tail = (shrunk_wide * end_growth).astype(BF16)
        values = value_ref[:, cols].astype(BF16)
        grad = grad_ref[:, cols]
        state = states_ref[0, h]
        flow = flow_ref[h]
        low_flow = flow.astype(BF16)
        scores = jnp.where(mask, dot(queries, shrunk, NT), 0.0).astype(BF16)
        grad_scores = jnp.where(mask, dot(grad, values, NT), 0.0).astype(BF16)
        to_queries = dot(grad, state.astype(BF16)) + dot(grad_scores, shrunk)
        to_keys = dot(grad_scores, queries, TN) + end_growth * dot(values, low_flow)
        grad_value_ref[:, cols] = (dot(scores, grad, TN) + dot(tail, low_flow, NT)).astype(BF16)
        grad_query_ref[:, cols] = (to_queries * growth * slope(pre, sig)).astype(BF16)
        terms = queries.astype(F32) * to_queries - shrunk.astype(F32) * to_keys
        high = terms.astype(BF16)
        rest = (terms - high.astype(F32)).astype(BF16)
        suffix = dot(lower, high, TN) + dot(lower, rest, TN)
        crossing = jnp.sum(flow * after_ref[h], axis=0, keepdims=True)
        pressure = jnp.where(live, to_keys * shrink - (suffix + crossing) / remain, 0.0)
        gap_part_ref[:, cols] += jnp.sum(closing * pressure, axis=0, keepdims=True)
        grad_forget_ref[:, cols] = (-closing * (1.0 - closing) * gap * pressure).astype(BF16)
        flow_ref[h] = end_growth * flow + dot(grad, queries, TN)
        after_ref[h] = state


def plain_call(kernel, name, grid, in_specs, out_specs, out_shape, scratch, flops, moved):
    return pl.pallas_call(
        kernel,
        grid_spec=pltpu.PrefetchScalarGridSpec(
            num_scalar_prefetch=1, grid=grid, in_specs=in_specs, out_specs=out_specs, scratch_shapes=scratch
        ),
        out_shape=out_shape,
        compiler_params=pltpu.CompilerParams(
            dimension_semantics=("arbitrary",), vmem_limit_bytes=VMEM_BYTES
        ),
        cost_estimate=pl.CostEstimate(flops=flops, bytes_accessed=moved, transcendentals=flops // 64),
        name=name,
    )


def combine(earlier, later):
    return (earlier[0] * later[0], later[0][:, None, :] * earlier[1] + later[1])


def from_earlier(state, decay, axis):
    size = lax.axis_size(axis)
    if size == 2:
        return lax.ppermute(state, axis, [(0, 1)])
    mine = lax.axis_index(axis)
    states, decays = lax.all_gather(state, axis), lax.all_gather(decay, axis)
    total = jnp.zeros_like(state)
    for k in range(size):
        new = decays[k][:, None, :] * total + states[k]
        total = jnp.where(k < mine, new, total)
    return total


def from_later(state, decay, axis):
    size = lax.axis_size(axis)
    if size == 2:
        return lax.ppermute(state, axis, [(1, 0)])
    mine = lax.axis_index(axis)
    states, decays = lax.all_gather(state, axis), lax.all_gather(decay, axis)
    total = jnp.zeros_like(state)
    for k in reversed(range(size)):
        new = decays[k][:, None, :] * total + states[k]
        total = jnp.where(k > mine, new, total)
    return total


def per_device(
    inputs, lengths, w_query, w_forget, w_input, w_outgate, w_output, w_gate, w_up, w_down,
    norm_gain, ffn_gain, head_gain, forget_gap, cotangent,
):
    groups, span, width = inputs.shape
    rows = groups * span
    fsdp, ctx, tp = lax.axis_size("fsdp"), lax.axis_size("ctx"), lax.axis_size("tp")
    local = forget_gap.shape[0]
    heads = local // HEAD_DIM
    ff = w_gate.shape[1]
    length = min(128, span)
    chunks = span // length
    place = lax.axis_index("tp")
    half = rows // 2

    valid = jnp.clip(lengths - lax.axis_index("ctx") * span, 0, span).astype(jnp.int32)
    keep = (jnp.arange(rows, dtype=jnp.int32) < valid[0])[:, None]
    x = inputs.reshape(rows, width)
    grad_low = jnp.where(keep, cotangent.reshape(rows, width), jnp.zeros((), BF16))
    gap = forget_gap.reshape(1, local)
    head_row = head_gain.reshape(1, HEAD_DIM)

    w_four, w_out = gather_weights(
        [w_query, w_forget, w_input, w_outgate, w_output],
        [(fsdp * w_query.shape[0], 4 * local), (local, width)],
        [(0, 0, 0), (0, 0, local), (0, 0, 2 * local), (0, 0, 3 * local), (1, 1, 0)],
        1,
    )

    wide = x.astype(F32)
    normed = (wide * rms(wide) * norm_gain).astype(BF16)
    pre = dot(normed, w_four)

    def column(j):
        return pl.BlockSpec((length, local), lambda i, *_: (i, j))

    def column_back(j):
        return pl.BlockSpec((length, local), lambda i, *_: (chunks - 1 - i, j))

    fixed = lambda shape: pl.BlockSpec(shape, lambda i, *_: (0,) * len(shape))
    state_shape = (heads, HEAD_DIM, HEAD_DIM)
    work = 2 * rows * local * HEAD_DIM
    moved = rows * local * 4

    local_end = plain_call(
        functools.partial(span_end_kernel, heads, length), "span_end", (chunks,),
        [column(1), column(2), fixed((1, local))], fixed(state_shape),
        jax.ShapeDtypeStruct(state_shape, F32), [], 3 * work, 2 * moved,
    )(valid, pre, pre, gap)
    span_decay = None
    if ctx > 2:
        keep_rows = keep.astype(F32)
        closing = jax.nn.sigmoid(-pre[:, local : 2 * local])
        logs = jnp.log(1.0 - gap * closing) * keep_rows
        span_decay = jnp.exp(jnp.sum(logs, axis=0)).reshape(heads, HEAD_DIM)
    start = from_earlier(local_end, span_decay, "ctx")
    gated, mixed, states = plain_call(
        functools.partial(mix_kernel, heads, length), "mix", (chunks,),
        [column(0), column(1), column(2), column(3), fixed((1, local)), fixed((1, HEAD_DIM)), fixed(state_shape)],
        [column(0), column(0), pl.BlockSpec((1,) + state_shape, lambda i, *_: (i, 0, 0, 0))],
        [
            jax.ShapeDtypeStruct((rows, local), BF16),
            jax.ShapeDtypeStruct((rows, local), F32),
            jax.ShapeDtypeStruct((chunks,) + state_shape, F32),
        ],
        [pltpu.VMEM(state_shape, F32)], 6 * work, 6 * moved,
    )(valid, pre, pre, pre, pre, gap, head_row, start)
    if ctx == 2:
        keep_rows = keep.astype(F32)
        closing = jax.nn.sigmoid(-pre[:, local : 2 * local])
        logs = jnp.log(1.0 - gap * closing) * keep_rows
        span_decay = jnp.exp(jnp.sum(logs, axis=0)).reshape(heads, HEAD_DIM)
    state_end = local_end + span_decay[:, None, :] * start

    branch = dot(gated, w_out).astype(BF16)
    normed_two, middle, w_both, w_back = line_sum(
        "sum_branch", branch, [x, ffn_gain.reshape(1, width)], [((half, width), F32)], middle_rows, 2,
        gather=(
            [w_gate, w_up, w_down],
            [(fsdp * w_gate.shape[0], 2 * ff), (ff, width)],
            [(0, 0, 0), (0, 0, ff), (1, 1, 0)],
        ),
    )

    both = dot(normed_two, w_both)
    gate_hidden, up_hidden = both[:, :ff], both[:, ff:]
    sig = jax.nn.sigmoid(gate_hidden)
    act = gate_hidden * sig
    hidden = (act * up_hidden).astype(BF16)
    mine = jnp.concatenate(
        [jnp.where(place == 0, middle, 0.0), jnp.where(place == tp - 1, middle, 0.0)], axis=0
    )
    feed = (dot(hidden, w_back) + mine).astype(BF16)
    result = lax.psum(feed, "tp").reshape(groups, span, width)

    grad_hidden = dot(grad_low, w_back, NT)
    grad_gate = (grad_hidden * up_hidden * slope(gate_hidden, sig)).astype(BF16)
    grad_up = (grad_hidden * act).astype(BF16)
    grad_both = jnp.concatenate([grad_gate, grad_up], axis=1)
    part_two = dot(grad_both, w_both, NT).astype(BF16)
    grad_w_down = dot(hidden, grad_low, TN).astype(BF16)
    grad_w_both = dot(normed_two, grad_both, TN).astype(BF16)
    both_axes = ("fsdp", "ctx")

    def scattered(grads, dims):
        if ctx == 2:
            return (grads, dims), None
        return None, [
            lax.psum_scatter(g, both_axes, scatter_dimension=d, tiled=True).astype(F32) for g, d in zip(grads, dims)
        ]

    job, sums_ffn = scattered([grad_w_both, grad_w_down], [0, 1])
    grad_branch, grad_middle, ffn_gain_part, *more = line_sum(
        "sum_norm_two", part_two, [middle, grad_low, ffn_gain.reshape(1, width)],
        [((half, width), F32), ((half // min(32, half), width), F32)], grad_middle_rows, 3, scatter=job,
    )
    out_both, out_down = sums_ffn or more

    grad_gated = dot(grad_branch, w_out, NT)
    grad_outgate, grad_mixed, head_part, local_begin = plain_call(
        functools.partial(span_begin_kernel, heads, length), "span_begin", (chunks,),
        [column_back(0), column_back(0), column_back(0), column_back(1), column_back(3), fixed((1, local)),
         fixed((1, HEAD_DIM))],
        [column_back(0), column_back(0), fixed((1, HEAD_DIM)), fixed(state_shape)],
        [
            jax.ShapeDtypeStruct((rows, local), BF16),
            jax.ShapeDtypeStruct((rows, local), BF16),
            jax.ShapeDtypeStruct((1, HEAD_DIM), F32),
            jax.ShapeDtypeStruct(state_shape, F32),
        ],
        [], 3 * work, 6 * moved,
    )(valid, grad_gated, mixed, pre, pre, pre, gap, head_row)
    grad_end = from_later(local_begin, span_decay, "ctx")
    grad_query, grad_forget, grad_value, gap_part = plain_call(
        functools.partial(mix_back_kernel, heads, length), "mix_back", (chunks,),
        [column_back(0), column_back(0), column_back(1), column_back(2), fixed((1, local)),
         pl.BlockSpec((1,) + state_shape, lambda i, *_: (chunks - 1 - i, 0, 0, 0)), fixed(state_shape),
         fixed(state_shape)],
        [column_back(0), column_back(0), column_back(0), fixed((1, local))],
        [jax.ShapeDtypeStruct((rows, local), BF16)] * 3 + [jax.ShapeDtypeStruct((1, local), F32)],
        [pltpu.VMEM(state_shape, F32), pltpu.VMEM(state_shape, F32)], 12 * work, 6 * moved,
    )(valid, grad_mixed, pre, pre, pre, gap, states, state_end, grad_end)

    grad_four = jnp.concatenate([grad_query, grad_forget, grad_value, grad_outgate], axis=1)
    part_one = dot(grad_four, w_four, NT).astype(BF16)
    grad_w_output = dot(gated, grad_branch, TN).astype(BF16)
    grad_w_four = dot(normed, grad_four, TN).astype(BF16)
    job, sums_mix = scattered([grad_w_four, grad_w_output], [0, 1])
    input_grad, norm_gain_part, *more = line_sum(
        "sum_norm_one", part_one, [x, grad_middle, norm_gain.reshape(1, width)],
        [((half // min(32, half), width), F32)], input_grad_rows, 4, scatter=job,
    )
    out_four, out_output = sums_mix or more
    input_grad = input_grad.reshape(groups, span, width)

    owner = jnp.logical_or(place == 0, place == tp - 1)
    sums = jnp.concatenate(
        [
            jnp.where(owner, jnp.sum(norm_gain_part, axis=0), 0.0),
            jnp.where(owner, jnp.sum(ffn_gain_part, axis=0), 0.0),
            head_part[0],
            lax.dynamic_update_slice(jnp.zeros((tp * local,), F32), gap_part[0], (place * local,)),
        ]
    )
    sums = small_sum(sums, 5)
    grad_norm_gain, grad_ffn_gain = sums[:width], sums[width : 2 * width]
    grad_head_gain = sums[2 * width : 2 * width + HEAD_DIM]
    grad_gap = lax.dynamic_slice(sums, (2 * width + HEAD_DIM + place * local,), (local,))
    return (
        result,
        input_grad,
        out_four[:, :local],
        out_four[:, local : 2 * local],
        out_four[:, 2 * local : 3 * local],
        out_four[:, 3 * local :],
        out_output,
        out_both[:, :ff],
        out_both[:, ff:],
        out_down,
        grad_norm_gain,
        grad_ffn_gain,
        grad_head_gain,
        grad_gap,
    )


def solution(mesh):
    tokens = P("fsdp", "ctx", None)
    inward, outward = P("fsdp", "tp"), P("tp", "fsdp")
    grad_in, grad_back = P(("fsdp", "ctx"), "tp"), P("tp", ("fsdp", "ctx"))
    return jax.shard_map(
        per_device,
        mesh=mesh,
        in_specs=(tokens, P("fsdp")) + (inward,) * 4 + (outward, inward, inward, outward)
        + (P(), P(), P(), P("tp"), tokens),
        out_specs=(tokens, tokens) + (grad_in,) * 4 + (grad_back, grad_in, grad_in, grad_back)
        + (P(), P(), P(), P("tp")),
        check_vma=False,
    )
```

```python
import functools

import jax
import jax.numpy as jnp
from jax import lax
from jax.experimental import pallas as pl
from jax.experimental.pallas import tpu as pltpu
from jax.sharding import PartitionSpec as P

HEAD_DIM = 128
EPSILON = 1e-05
F32 = jnp.float32
BF16 = jnp.bfloat16
BY_AXIS = pl.DeviceIdType.MESH
VMEM_BYTES = 67043328
ANY = pl.BlockSpec(memory_space=pl.ANY)
WHOLE = pl.BlockSpec(memory_space=pltpu.VMEM)


def dot(left, right, dims=((1,), (0,))):
    return lax.dot_general(left, right, (dims, ((), ())), preferred_element_type=F32)


NN = ((1,), (0,))
NT = ((1,), (1,))
TN = ((0,), (0,))


def sigmoid(value):
    return 1.0 / (1.0 + jnp.exp(-value))


def slope(pre, sig):
    return sig * (1.0 + pre * (1.0 - sig))


def ones_times(ones, value):
    high = value.astype(BF16)
    rest = (value - high.astype(F32)).astype(BF16)
    return dot(ones, high) + dot(ones, rest)


def ring_place(index, size, folded):
    if folded:
        return index + (index // 2) * (1 - 2 * (index % 2))
    return index


class RingGather:
    def __init__(self, shards, outs, where, sems, size, folded):
        self.shards, self.outs, self.where, self.size = shards, outs, where, size
        self.ring_send, self.ring_recv, self.pair_send, self.pair_recv, self.local = sems
        self.place = ring_place(lax.axis_index("fsdp"), size, folded)
        self.folded = folded
        self.core = lax.axis_index("ctx") % 2
        self.pair = lax.axis_index("ctx") + 1 - 2 * self.core

    def device(self, place):
        return ring_place(lax.rem(place + 2 * self.size, self.size), self.size, self.folded)

    def peers(self):
        return [
            {"fsdp": self.device(self.place + 1)},
            {"fsdp": self.device(self.place - 1)},
            {"ctx": self.pair},
        ]

    def rows(self, i, core, way):
        quarter = self.shards[i].shape[0] // 4
        return pl.multiple_of((2 * way + core) * quarter, 16), quarter

    def in_shard(self, i, core, way):
        at, length = self.rows(i, core, way)
        return self.shards[i].at[pl.ds(at, length), :]

    def in_out(self, i, block, core, way):
        out, dim, column = self.where[i]
        at, length = self.rows(i, core, way)
        deep, wide = self.shards[i].shape
        if dim == 0:
            start = pl.multiple_of(block * deep + at, 16)
            return self.outs[out].at[pl.ds(start, length), pl.ds(column, wide)]
        start = pl.multiple_of(block * wide, 128)
        return self.outs[out].at[pl.ds(at, length), pl.ds(start, wide)]

    def own_block(self, i):
        out, dim, column = self.where[i]
        deep, wide = self.shards[i].shape
        block = self.device(self.place)
        if dim == 0:
            start = pl.multiple_of(block * deep, 16)
            return self.outs[out].at[pl.ds(start, deep), pl.ds(column, wide)]
        return self.outs[out].at[:, pl.ds(pl.multiple_of(block * wide, 128), wide)]

    def local_copy(self, i):
        return pltpu.make_async_copy(self.shards[i], self.own_block(i), self.local.at[i])

    def ring(self, i, way, step):
        sign = 1 - 2 * way
        block = self.device(self.place - sign * step)
        there = self.in_out(i, block, self.core, way)
        here = self.in_shard(i, self.core, way) if step == 0 else there
        at = (i * 2 + way) * (self.size - 1) + step
        return pltpu.make_async_remote_copy(
            src_ref=here,
            dst_ref=there,
            send_sem=self.ring_send.at[at],
            recv_sem=self.ring_recv.at[at],
            device_id={"fsdp": self.device(self.place + sign)},
            device_id_type=BY_AXIS,
        )

    def across(self, i, way, step, core):
        sign = 1 - 2 * way
        block = self.device(self.place - sign * (step + 1))
        piece = self.in_out(i, block, core, way)
        at = (i * 2 + way) * (self.size - 1) + step
        return pltpu.make_async_remote_copy(
            src_ref=piece,
            dst_ref=piece,
            send_sem=self.pair_send.at[at],
            recv_sem=self.pair_recv.at[at],
            device_id={"ctx": self.pair},
            device_id_type=BY_AXIS,
        )

    def each(self):
        return [(i, way) for i in range(len(self.shards)) for way in range(2)]

    def start(self):
        for i, way in self.each():
            self.ring(i, way, 0).start()
        for i in range(len(self.shards)):
            self.local_copy(i).start()

    def advance(self, step):
        for i, way in self.each():
            arrived = self.ring(i, way, step)
            arrived.wait_recv()
            if step + 1 < self.size - 1:
                self.ring(i, way, step + 1).start()
            self.across(i, way, step, self.core).start()

    def wait_across(self, arrays, step):
        for i in arrays:
            for way in range(2):
                self.across(i, way, step, 1 - self.core).wait_recv()

    def finish(self, waited=()):
        for i, way in self.each():
            for step in range(self.size - 1):
                self.ring(i, way, step).wait_send()
                self.across(i, way, step, self.core).wait_send()
                if i not in waited:
                    self.across(i, way, step, 1 - self.core).wait_recv()
        for i in range(len(self.shards)):
            if i not in waited:
                self.local_copy(i).wait()

    @staticmethod
    def scratch(count, size):
        copies = count * 2 * (size - 1)
        return [pltpu.SemaphoreType.DMA((copies,)) for _ in range(4)] + [
            pltpu.SemaphoreType.DMA((count,))
        ]


class RingScatter:
    def __init__(self, grads, outs, dims, scratch, sems, size, folded):
        self.grads, self.outs, self.dims, self.size, self.folded = grads, outs, dims, size, folded
        count = len(grads)
        self.own, self.came, self.passed = scratch[:count], scratch[count : 2 * count], scratch[2 * count :]
        self.pair_send, self.pair_recv, self.local, self.ring_send, self.ring_recv = sems
        self.place = ring_place(lax.axis_index("fsdp"), size, folded)
        self.core = lax.axis_index("ctx")

    device = RingGather.device

    def peers(self):
        return [
            {"fsdp": self.device(self.place + 1)},
            {"fsdp": self.device(self.place - 1)},
            {"ctx": 1 - self.core},
        ]

    def block(self, i, offset, core):
        index = self.device(self.place + offset) * 2 + core
        extent = self.outs[i].shape[self.dims[i]]
        start = pl.multiple_of(index * extent, extent)
        if self.dims[i] == 0:
            return self.grads[i].at[pl.ds(start, extent), :]
        return self.grads[i].at[:, pl.ds(start, extent)]

    def local_copy(self, i, offset):
        return pltpu.make_async_copy(
            self.block(i, offset, self.core), self.own[i].at[offset], self.local.at[i * self.size + offset]
        )

    def across(self, i, offset):
        at = i * self.size + offset
        give = self.own[i].at[0, offset] if self.grads[i] is None else self.block(i, offset, 1 - self.core)
        return pltpu.make_async_remote_copy(
            src_ref=give,
            dst_ref=self.came[i].at[offset],
            send_sem=self.pair_send.at[at],
            recv_sem=self.pair_recv.at[at],
            device_id={"ctx": 1 - self.core},
            device_id_type=BY_AXIS,
        )

    def offset(self, way, step):
        return (-(step + 1) if way == 0 else step + 1) % self.size

    def ring(self, i, way, step):
        half = self.outs[i].shape[0] // 2
        at = (i * 2 + way) * (self.size - 1) + step
        return pltpu.make_async_remote_copy(
            src_ref=self.came[i].at[self.offset(way, step), pl.ds(way * half, half), :],
            dst_ref=self.passed[i].at[way, step],
            send_sem=self.ring_send.at[at],
            recv_sem=self.ring_recv.at[at],
            device_id={"fsdp": self.device(self.place + 1 - 2 * way)},
            device_id_type=BY_AXIS,
        )

    def order(self):
        used = []
        for step in range(self.size):
            for way in range(2):
                if self.offset(way, step) not in used:
                    used.append(self.offset(way, step))
        return used

    def start(self):
        for offset in self.order():
            for i in range(len(self.grads)):
                self.across(i, offset).start()
                self.local_copy(i, offset).start()

    def advance(self, step):
        before = {self.offset(way, s) for s in range(step) for way in range(2)}
        fresh = {self.offset(way, step) for way in range(2)} - before
        for i in range(len(self.grads)):
            for offset in sorted(fresh):
                self.across(i, offset).wait_recv()
                if self.grads[i] is not None:
                    self.local_copy(i, offset).wait()
            for way in range(2):
                if step > 0:
                    self.ring(i, way, step - 1).wait_recv()
                self.add(i, way, step)
                if step < self.size - 1:
                    self.ring(i, way, step).start()

    def add(self, i, way, step):
        half = self.outs[i].shape[0] // 2
        offset = self.offset(way, step)
        own, came, passed, out = self.own[i], self.came[i], self.passed[i], self.outs[i]

        @pl.loop(0, half // 16)
        def _(r):
            rows = pl.ds(pl.multiple_of(way * half + r * 16, 16), 16)
            kept = own[offset, rows, :] if self.grads[i] is not None else own[1, offset, rows, :]
            total = kept.astype(F32) + came[offset, rows, :].astype(F32)
            if step > 0:
                total += passed[way, step - 1, pl.ds(pl.multiple_of(r * 16, 16), 16), :].astype(F32)
            if step < self.size - 1:
                came[offset, rows, :] = total.astype(BF16)
            else:
                out[rows, :] = total

    def finish(self):
        for i in range(len(self.grads)):
            for offset in range(self.size):
                self.across(i, offset).wait_send()
            for way in range(2):
                for step in range(self.size - 1):
                    self.ring(i, way, step).wait_send()

    @staticmethod
    def out_shape(grad, dim, size):
        deep, wide = grad.shape
        return (deep // (2 * size), wide) if dim == 0 else (deep, wide // (2 * size))

    @staticmethod
    def buffers(shapes, size):
        full = [pltpu.VMEM((size,) + s, BF16) for s in shapes]
        return full + full + [pltpu.VMEM((2, size - 1, s[0] // 2, s[1]), BF16) for s in shapes]

    @staticmethod
    def scratch(count, size):
        return [pltpu.SemaphoreType.DMA((count * size,)) for _ in range(3)] + [
            pltpu.SemaphoreType.DMA((count * 2 * (size - 1),)) for _ in range(2)
        ]


def meet(peers):
    barrier = pltpu.get_barrier_semaphore()
    total = 0
    for condition, peer in peers:
        if condition is None:
            pl.semaphore_signal(barrier, inc=1, device_id=peer, device_id_type=BY_AXIS)
            total = total + 1
        else:

            @pl.when(condition)
            def _():
                pl.semaphore_signal(barrier, inc=1, device_id=peer, device_id_type=BY_AXIS)

            total = total + condition.astype(jnp.int32)
    pl.semaphore_wait(barrier, total)


def project(x, cotangent, gain, valid, shards, w_out_shard, collective_id):
    size = lax.axis_size("fsdp")
    rows, width = x.shape
    deep, local = shards[0].shape
    count = len(shards)
    total = count * local
    half = deep // 2
    tile = min(512, total)
    step_rows = min(64, rows)
    copies = 1 + 2 * (size - 1)

    def kernel(
        valid_ref, gain_ref, x_ref, cot_ref, *refs
    ):
        shard_refs, refs = refs[: count + 1], refs[count + 1 :]
        pre_ref, normed_ref, grad_ref, four_ref, out_ref = refs[:5]
        x_here, grad_here, normed, acc, four, in_sem, save_sem, four_sem, pre_sem = refs[5:14]
        where = [(0, 0, i * local) for i in range(count)] + [(1, 1, 0)]
        job = RingGather(shard_refs, [four, out_ref], where, refs[14:], size, size == 4)
        loads = [
            pltpu.make_async_copy(x_ref, x_here, in_sem.at[0]),
            pltpu.make_async_copy(cot_ref, grad_here, in_sem.at[1]),
        ]
        for load in loads:
            load.start()
        meet([(None, peer) for peer in job.peers()])
        job.start()
        loads[0].wait()

        @pl.loop(0, rows // step_rows)
        def _(r):
            at = pl.ds(pl.multiple_of(r * step_rows, step_rows), step_rows)
            wide = x_here[at, :].astype(F32)
            normed[at, :] = (wide * rms(wide) * gain_ref[...]).astype(BF16)

        saves = [
            pltpu.make_async_copy(normed, normed_ref, save_sem.at[0]),
            pltpu.make_async_copy(grad_here, grad_ref, save_sem.at[1]),
        ]
        saves[0].start()

        def save_four(start, length, number):
            at = pl.ds(start, length)
            return pltpu.make_async_copy(four.at[at, :], four_ref.at[at, :], four_sem.at[number])

        def save_pre(n):
            at = pl.ds(pl.multiple_of(n * tile, tile), tile)
            return pltpu.make_async_copy(acc.at[:, at], pre_ref.at[:, at], pre_sem.at[n])

        def multiply(start, length, first, last):
            @pl.loop(0, total // tile)
            def _(n):
                cols = pl.ds(pl.multiple_of(n * tile, tile), tile)
                deep_at = pl.ds(start, length)
                term = dot(normed[:, deep_at], four[deep_at, cols])
                acc[:, cols] = term if first else acc[:, cols] + term
                if last:
                    save_pre(n).start()

        for i in range(count):
            job.local_copy(i).wait()
        own = pl.multiple_of(job.device(job.place) * deep, deep)
        save_four(own, deep, 0).start()
        multiply(own, deep, True, False)
        loads[1].wait()

        @pl.loop(0, rows // step_rows)
        def _(r):
            at = pl.ds(pl.multiple_of(r * step_rows, step_rows), step_rows)
            row = lax.broadcasted_iota(jnp.int32, (step_rows, width), 0) + r * step_rows
            wide = grad_here[at, :].astype(F32)
            grad_here[at, :] = jnp.where(row < valid_ref[0], wide, 0.0).astype(BF16)

        saves[1].start()
        for step in range(size - 1):
            job.advance(step)
            job.wait_across(range(count), step)
            for way in range(2):
                block = job.device(job.place - (1 - 2 * way) * (step + 1))
                start = pl.multiple_of(block * deep + way * half, half)
                save_four(start, half, 1 + 2 * step + way).start()
                multiply(start, half, False, step == size - 2 and way == 1)
        job.finish(range(count))
        for save in saves:
            save.wait()
        save_four(own, deep, 0).wait()
        for step in range(size - 1):
            for way in range(2):
                save_four(0, half, 1 + 2 * step + way).wait()
        for n in range(total // tile):
            save_pre(n).wait()

    return pl.pallas_call(
        kernel,
        out_shape=[
            jax.ShapeDtypeStruct((rows, total), F32),
            jax.ShapeDtypeStruct((rows, width), BF16),
            jax.ShapeDtypeStruct((rows, width), BF16),
            jax.ShapeDtypeStruct((width, total), BF16),
            jax.ShapeDtypeStruct((w_out_shard.shape[0], width), BF16),
        ],
        in_specs=[pl.BlockSpec(memory_space=pltpu.SMEM), WHOLE, ANY, ANY] + [WHOLE] * (count + 1),
        out_specs=[ANY] * 5,
        scratch_shapes=[
            pltpu.VMEM((rows, width), BF16),
            pltpu.VMEM((rows, width), BF16),
            pltpu.VMEM((rows, width), BF16),
            pltpu.VMEM((rows, total), F32),
            pltpu.VMEM((width, total), BF16),
            pltpu.SemaphoreType.DMA((2,)),
            pltpu.SemaphoreType.DMA((2,)),
            pltpu.SemaphoreType.DMA((copies,)),
            pltpu.SemaphoreType.DMA((total // tile,)),
        ]
        + RingGather.scratch(count + 1, size),
        compiler_params=pltpu.CompilerParams(
            collective_id=collective_id, has_side_effects=True, vmem_limit_bytes=VMEM_BYTES
        ),
        name="project",
    )(valid, gain, x, cotangent, *shards, w_out_shard)


class GatherJob:
    def __init__(self, shards, out_shapes, where):
        self.size = lax.axis_size("fsdp")
        self.inputs, self.in_specs = shards, [WHOLE] * len(shards)
        self.out_shape = [jax.ShapeDtypeStruct(s, BF16) for s in out_shapes]
        self.out_specs = [ANY] * len(out_shapes)
        self.scratch = RingGather.scratch(len(shards), self.size)
        self.where = where

    def bind(self, ins, outs, scratch):
        self.job = RingGather(ins, outs, self.where, scratch, self.size, self.size == 4)

    def peers(self):
        return self.job.peers()

    def tasks(self):
        return []

    def cuts(self, steps):
        return [((2 * steps - 2) * (i + 1)) // self.size for i in range(self.size - 1)]

    def start(self):
        self.job.start()

    def advance(self, number):
        self.job.advance(number)

    def finish(self):
        self.job.finish()


class ScatterJob(GatherJob):
    def __init__(self, grads, dims):
        self.size = lax.axis_size("fsdp")
        self.dims = dims
        shapes = [RingScatter.out_shape(g, d, self.size) for g, d in zip(grads, dims)]
        self.inputs, self.in_specs = grads, [ANY] * len(grads)
        self.out_shape = [jax.ShapeDtypeStruct(s, F32) for s in shapes]
        self.out_specs = [WHOLE] * len(grads)
        self.scratch = RingScatter.buffers(shapes, self.size) + RingScatter.scratch(len(grads), self.size)

    def bind(self, ins, outs, scratch):
        self.job = RingScatter(
            ins, outs, self.dims, scratch[:-5], scratch[-5:], self.size, self.size == 4
        )

    def cuts(self, steps):
        first, last = (2 * steps) // 5, 2 * steps - 2
        return [first + ((last - first) * i) // (self.size - 1) for i in range(self.size)]


class ProductJob:
    def __init__(self, left_at, right_at, dims, shape, tile):
        self.left_at, self.right_at, self.dims, self.shape, self.tile = left_at, right_at, dims, shape, tile
        self.inputs, self.in_specs = [], []
        self.out_shape, self.out_specs = [jax.ShapeDtypeStruct(shape, BF16)], [ANY]
        self.scratch = [pltpu.VMEM((2, tile, shape[1]), BF16), pltpu.SemaphoreType.DMA((2,))]

    def bind(self, ins, outs, scratch):
        (self.out,) = outs
        self.stage, self.sem = scratch

    def peers(self):
        return []

    def cuts(self, steps):
        return []

    def start(self):
        pass

    def tasks(self):
        return [(self.shape[0] // self.tile, self.act, (self.left_at, self.right_at))]

    def copy(self, i):
        where = pl.ds(pl.multiple_of(i * self.tile, self.tile), self.tile)
        return pltpu.make_async_copy(self.stage.at[i % 2], self.out.at[where, :], self.sem.at[i % 2])

    def act(self, i):
        @pl.when(i >= 2)
        def _():
            self.copy(i - 2).wait()

        where = pl.ds(pl.multiple_of(i * self.tile, self.tile), self.tile)
        product_tile(self.operands[self.left_at], self.operands[self.right_at], self.dims, where, self.stage.at[i % 2])
        self.copy(i).start()

    def finish(self):
        tiles = self.shape[0] // self.tile
        for i in range(max(0, tiles - 2), tiles):
            self.copy(i).wait()


def product_tile(left, right, dims, where, out):
    rows = left[:, where].T if dims == TN else left[where, :]
    width = out.shape[-1]
    for start in range(0, width, 512):
        cols = slice(start, min(start + 512, width))
        if dims == NT:
            out[:, cols] = dot(rows, right[cols, :], NT).astype(out.dtype)
        else:
            out[:, cols] = dot(rows, right[:, cols]).astype(out.dtype)


class ProductScatterJob(ScatterJob):
    def __init__(self, pairs, shapes, dims):
        self.size = lax.axis_size("fsdp")
        self.pairs, self.dims = pairs, dims
        shapes = [RingScatter.out_shape(jax.ShapeDtypeStruct(s, BF16), d, self.size) for s, d in zip(shapes, dims)]
        self.inputs, self.in_specs = [], []
        self.out_shape = [jax.ShapeDtypeStruct(s, F32) for s in shapes]
        self.out_specs = [WHOLE] * len(shapes)
        self.scratch = [pltpu.VMEM((2, self.size) + s, BF16) for s in shapes]
        self.scratch += [pltpu.VMEM((self.size,) + s, BF16) for s in shapes]
        self.scratch += [pltpu.VMEM((2, self.size - 1, s[0] // 2, s[1]), BF16) for s in shapes]
        self.scratch += RingScatter.scratch(len(shapes), self.size)

    def bind(self, ins, outs, scratch):
        self.job = RingScatter(
            [None] * len(outs), outs, self.dims, scratch[:-5], scratch[-5:], self.size, self.size == 4
        )

    def cuts(self, steps):
        first, last = min(self.ready_at + 2, 2 * steps - 8), 2 * steps - 3
        return [first + ((last - first) * i) // (self.size - 1) for i in range(self.size)]

    def start(self):
        pass

    def tasks(self):
        made = []
        for i in sorted(range(len(self.pairs)), key=lambda i: -self.dims[i]):
            tiles = 2 * self.size if self.dims[i] == 0 else self.size
            made.append((tiles, functools.partial(self.act, i), self.pairs[i]))
        return made

    def act(self, i, t):
        job = self.job
        left, right = (self.operands[p] for p in self.pairs[i])
        if self.dims[i] == 0:
            offset, mine = lax.rem(t // 2 + 1, self.size), t % 2
            core = mine * job.core + (1 - mine) * (1 - job.core)
            extent = job.outs[i].shape[0]
            index = job.device(job.place + offset) * 2 + core
            where = pl.ds(pl.multiple_of(index * extent, extent), extent)
            product_tile(left, right, TN, where, job.own[i].at[mine, offset])

            @pl.when(mine == 0)
            def _():
                job.across(i, offset).start()
        else:
            offset = lax.rem(t + 1, self.size)
            extent = job.outs[i].shape[1]
            start = pl.multiple_of(job.device(job.place + offset) * 2 * extent, 2 * extent)
            tile = dot(left[...].T, right[:, pl.ds(start, 2 * extent)]).astype(BF16)
            for core in range(2):
                mine = 1 - core + (2 * core - 1) * job.core
                job.own[i][mine, offset] = tile[:, core * extent : (core + 1) * extent]
            job.across(i, offset).start()


class VectorJob:
    def __init__(self, others):
        self.axes = [(axis, lax.axis_size(axis)) for axis in ("ctx", "fsdp", "tp")]
        self.inputs, self.in_specs = [others], [WHOLE]
        self.out_shape, self.out_specs = [jax.ShapeDtypeStruct(others.shape, F32)], [WHOLE]
        self.scratch = [pltpu.VMEM((size,) + others.shape, F32) for _, size in self.axes] + [
            pltpu.SemaphoreType.DMA((size - 1,)) for _, size in self.axes
        ] * 2

    def bind(self, ins, outs, scratch):
        self.others, self.out = ins[0], outs[0]
        self.slots, self.sends, self.recvs = scratch[:3], scratch[3:6], scratch[6:]

    def peers(self):
        return [
            {axis: lax.rem(lax.axis_index(axis) + step, size)} for axis, size in self.axes for step in range(1, size)
        ]

    def cuts(self, steps):
        return [steps + (steps * (i + 1)) // 6 for i in range(len(self.axes) + 1)]

    def tasks(self):
        return []

    def start(self):
        pass

    def copies(self, number):
        axis, size = self.axes[number]
        mine = lax.axis_index(axis)
        return [
            pltpu.make_async_remote_copy(
                src_ref=self.slots[number].at[mine],
                dst_ref=self.slots[number].at[mine],
                send_sem=self.sends[number].at[step - 1],
                recv_sem=self.recvs[number].at[step - 1],
                device_id={axis: lax.rem(mine + step, size)},
                device_id_type=BY_AXIS,
            )
            for step in range(1, size)
        ]

    def advance(self, number):
        if number == 0:
            total = self.others[...] + self.extra()
        else:
            for copy in self.copies(number - 1):
                copy.wait_recv()
            slot = self.slots[number - 1]
            total = slot[0]
            for k in range(1, self.axes[number - 1][1]):
                total = total + slot[k]
        if number == len(self.axes):
            self.out[...] = total
            return
        self.slots[number][lax.axis_index(self.axes[number][0])] = total
        for copy in self.copies(number):
            copy.start()

    def finish(self):
        for number in range(len(self.axes)):
            for copy in self.copies(number):
                copy.wait_send()


def line_sum(
    name, part, halves, gain, n_out, epilogue, collective_id, jobs=(), operands=(), chunk=32, skew=2
):
    size = lax.axis_size("tp")
    product = isinstance(part, tuple)
    if product:
        left_at, right_at, part_dims = part
        rows = operands[left_at].shape[0]
        width = operands[right_at].shape[1 - part_dims[1][0]]
    else:
        rows, width = part.shape
    half = rows // 2
    chunk = min(chunk, half)
    count = half // chunk
    group = min(128, half)
    groups = half // group
    per_group = group // chunk
    vector = [job for job in jobs if isinstance(job, VectorJob)]

    def kernel(*refs):
        refs = list(refs)

        def take(n):
            taken = refs[:n]
            del refs[:n]
            return taken

        part_refs, (gain_ref,) = take(0 if product else 1), take(1)
        half_refs = take(len(halves))
        operand_refs = take(len(operands))
        job_ins = [take(len(job.inputs)) for job in jobs]
        (out_ref,) = take(1)
        own_refs = take(n_out)
        (gain_part_ref,) = take(1)
        job_outs = [take(len(job.out_shape)) for job in jobs]
        part_here, came, sum_send, sum_recv, back_send, back_recv, operand_sem, half_sem, own_sem, part_sem = take(10)
        half_here = take(len(halves))
        operand_here = take(len(operands))
        own_here = take(n_out)
        job_scratch = [take(len(job.scratch)) for job in jobs]
        place = lax.axis_index("tp")
        first, last = place == 0, place == size - 1
        source = (first, last)
        owner = (last, first)
        ahead = (place + 1, place - 1)
        behind = (place - 1, place + 1)
        base = (half, 0)

        loaded = set()

        def operand_copy(i):
            return pltpu.make_async_copy(operand_refs[i], operand_here[i], operand_sem.at[i])

        def need(places):
            for i in places:
                if i not in loaded:
                    operand_copy(i).wait()
                    loaded.add(i)

        def half_copy(way, i):
            start = base[way] if half_refs[i].shape[0] == rows else 0
            return pltpu.make_async_copy(half_refs[i].at[pl.ds(start, half), :], half_here[i], half_sem.at[i])

        def part_copy(way, g):
            where = pl.ds(pl.multiple_of(base[way] + g * group, group), group)
            return pltpu.make_async_copy(part_refs[0].at[where, :], part_here.at[where, :], part_sem.at[way, g])

        if not product:
            for g in range(groups):
                for way in range(2):

                    @pl.when(jnp.logical_not(source[way]))
                    def _():
                        part_copy(way, g).start()

        for i in range(len(operands)):
            operand_copy(i).start()

        for way in range(2):

            @pl.when(owner[way])
            def _():
                for i in range(len(halves)):
                    half_copy(way, i).start()

        for ins, outs, scratch, job in zip(job_ins, job_outs, job_scratch, jobs):
            job.operands = operand_here
            job.bind(ins, outs, scratch)
        peers = [(jnp.logical_not(first), {"tp": place - 1}), (jnp.logical_not(last), {"tp": place + 1})]
        meet(peers + [(None, peer) for job in jobs for peer in job.peers()])

        def at(way, k):
            return pl.ds(pl.multiple_of(k * chunk + base[way], chunk), chunk)

        def onward(way, k, from_part):
            return pltpu.make_async_remote_copy(
                src_ref=(part_here if product else part_refs[0]).at[at(way, k), :] if from_part else came.at[way, k],
                dst_ref=came.at[way, k],
                send_sem=sum_send.at[way, k],
                recv_sem=sum_recv.at[way, k],
                device_id={"tp": ahead[way]},
                device_id_type=BY_AXIS,
            )

        def back(way, k):
            piece = out_ref.at[at(way, k), :]
            return pltpu.make_async_remote_copy(
                src_ref=piece,
                dst_ref=piece,
                send_sem=back_send.at[way, k],
                recv_sem=back_recv.at[way, k],
                device_id={"tp": behind[way]},
                device_id_type=BY_AXIS,
            )

        def own_copy(k):
            where = pl.ds(pl.multiple_of(k * chunk, chunk), chunk)
            return pltpu.make_async_copy(own_here[0].at[where, :], own_refs[0].at[where, :], own_sem.at[k])

        def part_rows(j):
            way, g = j % 2, j // 2
            where = pl.ds(pl.multiple_of((1 - way) * half + g * group, group), group)
            left = operand_here[left_at][where, :]
            for start in range(0, width, 512):
                cols = slice(start, min(start + 512, width))
                right = operand_here[right_at]
                right = right[:, cols] if part_dims == NN else right[cols, :]
                part_here[where, cols] = dot(left, right, part_dims).astype(BF16)
            for w in range(2):

                @pl.when(jnp.logical_and(source[w], way == w))
                def _():
                    @pl.loop(0, per_group)
                    def _(k):
                        onward(w, g * per_group + k, True).start()

        tasks, at_step = [], 0
        if product:
            need((left_at, right_at))

            @pl.loop(0, 2)
            def _(j):
                part_rows(j)

            tasks, at_step = [(0, 2 * groups - 2, lambda i: part_rows(i + 2), ())], 2 * groups - 2
        else:
            for way in range(2):

                @pl.when(source[way])
                def _():
                    @pl.loop(0, count)
                    def _(k):
                        onward(way, k, True).start()

        for job in jobs:
            job.start()
        gain_part_ref[...] = jnp.zeros_like(gain_part_ref)

        away = (place - 1, size - 2 - place)

        def each_way(step, lead, act):
            for way in range(2):
                k = step - skew * lead[way]

                @pl.when(jnp.logical_and(k >= 0, k < count))
                def _():
                    act(way, k)

        def add(way, k):
            @pl.when(jnp.logical_not(source[way]))
            def _():
                if not product:

                    @pl.when(k % per_group == 0)
                    def _():
                        part_copy(way, k // per_group).wait()

                onward(way, k, False).wait_recv()
                total = came[way, k].astype(F32) + part_here[at(way, k), :].astype(F32)

                @pl.when(owner[way])
                def _():
                    @pl.when(k == 0)
                    def _():
                        for i in range(len(halves)):
                            half_copy(way, i).wait()

                    own = pl.ds(pl.multiple_of(k * chunk, chunk), chunk)
                    out_ref[at(way, k), :] = epilogue(
                        half_here, gain_ref[...], own_here[0] if n_out else None, gain_part_ref, own, total
                    )
                    back(way, k).start()
                    if n_out:
                        own_copy(k).start()

                @pl.when(jnp.logical_not(owner[way]))
                def _():
                    came[way, k] = total.astype(BF16)
                    onward(way, k, False).start()

        def spread(way, k):
            @pl.when(jnp.logical_not(owner[way]))
            def _():
                back(way, k).wait_recv()

                @pl.when(jnp.logical_not(source[way]))
                def _():
                    back(way, k).start()

        steps = count + skew * (size - 2)
        for job in vector:
            job.extra = lambda: jnp.where(
                lax.broadcasted_iota(jnp.int32, (8, width), 0) == 0, gain_part_ref[...], 0.0
            )
        for job in jobs:
            for tiles, act, needs in job.tasks():
                tasks.append((at_step, tiles, act, needs))
                at_step += tiles
            job.ready_at = at_step
        acts = sorted((cut, n, i) for n, job in enumerate(jobs) for i, cut in enumerate(job.cuts(steps)))
        bounds = {t[0] for t in tasks} | {t[0] + t[1] for t in tasks}
        for number, (act, lead) in enumerate([(add, away), (spread, (away[1], away[0]))]):
            low, high = number * steps, (number + 1) * steps
            here = [a for a in acts if low <= a[0] < high]
            edges = sorted({low, high} | {a[0] for a in here} | {e for e in bounds if low < e < high})
            for left, right in zip(edges[:-1], edges[1:]):
                for cut, n, i in here:
                    if cut == left:
                        jobs[n].advance(i)
                active = [t for t in tasks if t[0] <= left and right <= t[0] + t[1]]
                for t in active:
                    need(t[3])

                @pl.loop(left - low, right - low)
                def _(step):
                    each_way(step, lead, act)
                    for t in active:
                        t[2](step + low - t[0])

        for first_step, tiles, act, needs in tasks:
            done = min(max(2 * steps - first_step, 0), tiles)
            if done < tiles:
                need(needs)

                @pl.loop(done, tiles)
                def _(i):
                    act(i)

        need(range(len(operands)))
        for job in jobs:
            job.finish()

        for way in range(2):

            @pl.when(jnp.logical_not(owner[way]))
            def _():
                @pl.loop(0, count)
                def _(k):
                    onward(way, k, False).wait_send()

            @pl.when(jnp.logical_not(source[way]))
            def _():
                @pl.loop(0, count)
                def _(k):
                    back(way, k).wait_send()

            if n_out:

                @pl.when(owner[way])
                def _():
                    @pl.loop(0, count)
                    def _(k):
                        own_copy(k).wait()

    scratch = [
        pltpu.VMEM((rows, width), BF16),
        pltpu.VMEM((2, count, chunk, width), BF16),
        *[pltpu.SemaphoreType.DMA((2, count)) for _ in range(4)],
        pltpu.SemaphoreType.DMA((max(1, len(operands)),)),
        pltpu.SemaphoreType.DMA((max(1, len(halves)),)),
        pltpu.SemaphoreType.DMA((count,)),
        pltpu.SemaphoreType.DMA((2, groups)),
        *[pltpu.VMEM((half, width), h.dtype) for h in halves],
        *[pltpu.VMEM(o.shape, o.dtype) for o in operands],
        *[pltpu.VMEM((half, width), F32)] * n_out,
    ]
    return pl.pallas_call(
        kernel,
        out_shape=[jax.ShapeDtypeStruct((rows, width), BF16)]
        + [jax.ShapeDtypeStruct((half, width), F32)] * n_out
        + [jax.ShapeDtypeStruct((8, width), F32)]
        + [shape for job in jobs for shape in job.out_shape],
        in_specs=[ANY] * (not product) + [WHOLE] + [ANY] * (len(halves) + len(operands)) + [spec for job in jobs for spec in job.in_specs],
        out_specs=[WHOLE] + [ANY] * n_out + [WHOLE] + [spec for job in jobs for spec in job.out_specs],
        scratch_shapes=scratch + [shape for job in jobs for shape in job.scratch],
        compiler_params=pltpu.CompilerParams(
            collective_id=collective_id, has_side_effects=True, vmem_limit_bytes=VMEM_BYTES
        ),
        name=name,
    )(*([] if product else [part]), gain, *halves, *operands, *[array for job in jobs for array in job.inputs])


def rms(value):
    return lax.rsqrt(jnp.mean(value * value, axis=-1, keepdims=True) + EPSILON)


def middle_rows(halves, gain, own_ref, gain_part_ref, own, total):
    middle = halves[0][own, :].astype(F32) + total
    own_ref[own, :] = middle
    return (middle * rms(middle) * gain).astype(BF16)


def output_rows(halves, gain, own_ref, gain_part_ref, own, total):
    return (halves[0][own, :] + total).astype(BF16)


def norm_back(grad, value, gain, gain_part_ref):
    inverse = rms(value)
    scaled = value * inverse
    weighted = grad * gain
    gain_part_ref[0:1, :] += jnp.sum(grad * scaled, axis=0, keepdims=True)
    return inverse * (weighted - scaled * jnp.mean(weighted * scaled, axis=-1, keepdims=True))


def grad_middle_rows(halves, gain, own_ref, gain_part_ref, own, total):
    back = norm_back(total, halves[0][own, :], gain, gain_part_ref)
    grad_middle = halves[1][own, :].astype(F32) + back
    own_ref[own, :] = grad_middle
    return grad_middle.astype(BF16)


def input_grad_rows(halves, gain, own_ref, gain_part_ref, own, total):
    back = norm_back(total, halves[0][own, :].astype(F32), gain, gain_part_ref)
    return (halves[1][own, :] + back).astype(BF16)


def lower_ones(length):
    at = lax.broadcasted_iota(jnp.int32, (length, length), 0)
    before = lax.broadcasted_iota(jnp.int32, (length, length), 1)
    return at >= before


def chunk_decay(forget, gap, live, lower):
    closing = sigmoid(-forget)
    opened = gap * closing
    remain = 1.0 - opened
    decay = jnp.where(live, jnp.log(remain), 0.0)
    keys = jnp.where(live, opened, 0.0)
    return closing, remain, keys, ones_times(lower, decay)


def rows_live(valid_ref, chunk_index, length):
    at = lax.broadcasted_iota(jnp.int32, (length, HEAD_DIM), 0) + chunk_index * length
    return at < valid_ref[0]


def span_end_kernel(heads, length, valid_ref, forget_ref, value_ref, gap_ref, end_ref):
    index = pl.program_id(0)

    @pl.when(index == 0)
    def _():
        end_ref[...] = jnp.zeros_like(end_ref)

    live = rows_live(valid_ref, index, length)
    lower = lower_ones(length).astype(BF16)
    for h in range(heads):
        cols = slice(h * HEAD_DIM, (h + 1) * HEAD_DIM)
        _, _, keys, cumulative = chunk_decay(forget_ref[:, cols], gap_ref[:, cols], live, lower)
        total = cumulative[length - 1 :, :]
        tail = (keys * jnp.exp(total - cumulative)).astype(BF16)
        end_ref[h] = jnp.exp(total) * end_ref[h] + dot(value_ref[:, cols].astype(BF16), tail, TN)


def mix_kernel(
    heads, length, valid_ref, query_ref, forget_ref, value_ref, gate_ref, gap_ref, gain_ref, start_ref,
    gated_ref, mixed_ref, states_ref, end_ref, state_ref,
):
    index = pl.program_id(0)

    @pl.when(index == 0)
    def _():
        state_ref[...] = start_ref[...]

    live = rows_live(valid_ref, index, length)
    mask = lower_ones(length)
    lower = mask.astype(BF16)
    for h in range(heads):
        cols = slice(h * HEAD_DIM, (h + 1) * HEAD_DIM)
        _, _, keys, cumulative = chunk_decay(forget_ref[:, cols], gap_ref[:, cols], live, lower)
        pre = query_ref[:, cols]
        queries = (pre * sigmoid(pre) * jnp.exp(cumulative)).astype(BF16)
        shrunk = keys * jnp.exp(-cumulative)
        values = value_ref[:, cols].astype(BF16)
        state = state_ref[h]
        states_ref[0, h] = state
        scores = jnp.where(mask, dot(queries, shrunk.astype(BF16), NT), 0.0).astype(BF16)
        mixed = dot(scores, values) + dot(queries, state.astype(BF16), NT)
        mixed_ref[:, cols] = mixed
        growth = jnp.exp(cumulative[length - 1 :, :])
        state_ref[h] = growth * state + dot(values, (shrunk * growth).astype(BF16), TN)
        gate = gate_ref[:, cols]
        gated_ref[:, cols] = (mixed * rms(mixed) * gain_ref[...] * (gate * sigmoid(gate))).astype(BF16)

    @pl.when(index == pl.num_programs(0) - 1)
    def _():
        end_ref[...] = state_ref[...]


def span_begin_kernel(
    heads, length, valid_ref, grad_ref, mixed_ref, query_ref, forget_ref, gate_ref, gap_ref, gain_ref,
    grad_gate_ref, grad_mixed_ref, gain_part_ref, begin_ref,
):
    step = pl.program_id(0)
    index = pl.num_programs(0) - 1 - step

    @pl.when(step == 0)
    def _():
        begin_ref[...] = jnp.zeros_like(begin_ref)
        gain_part_ref[...] = jnp.zeros_like(gain_part_ref)

    live = rows_live(valid_ref, index, length)
    lower = lower_ones(length).astype(BF16)
    gain = gain_ref[...]
    for h in range(heads):
        cols = slice(h * HEAD_DIM, (h + 1) * HEAD_DIM)
        mixed = mixed_ref[:, cols]
        inverse = rms(mixed)
        scaled = mixed * inverse
        gate = gate_ref[:, cols]
        sig = sigmoid(gate)
        grad = grad_ref[:, cols].astype(F32)
        grad_gate_ref[:, cols] = (grad * scaled * gain * slope(gate, sig)).astype(BF16)
        grad_scaled = grad * (gate * sig)
        gain_part_ref[...] += jnp.sum(grad_scaled * scaled, axis=0, keepdims=True)
        weighted = grad_scaled * gain
        grad_mixed = inverse * (weighted - scaled * jnp.mean(weighted * scaled, axis=-1, keepdims=True))
        grad_mixed = grad_mixed.astype(BF16)
        grad_mixed_ref[:, cols] = grad_mixed
        _, _, _, cumulative = chunk_decay(forget_ref[:, cols], gap_ref[:, cols], live, lower)
        pre = query_ref[:, cols]
        queries = (pre * sigmoid(pre) * jnp.exp(cumulative)).astype(BF16)
        growth = jnp.exp(cumulative[length - 1 :, :])
        begin_ref[h] = growth * begin_ref[h] + dot(grad_mixed, queries, TN)


def mix_back_kernel(
    heads, length, valid_ref, grad_ref, query_ref, forget_ref, value_ref, gap_ref, states_ref, last_ref, end_ref,
    grad_query_ref, grad_forget_ref, grad_value_ref, gap_part_ref, flow_ref, after_ref,
):
    step = pl.program_id(0)
    index = pl.num_programs(0) - 1 - step

    @pl.when(step == 0)
    def _():
        flow_ref[...] = end_ref[...]
        after_ref[...] = last_ref[...]
        gap_part_ref[...] = jnp.zeros_like(gap_part_ref)

    live = rows_live(valid_ref, index, length)
    mask = lower_ones(length)
    lower = mask.astype(BF16)
    for h in range(heads):
        cols = slice(h * HEAD_DIM, (h + 1) * HEAD_DIM)
        gap = gap_ref[:, cols]
        closing, remain, keys, cumulative = chunk_decay(forget_ref[:, cols], gap, live, lower)
        pre = query_ref[:, cols]
        sig = sigmoid(pre)
        growth = jnp.exp(cumulative)
        shrink = jnp.exp(-cumulative)
        end_growth = growth[length - 1 :, :]
        queries = (pre * sig * growth).astype(BF16)
        shrunk_wide = keys * shrink
        shrunk = shrunk_wide.astype(BF16)
        tail = (shrunk_wide * end_growth).astype(BF16)
        values = value_ref[:, cols].astype(BF16)
        grad = grad_ref[:, cols]
        state = states_ref[0, h]
        flow = flow_ref[h]
        low_flow = flow.astype(BF16)
        scores = jnp.where(mask, dot(queries, shrunk, NT), 0.0).astype(BF16)
        grad_scores = jnp.where(mask, dot(grad, values, NT), 0.0).astype(BF16)
        to_queries = dot(grad, state.astype(BF16)) + dot(grad_scores, shrunk)
        to_keys = dot(grad_scores, queries, TN) + end_growth * dot(values, low_flow)
        grad_value_ref[:, cols] = (dot(scores, grad, TN) + dot(tail, low_flow, NT)).astype(BF16)
        grad_query_ref[:, cols] = (to_queries * growth * slope(pre, sig)).astype(BF16)
        terms = queries.astype(F32) * to_queries - shrunk.astype(F32) * to_keys
        high = terms.astype(BF16)
        rest = (terms - high.astype(F32)).astype(BF16)
        suffix = dot(lower, high, TN) + dot(lower, rest, TN)
        crossing = jnp.sum(flow * after_ref[h], axis=0, keepdims=True)
        pressure = jnp.where(live, to_keys * shrink - (suffix + crossing) / remain, 0.0)
        gap_part_ref[:, cols] += jnp.sum(closing * pressure, axis=0, keepdims=True)
        grad_forget_ref[:, cols] = (-closing * (1.0 - closing) * gap * pressure).astype(BF16)
        flow_ref[h] = end_growth * flow + dot(grad, queries, TN)
        after_ref[h] = state


def plain_call(kernel, name, grid, in_specs, out_specs, out_shape, scratch, flops, moved):
    return pl.pallas_call(
        kernel,
        grid_spec=pltpu.PrefetchScalarGridSpec(
            num_scalar_prefetch=1, grid=grid, in_specs=in_specs, out_specs=out_specs, scratch_shapes=scratch
        ),
        out_shape=out_shape,
        compiler_params=pltpu.CompilerParams(
            dimension_semantics=("arbitrary",), vmem_limit_bytes=VMEM_BYTES
        ),
        cost_estimate=pl.CostEstimate(flops=flops, bytes_accessed=moved, transcendentals=flops // 64),
        name=name,
    )


def combine(earlier, later):
    return (earlier[0] * later[0], later[0][:, None, :] * earlier[1] + later[1])


def from_earlier(state, decay, axis):
    size = lax.axis_size(axis)
    if size == 2:
        return lax.ppermute(state, axis, [(0, 1)])
    mine = lax.axis_index(axis)
    states, decays = lax.all_gather(state, axis), lax.all_gather(decay, axis)
    total = jnp.zeros_like(state)
    for k in range(size):
        new = decays[k][:, None, :] * total + states[k]
        total = jnp.where(k < mine, new, total)
    return total


def from_later(state, decay, axis):
    size = lax.axis_size(axis)
    if size == 2:
        return lax.ppermute(state, axis, [(1, 0)])
    mine = lax.axis_index(axis)
    states, decays = lax.all_gather(state, axis), lax.all_gather(decay, axis)
    total = jnp.zeros_like(state)
    for k in reversed(range(size)):
        new = decays[k][:, None, :] * total + states[k]
        total = jnp.where(k > mine, new, total)
    return total


def per_device(
    inputs, lengths, w_query, w_forget, w_input, w_outgate, w_output, w_gate, w_up, w_down,
    norm_gain, ffn_gain, head_gain, forget_gap, cotangent,
):
    groups, span, width = inputs.shape
    rows = groups * span
    fsdp, ctx, tp = lax.axis_size("fsdp"), lax.axis_size("ctx"), lax.axis_size("tp")
    local = forget_gap.shape[0]
    heads = local // HEAD_DIM
    ff = w_gate.shape[1]
    length = min(128, span)
    chunks = span // length
    place = lax.axis_index("tp")
    half = rows // 2

    valid = jnp.clip(lengths - lax.axis_index("ctx") * span, 0, span).astype(jnp.int32)
    x = inputs.reshape(rows, width)
    gap = forget_gap.reshape(1, local)
    head_row = head_gain.reshape(1, HEAD_DIM)
    norm_row, ffn_row = norm_gain.reshape(1, width), ffn_gain.reshape(1, width)

    pre, normed, grad_low, w_four, w_out = project(
        x, cotangent.reshape(rows, width), norm_row, valid, [w_query, w_forget, w_input, w_outgate], w_output, 1
    )

    def column(j):
        return pl.BlockSpec((length, local), lambda i, *_: (i, j))

    def column_back(j):
        return pl.BlockSpec((length, local), lambda i, *_: (chunks - 1 - i, j))

    fixed = lambda shape: pl.BlockSpec(shape, lambda i, *_: (0,) * len(shape))
    state_shape = (heads, HEAD_DIM, HEAD_DIM)
    work = 2 * rows * local * HEAD_DIM
    moved = rows * local * 4

    local_end = plain_call(
        functools.partial(span_end_kernel, heads, length), "span_end", (chunks,),
        [column(1), column(2), fixed((1, local))], fixed(state_shape),
        jax.ShapeDtypeStruct(state_shape, F32), [], 3 * work, 2 * moved,
    )(valid, pre, pre, gap)
    span_decay = None
    if ctx > 2:
        keep = (jnp.arange(rows, dtype=jnp.int32) < valid[0])[:, None]
        closing = jax.nn.sigmoid(-pre[:, local : 2 * local])
        logs = jnp.where(keep, jnp.log(1.0 - gap * closing), 0.0)
        span_decay = jnp.exp(jnp.sum(logs, axis=0)).reshape(heads, HEAD_DIM)
    start = from_earlier(local_end, span_decay, "ctx")
    gated, mixed, states, state_end = plain_call(
        functools.partial(mix_kernel, heads, length), "mix", (chunks,),
        [column(0), column(1), column(2), column(3), fixed((1, local)), fixed((1, HEAD_DIM)), fixed(state_shape)],
        [column(0), column(0), pl.BlockSpec((1,) + state_shape, lambda i, *_: (i, 0, 0, 0)), fixed(state_shape)],
        [
            jax.ShapeDtypeStruct((rows, local), BF16),
            jax.ShapeDtypeStruct((rows, local), F32),
            jax.ShapeDtypeStruct((chunks,) + state_shape, F32),
            jax.ShapeDtypeStruct(state_shape, F32),
        ],
        [pltpu.VMEM(state_shape, F32)], 6 * work, 6 * moved,
    )(valid, pre, pre, pre, pre, gap, head_row, start)

    normed_two, middle, _, w_both, w_back = line_sum(
        "sum_branch", (0, 1, NN), [x], ffn_row, 1, middle_rows, 2,
        [
            GatherJob(
                [w_gate, w_up, w_down],
                [(fsdp * w_gate.shape[0], 2 * ff), (ff, width)],
                [(0, 0, 0), (0, 0, ff), (1, 1, 0)],
            )
        ],
        [gated, w_out],
    )

    both = dot(normed_two, w_both)
    gate_hidden, up_hidden = both[:, :ff], both[:, ff:]
    sig = jax.nn.sigmoid(gate_hidden)
    act = gate_hidden * sig
    hidden = (act * up_hidden).astype(BF16)

    grad_hidden = dot(grad_low, w_back, NT)
    grad_gate = (grad_hidden * up_hidden * slope(gate_hidden, sig)).astype(BF16)
    grad_up = (grad_hidden * act).astype(BF16)
    grad_both = jnp.concatenate([grad_gate, grad_up], axis=1)
    result, _, part_two, grad_w_down, grad_w_both = line_sum(
        "sum_feed", (0, 1, NN), [middle], ffn_row, 0, output_rows, 5,
        [
            ProductJob(2, 3, NT, (rows, width), min(128, rows)),
            ProductJob(0, 4, TN, (ff, width), 128),
            ProductJob(5, 2, TN, (width, 2 * ff), 256),
        ],
        [hidden, w_back, grad_both, w_both, grad_low, normed_two],
    )
    result = result.reshape(groups, span, width)
    both_axes = ("fsdp", "ctx")

    def scattered(grads, dims):
        if ctx == 2:
            return [ScatterJob(grads, dims)], None
        return [], [
            lax.psum_scatter(g, both_axes, scatter_dimension=d, tiled=True).astype(F32) for g, d in zip(grads, dims)
        ]

    job, sums_ffn = scattered([grad_w_both, grad_w_down], [0, 1])
    grad_branch, grad_middle, ffn_gain_part, *more = line_sum(
        "sum_norm_two", part_two, [middle, grad_low], ffn_row, 1, grad_middle_rows, 3, job
    )
    out_both, out_down = sums_ffn or more
    grad_gated = dot(grad_branch, w_out, NT)
    grad_outgate, grad_mixed, head_part, local_begin = plain_call(
        functools.partial(span_begin_kernel, heads, length), "span_begin", (chunks,),
        [column_back(0), column_back(0), column_back(0), column_back(1), column_back(3), fixed((1, local)),
         fixed((1, HEAD_DIM))],
        [column_back(0), column_back(0), fixed((1, HEAD_DIM)), fixed(state_shape)],
        [
            jax.ShapeDtypeStruct((rows, local), BF16),
            jax.ShapeDtypeStruct((rows, local), BF16),
            jax.ShapeDtypeStruct((1, HEAD_DIM), F32),
            jax.ShapeDtypeStruct(state_shape, F32),
        ],
        [], 3 * work, 6 * moved,
    )(valid, grad_gated, mixed, pre, pre, pre, gap, head_row)
    grad_end = from_later(local_begin, span_decay, "ctx")
    grad_query, grad_forget, grad_value, gap_part = plain_call(
        functools.partial(mix_back_kernel, heads, length), "mix_back", (chunks,),
        [column_back(0), column_back(0), column_back(1), column_back(2), fixed((1, local)),
         pl.BlockSpec((1,) + state_shape, lambda i, *_: (chunks - 1 - i, 0, 0, 0)), fixed(state_shape),
         fixed(state_shape)],
        [column_back(0), column_back(0), column_back(0), fixed((1, local))],
        [jax.ShapeDtypeStruct((rows, local), BF16)] * 3 + [jax.ShapeDtypeStruct((1, local), F32)],
        [pltpu.VMEM(state_shape, F32), pltpu.VMEM(state_shape, F32)], 12 * work, 6 * moved,
    )(valid, grad_mixed, pre, pre, pre, gap, states, state_end, grad_end)

    grad_four = jnp.concatenate([grad_query, grad_forget, grad_value, grad_outgate], axis=1)
    owner = jnp.logical_or(place == 0, place == tp - 1)
    gap_row = lax.dynamic_update_slice(jnp.zeros((tp * local,), F32), gap_part[0], (place * local,))
    small = jnp.zeros((8, width), F32)
    small = small.at[1].set(jnp.where(owner, ffn_gain_part[0], 0.0))
    small = small.at[2, :HEAD_DIM].set(head_part[0]).at[3, : tp * local].set(gap_row)
    jobs, operands, sums_mix = [VectorJob(small)], [grad_four, w_four], None
    if ctx == 2:
        shapes = [(width, 4 * local), (local, width)]
        jobs.append(ProductScatterJob([(2, 0), (3, 4)], shapes, [0, 1]))
        operands += [normed, gated, grad_branch]
    else:
        grads = [dot(normed, grad_four, TN).astype(BF16), dot(gated, grad_branch, TN).astype(BF16)]
        _, sums_mix = scattered(grads, [0, 1])
    input_grad, _, sums, *more = line_sum(
        "sum_norm_one", (0, 1, NT), [x, grad_middle], norm_row, 0, input_grad_rows, 4, jobs, operands
    )
    out_four, out_output = sums_mix or more
    input_grad = input_grad.reshape(groups, span, width)
    grad_norm_gain, grad_ffn_gain, grad_head_gain = sums[0], sums[1], sums[2, :HEAD_DIM]
    grad_gap = lax.dynamic_slice(sums[3], (place * local,), (local,))
    return (
        result,
        input_grad,
        out_four[:, :local],
        out_four[:, local : 2 * local],
        out_four[:, 2 * local : 3 * local],
        out_four[:, 3 * local :],
        out_output,
        out_both[:, :ff],
        out_both[:, ff:],
        out_down,
        grad_norm_gain,
        grad_ffn_gain,
        grad_head_gain,
        grad_gap,
    )


def solution(mesh):
    tokens = P("fsdp", "ctx", None)
    inward, outward = P("fsdp", "tp"), P("tp", "fsdp")
    grad_in, grad_back = P(("fsdp", "ctx"), "tp"), P("tp", ("fsdp", "ctx"))
    return jax.shard_map(
        per_device,
        mesh=mesh,
        in_specs=(tokens, P("fsdp")) + (inward,) * 4 + (outward, inward, inward, outward)
        + (P(), P(), P(), P("tp"), tokens),
        out_specs=(tokens, tokens) + (grad_in,) * 4 + (grad_back, grad_in, grad_in, grad_back)
        + (P(), P(), P(), P("tp")),
        check_vma=False,
    )
```

```python
import functools

import jax
import jax.numpy as jnp
from jax import lax
from jax.experimental import pallas as pl
from jax.experimental.pallas import tpu as pltpu
from jax.sharding import PartitionSpec as P

HEAD_DIM = 128
EPSILON = 1e-05
F32 = jnp.float32
BF16 = jnp.bfloat16
BY_AXIS = pl.DeviceIdType.MESH
VMEM_BYTES = 67043328
ANY = pl.BlockSpec(memory_space=pl.ANY)
WHOLE = pl.BlockSpec(memory_space=pltpu.VMEM)


def dot(left, right, dims=((1,), (0,))):
    return lax.dot_general(left, right, (dims, ((), ())), preferred_element_type=F32)


NN = ((1,), (0,))
NT = ((1,), (1,))
TN = ((0,), (0,))


def sigmoid(value):
    return 1.0 / (1.0 + jnp.exp(-value))


def slope(pre, sig):
    return sig * (1.0 + pre * (1.0 - sig))


def ones_times(ones, value):
    high = value.astype(BF16)
    rest = (value - high.astype(F32)).astype(BF16)
    return dot(ones, high) + dot(ones, rest)


def ring_place(index, size, folded):
    if folded:
        return index + (index // 2) * (1 - 2 * (index % 2))
    return index


class RingGather:
    def __init__(self, shards, outs, where, sems, size, folded):
        self.shards, self.outs, self.where, self.size = shards, outs, where, size
        self.ring_send, self.ring_recv, self.pair_send, self.pair_recv, self.local = sems
        self.place = ring_place(lax.axis_index("fsdp"), size, folded)
        self.folded = folded
        self.core = lax.axis_index("ctx") % 2
        self.pair = lax.axis_index("ctx") + 1 - 2 * self.core

    def device(self, place):
        return ring_place(lax.rem(place + 2 * self.size, self.size), self.size, self.folded)

    def peers(self):
        return [
            {"fsdp": self.device(self.place + 1)},
            {"fsdp": self.device(self.place - 1)},
            {"ctx": self.pair},
        ]

    def rows(self, i, core, way):
        quarter = self.shards[i].shape[0] // 4
        return pl.multiple_of((2 * way + core) * quarter, 16), quarter

    def in_shard(self, i, core, way):
        at, length = self.rows(i, core, way)
        return self.shards[i].at[pl.ds(at, length), :]

    def in_out(self, i, block, core, way):
        out, dim, column = self.where[i]
        at, length = self.rows(i, core, way)
        deep, wide = self.shards[i].shape
        if dim == 0:
            start = pl.multiple_of(block * deep + at, 16)
            return self.outs[out].at[pl.ds(start, length), pl.ds(column, wide)]
        start = pl.multiple_of(block * wide, 128)
        return self.outs[out].at[pl.ds(at, length), pl.ds(start, wide)]

    def own_block(self, i):
        out, dim, column = self.where[i]
        deep, wide = self.shards[i].shape
        block = self.device(self.place)
        if dim == 0:
            start = pl.multiple_of(block * deep, 16)
            return self.outs[out].at[pl.ds(start, deep), pl.ds(column, wide)]
        return self.outs[out].at[:, pl.ds(pl.multiple_of(block * wide, 128), wide)]

    def local_copy(self, i):
        return pltpu.make_async_copy(self.shards[i], self.own_block(i), self.local.at[i])

    def ring(self, i, way, step):
        sign = 1 - 2 * way
        block = self.device(self.place - sign * step)
        there = self.in_out(i, block, self.core, way)
        here = self.in_shard(i, self.core, way) if step == 0 else there
        at = (i * 2 + way) * (self.size - 1) + step
        return pltpu.make_async_remote_copy(
            src_ref=here,
            dst_ref=there,
            send_sem=self.ring_send.at[at],
            recv_sem=self.ring_recv.at[at],
            device_id={"fsdp": self.device(self.place + sign)},
            device_id_type=BY_AXIS,
        )

    def across(self, i, way, step, core):
        sign = 1 - 2 * way
        block = self.device(self.place - sign * (step + 1))
        piece = self.in_out(i, block, core, way)
        at = (i * 2 + way) * (self.size - 1) + step
        return pltpu.make_async_remote_copy(
            src_ref=piece,
            dst_ref=piece,
            send_sem=self.pair_send.at[at],
            recv_sem=self.pair_recv.at[at],
            device_id={"ctx": self.pair},
            device_id_type=BY_AXIS,
        )

    def each(self):
        return [(i, way) for i in range(len(self.shards)) for way in range(2)]

    def start(self):
        for i, way in self.each():
            self.ring(i, way, 0).start()
        for i in range(len(self.shards)):
            self.local_copy(i).start()

    def advance(self, step):
        for i, way in self.each():
            arrived = self.ring(i, way, step)
            arrived.wait_recv()
            if step + 1 < self.size - 1:
                self.ring(i, way, step + 1).start()
            self.across(i, way, step, self.core).start()

    def wait_across(self, arrays, step):
        for i in arrays:
            for way in range(2):
                self.across(i, way, step, 1 - self.core).wait_recv()

    def finish(self, waited=()):
        for i, way in self.each():
            for step in range(self.size - 1):
                self.ring(i, way, step).wait_send()
                self.across(i, way, step, self.core).wait_send()
                if i not in waited:
                    self.across(i, way, step, 1 - self.core).wait_recv()
        for i in range(len(self.shards)):
            if i not in waited:
                self.local_copy(i).wait()

    @staticmethod
    def scratch(count, size):
        copies = count * 2 * (size - 1)
        return [pltpu.SemaphoreType.DMA((copies,)) for _ in range(4)] + [
            pltpu.SemaphoreType.DMA((count,))
        ]


class RingScatter:
    def __init__(self, grads, outs, dims, scratch, sems, size, folded):
        self.grads, self.outs, self.dims, self.size, self.folded = grads, outs, dims, size, folded
        count = len(grads)
        self.own, self.came, self.passed = scratch[:count], scratch[count : 2 * count], scratch[2 * count :]
        self.pair_send, self.pair_recv, self.local, self.ring_send, self.ring_recv = sems
        self.place = ring_place(lax.axis_index("fsdp"), size, folded)
        self.core = lax.axis_index("ctx")

    device = RingGather.device

    def peers(self):
        return [
            {"fsdp": self.device(self.place + 1)},
            {"fsdp": self.device(self.place - 1)},
            {"ctx": 1 - self.core},
        ]

    def block(self, i, offset, core):
        index = self.device(self.place + offset) * 2 + core
        extent = self.outs[i].shape[self.dims[i]]
        start = pl.multiple_of(index * extent, extent)
        if self.dims[i] == 0:
            return self.grads[i].at[pl.ds(start, extent), :]
        return self.grads[i].at[:, pl.ds(start, extent)]

    def local_copy(self, i, offset):
        return pltpu.make_async_copy(
            self.block(i, offset, self.core), self.own[i].at[offset], self.local.at[i * self.size + offset]
        )

    def across(self, i, offset):
        at = i * self.size + offset
        give = self.own[i].at[0, offset] if self.grads[i] is None else self.block(i, offset, 1 - self.core)
        return pltpu.make_async_remote_copy(
            src_ref=give,
            dst_ref=self.came[i].at[offset],
            send_sem=self.pair_send.at[at],
            recv_sem=self.pair_recv.at[at],
            device_id={"ctx": 1 - self.core},
            device_id_type=BY_AXIS,
        )

    def offset(self, way, step):
        return (-(step + 1) if way == 0 else step + 1) % self.size

    def ring(self, i, way, step):
        half = self.outs[i].shape[0] // 2
        at = (i * 2 + way) * (self.size - 1) + step
        return pltpu.make_async_remote_copy(
            src_ref=self.came[i].at[self.offset(way, step), pl.ds(way * half, half), :],
            dst_ref=self.passed[i].at[way, step],
            send_sem=self.ring_send.at[at],
            recv_sem=self.ring_recv.at[at],
            device_id={"fsdp": self.device(self.place + 1 - 2 * way)},
            device_id_type=BY_AXIS,
        )

    def order(self):
        used = []
        for step in range(self.size):
            for way in range(2):
                if self.offset(way, step) not in used:
                    used.append(self.offset(way, step))
        return used

    def start(self):
        for offset in self.order():
            for i in range(len(self.grads)):
                self.across(i, offset).start()
                self.local_copy(i, offset).start()

    def advance(self, step):
        before = {self.offset(way, s) for s in range(step) for way in range(2)}
        fresh = {self.offset(way, step) for way in range(2)} - before
        for i in range(len(self.grads)):
            for offset in sorted(fresh):
                self.across(i, offset).wait_recv()
                if self.grads[i] is not None:
                    self.local_copy(i, offset).wait()
            for way in range(2):
                if step > 0:
                    self.ring(i, way, step - 1).wait_recv()
                self.add(i, way, step)
                if step < self.size - 1:
                    self.ring(i, way, step).start()

    def add(self, i, way, step):
        half = self.outs[i].shape[0] // 2
        offset = self.offset(way, step)
        own, came, passed, out = self.own[i], self.came[i], self.passed[i], self.outs[i]

        @pl.loop(0, half // 16)
        def _(r):
            rows = pl.ds(pl.multiple_of(way * half + r * 16, 16), 16)
            kept = own[offset, rows, :] if self.grads[i] is not None else own[1, offset, rows, :]
            total = kept.astype(F32) + came[offset, rows, :].astype(F32)
            if step > 0:
                total += passed[way, step - 1, pl.ds(pl.multiple_of(r * 16, 16), 16), :].astype(F32)
            if step < self.size - 1:
                came[offset, rows, :] = total.astype(BF16)
            else:
                out[rows, :] = total

    def finish(self):
        for i in range(len(self.grads)):
            for offset in range(self.size):
                self.across(i, offset).wait_send()
            for way in range(2):
                for step in range(self.size - 1):
                    self.ring(i, way, step).wait_send()

    @staticmethod
    def out_shape(grad, dim, size):
        deep, wide = grad.shape
        return (deep // (2 * size), wide) if dim == 0 else (deep, wide // (2 * size))

    @staticmethod
    def buffers(shapes, size):
        full = [pltpu.VMEM((size,) + s, BF16) for s in shapes]
        return full + full + [pltpu.VMEM((2, size - 1, s[0] // 2, s[1]), BF16) for s in shapes]

    @staticmethod
    def scratch(count, size):
        return [pltpu.SemaphoreType.DMA((count * size,)) for _ in range(3)] + [
            pltpu.SemaphoreType.DMA((count * 2 * (size - 1),)) for _ in range(2)
        ]


def meet(peers):
    barrier = pltpu.get_barrier_semaphore()
    total = 0
    for condition, peer in peers:
        if condition is None:
            pl.semaphore_signal(barrier, inc=1, device_id=peer, device_id_type=BY_AXIS)
            total = total + 1
        else:

            @pl.when(condition)
            def _():
                pl.semaphore_signal(barrier, inc=1, device_id=peer, device_id_type=BY_AXIS)

            total = total + condition.astype(jnp.int32)
    pl.semaphore_wait(barrier, total)


def project(x, cotangent, gain, valid, shards, w_out_shard, collective_id):
    size = lax.axis_size("fsdp")
    rows, width = x.shape
    deep, local = shards[0].shape
    count = len(shards)
    total = count * local
    half = deep // 2
    tile = min(512, total)
    step_rows = min(64, rows)
    row_tile = min(512, rows)
    copies = 1 + 2 * (size - 1)

    def kernel(
        valid_ref, gain_ref, x_ref, cot_ref, *refs
    ):
        shard_refs, refs = refs[: count + 1], refs[count + 1 :]
        pre_ref, normed_ref, grad_ref, four_ref, out_ref = refs[:5]
        x_here, grad_here, normed, acc, four, in_sem, save_sem, four_sem, pre_sem = refs[5:14]
        where = [(0, 0, i * local) for i in range(count)] + [(1, 1, 0)]
        job = RingGather(shard_refs, [four, out_ref], where, refs[14:], size, size == 4)
        loads = [
            pltpu.make_async_copy(x_ref, x_here, in_sem.at[0]),
            pltpu.make_async_copy(cot_ref, grad_here, in_sem.at[1]),
        ]
        for load in loads:
            load.start()
        meet([(None, peer) for peer in job.peers()])
        job.start()
        loads[0].wait()

        @pl.loop(0, rows // step_rows)
        def _(r):
            at = pl.ds(pl.multiple_of(r * step_rows, step_rows), step_rows)
            wide = x_here[at, :].astype(F32)
            normed[at, :] = (wide * rms(wide) * gain_ref[...]).astype(BF16)

        saves = [
            pltpu.make_async_copy(normed, normed_ref, save_sem.at[0]),
            pltpu.make_async_copy(grad_here, grad_ref, save_sem.at[1]),
        ]
        saves[0].start()

        def save_four(start, length, number):
            at = pl.ds(start, length)
            return pltpu.make_async_copy(four.at[at, :], four_ref.at[at, :], four_sem.at[number])

        def save_pre(n):
            at = pl.ds(pl.multiple_of(n * tile, tile), tile)
            return pltpu.make_async_copy(acc.at[:, at], pre_ref.at[:, at], pre_sem.at[n])

        def multiply(start, length, first, last):
            @pl.loop(0, total // tile)
            def _(n):
                cols = pl.ds(pl.multiple_of(n * tile, tile), tile)
                deep_at = pl.ds(start, length)

                @pl.loop(0, rows // row_tile)
                def _(r):
                    at = pl.ds(pl.multiple_of(r * row_tile, row_tile), row_tile)
                    term = dot(normed[at, deep_at], four[deep_at, cols])
                    acc[at, cols] = term if first else acc[at, cols] + term

                if last:
                    save_pre(n).start()

        for i in range(count):
            job.local_copy(i).wait()
        own = pl.multiple_of(job.device(job.place) * deep, deep)
        save_four(own, deep, 0).start()
        multiply(own, deep, True, False)
        loads[1].wait()

        @pl.loop(0, rows // step_rows)
        def _(r):
            at = pl.ds(pl.multiple_of(r * step_rows, step_rows), step_rows)
            row = lax.broadcasted_iota(jnp.int32, (step_rows, width), 0) + r * step_rows
            wide = grad_here[at, :].astype(F32)
            grad_here[at, :] = jnp.where(row < valid_ref[0], wide, 0.0).astype(BF16)

        saves[1].start()
        for step in range(size - 1):
            job.advance(step)
            job.wait_across(range(count), step)
            for way in range(2):
                block = job.device(job.place - (1 - 2 * way) * (step + 1))
                start = pl.multiple_of(block * deep + way * half, half)
                save_four(start, half, 1 + 2 * step + way).start()
                multiply(start, half, False, step == size - 2 and way == 1)
        job.finish(range(count))
        for save in saves:
            save.wait()
        save_four(own, deep, 0).wait()
        for step in range(size - 1):
            for way in range(2):
                save_four(0, half, 1 + 2 * step + way).wait()
        for n in range(total // tile):
            save_pre(n).wait()

    return pl.pallas_call(
        kernel,
        out_shape=[
            jax.ShapeDtypeStruct((rows, total), F32),
            jax.ShapeDtypeStruct((rows, width), BF16),
            jax.ShapeDtypeStruct((rows, width), BF16),
            jax.ShapeDtypeStruct((width, total), BF16),
            jax.ShapeDtypeStruct((w_out_shard.shape[0], width), BF16),
        ],
        in_specs=[pl.BlockSpec(memory_space=pltpu.SMEM), WHOLE, ANY, ANY] + [WHOLE] * (count + 1),
        out_specs=[ANY] * 5,
        scratch_shapes=[
            pltpu.VMEM((rows, width), BF16),
            pltpu.VMEM((rows, width), BF16),
            pltpu.VMEM((rows, width), BF16),
            pltpu.VMEM((rows, total), F32),
            pltpu.VMEM((width, total), BF16),
            pltpu.SemaphoreType.DMA((2,)),
            pltpu.SemaphoreType.DMA((2,)),
            pltpu.SemaphoreType.DMA((copies,)),
            pltpu.SemaphoreType.DMA((total // tile,)),
        ]
        + RingGather.scratch(count + 1, size),
        compiler_params=pltpu.CompilerParams(
            collective_id=collective_id, has_side_effects=True, vmem_limit_bytes=VMEM_BYTES
        ),
        name="project",
    )(valid, gain, x, cotangent, *shards, w_out_shard)


class GatherJob:
    def __init__(self, shards, out_shapes, where):
        self.size = lax.axis_size("fsdp")
        self.inputs, self.in_specs = shards, [WHOLE] * len(shards)
        self.out_shape = [jax.ShapeDtypeStruct(s, BF16) for s in out_shapes]
        self.out_specs = [ANY] * len(out_shapes)
        self.scratch = RingGather.scratch(len(shards), self.size)
        self.where = where

    def bind(self, ins, outs, scratch):
        self.job = RingGather(ins, outs, self.where, scratch, self.size, self.size == 4)

    def peers(self):
        return self.job.peers()

    def tasks(self):
        return []

    def cuts(self, steps):
        return [((2 * steps - 2) * (i + 1)) // self.size for i in range(self.size - 1)]

    def start(self):
        self.job.start()

    def advance(self, number):
        self.job.advance(number)

    def finish(self):
        self.job.finish()


class ScatterJob(GatherJob):
    def __init__(self, grads, dims):
        self.size = lax.axis_size("fsdp")
        self.dims = dims
        shapes = [RingScatter.out_shape(g, d, self.size) for g, d in zip(grads, dims)]
        self.inputs, self.in_specs = grads, [ANY] * len(grads)
        self.out_shape = [jax.ShapeDtypeStruct(s, F32) for s in shapes]
        self.out_specs = [WHOLE] * len(grads)
        self.scratch = RingScatter.buffers(shapes, self.size) + RingScatter.scratch(len(grads), self.size)

    def bind(self, ins, outs, scratch):
        self.job = RingScatter(
            ins, outs, self.dims, scratch[:-5], scratch[-5:], self.size, self.size == 4
        )

    def cuts(self, steps):
        first, last = (2 * steps) // 5, 2 * steps - 2
        return [first + ((last - first) * i) // (self.size - 1) for i in range(self.size)]


class ProductJob:
    def __init__(self, left_at, right_at, dims, shape, tile):
        self.left_at, self.right_at, self.dims, self.shape, self.tile = left_at, right_at, dims, shape, tile
        self.inputs, self.in_specs = [], []
        self.out_shape, self.out_specs = [jax.ShapeDtypeStruct(shape, BF16)], [ANY]
        self.scratch = [pltpu.VMEM((2, tile, shape[1]), BF16), pltpu.SemaphoreType.DMA((2,))]

    def bind(self, ins, outs, scratch):
        (self.out,) = outs
        self.stage, self.sem = scratch

    def peers(self):
        return []

    def cuts(self, steps):
        return []

    def start(self):
        pass

    def tasks(self):
        return [(self.shape[0] // self.tile, self.act, (self.left_at, self.right_at))]

    def copy(self, i):
        where = pl.ds(pl.multiple_of(i * self.tile, self.tile), self.tile)
        return pltpu.make_async_copy(self.stage.at[i % 2], self.out.at[where, :], self.sem.at[i % 2])

    def act(self, i):
        @pl.when(i >= 2)
        def _():
            self.copy(i - 2).wait()

        where = pl.ds(pl.multiple_of(i * self.tile, self.tile), self.tile)
        product_tile(self.operands[self.left_at], self.operands[self.right_at], self.dims, where, self.stage.at[i % 2])
        self.copy(i).start()

    def finish(self):
        tiles = self.shape[0] // self.tile
        for i in range(max(0, tiles - 2), tiles):
            self.copy(i).wait()


def product_tile(left, right, dims, where, out):
    rows = left[:, where].T if dims == TN else left[where, :]

    def act(cols):
        if dims == NT:
            out[:, cols] = dot(rows, right[cols, :], NT).astype(out.dtype)
        else:
            out[:, cols] = dot(rows, right[:, cols]).astype(out.dtype)

    by_columns(out.shape[-1], act)


def by_columns(width, act):
    step = min(512, width)

    @pl.loop(0, width // step)
    def _(n):
        act(pl.ds(pl.multiple_of(n * step, step), step))

    if width % step:
        act(pl.ds(width - width % step, width % step))


class ProductScatterJob(ScatterJob):
    def __init__(self, pairs, shapes, dims):
        self.size = lax.axis_size("fsdp")
        self.pairs, self.dims = pairs, dims
        shapes = [RingScatter.out_shape(jax.ShapeDtypeStruct(s, BF16), d, self.size) for s, d in zip(shapes, dims)]
        self.inputs, self.in_specs = [], []
        self.out_shape = [jax.ShapeDtypeStruct(s, F32) for s in shapes]
        self.out_specs = [WHOLE] * len(shapes)
        self.scratch = [pltpu.VMEM((2, self.size) + s, BF16) for s in shapes]
        self.scratch += [pltpu.VMEM((self.size,) + s, BF16) for s in shapes]
        self.scratch += [pltpu.VMEM((2, self.size - 1, s[0] // 2, s[1]), BF16) for s in shapes]
        self.scratch += RingScatter.scratch(len(shapes), self.size)

    def bind(self, ins, outs, scratch):
        self.job = RingScatter(
            [None] * len(outs), outs, self.dims, scratch[:-5], scratch[-5:], self.size, self.size == 4
        )

    def cuts(self, steps):
        first, last = min(self.ready_at + 2, 2 * steps - 8), 2 * steps - 3
        return [first + ((last - first) * i) // (self.size - 1) for i in range(self.size)]

    def start(self):
        pass

    def tasks(self):
        made = []
        for i in sorted(range(len(self.pairs)), key=lambda i: -self.dims[i]):
            tiles = 2 * self.size if self.dims[i] == 0 else self.size
            made.append((tiles, functools.partial(self.act, i), self.pairs[i]))
        return made

    def act(self, i, t):
        job = self.job
        left, right = (self.operands[p] for p in self.pairs[i])
        if self.dims[i] == 0:
            offset, mine = lax.rem(t // 2 + 1, self.size), t % 2
            core = mine * job.core + (1 - mine) * (1 - job.core)
            extent = job.outs[i].shape[0]
            index = job.device(job.place + offset) * 2 + core
            where = pl.ds(pl.multiple_of(index * extent, extent), extent)
            product_tile(left, right, TN, where, job.own[i].at[mine, offset])

            @pl.when(mine == 0)
            def _():
                job.across(i, offset).start()
        else:
            offset = lax.rem(t + 1, self.size)
            extent = job.outs[i].shape[1]
            start = pl.multiple_of(job.device(job.place + offset) * 2 * extent, 2 * extent)
            tile = dot(left[...].T, right[:, pl.ds(start, 2 * extent)]).astype(BF16)
            for core in range(2):
                mine = 1 - core + (2 * core - 1) * job.core
                job.own[i][mine, offset] = tile[:, core * extent : (core + 1) * extent]
            job.across(i, offset).start()


class MixBackJob:
    def __init__(self, valid, grad_branch, w_out, mixed, pre, states, gap, gain, state_end):
        self.rows, self.width = grad_branch.shape
        self.local = w_out.shape[0]
        self.chunks, self.heads = states.shape[:2]
        self.length = self.rows // self.chunks
        self.inputs = [valid, grad_branch, w_out, mixed, pre, states, gap, gain, state_end]
        self.in_specs = [pl.BlockSpec(memory_space=pltpu.SMEM)] + [ANY] * 5 + [WHOLE] * 3
        self.out_shape = [jax.ShapeDtypeStruct((self.rows, self.local), BF16)] * 4 + [
            jax.ShapeDtypeStruct((1, self.local), F32),
            jax.ShapeDtypeStruct((1, HEAD_DIM), F32),
        ]
        self.out_specs = [ANY] * 4 + [WHOLE] * 2
        state = states.shape[1:]
        self.scratch = [
            pltpu.VMEM(w_out.shape, BF16),
            pltpu.VMEM((2, self.length, self.width), BF16),
            pltpu.VMEM((2, self.length, self.local), F32),
            pltpu.VMEM((2, self.length, 4 * self.local), F32),
            pltpu.VMEM((2,) + state, F32),
            pltpu.VMEM((self.length, self.local), F32),
            pltpu.VMEM((self.rows, self.local), BF16),
            *[pltpu.VMEM(state, F32)] * 4,
            pltpu.VMEM((2, 4, self.length, self.local), BF16),
            pltpu.SemaphoreType.DMA((2, 4)),
            pltpu.SemaphoreType.DMA((2, 4)),
            pltpu.SemaphoreType.DMA((3,)),
        ]

    def bind(self, ins, outs, scratch):
        self.valid, self.grad_branch, self.w_out, self.mixed, self.pre, self.states, self.gap, self.gain, self.last = ins
        self.outs, (self.gap_part, self.gain_part) = outs[:4], outs[4:]
        self.w_here, self.grad_here, self.mixed_here, self.pre_here, self.states_here = scratch[:5]
        self.gated, self.grad_mixed, self.begin, self.came, self.flow, self.after = scratch[5:11]
        self.stage, self.in_sem, self.out_sem, self.sem = scratch[11:]
        self.core = lax.axis_index("ctx")

    def peers(self):
        return [{"ctx": 1 - self.core}]

    def cuts(self, steps):
        return []

    def w_copy(self):
        return pltpu.make_async_copy(self.w_out, self.w_here, self.sem.at[0])

    def across(self):
        return pltpu.make_async_remote_copy(
            src_ref=self.begin,
            dst_ref=self.came,
            send_sem=self.sem.at[1],
            recv_sem=self.sem.at[2],
            device_id={"ctx": 1 - self.core},
            device_id_type=BY_AXIS,
        )

    def where(self, i):
        return pl.ds(pl.multiple_of((self.chunks - 1 - i) * self.length, self.length), self.length)

    def loads(self, phase, i):
        slot = i % 2
        copies = [pltpu.make_async_copy(self.pre.at[self.where(i), :], self.pre_here.at[slot], self.in_sem.at[slot, 0])]
        if phase == 0:
            whole = (self.grad_branch, self.grad_here, 1), (self.mixed, self.mixed_here, 2)
            for source, here, n in whole:
                copies.append(
                    pltpu.make_async_copy(source.at[self.where(i), :], here.at[slot], self.in_sem.at[slot, n])
                )
        else:
            copies.append(
                pltpu.make_async_copy(
                    self.states.at[self.chunks - 1 - i], self.states_here.at[slot], self.in_sem.at[slot, 3]
                )
            )
        return copies

    def begin_loads(self, phase, i):
        for copy in self.loads(phase, i):
            copy.start()

    def end_loads(self, phase, i):
        for copy in self.loads(phase, i):
            copy.wait()

    def save(self, k, i):
        slot = i % 2
        return pltpu.make_async_copy(
            self.stage.at[slot, k], self.outs[k].at[self.where(i), :], self.out_sem.at[slot, k]
        )

    def start(self):
        self.w_copy().start()
        for i in range(2):
            self.begin_loads(0, i)

    def tasks(self):
        return [(self.chunks, self.act_begin, ()), (1, lambda i: None, ()), (2 * self.chunks, self.act_back, ())]

    def column(self, slot, k, start=0, wide=None):
        return self.pre_here.at[slot, :, pl.ds(k * self.local + start, wide or self.local)]

    def act_begin(self, i):
        slot = i % 2

        @pl.when(i == 0)
        def _():
            self.w_copy().wait()

        self.end_loads(0, i)

        @pl.when(i >= 2)
        def _():
            self.save(3, i - 2).wait()

        self.gated[...] = dot(self.grad_here[slot], self.w_here[...], NT)
        span_begin_chunk(
            self.heads, self.length, i, self.chunks, self.valid, self.gated, self.mixed_here.at[slot],
            self.column(slot, 0), self.column(slot, 1), self.column(slot, 3), self.gap, self.gain,
            self.stage.at[slot, 3], self.grad_mixed.at[self.where(i), :], self.gain_part, self.begin,
        )
        self.save(3, i).start()

        @pl.when(i + 2 < self.chunks)
        def _():
            self.begin_loads(0, i + 2)

        @pl.when(i + 2 >= self.chunks)
        def _():
            self.begin_loads(1, i + 2 - self.chunks)

        @pl.when(i == self.chunks - 1)
        def _():
            self.across().start()

    def act_back(self, t):
        i, part = t // 2, t % 2
        slot = i % 2

        @pl.when(t == 0)
        def _():
            self.across().wait_recv()
            self.came[...] = jnp.where(self.core == 0, self.came[...], 0.0)

        @pl.when(part == 0)
        def _():
            self.end_loads(1, i)

            @pl.when(i >= 2)
            def _():
                for k in range(3):
                    self.save(k, i - 2).wait()

        heads, wide = self.heads // 2, self.local // 2
        start = pl.multiple_of(part * wide, HEAD_DIM)
        cols, some = pl.ds(start, wide), pl.ds(part * heads, heads)
        mix_back_chunk(
            heads, self.length, i, self.chunks, self.valid, self.grad_mixed.at[self.where(i), cols],
            *[self.column(slot, k, start, wide) for k in range(3)], self.gap.at[:, cols],
            self.states_here.at[pl.ds(slot, 1), some], self.last.at[some], self.came.at[some],
            *[self.stage.at[slot, k, :, cols] for k in range(3)],
            self.gap_part.at[:, cols], self.flow.at[some], self.after.at[some],
        )

        @pl.when(part == 1)
        def _():
            for k in range(3):
                self.save(k, i).start()

            @pl.when(i + 2 < self.chunks)
            def _():
                self.begin_loads(1, i + 2)

    def finish(self):
        for i in range(self.chunks - 2, self.chunks):
            for k in range(4):
                self.save(k, i).wait()
        self.across().wait_send()


class VectorJob:
    def __init__(self, full, short, split):
        self.axes = [(axis, lax.axis_size(axis)) for axis in ("ctx", "fsdp", "tp")]
        self.inputs, self.in_specs = [full, short, split], [WHOLE] * 3
        self.out_shape, self.out_specs = [jax.ShapeDtypeStruct(full.shape, F32)], [WHOLE]
        self.scratch = [pltpu.VMEM((size,) + full.shape, F32) for _, size in self.axes] + [
            pltpu.SemaphoreType.DMA((size - 1,)) for _, size in self.axes
        ] * 2

    def bind(self, ins, outs, scratch):
        self.full, self.short, self.split = ins
        (self.out,) = outs
        self.slots, self.sends, self.recvs = scratch[:3], scratch[3:6], scratch[6:]

    def peers(self):
        return [
            {axis: lax.rem(lax.axis_index(axis) + step, size)} for axis, size in self.axes for step in range(1, size)
        ]

    def cuts(self, steps):
        return [steps + (steps * (i + 1)) // 6 for i in range(len(self.axes) + 1)]

    def tasks(self):
        return []

    def start(self):
        pass

    def copies(self, number):
        axis, size = self.axes[number]
        mine = lax.axis_index(axis)
        return [
            pltpu.make_async_remote_copy(
                src_ref=self.slots[number].at[mine],
                dst_ref=self.slots[number].at[mine],
                send_sem=self.sends[number].at[step - 1],
                recv_sem=self.recvs[number].at[step - 1],
                device_id={axis: lax.rem(mine + step, size)},
                device_id_type=BY_AXIS,
            )
            for step in range(1, size)
        ]

    def advance(self, number):
        if number == 0:
            mine = lax.axis_index(self.axes[0][0])
            slot, local = self.slots[0], self.split.shape[1]
            slot[mine] = self.extra()
            slot[mine, 1:2, :] = self.full[0:1, :]
            slot[mine, 2:3, : self.short.shape[1]] = self.short[...]
            slot[mine, 3:4, pl.ds(pl.multiple_of(lax.axis_index("tp") * local, local), local)] = self.split[...]
        else:
            for copy in self.copies(number - 1):
                copy.wait_recv()
            slot = self.slots[number - 1]
            total = slot[0]
            for k in range(1, self.axes[number - 1][1]):
                total = total + slot[k]
        if number == len(self.axes):
            self.out[...] = total
            return
        if number > 0:
            self.slots[number][lax.axis_index(self.axes[number][0])] = total
        for copy in self.copies(number):
            copy.start()

    def finish(self):
        for number in range(len(self.axes)):
            for copy in self.copies(number):
                copy.wait_send()


def line_sum(
    name, part, halves, gain, n_out, epilogue, collective_id, jobs=(), operands=(), chunk=32, skew=2
):
    size = lax.axis_size("tp")
    product = isinstance(part, tuple)
    operands = [o if isinstance(o, tuple) else (o,) for o in operands]
    operand_shapes = [(o[0].shape[0], sum(p.shape[1] for p in o)) for o in operands]
    pieces = [p for o in operands for p in o]
    if product:
        left_at, right_at, part_dims = part
        rows = operand_shapes[left_at][0]
        width = operand_shapes[right_at][1 - part_dims[1][0]]
    else:
        rows, width = part.shape
    half = rows // 2
    chunk = min(chunk, half)
    count = half // chunk
    group = min(128, half)
    groups = half // group
    per_group = group // chunk
    vector = [job for job in jobs if isinstance(job, VectorJob)]

    def kernel(*refs):
        refs = list(refs)

        def take(n):
            taken = refs[:n]
            del refs[:n]
            return taken

        part_refs, (gain_ref,) = take(0 if product else 1), take(1)
        half_refs = take(len(halves))
        operand_refs = take(len(pieces))
        job_ins = [take(len(job.inputs)) for job in jobs]
        (out_ref,) = take(1)
        own_refs = take(n_out)
        (gain_part_ref,) = take(1)
        job_outs = [take(len(job.out_shape)) for job in jobs]
        part_here, came, sum_send, sum_recv, back_send, back_recv, operand_sem, half_sem, own_sem, part_sem = take(10)
        half_here = take(len(halves))
        operand_here = take(len(operands))
        own_here = take(n_out)
        job_scratch = [take(len(job.scratch)) for job in jobs]
        place = lax.axis_index("tp")
        first, last = place == 0, place == size - 1
        source = (first, last)
        owner = (last, first)
        ahead = (place + 1, place - 1)
        behind = (place - 1, place + 1)
        base = (half, 0)

        loaded = set()

        def operand_copies(i):
            first, column = sum(len(o) for o in operands[:i]), 0
            for n, piece in enumerate(operands[i], first):
                where = operand_here[i].at[:, pl.ds(column, piece.shape[1])]
                yield pltpu.make_async_copy(operand_refs[n], where, operand_sem.at[n])
                column += piece.shape[1]

        def need(places):
            for i in places:
                if i not in loaded:
                    for copy in operand_copies(i):
                        copy.wait()
                    loaded.add(i)

        def half_copy(way, i):
            start = base[way] if half_refs[i].shape[0] == rows else 0
            return pltpu.make_async_copy(half_refs[i].at[pl.ds(start, half), :], half_here[i], half_sem.at[i])

        def part_copy(way, g):
            where = pl.ds(pl.multiple_of(base[way] + g * group, group), group)
            return pltpu.make_async_copy(part_refs[0].at[where, :], part_here.at[where, :], part_sem.at[way, g])

        if not product:
            for g in range(groups):
                for way in range(2):

                    @pl.when(jnp.logical_not(source[way]))
                    def _():
                        part_copy(way, g).start()

        def load(places):
            for i in places:
                for copy in operand_copies(i):
                    copy.start()

        early = (left_at, right_at) if product else ()
        load(early)
        for ins, outs, scratch, job in zip(job_ins, job_outs, job_scratch, jobs):
            job.operands = operand_here
            job.bind(ins, outs, scratch)
        peers = [(jnp.logical_not(first), {"tp": place - 1}), (jnp.logical_not(last), {"tp": place + 1})]
        meet(peers + [(None, peer) for job in jobs for peer in job.peers()])

        def at(way, k):
            return pl.ds(pl.multiple_of(k * chunk + base[way], chunk), chunk)

        def onward(way, k, from_part):
            return pltpu.make_async_remote_copy(
                src_ref=(part_here if product else part_refs[0]).at[at(way, k), :] if from_part else came.at[way, k],
                dst_ref=came.at[way, k],
                send_sem=sum_send.at[way, k],
                recv_sem=sum_recv.at[way, k],
                device_id={"tp": ahead[way]},
                device_id_type=BY_AXIS,
            )

        def back(way, k):
            piece = out_ref.at[at(way, k), :]
            return pltpu.make_async_remote_copy(
                src_ref=piece,
                dst_ref=piece,
                send_sem=back_send.at[way, k],
                recv_sem=back_recv.at[way, k],
                device_id={"tp": behind[way]},
                device_id_type=BY_AXIS,
            )

        def own_copy(k):
            where = pl.ds(pl.multiple_of(k * chunk, chunk), chunk)
            return pltpu.make_async_copy(own_here[0].at[where, :], own_refs[0].at[where, :], own_sem.at[k])

        def part_rows(j):
            way, g = lax.rem(j + jnp.where(place < size // 2, 0, 1), 2), j // 2
            where = pl.ds(pl.multiple_of((1 - way) * half + g * group, group), group)
            left = operand_here[left_at][where, :]
            for start in range(0, width, 512):
                cols = slice(start, min(start + 512, width))
                right = operand_here[right_at]
                right = right[:, cols] if part_dims == NN else right[cols, :]
                part_here[where, cols] = dot(left, right, part_dims).astype(BF16)
            for w in range(2):

                @pl.when(jnp.logical_and(source[w], way == w))
                def _():
                    @pl.loop(0, per_group)
                    def _(k):
                        onward(w, g * per_group + k, True).start()

        tasks, at_step = [], 0
        need(early)
        load([i for i in range(len(operands)) if i not in early])
        for way in range(2):

            @pl.when(owner[way])
            def _():
                for i in range(len(halves)):
                    half_copy(way, i).start()

        if product:
            tasks, at_step = [(-2, 2 * groups, part_rows, ())], 2 * groups - 2
        else:
            for way in range(2):

                @pl.when(source[way])
                def _():
                    @pl.loop(0, count)
                    def _(k):
                        onward(way, k, True).start()

        for job in jobs:
            job.start()
        gain_part_ref[...] = jnp.zeros_like(gain_part_ref)

        away = (place - 1, size - 2 - place)

        def each_way(step, lead, act):
            for way in range(2):
                k = step - skew * lead[way]

                @pl.when(jnp.logical_and(k >= 0, k < count))
                def _():
                    act(way, k)

        def add(way, k):
            @pl.when(jnp.logical_not(source[way]))
            def _():
                if not product:

                    @pl.when(k % per_group == 0)
                    def _():
                        part_copy(way, k // per_group).wait()

                onward(way, k, False).wait_recv()
                total = came[way, k].astype(F32) + part_here[at(way, k), :].astype(F32)

                @pl.when(owner[way])
                def _():
                    @pl.when(k == 0)
                    def _():
                        for i in range(len(halves)):
                            half_copy(way, i).wait()

                    own = pl.ds(pl.multiple_of(k * chunk, chunk), chunk)
                    out_ref[at(way, k), :] = epilogue(
                        half_here, gain_ref[...], own_here[0] if n_out else None, gain_part_ref, own, total
                    )
                    back(way, k).start()
                    if n_out:
                        own_copy(k).start()

                @pl.when(jnp.logical_not(owner[way]))
                def _():
                    came[way, k] = total.astype(BF16)
                    onward(way, k, False).start()

        def spread(way, k):
            @pl.when(jnp.logical_not(owner[way]))
            def _():
                back(way, k).wait_recv()

                @pl.when(jnp.logical_not(source[way]))
                def _():
                    back(way, k).start()

        steps = count + skew * (size - 2)
        for job in vector:
            job.extra = lambda: jnp.where(
                lax.broadcasted_iota(jnp.int32, (8, width), 0) == 0, gain_part_ref[...], 0.0
            )
        for job in jobs:
            for tiles, act, needs in job.tasks():
                tasks.append((at_step, tiles, act, needs))
                at_step += tiles
            job.ready_at = at_step
        acts = sorted((cut, n, i) for n, job in enumerate(jobs) for i, cut in enumerate(job.cuts(steps)))
        bounds = {t[0] for t in tasks} | {t[0] + t[1] for t in tasks}
        for number, (act, lead) in enumerate([(add, away), (spread, (away[1], away[0]))]):
            base_step, high = number * steps, (number + 1) * steps
            low = min([base_step] + [t[0] for t in tasks if number == 0])
            here = [a for a in acts if low <= a[0] < high]
            edges = sorted({low, high} | {a[0] for a in here} | {e for e in bounds if low < e < high})
            for left, right in zip(edges[:-1], edges[1:]):
                for cut, n, i in here:
                    if cut == left:
                        jobs[n].advance(i)
                active = [t for t in tasks if t[0] <= left and right <= t[0] + t[1]]
                for t in active:
                    need(t[3])

                @pl.loop(left - base_step, right - base_step)
                def _(step):
                    each_way(step, lead, act)
                    for t in active:
                        t[2](step + base_step - t[0])

        for first_step, tiles, act, needs in tasks:
            done = min(max(2 * steps - first_step, 0), tiles)
            if done < tiles:
                need(needs)

                @pl.loop(done, tiles)
                def _(i):
                    act(i)

        need(range(len(operands)))
        for job in jobs:
            job.finish()

        for way in range(2):

            @pl.when(jnp.logical_not(owner[way]))
            def _():
                @pl.loop(0, count)
                def _(k):
                    onward(way, k, False).wait_send()

            @pl.when(jnp.logical_not(source[way]))
            def _():
                @pl.loop(0, count)
                def _(k):
                    back(way, k).wait_send()

            if n_out:

                @pl.when(owner[way])
                def _():
                    @pl.loop(0, count)
                    def _(k):
                        own_copy(k).wait()

    scratch = [
        pltpu.VMEM((rows, width), BF16),
        pltpu.VMEM((2, count, chunk, width), BF16),
        *[pltpu.SemaphoreType.DMA((2, count)) for _ in range(4)],
        pltpu.SemaphoreType.DMA((max(1, len(pieces)),)),
        pltpu.SemaphoreType.DMA((max(1, len(halves)),)),
        pltpu.SemaphoreType.DMA((count,)),
        pltpu.SemaphoreType.DMA((2, groups)),
        *[pltpu.VMEM((half, width), h.dtype) for h in halves],
        *[pltpu.VMEM(shape, o[0].dtype) for shape, o in zip(operand_shapes, operands)],
        *[pltpu.VMEM((half, width), F32)] * n_out,
    ]
    return pl.pallas_call(
        kernel,
        out_shape=[jax.ShapeDtypeStruct((rows, width), BF16)]
        + [jax.ShapeDtypeStruct((half, width), F32)] * n_out
        + [jax.ShapeDtypeStruct((8, width), F32)]
        + [shape for job in jobs for shape in job.out_shape],
        in_specs=[ANY] * (not product) + [WHOLE] + [ANY] * (len(halves) + len(pieces)) + [spec for job in jobs for spec in job.in_specs],
        out_specs=[WHOLE] + [ANY] * n_out + [WHOLE] + [spec for job in jobs for spec in job.out_specs],
        scratch_shapes=scratch + [shape for job in jobs for shape in job.scratch],
        compiler_params=pltpu.CompilerParams(
            collective_id=collective_id, has_side_effects=True, vmem_limit_bytes=VMEM_BYTES
        ),
        name=name,
    )(*([] if product else [part]), gain, *halves, *pieces, *[array for job in jobs for array in job.inputs])


def rms(value):
    return lax.rsqrt(jnp.mean(value * value, axis=-1, keepdims=True) + EPSILON)


def middle_rows(halves, gain, own_ref, gain_part_ref, own, total):
    middle = halves[0][own, :].astype(F32) + total
    own_ref[own, :] = middle
    return (middle * rms(middle) * gain).astype(BF16)


def output_rows(halves, gain, own_ref, gain_part_ref, own, total):
    return (halves[0][own, :] + total).astype(BF16)


def norm_back(grad, value, gain, gain_part_ref):
    inverse = rms(value)
    scaled = value * inverse
    weighted = grad * gain
    gain_part_ref[0:1, :] += jnp.sum(grad * scaled, axis=0, keepdims=True)
    return inverse * (weighted - scaled * jnp.mean(weighted * scaled, axis=-1, keepdims=True))


def grad_middle_rows(halves, gain, own_ref, gain_part_ref, own, total):
    back = norm_back(total, halves[0][own, :], gain, gain_part_ref)
    grad_middle = halves[1][own, :].astype(F32) + back
    own_ref[own, :] = grad_middle
    return grad_middle.astype(BF16)


def input_grad_rows(halves, gain, own_ref, gain_part_ref, own, total):
    back = norm_back(total, halves[0][own, :].astype(F32), gain, gain_part_ref)
    return (halves[1][own, :] + back).astype(BF16)


def lower_ones(length):
    at = lax.broadcasted_iota(jnp.int32, (length, length), 0)
    before = lax.broadcasted_iota(jnp.int32, (length, length), 1)
    return at >= before


def chunk_decay(forget, gap, live, lower):
    closing = sigmoid(-forget)
    opened = gap * closing
    remain = 1.0 - opened
    decay = jnp.where(live, jnp.log(remain), 0.0)
    keys = jnp.where(live, opened, 0.0)
    return closing, remain, keys, ones_times(lower, decay)


def rows_live(valid_ref, chunk_index, length):
    at = lax.broadcasted_iota(jnp.int32, (length, HEAD_DIM), 0) + chunk_index * length
    return at < valid_ref[0]


def span_end_kernel(heads, length, valid_ref, forget_ref, value_ref, gap_ref, end_ref):
    index = pl.program_id(0)

    @pl.when(index == 0)
    def _():
        end_ref[...] = jnp.zeros_like(end_ref)

    live = rows_live(valid_ref, index, length)
    lower = lower_ones(length).astype(BF16)
    for h in range(heads):
        cols = slice(h * HEAD_DIM, (h + 1) * HEAD_DIM)
        _, _, keys, cumulative = chunk_decay(forget_ref[:, cols], gap_ref[:, cols], live, lower)
        total = cumulative[length - 1 :, :]
        tail = (keys * jnp.exp(total - cumulative)).astype(BF16)
        end_ref[h] = jnp.exp(total) * end_ref[h] + dot(value_ref[:, cols].astype(BF16), tail, TN)


def mix_kernel(
    heads, length, valid_ref, query_ref, forget_ref, value_ref, gate_ref, gap_ref, gain_ref, start_ref,
    gated_ref, mixed_ref, states_ref, end_ref, state_ref,
):
    index = pl.program_id(0)

    @pl.when(index == 0)
    def _():
        state_ref[...] = start_ref[...]

    live = rows_live(valid_ref, index, length)
    mask = lower_ones(length)
    lower = mask.astype(BF16)
    for h in range(heads):
        cols = slice(h * HEAD_DIM, (h + 1) * HEAD_DIM)
        _, _, keys, cumulative = chunk_decay(forget_ref[:, cols], gap_ref[:, cols], live, lower)
        pre = query_ref[:, cols]
        queries = (pre * sigmoid(pre) * jnp.exp(cumulative)).astype(BF16)
        shrunk = keys * jnp.exp(-cumulative)
        values = value_ref[:, cols].astype(BF16)
        state = state_ref[h]
        states_ref[0, h] = state
        scores = jnp.where(mask, dot(queries, shrunk.astype(BF16), NT), 0.0).astype(BF16)
        mixed = dot(scores, values) + dot(queries, state.astype(BF16), NT)
        mixed_ref[:, cols] = mixed
        growth = jnp.exp(cumulative[length - 1 :, :])
        state_ref[h] = growth * state + dot(values, (shrunk * growth).astype(BF16), TN)
        gate = gate_ref[:, cols]
        gated_ref[:, cols] = (mixed * rms(mixed) * gain_ref[...] * (gate * sigmoid(gate))).astype(BF16)

    @pl.when(index == pl.num_programs(0) - 1)
    def _():
        end_ref[...] = state_ref[...]


def span_begin_kernel(heads, length, *refs):
    span_begin_chunk(heads, length, pl.program_id(0), pl.num_programs(0), *refs)


def span_begin_chunk(
    heads, length, step, steps, valid_ref, grad_ref, mixed_ref, query_ref, forget_ref, gate_ref, gap_ref, gain_ref,
    grad_gate_ref, grad_mixed_ref, gain_part_ref, begin_ref,
):
    index = steps - 1 - step

    @pl.when(step == 0)
    def _():
        begin_ref[...] = jnp.zeros_like(begin_ref)
        gain_part_ref[...] = jnp.zeros_like(gain_part_ref)

    live = rows_live(valid_ref, index, length)
    lower = lower_ones(length).astype(BF16)
    gain = gain_ref[...]
    for h in range(heads):
        cols = slice(h * HEAD_DIM, (h + 1) * HEAD_DIM)
        mixed = mixed_ref[:, cols]
        inverse = rms(mixed)
        scaled = mixed * inverse
        gate = gate_ref[:, cols]
        sig = sigmoid(gate)
        grad = grad_ref[:, cols].astype(F32)
        grad_gate_ref[:, cols] = (grad * scaled * gain * slope(gate, sig)).astype(BF16)
        grad_scaled = grad * (gate * sig)
        gain_part_ref[...] += jnp.sum(grad_scaled * scaled, axis=0, keepdims=True)
        weighted = grad_scaled * gain
        grad_mixed = inverse * (weighted - scaled * jnp.mean(weighted * scaled, axis=-1, keepdims=True))
        grad_mixed = grad_mixed.astype(BF16)
        grad_mixed_ref[:, cols] = grad_mixed
        _, _, _, cumulative = chunk_decay(forget_ref[:, cols], gap_ref[:, cols], live, lower)
        pre = query_ref[:, cols]
        queries = (pre * sigmoid(pre) * jnp.exp(cumulative)).astype(BF16)
        growth = jnp.exp(cumulative[length - 1 :, :])
        begin_ref[h] = growth * begin_ref[h] + dot(grad_mixed, queries, TN)


def mix_back_kernel(heads, length, *refs):
    mix_back_chunk(heads, length, pl.program_id(0), pl.num_programs(0), *refs)


def mix_back_chunk(
    heads, length, step, steps, valid_ref, grad_ref, query_ref, forget_ref, value_ref, gap_ref, states_ref, last_ref,
    end_ref, grad_query_ref, grad_forget_ref, grad_value_ref, gap_part_ref, flow_ref, after_ref,
):
    index = steps - 1 - step

    @pl.when(step == 0)
    def _():
        flow_ref[...] = end_ref[...]
        after_ref[...] = last_ref[...]
        gap_part_ref[...] = jnp.zeros_like(gap_part_ref)

    live = rows_live(valid_ref, index, length)
    mask = lower_ones(length)
    lower = mask.astype(BF16)
    for h in range(heads):
        cols = slice(h * HEAD_DIM, (h + 1) * HEAD_DIM)
        gap = gap_ref[:, cols]
        closing, remain, keys, cumulative = chunk_decay(forget_ref[:, cols], gap, live, lower)
        pre = query_ref[:, cols]
        sig = sigmoid(pre)
        growth = jnp.exp(cumulative)
        shrink = jnp.exp(-cumulative)
        end_growth = growth[length - 1 :, :]
        queries = (pre * sig * growth).astype(BF16)
        shrunk_wide = keys * shrink
        shrunk = shrunk_wide.astype(BF16)
        tail = (shrunk_wide * end_growth).astype(BF16)
        values = value_ref[:, cols].astype(BF16)
        grad = grad_ref[:, cols]
        state = states_ref[0, h]
        flow = flow_ref[h]
        low_flow = flow.astype(BF16)
        scores = jnp.where(mask, dot(queries, shrunk, NT), 0.0).astype(BF16)
        grad_scores = jnp.where(mask, dot(grad, values, NT), 0.0).astype(BF16)
        to_queries = dot(grad, state.astype(BF16)) + dot(grad_scores, shrunk)
        to_keys = dot(grad_scores, queries, TN) + end_growth * dot(values, low_flow)
        grad_value_ref[:, cols] = (dot(scores, grad, TN) + dot(tail, low_flow, NT)).astype(BF16)
        grad_query_ref[:, cols] = (to_queries * growth * slope(pre, sig)).astype(BF16)
        terms = queries.astype(F32) * to_queries - shrunk.astype(F32) * to_keys
        high = terms.astype(BF16)
        rest = (terms - high.astype(F32)).astype(BF16)
        suffix = dot(lower, high, TN) + dot(lower, rest, TN)
        crossing = jnp.sum(flow * after_ref[h], axis=0, keepdims=True)
        pressure = jnp.where(live, to_keys * shrink - (suffix + crossing) / remain, 0.0)
        gap_part_ref[:, cols] += jnp.sum(closing * pressure, axis=0, keepdims=True)
        grad_forget_ref[:, cols] = (-closing * (1.0 - closing) * gap * pressure).astype(BF16)
        flow_ref[h] = end_growth * flow + dot(grad, queries, TN)
        after_ref[h] = state


def plain_call(kernel, name, grid, in_specs, out_specs, out_shape, scratch, flops, moved):
    return pl.pallas_call(
        kernel,
        grid_spec=pltpu.PrefetchScalarGridSpec(
            num_scalar_prefetch=1, grid=grid, in_specs=in_specs, out_specs=out_specs, scratch_shapes=scratch
        ),
        out_shape=out_shape,
        compiler_params=pltpu.CompilerParams(
            dimension_semantics=("arbitrary",), vmem_limit_bytes=VMEM_BYTES
        ),
        cost_estimate=pl.CostEstimate(flops=flops, bytes_accessed=moved, transcendentals=flops // 64),
        name=name,
    )


def combine(earlier, later):
    return (earlier[0] * later[0], later[0][:, None, :] * earlier[1] + later[1])


def from_earlier(state, decay, axis):
    size = lax.axis_size(axis)
    if size == 2:
        return lax.ppermute(state, axis, [(0, 1)])
    mine = lax.axis_index(axis)
    states, decays = lax.all_gather(state, axis), lax.all_gather(decay, axis)
    total = jnp.zeros_like(state)
    for k in range(size):
        new = decays[k][:, None, :] * total + states[k]
        total = jnp.where(k < mine, new, total)
    return total


def from_later(state, decay, axis):
    size = lax.axis_size(axis)
    if size == 2:
        return lax.ppermute(state, axis, [(1, 0)])
    mine = lax.axis_index(axis)
    states, decays = lax.all_gather(state, axis), lax.all_gather(decay, axis)
    total = jnp.zeros_like(state)
    for k in reversed(range(size)):
        new = decays[k][:, None, :] * total + states[k]
        total = jnp.where(k > mine, new, total)
    return total


def per_device(
    inputs, lengths, w_query, w_forget, w_input, w_outgate, w_output, w_gate, w_up, w_down,
    norm_gain, ffn_gain, head_gain, forget_gap, cotangent,
):
    groups, span, width = inputs.shape
    rows = groups * span
    fsdp, ctx, tp = lax.axis_size("fsdp"), lax.axis_size("ctx"), lax.axis_size("tp")
    local = forget_gap.shape[0]
    heads = local // HEAD_DIM
    ff = w_gate.shape[1]
    length = min(128, span)
    chunks = span // length
    place = lax.axis_index("tp")

    valid = jnp.clip(lengths - lax.axis_index("ctx") * span, 0, span).astype(jnp.int32)
    x = inputs.reshape(rows, width)
    gap = forget_gap.reshape(1, local)
    head_row = head_gain.reshape(1, HEAD_DIM)
    norm_row, ffn_row = norm_gain.reshape(1, width), ffn_gain.reshape(1, width)

    pre, normed, grad_low, w_four, w_out = project(
        x, cotangent.reshape(rows, width), norm_row, valid, [w_query, w_forget, w_input, w_outgate], w_output, 1
    )

    def column(j):
        return pl.BlockSpec((length, local), lambda i, *_: (i, j))

    def column_back(j):
        return pl.BlockSpec((length, local), lambda i, *_: (chunks - 1 - i, j))

    fixed = lambda shape: pl.BlockSpec(shape, lambda i, *_: (0,) * len(shape))
    state_shape = (heads, HEAD_DIM, HEAD_DIM)
    work = 2 * rows * local * HEAD_DIM
    moved = rows * local * 4

    local_end = plain_call(
        functools.partial(span_end_kernel, heads, length), "span_end", (chunks,),
        [column(1), column(2), fixed((1, local))], fixed(state_shape),
        jax.ShapeDtypeStruct(state_shape, F32), [], 3 * work, 2 * moved,
    )(valid, pre, pre, gap)
    span_decay = None
    if ctx > 2:
        keep = (jnp.arange(rows, dtype=jnp.int32) < valid[0])[:, None]
        closing = jax.nn.sigmoid(-pre[:, local : 2 * local])
        logs = jnp.where(keep, jnp.log(1.0 - gap * closing), 0.0)
        span_decay = jnp.exp(jnp.sum(logs, axis=0)).reshape(heads, HEAD_DIM)
    start = from_earlier(local_end, span_decay, "ctx")
    gated, mixed, states, state_end = plain_call(
        functools.partial(mix_kernel, heads, length), "mix", (chunks,),
        [column(0), column(1), column(2), column(3), fixed((1, local)), fixed((1, HEAD_DIM)), fixed(state_shape)],
        [column(0), column(0), pl.BlockSpec((1,) + state_shape, lambda i, *_: (i, 0, 0, 0)), fixed(state_shape)],
        [
            jax.ShapeDtypeStruct((rows, local), BF16),
            jax.ShapeDtypeStruct((rows, local), F32),
            jax.ShapeDtypeStruct((chunks,) + state_shape, F32),
            jax.ShapeDtypeStruct(state_shape, F32),
        ],
        [pltpu.VMEM(state_shape, F32)], 6 * work, 6 * moved,
    )(valid, pre, pre, pre, pre, gap, head_row, start)

    normed_two, middle, _, w_both, w_back = line_sum(
        "sum_branch", (0, 1, NN), [x], ffn_row, 1, middle_rows, 2,
        [
            GatherJob(
                [w_gate, w_up, w_down],
                [(fsdp * w_gate.shape[0], 2 * ff), (ff, width)],
                [(0, 0, 0), (0, 0, ff), (1, 1, 0)],
            )
        ],
        [gated, w_out],
    )

    both = dot(normed_two, w_both)
    gate_hidden, up_hidden = both[:, :ff], both[:, ff:]
    sig = jax.nn.sigmoid(gate_hidden)
    act = gate_hidden * sig
    hidden = (act * up_hidden).astype(BF16)

    grad_hidden = dot(grad_low, w_back, NT)
    grad_gate = (grad_hidden * up_hidden * slope(gate_hidden, sig)).astype(BF16)
    grad_up = (grad_hidden * act).astype(BF16)
    both_axes = ("fsdp", "ctx")

    def scattered(grads, dims):
        if ctx == 2:
            return [ScatterJob(grads, dims)], None
        return [], [
            lax.psum_scatter(g, both_axes, scatter_dimension=d, tiled=True).astype(F32) for g, d in zip(grads, dims)
        ]

    grad_branch, grad_middle, ffn_gain_part, grad_w_down, grad_w_both = line_sum(
        "sum_norm_two", (0, 1, NT), [middle, grad_low], ffn_row, 1, grad_middle_rows, 3,
        [ProductJob(2, 3, TN, (ff, width), 128), ProductJob(4, 0, TN, (width, 2 * ff), 128)],
        [(grad_gate, grad_up), w_both, hidden, grad_low, normed_two],
    )

    jobs, sums_ffn = scattered([grad_w_both, grad_w_down], [0, 1])
    if ctx == 2:
        jobs.append(MixBackJob(valid, grad_branch, w_out, mixed, pre, states, gap, head_row, state_end))
    result, _, *more = line_sum(
        "sum_feed", (0, 1, NN), [middle], ffn_row, 0, output_rows, 5, jobs, [hidden, w_back]
    )
    result = result.reshape(groups, span, width)
    if ctx == 2:
        out_both, out_down, grad_query, grad_forget, grad_value, grad_outgate, gap_part, head_part = more
    else:
        out_both, out_down = sums_ffn
        grad_gated = dot(grad_branch, w_out, NT)
        grad_outgate, grad_mixed, head_part, local_begin = plain_call(
            functools.partial(span_begin_kernel, heads, length), "span_begin", (chunks,),
            [column_back(0), column_back(0), column_back(0), column_back(1), column_back(3), fixed((1, local)),
             fixed((1, HEAD_DIM))],
            [column_back(0), column_back(0), fixed((1, HEAD_DIM)), fixed(state_shape)],
            [
                jax.ShapeDtypeStruct((rows, local), BF16),
                jax.ShapeDtypeStruct((rows, local), BF16),
                jax.ShapeDtypeStruct((1, HEAD_DIM), F32),
                jax.ShapeDtypeStruct(state_shape, F32),
            ],
            [], 3 * work, 6 * moved,
        )(valid, grad_gated, mixed, pre, pre, pre, gap, head_row)
        grad_end = from_later(local_begin, span_decay, "ctx")
        grad_query, grad_forget, grad_value, gap_part = plain_call(
            functools.partial(mix_back_kernel, heads, length), "mix_back", (chunks,),
            [column_back(0), column_back(0), column_back(1), column_back(2), fixed((1, local)),
             pl.BlockSpec((1,) + state_shape, lambda i, *_: (chunks - 1 - i, 0, 0, 0)), fixed(state_shape),
             fixed(state_shape)],
            [column_back(0), column_back(0), column_back(0), fixed((1, local))],
            [jax.ShapeDtypeStruct((rows, local), BF16)] * 3 + [jax.ShapeDtypeStruct((1, local), F32)],
            [pltpu.VMEM(state_shape, F32), pltpu.VMEM(state_shape, F32)], 12 * work, 6 * moved,
        )(valid, grad_mixed, pre, pre, pre, gap, states, state_end, grad_end)

    grad_four = (grad_query, grad_forget, grad_value, grad_outgate)
    jobs, operands, sums_mix = [VectorJob(ffn_gain_part, head_part, gap_part)], [grad_four, w_four], None
    if ctx == 2:
        shapes = [(width, 4 * local), (local, width)]
        jobs.append(ProductScatterJob([(2, 0), (3, 4)], shapes, [0, 1]))
        operands += [normed, gated, grad_branch]
    else:
        grads = [dot(normed, jnp.concatenate(grad_four, axis=1), TN).astype(BF16), dot(gated, grad_branch, TN).astype(BF16)]
        _, sums_mix = scattered(grads, [0, 1])
    input_grad, _, sums, *more = line_sum(
        "sum_norm_one", (0, 1, NT), [x, grad_middle], norm_row, 0, input_grad_rows, 4, jobs, operands
    )
    out_four, out_output = sums_mix or more
    input_grad = input_grad.reshape(groups, span, width)
    grad_norm_gain, grad_ffn_gain, grad_head_gain = sums[0], sums[1], sums[2, :HEAD_DIM]
    grad_gap = lax.dynamic_slice(sums[3], (place * local,), (local,))
    return (
        result,
        input_grad,
        out_four[:, :local],
        out_four[:, local : 2 * local],
        out_four[:, 2 * local : 3 * local],
        out_four[:, 3 * local :],
        out_output,
        out_both[:, :ff],
        out_both[:, ff:],
        out_down,
        grad_norm_gain,
        grad_ffn_gain,
        grad_head_gain,
        grad_gap,
    )


def solution(mesh):
    tokens = P("fsdp", "ctx", None)
    inward, outward = P("fsdp", "tp"), P("tp", "fsdp")
    grad_in, grad_back = P(("fsdp", "ctx"), "tp"), P("tp", ("fsdp", "ctx"))
    return jax.shard_map(
        per_device,
        mesh=mesh,
        in_specs=(tokens, P("fsdp")) + (inward,) * 4 + (outward, inward, inward, outward)
        + (P(), P(), P(), P("tp"), tokens),
        out_specs=(tokens, tokens) + (grad_in,) * 4 + (grad_back, grad_in, grad_in, grad_back)
        + (P(), P(), P(), P("tp")),
        check_vma=False,
    )
```

```python
import functools

import jax
import jax.numpy as jnp
from jax import lax
from jax.experimental import pallas as pl
from jax.experimental.pallas import tpu as pltpu
from jax.sharding import PartitionSpec as P

HEAD_DIM = 128
EPSILON = 1e-05
F32 = jnp.float32
BF16 = jnp.bfloat16
BY_AXIS = pl.DeviceIdType.MESH
VMEM_BYTES = 67043328
ANY = pl.BlockSpec(memory_space=pl.ANY)
WHOLE = pl.BlockSpec(memory_space=pltpu.VMEM)


def dot(left, right, dims=((1,), (0,))):
    return lax.dot_general(left, right, (dims, ((), ())), preferred_element_type=F32)


NN = ((1,), (0,))
NT = ((1,), (1,))
TN = ((0,), (0,))


def sigmoid(value):
    return 1.0 / (1.0 + jnp.exp(-value))


def slope(pre, sig):
    return sig * (1.0 + pre * (1.0 - sig))


def ones_times(ones, value):
    high = value.astype(BF16)
    rest = (value - high.astype(F32)).astype(BF16)
    return dot(ones, high) + dot(ones, rest)


def ring_place(index, size, folded):
    if folded:
        return index + (index // 2) * (1 - 2 * (index % 2))
    return index


class RingGather:
    def __init__(self, shards, outs, where, sems, size, folded):
        self.shards, self.outs, self.where, self.size = shards, outs, where, size
        self.ring_send, self.ring_recv, self.pair_send, self.pair_recv, self.local = sems
        self.place = ring_place(lax.axis_index("fsdp"), size, folded)
        self.folded = folded
        self.core = lax.axis_index("ctx") % 2
        self.pair = lax.axis_index("ctx") + 1 - 2 * self.core

    def device(self, place):
        return ring_place(lax.rem(place + 2 * self.size, self.size), self.size, self.folded)

    def peers(self):
        return [
            {"fsdp": self.device(self.place + 1)},
            {"fsdp": self.device(self.place - 1)},
            {"ctx": self.pair},
        ]

    def rows(self, i, core, way):
        quarter = self.shards[i].shape[0] // 4
        return pl.multiple_of((2 * way + core) * quarter, 16), quarter

    def in_shard(self, i, core, way):
        at, length = self.rows(i, core, way)
        return self.shards[i].at[pl.ds(at, length), :]

    def in_out(self, i, block, core, way):
        out, dim, column = self.where[i]
        at, length = self.rows(i, core, way)
        deep, wide = self.shards[i].shape
        if dim == 0:
            start = pl.multiple_of(block * deep + at, 16)
            return self.outs[out].at[pl.ds(start, length), pl.ds(column, wide)]
        start = pl.multiple_of(block * wide, 128)
        return self.outs[out].at[pl.ds(at, length), pl.ds(start, wide)]

    def own_block(self, i):
        out, dim, column = self.where[i]
        deep, wide = self.shards[i].shape
        block = self.device(self.place)
        if dim == 0:
            start = pl.multiple_of(block * deep, 16)
            return self.outs[out].at[pl.ds(start, deep), pl.ds(column, wide)]
        return self.outs[out].at[:, pl.ds(pl.multiple_of(block * wide, 128), wide)]

    def local_copy(self, i):
        return pltpu.make_async_copy(self.shards[i], self.own_block(i), self.local.at[i])

    def ring(self, i, way, step):
        sign = 1 - 2 * way
        block = self.device(self.place - sign * step)
        there = self.in_out(i, block, self.core, way)
        here = self.in_shard(i, self.core, way) if step == 0 else there
        at = (i * 2 + way) * (self.size - 1) + step
        return pltpu.make_async_remote_copy(
            src_ref=here,
            dst_ref=there,
            send_sem=self.ring_send.at[at],
            recv_sem=self.ring_recv.at[at],
            device_id={"fsdp": self.device(self.place + sign)},
            device_id_type=BY_AXIS,
        )

    def across(self, i, way, step, core):
        sign = 1 - 2 * way
        block = self.device(self.place - sign * (step + 1))
        piece = self.in_out(i, block, core, way)
        at = (i * 2 + way) * (self.size - 1) + step
        return pltpu.make_async_remote_copy(
            src_ref=piece,
            dst_ref=piece,
            send_sem=self.pair_send.at[at],
            recv_sem=self.pair_recv.at[at],
            device_id={"ctx": self.pair},
            device_id_type=BY_AXIS,
        )

    def each(self):
        return [(i, way) for i in range(len(self.shards)) for way in range(2)]

    def start(self):
        for i, way in self.each():
            self.ring(i, way, 0).start()
        for i in range(len(self.shards)):
            self.local_copy(i).start()

    def advance(self, step):
        for i, way in self.each():
            arrived = self.ring(i, way, step)
            arrived.wait_recv()
            if step + 1 < self.size - 1:
                self.ring(i, way, step + 1).start()
            self.across(i, way, step, self.core).start()

    def wait_across(self, arrays, step):
        for i in arrays:
            for way in range(2):
                self.across(i, way, step, 1 - self.core).wait_recv()

    def finish(self, waited=()):
        for i, way in self.each():
            for step in range(self.size - 1):
                self.ring(i, way, step).wait_send()
                self.across(i, way, step, self.core).wait_send()
                if i not in waited:
                    self.across(i, way, step, 1 - self.core).wait_recv()
        for i in range(len(self.shards)):
            if i not in waited:
                self.local_copy(i).wait()

    @staticmethod
    def scratch(count, size):
        copies = count * 2 * (size - 1)
        return [pltpu.SemaphoreType.DMA((copies,)) for _ in range(4)] + [
            pltpu.SemaphoreType.DMA((count,))
        ]


class RingScatter:
    def __init__(self, grads, outs, dims, scratch, sems, size, folded):
        self.grads, self.outs, self.dims, self.size, self.folded = grads, outs, dims, size, folded
        count = len(grads)
        self.own, self.came, self.passed = scratch[:count], scratch[count : 2 * count], scratch[2 * count :]
        self.pair_send, self.pair_recv, self.local, self.ring_send, self.ring_recv = sems
        self.place = ring_place(lax.axis_index("fsdp"), size, folded)
        self.core = lax.axis_index("ctx")

    device = RingGather.device

    def peers(self):
        return [
            {"fsdp": self.device(self.place + 1)},
            {"fsdp": self.device(self.place - 1)},
            {"ctx": 1 - self.core},
        ]

    def block(self, i, offset, core):
        index = self.device(self.place + offset) * 2 + core
        extent = self.outs[i].shape[self.dims[i]]
        start = pl.multiple_of(index * extent, extent)
        if self.dims[i] == 0:
            return self.grads[i].at[pl.ds(start, extent), :]
        return self.grads[i].at[:, pl.ds(start, extent)]

    def local_copy(self, i, offset):
        return pltpu.make_async_copy(
            self.block(i, offset, self.core), self.own[i].at[offset], self.local.at[i * self.size + offset]
        )

    def across(self, i, offset):
        at = i * self.size + offset
        give = self.own[i].at[0, offset] if self.grads[i] is None else self.block(i, offset, 1 - self.core)
        return pltpu.make_async_remote_copy(
            src_ref=give,
            dst_ref=self.came[i].at[offset],
            send_sem=self.pair_send.at[at],
            recv_sem=self.pair_recv.at[at],
            device_id={"ctx": 1 - self.core},
            device_id_type=BY_AXIS,
        )

    def offset(self, way, step):
        return (-(step + 1) if way == 0 else step + 1) % self.size

    def ring(self, i, way, step):
        half = self.outs[i].shape[0] // 2
        at = (i * 2 + way) * (self.size - 1) + step
        return pltpu.make_async_remote_copy(
            src_ref=self.came[i].at[self.offset(way, step), pl.ds(way * half, half), :],
            dst_ref=self.passed[i].at[way, step],
            send_sem=self.ring_send.at[at],
            recv_sem=self.ring_recv.at[at],
            device_id={"fsdp": self.device(self.place + 1 - 2 * way)},
            device_id_type=BY_AXIS,
        )

    def order(self):
        used = []
        for step in range(self.size):
            for way in range(2):
                if self.offset(way, step) not in used:
                    used.append(self.offset(way, step))
        return used

    def start(self):
        for offset in self.order():
            for i in range(len(self.grads)):
                self.across(i, offset).start()
                self.local_copy(i, offset).start()

    def advance(self, step):
        before = {self.offset(way, s) for s in range(step) for way in range(2)}
        fresh = {self.offset(way, step) for way in range(2)} - before
        for i in range(len(self.grads)):
            for offset in sorted(fresh):
                self.across(i, offset).wait_recv()
                if self.grads[i] is not None:
                    self.local_copy(i, offset).wait()
            for way in range(2):
                if step > 0:
                    self.ring(i, way, step - 1).wait_recv()
                self.add(i, way, step)
                if step < self.size - 1:
                    self.ring(i, way, step).start()

    def add(self, i, way, step):
        half = self.outs[i].shape[0] // 2
        offset = self.offset(way, step)
        own, came, passed, out = self.own[i], self.came[i], self.passed[i], self.outs[i]

        @pl.loop(0, half // 16)
        def _(r):
            rows = pl.ds(pl.multiple_of(way * half + r * 16, 16), 16)
            kept = own[offset, rows, :] if self.grads[i] is not None else own[1, offset, rows, :]
            total = kept.astype(F32) + came[offset, rows, :].astype(F32)
            if step > 0:
                total += passed[way, step - 1, pl.ds(pl.multiple_of(r * 16, 16), 16), :].astype(F32)
            if step < self.size - 1:
                came[offset, rows, :] = total.astype(BF16)
            else:
                out[rows, :] = total

    def finish(self):
        for i in range(len(self.grads)):
            for offset in range(self.size):
                self.across(i, offset).wait_send()
            for way in range(2):
                for step in range(self.size - 1):
                    self.ring(i, way, step).wait_send()

    @staticmethod
    def out_shape(grad, dim, size):
        deep, wide = grad.shape
        return (deep // (2 * size), wide) if dim == 0 else (deep, wide // (2 * size))

    @staticmethod
    def buffers(shapes, size):
        full = [pltpu.VMEM((size,) + s, BF16) for s in shapes]
        return full + full + [pltpu.VMEM((2, size - 1, s[0] // 2, s[1]), BF16) for s in shapes]

    @staticmethod
    def scratch(count, size):
        return [pltpu.SemaphoreType.DMA((count * size,)) for _ in range(3)] + [
            pltpu.SemaphoreType.DMA((count * 2 * (size - 1),)) for _ in range(2)
        ]


def meet(peers):
    barrier = pltpu.get_barrier_semaphore()
    total = 0
    for condition, peer in peers:
        if condition is None:
            pl.semaphore_signal(barrier, inc=1, device_id=peer, device_id_type=BY_AXIS)
            total = total + 1
        else:

            @pl.when(condition)
            def _():
                pl.semaphore_signal(barrier, inc=1, device_id=peer, device_id_type=BY_AXIS)

            total = total + condition.astype(jnp.int32)
    pl.semaphore_wait(barrier, total)


def project(x, cotangent, gain, valid, shards, w_out_shard, collective_id):
    size = lax.axis_size("fsdp")
    rows, width = x.shape
    deep, local = shards[0].shape
    count = len(shards)
    total = count * local
    half = deep // 2
    tile = min(512, total)
    step_rows = min(64, rows)
    row_tile = min(512, rows)
    copies = 1 + 2 * (size - 1)

    def kernel(
        valid_ref, gain_ref, x_ref, cot_ref, *refs
    ):
        shard_refs, refs = refs[: count + 1], refs[count + 1 :]
        pre_ref, normed_ref, grad_ref, four_ref, out_ref = refs[:5]
        x_here, grad_here, normed, acc, four, in_sem, save_sem, four_sem, pre_sem = refs[5:14]
        where = [(0, 0, i * local) for i in range(count)] + [(1, 1, 0)]
        job = RingGather(shard_refs, [four, out_ref], where, refs[14:], size, size == 4)
        loads = [
            pltpu.make_async_copy(x_ref, x_here, in_sem.at[0]),
            pltpu.make_async_copy(cot_ref, grad_here, in_sem.at[1]),
        ]
        for load in loads:
            load.start()
        meet([(None, peer) for peer in job.peers()])
        job.start()
        loads[0].wait()

        @pl.loop(0, rows // step_rows)
        def _(r):
            at = pl.ds(pl.multiple_of(r * step_rows, step_rows), step_rows)
            wide = x_here[at, :].astype(F32)
            normed[at, :] = (wide * rms(wide) * gain_ref[...]).astype(BF16)

        saves = [
            pltpu.make_async_copy(normed, normed_ref, save_sem.at[0]),
            pltpu.make_async_copy(grad_here, grad_ref, save_sem.at[1]),
        ]
        saves[0].start()

        def save_four(start, length, number):
            at = pl.ds(start, length)
            return pltpu.make_async_copy(four.at[at, :], four_ref.at[at, :], four_sem.at[number])

        def save_pre(n):
            at = pl.ds(pl.multiple_of(n * tile, tile), tile)
            return pltpu.make_async_copy(acc.at[:, at], pre_ref.at[:, at], pre_sem.at[n])

        def multiply(start, length, first, last):
            @pl.loop(0, total // tile)
            def _(n):
                cols = pl.ds(pl.multiple_of(n * tile, tile), tile)
                deep_at = pl.ds(start, length)

                @pl.loop(0, rows // row_tile)
                def _(r):
                    at = pl.ds(pl.multiple_of(r * row_tile, row_tile), row_tile)
                    term = dot(normed[at, deep_at], four[deep_at, cols])
                    acc[at, cols] = term if first else acc[at, cols] + term

                if last:
                    save_pre(n).start()

        for i in range(count):
            job.local_copy(i).wait()
        own = pl.multiple_of(job.device(job.place) * deep, deep)
        save_four(own, deep, 0).start()
        multiply(own, deep, True, False)
        loads[1].wait()

        @pl.loop(0, rows // step_rows)
        def _(r):
            at = pl.ds(pl.multiple_of(r * step_rows, step_rows), step_rows)
            row = lax.broadcasted_iota(jnp.int32, (step_rows, width), 0) + r * step_rows
            wide = grad_here[at, :].astype(F32)
            grad_here[at, :] = jnp.where(row < valid_ref[0], wide, 0.0).astype(BF16)

        saves[1].start()
        for step in range(size - 1):
            job.advance(step)
            job.wait_across(range(count), step)
            for way in range(2):
                block = job.device(job.place - (1 - 2 * way) * (step + 1))
                start = pl.multiple_of(block * deep + way * half, half)
                save_four(start, half, 1 + 2 * step + way).start()
                multiply(start, half, False, step == size - 2 and way == 1)
        job.finish(range(count))
        for save in saves:
            save.wait()
        save_four(own, deep, 0).wait()
        for step in range(size - 1):
            for way in range(2):
                save_four(0, half, 1 + 2 * step + way).wait()
        for n in range(total // tile):
            save_pre(n).wait()

    return pl.pallas_call(
        kernel,
        out_shape=[
            jax.ShapeDtypeStruct((rows, total), F32),
            jax.ShapeDtypeStruct((rows, width), BF16),
            jax.ShapeDtypeStruct((rows, width), BF16),
            jax.ShapeDtypeStruct((width, total), BF16),
            jax.ShapeDtypeStruct((w_out_shard.shape[0], width), BF16),
        ],
        in_specs=[pl.BlockSpec(memory_space=pltpu.SMEM), WHOLE, ANY, ANY] + [WHOLE] * (count + 1),
        out_specs=[ANY] * 5,
        scratch_shapes=[
            pltpu.VMEM((rows, width), BF16),
            pltpu.VMEM((rows, width), BF16),
            pltpu.VMEM((rows, width), BF16),
            pltpu.VMEM((rows, total), F32),
            pltpu.VMEM((width, total), BF16),
            pltpu.SemaphoreType.DMA((2,)),
            pltpu.SemaphoreType.DMA((2,)),
            pltpu.SemaphoreType.DMA((copies,)),
            pltpu.SemaphoreType.DMA((total // tile,)),
        ]
        + RingGather.scratch(count + 1, size),
        compiler_params=pltpu.CompilerParams(
            collective_id=collective_id, has_side_effects=True, vmem_limit_bytes=VMEM_BYTES
        ),
        name="project",
    )(valid, gain, x, cotangent, *shards, w_out_shard)


class Job:
    first = 0

    def tasks(self):
        return []

    def follow(self, step, ways):
        pass


class ForwardJob(Job):
    def __init__(self, shards, grad_low, rows_in_group, first):
        self.size = lax.axis_size("fsdp")
        self.rows, self.width = grad_low.shape
        self.ff = shards[0].shape[1]
        self.group, self.first = rows_in_group, first
        self.inputs, self.in_specs = [*shards, grad_low], [ANY] * 4
        self.out_shape = [
            jax.ShapeDtypeStruct((self.width, 2 * self.ff), BF16),
            jax.ShapeDtypeStruct((self.ff, self.width), BF16),
            *[jax.ShapeDtypeStruct((self.rows, self.ff), BF16)] * 3,
        ]
        self.out_specs = [ANY] * 5
        self.scratch = [
            pltpu.VMEM((self.width, 2 * self.ff), BF16),
            pltpu.VMEM((self.ff, self.width), BF16),
            pltpu.VMEM((self.rows, self.width), BF16),
            pltpu.VMEM((2, self.group, 2 * self.ff), F32),
            pltpu.VMEM((2, 3, self.group, self.ff), BF16),
            pltpu.SemaphoreType.DMA((3,)),
            pltpu.SemaphoreType.DMA((2, 3)),
            *RingGather.scratch(2, self.size),
            *RingGather.scratch(1, self.size),
        ]

    def bind(self, ins, outs, scratch):
        self.grad_low = ins[3]
        self.both_out, self.back_out, *self.outs = outs
        self.both, self.back, self.grad_here, self.products, self.stage, self.sem, self.stage_sem = scratch[:7]
        size = self.size
        self.inward = RingGather(ins[:2], [self.both], [(0, 0, 0), (0, 0, self.ff)], scratch[7:12], size, size == 4)
        self.outward = RingGather(ins[2:3], [self.back], [(0, 1, 0)], scratch[12:], size, size == 4)

    def peers(self):
        return self.inward.peers()

    def cuts(self, steps):
        ring = self.size - 1
        ahead = [((16 * (i + 1)) // ring * steps) // 20 for i in range(ring)]
        return ahead + [((16 + (9 * (i + 1)) // ring) * steps) // 20 for i in range(ring)]

    def load(self):
        return pltpu.make_async_copy(self.grad_low, self.grad_here, self.sem.at[0])

    def keep(self):
        return [
            pltpu.make_async_copy(self.both, self.both_out, self.sem.at[1]),
            pltpu.make_async_copy(self.back, self.back_out, self.sem.at[2]),
        ]

    def start(self):
        self.inward.start()
        self.load().start()

    def advance(self, number):
        ring = self.size - 1
        if number < ring:
            self.inward.advance(number)
            if number == max(0, ring - 2):
                self.outward.start()
            return
        self.outward.advance(number - ring)
        if number == 2 * ring - 1:
            for step in range(ring):
                self.inward.wait_across(range(2), step)
                self.outward.wait_across(range(1), step)
            for i in range(2):
                self.inward.local_copy(i).wait()
            self.outward.local_copy(0).wait()
            self.load().wait()
            for copy in self.keep():
                copy.start()

    def save(self, way, k, at):
        return pltpu.make_async_copy(self.stage.at[way, k], self.outs[k].at[at, :], self.stage_sem.at[way, k])

    def follow(self, step, ways):
        normed, begins, periods, groups, bases = ways

        @pl.loop(0, 2)
        def _(way):
            begin, period, base = (jnp.where(way == 0, pair[0], pair[1]) for pair in (begins, periods, bases))
            k = step - begin
            g = lax.div(k, period)
            part = lax.rem(k, period)
            busy = jnp.logical_and(k >= 0, g < groups)
            at = pl.ds(pl.multiple_of(base + g * self.group, self.group), self.group)

            @pl.when(jnp.logical_and(busy, part == 0))
            def _():
                product_tile(normed, self.both, NN, at, self.products.at[way])

            @pl.when(jnp.logical_and(busy, part == 1))
            def _():
                @pl.when(g > 0)
                def _():
                    for n in range(3):
                        self.save(way, n, at).wait()

                grad_rows = self.grad_here[at, :]
                products, stage, ff = self.products.at[way], self.stage.at[way], self.ff
                wide = min(512, ff)
                for start in range(0, ff, wide):
                    length = min(wide, ff - start)
                    cols = slice(start, start + length)
                    gate, up = products[:, cols], products[:, ff + start : ff + start + length]
                    grad = dot(grad_rows, self.back[cols, :], NT)
                    sig = sigmoid(gate)
                    value = gate * sig
                    stage[0, :, cols] = (value * up).astype(BF16)
                    stage[1, :, cols] = (grad * up * slope(gate, sig)).astype(BF16)
                    stage[2, :, cols] = (grad * value).astype(BF16)
                for n in range(3):
                    self.save(way, n, at).start()

    def finish(self):
        for way in range(2):
            for n in range(3):
                self.save(way, n, pl.ds(0, self.group)).wait()
        for copy in self.keep():
            copy.wait()
        self.inward.finish(range(2))
        self.outward.finish(range(1))


class ScatterJob(Job):
    def __init__(self, grads, dims):
        self.size = lax.axis_size("fsdp")
        self.dims = dims
        shapes = [RingScatter.out_shape(g, d, self.size) for g, d in zip(grads, dims)]
        self.inputs, self.in_specs = grads, [ANY] * len(grads)
        self.out_shape = [jax.ShapeDtypeStruct(s, F32) for s in shapes]
        self.out_specs = [WHOLE] * len(grads)
        self.scratch = RingScatter.buffers(shapes, self.size) + RingScatter.scratch(len(grads), self.size)

    def bind(self, ins, outs, scratch):
        self.job = RingScatter(
            ins, outs, self.dims, scratch[:-5], scratch[-5:], self.size, self.size == 4
        )

    def peers(self):
        return self.job.peers()

    def start(self):
        self.job.start()

    def advance(self, number):
        self.job.advance(number)

    def finish(self):
        self.job.finish()

    def cuts(self, steps):
        first, last = (2 * steps) // 5, 2 * steps - 2
        return [first + ((last - first) * i) // (self.size - 1) for i in range(self.size)]


class ProductJob(Job):
    def __init__(self, left_at, right_at, dims, shape, tile):
        self.left_at, self.right_at, self.dims, self.shape, self.tile = left_at, right_at, dims, shape, tile
        self.inputs, self.in_specs = [], []
        self.out_shape, self.out_specs = [jax.ShapeDtypeStruct(shape, BF16)], [ANY]
        self.scratch = [pltpu.VMEM((2, tile, shape[1]), BF16), pltpu.SemaphoreType.DMA((2,))]

    def bind(self, ins, outs, scratch):
        (self.out,) = outs
        self.stage, self.sem = scratch

    def peers(self):
        return []

    def cuts(self, steps):
        return []

    def start(self):
        pass

    def tasks(self):
        return [(self.shape[0] // self.tile, self.act, (self.left_at, self.right_at))]

    def copy(self, i):
        where = pl.ds(pl.multiple_of(i * self.tile, self.tile), self.tile)
        return pltpu.make_async_copy(self.stage.at[i % 2], self.out.at[where, :], self.sem.at[i % 2])

    def act(self, i):
        @pl.when(i >= 2)
        def _():
            self.copy(i - 2).wait()

        where = pl.ds(pl.multiple_of(i * self.tile, self.tile), self.tile)
        product_tile(self.operands[self.left_at], self.operands[self.right_at], self.dims, where, self.stage.at[i % 2])
        self.copy(i).start()

    def finish(self):
        tiles = self.shape[0] // self.tile
        for i in range(max(0, tiles - 2), tiles):
            self.copy(i).wait()


def product_tile(left, right, dims, where, out):
    rows = left[:, where].T if dims == TN else left[where, :]

    def act(cols):
        if dims == NT:
            out[:, cols] = dot(rows, right[cols, :], NT).astype(out.dtype)
        else:
            out[:, cols] = dot(rows, right[:, cols]).astype(out.dtype)

    by_columns(out.shape[-1], act)


def by_columns(width, act):
    step = min(512, width)

    @pl.loop(0, width // step)
    def _(n):
        act(pl.ds(pl.multiple_of(n * step, step), step))

    if width % step:
        act(pl.ds(width - width % step, width % step))


class ProductScatterJob(ScatterJob):
    def __init__(self, pairs, shapes, dims):
        self.size = lax.axis_size("fsdp")
        self.pairs, self.dims = pairs, dims
        shapes = [RingScatter.out_shape(jax.ShapeDtypeStruct(s, BF16), d, self.size) for s, d in zip(shapes, dims)]
        self.inputs, self.in_specs = [], []
        self.out_shape = [jax.ShapeDtypeStruct(s, F32) for s in shapes]
        self.out_specs = [WHOLE] * len(shapes)
        self.scratch = [pltpu.VMEM((2, self.size) + s, BF16) for s in shapes]
        self.scratch += [pltpu.VMEM((self.size,) + s, BF16) for s in shapes]
        self.scratch += [pltpu.VMEM((2, self.size - 1, s[0] // 2, s[1]), BF16) for s in shapes]
        self.scratch += RingScatter.scratch(len(shapes), self.size)

    def bind(self, ins, outs, scratch):
        self.job = RingScatter(
            [None] * len(outs), outs, self.dims, scratch[:-5], scratch[-5:], self.size, self.size == 4
        )

    def cuts(self, steps):
        first, last = min(self.ready_at + 2, 2 * steps - 8), 2 * steps - 3
        return [first + ((last - first) * i) // (self.size - 1) for i in range(self.size)]

    def start(self):
        pass

    def tasks(self):
        made = []
        for i in sorted(range(len(self.pairs)), key=lambda i: -self.dims[i]):
            tiles = 2 * self.size if self.dims[i] == 0 else self.size
            made.append((tiles, functools.partial(self.act, i), self.pairs[i]))
        return made

    def act(self, i, t):
        job = self.job
        left, right = (self.operands[p] for p in self.pairs[i])
        if self.dims[i] == 0:
            offset, mine = lax.rem(t // 2 + 1, self.size), t % 2
            core = mine * job.core + (1 - mine) * (1 - job.core)
            extent = job.outs[i].shape[0]
            index = job.device(job.place + offset) * 2 + core
            where = pl.ds(pl.multiple_of(index * extent, extent), extent)
            product_tile(left, right, TN, where, job.own[i].at[mine, offset])

            @pl.when(mine == 0)
            def _():
                job.across(i, offset).start()
        else:
            offset = lax.rem(t + 1, self.size)
            extent = job.outs[i].shape[1]
            start = pl.multiple_of(job.device(job.place + offset) * 2 * extent, 2 * extent)
            tile = dot(left[...].T, right[:, pl.ds(start, 2 * extent)]).astype(BF16)
            for core in range(2):
                mine = 1 - core + (2 * core - 1) * job.core
                job.own[i][mine, offset] = tile[:, core * extent : (core + 1) * extent]
            job.across(i, offset).start()


class MixBackJob(Job):
    def __init__(self, valid, grad_branch, w_out, mixed, pre, states, gap, gain, state_end):
        self.rows, self.width = grad_branch.shape
        self.local = w_out.shape[0]
        self.chunks, self.heads = states.shape[:2]
        self.length = self.rows // self.chunks
        self.inputs = [valid, grad_branch, w_out, mixed, pre, states, gap, gain, state_end]
        self.in_specs = [pl.BlockSpec(memory_space=pltpu.SMEM)] + [ANY] * 5 + [WHOLE] * 3
        self.out_shape = [jax.ShapeDtypeStruct((self.rows, self.local), BF16)] * 4 + [
            jax.ShapeDtypeStruct((1, self.local), F32),
            jax.ShapeDtypeStruct((1, HEAD_DIM), F32),
        ]
        self.out_specs = [ANY] * 4 + [WHOLE] * 2
        state = states.shape[1:]
        self.scratch = [
            pltpu.VMEM(w_out.shape, BF16),
            pltpu.VMEM((2, self.length, self.width), BF16),
            pltpu.VMEM((2, self.length, self.local), F32),
            pltpu.VMEM((2, self.length, 4 * self.local), F32),
            pltpu.VMEM((2,) + state, F32),
            pltpu.VMEM((self.length, self.local), F32),
            pltpu.VMEM((self.rows, self.local), BF16),
            *[pltpu.VMEM(state, F32)] * 4,
            pltpu.VMEM((2, 4, self.length, self.local), BF16),
            pltpu.SemaphoreType.DMA((2, 4)),
            pltpu.SemaphoreType.DMA((2, 4)),
            pltpu.SemaphoreType.DMA((3,)),
        ]

    def bind(self, ins, outs, scratch):
        self.valid, self.grad_branch, self.w_out, self.mixed, self.pre, self.states, self.gap, self.gain, self.last = ins
        self.outs, (self.gap_part, self.gain_part) = outs[:4], outs[4:]
        self.w_here, self.grad_here, self.mixed_here, self.pre_here, self.states_here = scratch[:5]
        self.gated, self.grad_mixed, self.begin, self.came, self.flow, self.after = scratch[5:11]
        self.stage, self.in_sem, self.out_sem, self.sem = scratch[11:]
        self.core = lax.axis_index("ctx")

    def peers(self):
        return [{"ctx": 1 - self.core}]

    def cuts(self, steps):
        return []

    def w_copy(self):
        return pltpu.make_async_copy(self.w_out, self.w_here, self.sem.at[0])

    def across(self):
        return pltpu.make_async_remote_copy(
            src_ref=self.begin,
            dst_ref=self.came,
            send_sem=self.sem.at[1],
            recv_sem=self.sem.at[2],
            device_id={"ctx": 1 - self.core},
            device_id_type=BY_AXIS,
        )

    def where(self, i):
        return pl.ds(pl.multiple_of((self.chunks - 1 - i) * self.length, self.length), self.length)

    def loads(self, phase, i):
        slot = i % 2
        copies = [pltpu.make_async_copy(self.pre.at[self.where(i), :], self.pre_here.at[slot], self.in_sem.at[slot, 0])]
        if phase == 0:
            whole = (self.grad_branch, self.grad_here, 1), (self.mixed, self.mixed_here, 2)
            for source, here, n in whole:
                copies.append(
                    pltpu.make_async_copy(source.at[self.where(i), :], here.at[slot], self.in_sem.at[slot, n])
                )
        else:
            copies.append(
                pltpu.make_async_copy(
                    self.states.at[self.chunks - 1 - i], self.states_here.at[slot], self.in_sem.at[slot, 3]
                )
            )
        return copies

    def begin_loads(self, phase, i):
        for copy in self.loads(phase, i):
            copy.start()

    def end_loads(self, phase, i):
        for copy in self.loads(phase, i):
            copy.wait()

    def save(self, k, i):
        slot = i % 2
        return pltpu.make_async_copy(
            self.stage.at[slot, k], self.outs[k].at[self.where(i), :], self.out_sem.at[slot, k]
        )

    def start(self):
        self.w_copy().start()
        for i in range(2):
            self.begin_loads(0, i)

    def tasks(self):
        return [(self.chunks, self.act_begin, ()), (1, lambda i: None, ()), (2 * self.chunks, self.act_back, ())]

    def column(self, slot, k, start=0, wide=None):
        return self.pre_here.at[slot, :, pl.ds(k * self.local + start, wide or self.local)]

    def act_begin(self, i):
        slot = i % 2

        @pl.when(i == 0)
        def _():
            self.w_copy().wait()

        self.end_loads(0, i)

        @pl.when(i >= 2)
        def _():
            self.save(3, i - 2).wait()

        self.gated[...] = dot(self.grad_here[slot], self.w_here[...], NT)
        span_begin_chunk(
            self.heads, self.length, i, self.chunks, self.valid, self.gated, self.mixed_here.at[slot],
            self.column(slot, 0), self.column(slot, 1), self.column(slot, 3), self.gap, self.gain,
            self.stage.at[slot, 3], self.grad_mixed.at[self.where(i), :], self.gain_part, self.begin,
        )
        self.save(3, i).start()

        @pl.when(i + 2 < self.chunks)
        def _():
            self.begin_loads(0, i + 2)

        @pl.when(i + 2 >= self.chunks)
        def _():
            self.begin_loads(1, i + 2 - self.chunks)

        @pl.when(i == self.chunks - 1)
        def _():
            self.across().start()

    def act_back(self, t):
        i, part = t // 2, t % 2
        slot = i % 2

        @pl.when(t == 0)
        def _():
            self.across().wait_recv()
            self.came[...] = jnp.where(self.core == 0, self.came[...], 0.0)

        @pl.when(part == 0)
        def _():
            self.end_loads(1, i)

            @pl.when(i >= 2)
            def _():
                for k in range(3):
                    self.save(k, i - 2).wait()

        heads, wide = self.heads // 2, self.local // 2
        start = pl.multiple_of(part * wide, HEAD_DIM)
        cols, some = pl.ds(start, wide), pl.ds(part * heads, heads)
        mix_back_chunk(
            heads, self.length, i, self.chunks, self.valid, self.grad_mixed.at[self.where(i), cols],
            *[self.column(slot, k, start, wide) for k in range(3)], self.gap.at[:, cols],
            self.states_here.at[pl.ds(slot, 1), some], self.last.at[some], self.came.at[some],
            *[self.stage.at[slot, k, :, cols] for k in range(3)],
            self.gap_part.at[:, cols], self.flow.at[some], self.after.at[some],
        )

        @pl.when(part == 1)
        def _():
            for k in range(3):
                self.save(k, i).start()

            @pl.when(i + 2 < self.chunks)
            def _():
                self.begin_loads(1, i + 2)

    def finish(self):
        for i in range(self.chunks - 2, self.chunks):
            for k in range(4):
                self.save(k, i).wait()
        self.across().wait_send()


class VectorJob(Job):
    def __init__(self, full, short, split):
        self.axes = [(axis, lax.axis_size(axis)) for axis in ("ctx", "fsdp", "tp")]
        self.inputs, self.in_specs = [full, short, split], [WHOLE] * 3
        self.out_shape, self.out_specs = [jax.ShapeDtypeStruct(full.shape, F32)], [WHOLE]
        self.scratch = [pltpu.VMEM((size,) + full.shape, F32) for _, size in self.axes] + [
            pltpu.SemaphoreType.DMA((size - 1,)) for _, size in self.axes
        ] * 2

    def bind(self, ins, outs, scratch):
        self.full, self.short, self.split = ins
        (self.out,) = outs
        self.slots, self.sends, self.recvs = scratch[:3], scratch[3:6], scratch[6:]

    def peers(self):
        return [
            {axis: lax.rem(lax.axis_index(axis) + step, size)} for axis, size in self.axes for step in range(1, size)
        ]

    def cuts(self, steps):
        return [steps + (steps * (i + 1)) // 6 for i in range(len(self.axes) + 1)]

    def tasks(self):
        return []

    def start(self):
        pass

    def copies(self, number):
        axis, size = self.axes[number]
        mine = lax.axis_index(axis)
        return [
            pltpu.make_async_remote_copy(
                src_ref=self.slots[number].at[mine],
                dst_ref=self.slots[number].at[mine],
                send_sem=self.sends[number].at[step - 1],
                recv_sem=self.recvs[number].at[step - 1],
                device_id={axis: lax.rem(mine + step, size)},
                device_id_type=BY_AXIS,
            )
            for step in range(1, size)
        ]

    def advance(self, number):
        if number == 0:
            mine = lax.axis_index(self.axes[0][0])
            slot, local = self.slots[0], self.split.shape[1]
            slot[mine] = self.extra()
            slot[mine, 1:2, :] = self.full[0:1, :]
            slot[mine, 2:3, : self.short.shape[1]] = self.short[...]
            slot[mine, 3:4, pl.ds(pl.multiple_of(lax.axis_index("tp") * local, local), local)] = self.split[...]
        else:
            for copy in self.copies(number - 1):
                copy.wait_recv()
            slot = self.slots[number - 1]
            total = slot[0]
            for k in range(1, self.axes[number - 1][1]):
                total = total + slot[k]
        if number == len(self.axes):
            self.out[...] = total
            return
        if number > 0:
            self.slots[number][lax.axis_index(self.axes[number][0])] = total
        for copy in self.copies(number):
            copy.start()

    def finish(self):
        for number in range(len(self.axes)):
            for copy in self.copies(number):
                copy.wait_send()


def line_sum(
    name, part, halves, gain, n_out, epilogue, collective_id, jobs=(), operands=(), chunk=32, skew=2
):
    size = lax.axis_size("tp")
    product = isinstance(part, tuple)
    operands = [o if isinstance(o, tuple) else (o,) for o in operands]
    operand_shapes = [(o[0].shape[0], sum(p.shape[1] for p in o)) for o in operands]
    pieces = [p for o in operands for p in o]
    if product:
        left_at, right_at, part_dims = part
        rows = operand_shapes[left_at][0]
        width = operand_shapes[right_at][1 - part_dims[1][0]]
    else:
        rows, width = part.shape
    half = rows // 2
    chunk = min(chunk, half)
    count = half // chunk
    group = min(128, half)
    groups = half // group
    per_group = group // chunk
    vector = [job for job in jobs if isinstance(job, VectorJob)]

    def kernel(*refs):
        refs = list(refs)

        def take(n):
            taken = refs[:n]
            del refs[:n]
            return taken

        part_refs, (gain_ref,) = take(0 if product else 1), take(1)
        half_refs = take(len(halves))
        operand_refs = take(len(pieces))
        job_ins = [take(len(job.inputs)) for job in jobs]
        (out_ref,) = take(1)
        own_refs = take(n_out)
        (gain_part_ref,) = take(1)
        job_outs = [take(len(job.out_shape)) for job in jobs]
        part_here, came, sum_send, sum_recv, back_send, back_recv, operand_sem, half_sem, own_sem, part_sem = take(10)
        half_here = take(len(halves))
        operand_here = take(len(operands))
        own_here = take(n_out)
        job_scratch = [take(len(job.scratch)) for job in jobs]
        place = lax.axis_index("tp")
        first, last = place == 0, place == size - 1
        source = (first, last)
        owner = (last, first)
        ahead = (place + 1, place - 1)
        behind = (place - 1, place + 1)
        base = (half, 0)

        loaded = set()

        def operand_copies(i):
            first, column = sum(len(o) for o in operands[:i]), 0
            for n, piece in enumerate(operands[i], first):
                where = operand_here[i].at[:, pl.ds(column, piece.shape[1])]
                yield pltpu.make_async_copy(operand_refs[n], where, operand_sem.at[n])
                column += piece.shape[1]

        def need(places):
            for i in places:
                if i not in loaded:
                    for copy in operand_copies(i):
                        copy.wait()
                    loaded.add(i)

        def half_copy(way, i):
            start = base[way] if half_refs[i].shape[0] == rows else 0
            return pltpu.make_async_copy(half_refs[i].at[pl.ds(start, half), :], half_here[i], half_sem.at[i])

        def part_copy(way, g):
            where = pl.ds(pl.multiple_of(base[way] + g * group, group), group)
            return pltpu.make_async_copy(part_refs[0].at[where, :], part_here.at[where, :], part_sem.at[way, g])

        if not product:
            for g in range(groups):
                for way in range(2):

                    @pl.when(jnp.logical_not(source[way]))
                    def _():
                        part_copy(way, g).start()

        def load(places):
            for i in places:
                for copy in operand_copies(i):
                    copy.start()

        early = (left_at, right_at) if product else ()
        load(early)
        for ins, outs, scratch, job in zip(job_ins, job_outs, job_scratch, jobs):
            job.operands = operand_here
            job.bind(ins, outs, scratch)
        peers = [(jnp.logical_not(first), {"tp": place - 1}), (jnp.logical_not(last), {"tp": place + 1})]
        meet(peers + [(None, peer) for job in jobs for peer in job.peers()])

        def at(way, k):
            return pl.ds(pl.multiple_of(k * chunk + base[way], chunk), chunk)

        def onward(way, k, from_part):
            return pltpu.make_async_remote_copy(
                src_ref=(part_here if product else part_refs[0]).at[at(way, k), :] if from_part else came.at[way, k],
                dst_ref=came.at[way, k],
                send_sem=sum_send.at[way, k],
                recv_sem=sum_recv.at[way, k],
                device_id={"tp": ahead[way]},
                device_id_type=BY_AXIS,
            )

        def back(way, k):
            piece = out_ref.at[at(way, k), :]
            return pltpu.make_async_remote_copy(
                src_ref=piece,
                dst_ref=piece,
                send_sem=back_send.at[way, k],
                recv_sem=back_recv.at[way, k],
                device_id={"tp": behind[way]},
                device_id_type=BY_AXIS,
            )

        def own_copy(k):
            where = pl.ds(pl.multiple_of(k * chunk, chunk), chunk)
            return pltpu.make_async_copy(own_here[0].at[where, :], own_refs[0].at[where, :], own_sem.at[k])

        def part_rows(j):
            way, g = lax.rem(j + jnp.where(place < size // 2, 0, 1), 2), j // 2
            where = pl.ds(pl.multiple_of((1 - way) * half + g * group, group), group)
            left = operand_here[left_at][where, :]
            for start in range(0, width, 512):
                cols = slice(start, min(start + 512, width))
                right = operand_here[right_at]
                right = right[:, cols] if part_dims == NN else right[cols, :]
                part_here[where, cols] = dot(left, right, part_dims).astype(BF16)
            for w in range(2):

                @pl.when(jnp.logical_and(source[w], way == w))
                def _():
                    @pl.loop(0, per_group)
                    def _(k):
                        onward(w, g * per_group + k, True).start()

        tasks, at_step = [], 0
        need(early)
        load([i for i in range(len(operands)) if i not in early])
        for way in range(2):

            @pl.when(owner[way])
            def _():
                for i in range(len(halves)):
                    half_copy(way, i).start()

        if product:
            tasks, at_step = [(-2, 2 * groups, part_rows, ())], 2 * groups - 2
        else:
            for way in range(2):

                @pl.when(source[way])
                def _():
                    @pl.loop(0, count)
                    def _(k):
                        onward(way, k, True).start()

        for job in jobs:
            job.start()
        gain_part_ref[...] = jnp.zeros_like(gain_part_ref)

        away = (place - 1, size - 2 - place)

        def each_way(step, lead, act):
            for way in range(2):
                k = step - skew * lead[way]

                @pl.when(jnp.logical_and(k >= 0, k < count))
                def _():
                    act(way, k)

        def add(way, k):
            @pl.when(jnp.logical_not(source[way]))
            def _():
                if not product:

                    @pl.when(k % per_group == 0)
                    def _():
                        part_copy(way, k // per_group).wait()

                onward(way, k, False).wait_recv()
                total = came[way, k].astype(F32) + part_here[at(way, k), :].astype(F32)

                @pl.when(owner[way])
                def _():
                    @pl.when(k == 0)
                    def _():
                        for i in range(len(halves)):
                            half_copy(way, i).wait()

                    own = pl.ds(pl.multiple_of(k * chunk, chunk), chunk)
                    out_ref[at(way, k), :] = epilogue(
                        half_here, gain_ref[...], own_here[0] if n_out else None, gain_part_ref, own, total
                    )
                    back(way, k).start()
                    if n_out:
                        own_copy(k).start()

                @pl.when(jnp.logical_not(owner[way]))
                def _():
                    came[way, k] = total.astype(BF16)
                    onward(way, k, False).start()

        def spread(way, k):
            @pl.when(jnp.logical_not(owner[way]))
            def _():
                back(way, k).wait_recv()

                @pl.when(jnp.logical_not(source[way]))
                def _():
                    back(way, k).start()

        steps = count + skew * (size - 2)
        extra, followed = 0, None
        for job in jobs:
            if isinstance(job, ForwardJob):
                slowest = max(job.first, per_group + skew * (size - 2))
                extra = max(0, slowest + (groups - 1) * per_group + 2 - steps, job.first + 2 * groups - steps)
                arrivals = [jnp.maximum(job.first, per_group + skew * away[1 - way]) for way in range(2)]
                begins = [jnp.where(owner[way], job.first, arrivals[way]) for way in range(2)]
                followed = out_ref, begins, [jnp.where(o, 2, per_group) for o in owner], groups, base
        for job in vector:
            job.extra = lambda: jnp.where(
                lax.broadcasted_iota(jnp.int32, (8, width), 0) == 0, gain_part_ref[...], 0.0
            )
        for job in jobs:
            for tiles, act, needs in job.tasks():
                tasks.append((at_step, tiles, act, needs))
                at_step += tiles
            job.ready_at = at_step
        acts = sorted((cut, n, i) for n, job in enumerate(jobs) for i, cut in enumerate(job.cuts(steps)))
        bounds = {t[0] for t in tasks} | {t[0] + t[1] for t in tasks}
        for number, (act, lead) in enumerate([(add, away), (spread, (away[1], away[0]))]):
            base_step, high = number * steps, (number + 1) * steps + (extra if number else 0)
            low = min([base_step] + [t[0] for t in tasks if number == 0])
            here = [a for a in acts if low <= a[0] < high]
            edges = sorted({low, high} | {a[0] for a in here} | {e for e in bounds if low < e < high})
            for left, right in zip(edges[:-1], edges[1:]):
                for cut, n, i in here:
                    if cut == left:
                        jobs[n].advance(i)
                active = [t for t in tasks if t[0] <= left and right <= t[0] + t[1]]
                for t in active:
                    need(t[3])

                @pl.loop(left - base_step, right - base_step)
                def _(step):
                    each_way(step, lead, act)
                    for t in active:
                        t[2](step + base_step - t[0])
                    for job in jobs:
                        if number and right - base_step > job.first:
                            job.follow(step, followed)

        for first_step, tiles, act, needs in tasks:
            done = min(max(2 * steps - first_step, 0), tiles)
            if done < tiles:
                need(needs)

                @pl.loop(done, tiles)
                def _(i):
                    act(i)

        need(range(len(operands)))
        for job in jobs:
            job.finish()

        for way in range(2):

            @pl.when(jnp.logical_not(owner[way]))
            def _():
                @pl.loop(0, count)
                def _(k):
                    onward(way, k, False).wait_send()

            @pl.when(jnp.logical_not(source[way]))
            def _():
                @pl.loop(0, count)
                def _(k):
                    back(way, k).wait_send()

            if n_out:

                @pl.when(owner[way])
                def _():
                    @pl.loop(0, count)
                    def _(k):
                        own_copy(k).wait()

    scratch = [
        pltpu.VMEM((rows, width), BF16),
        pltpu.VMEM((2, count, chunk, width), BF16),
        *[pltpu.SemaphoreType.DMA((2, count)) for _ in range(4)],
        pltpu.SemaphoreType.DMA((max(1, len(pieces)),)),
        pltpu.SemaphoreType.DMA((max(1, len(halves)),)),
        pltpu.SemaphoreType.DMA((count,)),
        pltpu.SemaphoreType.DMA((2, groups)),
        *[pltpu.VMEM((half, width), h.dtype) for h in halves],
        *[pltpu.VMEM(shape, o[0].dtype) for shape, o in zip(operand_shapes, operands)],
        *[pltpu.VMEM((half, width), F32)] * n_out,
    ]
    return pl.pallas_call(
        kernel,
        out_shape=[jax.ShapeDtypeStruct((rows, width), BF16)]
        + [jax.ShapeDtypeStruct((half, width), F32)] * n_out
        + [jax.ShapeDtypeStruct((8, width), F32)]
        + [shape for job in jobs for shape in job.out_shape],
        in_specs=[ANY] * (not product) + [WHOLE] + [ANY] * (len(halves) + len(pieces)) + [spec for job in jobs for spec in job.in_specs],
        out_specs=[WHOLE] + [ANY] * n_out + [WHOLE] + [spec for job in jobs for spec in job.out_specs],
        scratch_shapes=scratch + [shape for job in jobs for shape in job.scratch],
        compiler_params=pltpu.CompilerParams(
            collective_id=collective_id, has_side_effects=True, vmem_limit_bytes=VMEM_BYTES
        ),
        name=name,
    )(*([] if product else [part]), gain, *halves, *pieces, *[array for job in jobs for array in job.inputs])


def rms(value):
    return lax.rsqrt(jnp.mean(value * value, axis=-1, keepdims=True) + EPSILON)


def middle_rows(halves, gain, own_ref, gain_part_ref, own, total):
    middle = halves[0][own, :].astype(F32) + total
    own_ref[own, :] = middle
    return (middle * rms(middle) * gain).astype(BF16)


def output_rows(halves, gain, own_ref, gain_part_ref, own, total):
    return (halves[0][own, :] + total).astype(BF16)


def norm_back(grad, value, gain, gain_part_ref):
    inverse = rms(value)
    scaled = value * inverse
    weighted = grad * gain
    gain_part_ref[0:1, :] += jnp.sum(grad * scaled, axis=0, keepdims=True)
    return inverse * (weighted - scaled * jnp.mean(weighted * scaled, axis=-1, keepdims=True))


def grad_middle_rows(halves, gain, own_ref, gain_part_ref, own, total):
    back = norm_back(total, halves[0][own, :], gain, gain_part_ref)
    grad_middle = halves[1][own, :].astype(F32) + back
    own_ref[own, :] = grad_middle
    return grad_middle.astype(BF16)


def input_grad_rows(halves, gain, own_ref, gain_part_ref, own, total):
    back = norm_back(total, halves[0][own, :].astype(F32), gain, gain_part_ref)
    return (halves[1][own, :] + back).astype(BF16)


def lower_ones(length):
    at = lax.broadcasted_iota(jnp.int32, (length, length), 0)
    before = lax.broadcasted_iota(jnp.int32, (length, length), 1)
    return at >= before


def chunk_decay(forget, gap, live, lower):
    closing = sigmoid(-forget)
    opened = gap * closing
    remain = 1.0 - opened
    decay = jnp.where(live, jnp.log(remain), 0.0)
    keys = jnp.where(live, opened, 0.0)
    return closing, remain, keys, ones_times(lower, decay)


def rows_live(valid_ref, chunk_index, length):
    at = lax.broadcasted_iota(jnp.int32, (length, HEAD_DIM), 0) + chunk_index * length
    return at < valid_ref[0]


def span_end_kernel(heads, length, valid_ref, forget_ref, value_ref, gap_ref, end_ref):
    index = pl.program_id(0)

    @pl.when(index == 0)
    def _():
        end_ref[...] = jnp.zeros_like(end_ref)

    live = rows_live(valid_ref, index, length)
    lower = lower_ones(length).astype(BF16)
    for h in range(heads):
        cols = slice(h * HEAD_DIM, (h + 1) * HEAD_DIM)
        _, _, keys, cumulative = chunk_decay(forget_ref[:, cols], gap_ref[:, cols], live, lower)
        total = cumulative[length - 1 :, :]
        tail = (keys * jnp.exp(total - cumulative)).astype(BF16)
        end_ref[h] = jnp.exp(total) * end_ref[h] + dot(value_ref[:, cols].astype(BF16), tail, TN)


def mix_kernel(
    heads, length, valid_ref, query_ref, forget_ref, value_ref, gate_ref, gap_ref, gain_ref, start_ref,
    gated_ref, mixed_ref, states_ref, end_ref, state_ref,
):
    index = pl.program_id(0)

    @pl.when(index == 0)
    def _():
        state_ref[...] = start_ref[...]

    live = rows_live(valid_ref, index, length)
    mask = lower_ones(length)
    lower = mask.astype(BF16)
    for h in range(heads):
        cols = slice(h * HEAD_DIM, (h + 1) * HEAD_DIM)
        _, _, keys, cumulative = chunk_decay(forget_ref[:, cols], gap_ref[:, cols], live, lower)
        pre = query_ref[:, cols]
        queries = (pre * sigmoid(pre) * jnp.exp(cumulative)).astype(BF16)
        shrunk = keys * jnp.exp(-cumulative)
        values = value_ref[:, cols].astype(BF16)
        state = state_ref[h]
        states_ref[0, h] = state
        scores = jnp.where(mask, dot(queries, shrunk.astype(BF16), NT), 0.0).astype(BF16)
        mixed = dot(scores, values) + dot(queries, state.astype(BF16), NT)
        mixed_ref[:, cols] = mixed
        growth = jnp.exp(cumulative[length - 1 :, :])
        state_ref[h] = growth * state + dot(values, (shrunk * growth).astype(BF16), TN)
        gate = gate_ref[:, cols]
        gated_ref[:, cols] = (mixed * rms(mixed) * gain_ref[...] * (gate * sigmoid(gate))).astype(BF16)

    @pl.when(index == pl.num_programs(0) - 1)
    def _():
        end_ref[...] = state_ref[...]


def span_begin_kernel(heads, length, *refs):
    span_begin_chunk(heads, length, pl.program_id(0), pl.num_programs(0), *refs)


def span_begin_chunk(
    heads, length, step, steps, valid_ref, grad_ref, mixed_ref, query_ref, forget_ref, gate_ref, gap_ref, gain_ref,
    grad_gate_ref, grad_mixed_ref, gain_part_ref, begin_ref,
):
    index = steps - 1 - step

    @pl.when(step == 0)
    def _():
        begin_ref[...] = jnp.zeros_like(begin_ref)
        gain_part_ref[...] = jnp.zeros_like(gain_part_ref)

    live = rows_live(valid_ref, index, length)
    lower = lower_ones(length).astype(BF16)
    gain = gain_ref[...]
    for h in range(heads):
        cols = slice(h * HEAD_DIM, (h + 1) * HEAD_DIM)
        mixed = mixed_ref[:, cols]
        inverse = rms(mixed)
        scaled = mixed * inverse
        gate = gate_ref[:, cols]
        sig = sigmoid(gate)
        grad = grad_ref[:, cols].astype(F32)
        grad_gate_ref[:, cols] = (grad * scaled * gain * slope(gate, sig)).astype(BF16)
        grad_scaled = grad * (gate * sig)
        gain_part_ref[...] += jnp.sum(grad_scaled * scaled, axis=0, keepdims=True)
        weighted = grad_scaled * gain
        grad_mixed = inverse * (weighted - scaled * jnp.mean(weighted * scaled, axis=-1, keepdims=True))
        grad_mixed = grad_mixed.astype(BF16)
        grad_mixed_ref[:, cols] = grad_mixed
        _, _, _, cumulative = chunk_decay(forget_ref[:, cols], gap_ref[:, cols], live, lower)
        pre = query_ref[:, cols]
        queries = (pre * sigmoid(pre) * jnp.exp(cumulative)).astype(BF16)
        growth = jnp.exp(cumulative[length - 1 :, :])
        begin_ref[h] = growth * begin_ref[h] + dot(grad_mixed, queries, TN)


def mix_back_kernel(heads, length, *refs):
    mix_back_chunk(heads, length, pl.program_id(0), pl.num_programs(0), *refs)


def mix_back_chunk(
    heads, length, step, steps, valid_ref, grad_ref, query_ref, forget_ref, value_ref, gap_ref, states_ref, last_ref,
    end_ref, grad_query_ref, grad_forget_ref, grad_value_ref, gap_part_ref, flow_ref, after_ref,
):
    index = steps - 1 - step

    @pl.when(step == 0)
    def _():
        flow_ref[...] = end_ref[...]
        after_ref[...] = last_ref[...]
        gap_part_ref[...] = jnp.zeros_like(gap_part_ref)

    live = rows_live(valid_ref, index, length)
    mask = lower_ones(length)
    lower = mask.astype(BF16)
    for h in range(heads):
        cols = slice(h * HEAD_DIM, (h + 1) * HEAD_DIM)
        gap = gap_ref[:, cols]
        closing, remain, keys, cumulative = chunk_decay(forget_ref[:, cols], gap, live, lower)
        pre = query_ref[:, cols]
        sig = sigmoid(pre)
        growth = jnp.exp(cumulative)
        shrink = jnp.exp(-cumulative)
        end_growth = growth[length - 1 :, :]
        queries = (pre * sig * growth).astype(BF16)
        shrunk_wide = keys * shrink
        shrunk = shrunk_wide.astype(BF16)
        tail = (shrunk_wide * end_growth).astype(BF16)
        values = value_ref[:, cols].astype(BF16)
        grad = grad_ref[:, cols]
        state = states_ref[0, h]
        flow = flow_ref[h]
        low_flow = flow.astype(BF16)
        scores = jnp.where(mask, dot(queries, shrunk, NT), 0.0).astype(BF16)
        grad_scores = jnp.where(mask, dot(grad, values, NT), 0.0).astype(BF16)
        to_queries = dot(grad, state.astype(BF16)) + dot(grad_scores, shrunk)
        to_keys = dot(grad_scores, queries, TN) + end_growth * dot(values, low_flow)
        grad_value_ref[:, cols] = (dot(scores, grad, TN) + dot(tail, low_flow, NT)).astype(BF16)
        grad_query_ref[:, cols] = (to_queries * growth * slope(pre, sig)).astype(BF16)
        terms = queries.astype(F32) * to_queries - shrunk.astype(F32) * to_keys
        high = terms.astype(BF16)
        rest = (terms - high.astype(F32)).astype(BF16)
        suffix = dot(lower, high, TN) + dot(lower, rest, TN)
        crossing = jnp.sum(flow * after_ref[h], axis=0, keepdims=True)
        pressure = jnp.where(live, to_keys * shrink - (suffix + crossing) / remain, 0.0)
        gap_part_ref[:, cols] += jnp.sum(closing * pressure, axis=0, keepdims=True)
        grad_forget_ref[:, cols] = (-closing * (1.0 - closing) * gap * pressure).astype(BF16)
        flow_ref[h] = end_growth * flow + dot(grad, queries, TN)
        after_ref[h] = state


def plain_call(kernel, name, grid, in_specs, out_specs, out_shape, scratch, flops, moved):
    return pl.pallas_call(
        kernel,
        grid_spec=pltpu.PrefetchScalarGridSpec(
            num_scalar_prefetch=1, grid=grid, in_specs=in_specs, out_specs=out_specs, scratch_shapes=scratch
        ),
        out_shape=out_shape,
        compiler_params=pltpu.CompilerParams(
            dimension_semantics=("arbitrary",), vmem_limit_bytes=VMEM_BYTES
        ),
        cost_estimate=pl.CostEstimate(flops=flops, bytes_accessed=moved, transcendentals=flops // 64),
        name=name,
    )


def combine(earlier, later):
    return (earlier[0] * later[0], later[0][:, None, :] * earlier[1] + later[1])


def from_earlier(state, decay, axis):
    size = lax.axis_size(axis)
    if size == 2:
        return lax.ppermute(state, axis, [(0, 1)])
    mine = lax.axis_index(axis)
    states, decays = lax.all_gather(state, axis), lax.all_gather(decay, axis)
    total = jnp.zeros_like(state)
    for k in range(size):
        new = decays[k][:, None, :] * total + states[k]
        total = jnp.where(k < mine, new, total)
    return total


def from_later(state, decay, axis):
    size = lax.axis_size(axis)
    if size == 2:
        return lax.ppermute(state, axis, [(1, 0)])
    mine = lax.axis_index(axis)
    states, decays = lax.all_gather(state, axis), lax.all_gather(decay, axis)
    total = jnp.zeros_like(state)
    for k in reversed(range(size)):
        new = decays[k][:, None, :] * total + states[k]
        total = jnp.where(k > mine, new, total)
    return total


def per_device(
    inputs, lengths, w_query, w_forget, w_input, w_outgate, w_output, w_gate, w_up, w_down,
    norm_gain, ffn_gain, head_gain, forget_gap, cotangent,
):
    groups, span, width = inputs.shape
    rows = groups * span
    fsdp, ctx, tp = lax.axis_size("fsdp"), lax.axis_size("ctx"), lax.axis_size("tp")
    local = forget_gap.shape[0]
    heads = local // HEAD_DIM
    ff = w_gate.shape[1]
    length = min(128, span)
    chunks = span // length
    place = lax.axis_index("tp")

    valid = jnp.clip(lengths - lax.axis_index("ctx") * span, 0, span).astype(jnp.int32)
    x = inputs.reshape(rows, width)
    gap = forget_gap.reshape(1, local)
    head_row = head_gain.reshape(1, HEAD_DIM)
    norm_row, ffn_row = norm_gain.reshape(1, width), ffn_gain.reshape(1, width)

    pre, normed, grad_low, w_four, w_out = project(
        x, cotangent.reshape(rows, width), norm_row, valid, [w_query, w_forget, w_input, w_outgate], w_output, 1
    )

    def column(j):
        return pl.BlockSpec((length, local), lambda i, *_: (i, j))

    def column_back(j):
        return pl.BlockSpec((length, local), lambda i, *_: (chunks - 1 - i, j))

    fixed = lambda shape: pl.BlockSpec(shape, lambda i, *_: (0,) * len(shape))
    state_shape = (heads, HEAD_DIM, HEAD_DIM)
    work = 2 * rows * local * HEAD_DIM
    moved = rows * local * 4

    local_end = plain_call(
        functools.partial(span_end_kernel, heads, length), "span_end", (chunks,),
        [column(1), column(2), fixed((1, local))], fixed(state_shape),
        jax.ShapeDtypeStruct(state_shape, F32), [], 3 * work, 2 * moved,
    )(valid, pre, pre, gap)
    span_decay = None
    if ctx > 2:
        keep = (jnp.arange(rows, dtype=jnp.int32) < valid[0])[:, None]
        closing = jax.nn.sigmoid(-pre[:, local : 2 * local])
        logs = jnp.where(keep, jnp.log(1.0 - gap * closing), 0.0)
        span_decay = jnp.exp(jnp.sum(logs, axis=0)).reshape(heads, HEAD_DIM)
    start = from_earlier(local_end, span_decay, "ctx")
    gated, mixed, states, state_end = plain_call(
        functools.partial(mix_kernel, heads, length), "mix", (chunks,),
        [column(0), column(1), column(2), column(3), fixed((1, local)), fixed((1, HEAD_DIM)), fixed(state_shape)],
        [column(0), column(0), pl.BlockSpec((1,) + state_shape, lambda i, *_: (i, 0, 0, 0)), fixed(state_shape)],
        [
            jax.ShapeDtypeStruct((rows, local), BF16),
            jax.ShapeDtypeStruct((rows, local), F32),
            jax.ShapeDtypeStruct((chunks,) + state_shape, F32),
            jax.ShapeDtypeStruct(state_shape, F32),
        ],
        [pltpu.VMEM(state_shape, F32)], 6 * work, 6 * moved,
    )(valid, pre, pre, pre, pre, gap, head_row, start)

    normed_two, middle, _, w_both, w_back, hidden, grad_gate, grad_up = line_sum(
        "sum_branch", (0, 1, NN), [x], ffn_row, 1, middle_rows, 2,
        [ForwardJob([w_gate, w_up, w_down], grad_low, min(128, rows // 2), 5)], [gated, w_out],
    )

    both_axes = ("fsdp", "ctx")

    def scattered(grads, dims):
        if ctx == 2:
            return [ScatterJob(grads, dims)], None
        return [], [
            lax.psum_scatter(g, both_axes, scatter_dimension=d, tiled=True).astype(F32) for g, d in zip(grads, dims)
        ]

    grad_branch, grad_middle, ffn_gain_part, grad_w_down, grad_w_both = line_sum(
        "sum_norm_two", (0, 1, NT), [middle, grad_low], ffn_row, 1, grad_middle_rows, 3,
        [ProductJob(2, 3, TN, (ff, width), 128), ProductJob(4, 0, TN, (width, 2 * ff), 128)],
        [(grad_gate, grad_up), w_both, hidden, grad_low, normed_two],
    )

    jobs, sums_ffn = scattered([grad_w_both, grad_w_down], [0, 1])
    if ctx == 2:
        jobs.append(MixBackJob(valid, grad_branch, w_out, mixed, pre, states, gap, head_row, state_end))
    result, _, *more = line_sum(
        "sum_feed", (0, 1, NN), [middle], ffn_row, 0, output_rows, 5, jobs, [hidden, w_back]
    )
    result = result.reshape(groups, span, width)
    if ctx == 2:
        out_both, out_down, grad_query, grad_forget, grad_value, grad_outgate, gap_part, head_part = more
    else:
        out_both, out_down = sums_ffn
        grad_gated = dot(grad_branch, w_out, NT)
        grad_outgate, grad_mixed, head_part, local_begin = plain_call(
            functools.partial(span_begin_kernel, heads, length), "span_begin", (chunks,),
            [column_back(0), column_back(0), column_back(0), column_back(1), column_back(3), fixed((1, local)),
             fixed((1, HEAD_DIM))],
            [column_back(0), column_back(0), fixed((1, HEAD_DIM)), fixed(state_shape)],
            [
                jax.ShapeDtypeStruct((rows, local), BF16),
                jax.ShapeDtypeStruct((rows, local), BF16),
                jax.ShapeDtypeStruct((1, HEAD_DIM), F32),
                jax.ShapeDtypeStruct(state_shape, F32),
            ],
            [], 3 * work, 6 * moved,
        )(valid, grad_gated, mixed, pre, pre, pre, gap, head_row)
        grad_end = from_later(local_begin, span_decay, "ctx")
        grad_query, grad_forget, grad_value, gap_part = plain_call(
            functools.partial(mix_back_kernel, heads, length), "mix_back", (chunks,),
            [column_back(0), column_back(0), column_back(1), column_back(2), fixed((1, local)),
             pl.BlockSpec((1,) + state_shape, lambda i, *_: (chunks - 1 - i, 0, 0, 0)), fixed(state_shape),
             fixed(state_shape)],
            [column_back(0), column_back(0), column_back(0), fixed((1, local))],
            [jax.ShapeDtypeStruct((rows, local), BF16)] * 3 + [jax.ShapeDtypeStruct((1, local), F32)],
            [pltpu.VMEM(state_shape, F32), pltpu.VMEM(state_shape, F32)], 12 * work, 6 * moved,
        )(valid, grad_mixed, pre, pre, pre, gap, states, state_end, grad_end)

    grad_four = (grad_query, grad_forget, grad_value, grad_outgate)
    jobs, operands, sums_mix = [VectorJob(ffn_gain_part, head_part, gap_part)], [grad_four, w_four], None
    if ctx == 2:
        shapes = [(width, 4 * local), (local, width)]
        jobs.append(ProductScatterJob([(2, 0), (3, 4)], shapes, [0, 1]))
        operands += [normed, gated, grad_branch]
    else:
        grads = [dot(normed, jnp.concatenate(grad_four, axis=1), TN).astype(BF16), dot(gated, grad_branch, TN).astype(BF16)]
        _, sums_mix = scattered(grads, [0, 1])
    input_grad, _, sums, *more = line_sum(
        "sum_norm_one", (0, 1, NT), [x, grad_middle], norm_row, 0, input_grad_rows, 4, jobs, operands
    )
    out_four, out_output = sums_mix or more
    input_grad = input_grad.reshape(groups, span, width)
    grad_norm_gain, grad_ffn_gain, grad_head_gain = sums[0], sums[1], sums[2, :HEAD_DIM]
    grad_gap = lax.dynamic_slice(sums[3], (place * local,), (local,))
    return (
        result,
        input_grad,
        out_four[:, :local],
        out_four[:, local : 2 * local],
        out_four[:, 2 * local : 3 * local],
        out_four[:, 3 * local :],
        out_output,
        out_both[:, :ff],
        out_both[:, ff:],
        out_down,
        grad_norm_gain,
        grad_ffn_gain,
        grad_head_gain,
        grad_gap,
    )


def solution(mesh):
    tokens = P("fsdp", "ctx", None)
    inward, outward = P("fsdp", "tp"), P("tp", "fsdp")
    grad_in, grad_back = P(("fsdp", "ctx"), "tp"), P("tp", ("fsdp", "ctx"))
    return jax.shard_map(
        per_device,
        mesh=mesh,
        in_specs=(tokens, P("fsdp")) + (inward,) * 4 + (outward, inward, inward, outward)
        + (P(), P(), P(), P("tp"), tokens),
        out_specs=(tokens, tokens) + (grad_in,) * 4 + (grad_back, grad_in, grad_in, grad_back)
        + (P(), P(), P(), P("tp")),
        check_vma=False,
    )
```

```python
import functools

import jax
import jax.numpy as jnp
from jax import lax
from jax.experimental import pallas as pl
from jax.experimental.pallas import tpu as pltpu
from jax.sharding import PartitionSpec as P

HEAD_DIM = 128
EPSILON = 1e-05
F32 = jnp.float32
BF16 = jnp.bfloat16
BY_AXIS = pl.DeviceIdType.MESH
VMEM_BYTES = 67043328
ANY = pl.BlockSpec(memory_space=pl.ANY)
WHOLE = pl.BlockSpec(memory_space=pltpu.VMEM)


def dot(left, right, dims=((1,), (0,))):
    return lax.dot_general(left, right, (dims, ((), ())), preferred_element_type=F32)


NN = ((1,), (0,))
NT = ((1,), (1,))
TN = ((0,), (0,))


def sigmoid(value):
    return 1.0 / (1.0 + jnp.exp(-value))


def slope(pre, sig):
    return sig * (1.0 + pre * (1.0 - sig))


def ones_times(ones, value):
    high = value.astype(BF16)
    rest = (value - high.astype(F32)).astype(BF16)
    return dot(ones, high) + dot(ones, rest)


def ring_place(index, size, folded):
    if folded:
        return index + (index // 2) * (1 - 2 * (index % 2))
    return index


class RingGather:
    def __init__(self, shards, outs, where, sems, size, folded):
        self.shards, self.outs, self.where, self.size = shards, outs, where, size
        self.ring_send, self.ring_recv, self.pair_send, self.pair_recv, self.local = sems
        self.place = ring_place(lax.axis_index("fsdp"), size, folded)
        self.folded = folded
        self.core = lax.axis_index("ctx") % 2
        self.pair = lax.axis_index("ctx") + 1 - 2 * self.core

    def device(self, place):
        return ring_place(lax.rem(place + 2 * self.size, self.size), self.size, self.folded)

    def peers(self):
        return [
            {"fsdp": self.device(self.place + 1)},
            {"fsdp": self.device(self.place - 1)},
            {"ctx": self.pair},
        ]

    def rows(self, i, core, way):
        quarter = self.shards[i].shape[0] // 4
        return pl.multiple_of((2 * way + core) * quarter, 16), quarter

    def in_shard(self, i, core, way):
        at, length = self.rows(i, core, way)
        return self.shards[i].at[pl.ds(at, length), :]

    def in_out(self, i, block, core, way):
        out, dim, column = self.where[i]
        at, length = self.rows(i, core, way)
        deep, wide = self.shards[i].shape
        if dim == 0:
            start = pl.multiple_of(block * deep + at, 16)
            return self.outs[out].at[pl.ds(start, length), pl.ds(column, wide)]
        start = pl.multiple_of(block * wide, 128)
        return self.outs[out].at[pl.ds(at, length), pl.ds(start, wide)]

    def own_block(self, i):
        out, dim, column = self.where[i]
        deep, wide = self.shards[i].shape
        block = self.device(self.place)
        if dim == 0:
            start = pl.multiple_of(block * deep, 16)
            return self.outs[out].at[pl.ds(start, deep), pl.ds(column, wide)]
        return self.outs[out].at[:, pl.ds(pl.multiple_of(block * wide, 128), wide)]

    def local_copy(self, i):
        return pltpu.make_async_copy(self.shards[i], self.own_block(i), self.local.at[i])

    def ring(self, i, way, step):
        sign = 1 - 2 * way
        block = self.device(self.place - sign * step)
        there = self.in_out(i, block, self.core, way)
        here = self.in_shard(i, self.core, way) if step == 0 else there
        at = (i * 2 + way) * (self.size - 1) + step
        return pltpu.make_async_remote_copy(
            src_ref=here,
            dst_ref=there,
            send_sem=self.ring_send.at[at],
            recv_sem=self.ring_recv.at[at],
            device_id={"fsdp": self.device(self.place + sign)},
            device_id_type=BY_AXIS,
        )

    def across(self, i, way, step, core):
        sign = 1 - 2 * way
        block = self.device(self.place - sign * (step + 1))
        piece = self.in_out(i, block, core, way)
        at = (i * 2 + way) * (self.size - 1) + step
        return pltpu.make_async_remote_copy(
            src_ref=piece,
            dst_ref=piece,
            send_sem=self.pair_send.at[at],
            recv_sem=self.pair_recv.at[at],
            device_id={"ctx": self.pair},
            device_id_type=BY_AXIS,
        )

    def each(self):
        return [(i, way) for i in range(len(self.shards)) for way in range(2)]

    def start(self):
        for i, way in self.each():
            self.ring(i, way, 0).start()
        for i in range(len(self.shards)):
            self.local_copy(i).start()

    def advance(self, step):
        for i, way in self.each():
            arrived = self.ring(i, way, step)
            arrived.wait_recv()
            if step + 1 < self.size - 1:
                self.ring(i, way, step + 1).start()
            self.across(i, way, step, self.core).start()

    def wait_across(self, arrays, step):
        for i in arrays:
            for way in range(2):
                self.across(i, way, step, 1 - self.core).wait_recv()

    def finish(self, waited=()):
        for i, way in self.each():
            for step in range(self.size - 1):
                self.ring(i, way, step).wait_send()
                self.across(i, way, step, self.core).wait_send()
                if i not in waited:
                    self.across(i, way, step, 1 - self.core).wait_recv()
        for i in range(len(self.shards)):
            if i not in waited:
                self.local_copy(i).wait()

    @staticmethod
    def scratch(count, size):
        copies = count * 2 * (size - 1)
        return [pltpu.SemaphoreType.DMA((copies,)) for _ in range(4)] + [
            pltpu.SemaphoreType.DMA((count,))
        ]


class RingScatter:
    def __init__(self, grads, results, dims, scratch, sems, size, folded):
        self.grads, self.results, self.dims, self.size, self.folded = grads, results, dims, size, folded
        count = len(grads)
        self.own, self.came, self.passed, self.outs = (scratch[n * count : (n + 1) * count] for n in range(4))
        self.pair_send, self.pair_recv, self.local, self.ring_send, self.ring_recv, self.saved = sems
        self.place = ring_place(lax.axis_index("fsdp"), size, folded)
        self.core = lax.axis_index("ctx")

    device = RingGather.device

    def peers(self):
        return [
            {"fsdp": self.device(self.place + 1)},
            {"fsdp": self.device(self.place - 1)},
            {"ctx": 1 - self.core},
        ]

    def block(self, i, offset, core):
        index = self.device(self.place + offset) * 2 + core
        extent = self.outs[i].shape[self.dims[i]]
        start = pl.multiple_of(index * extent, extent)
        if self.dims[i] == 0:
            return self.grads[i].at[pl.ds(start, extent), :]
        return self.grads[i].at[:, pl.ds(start, extent)]

    def local_copy(self, i, offset):
        return pltpu.make_async_copy(
            self.block(i, offset, self.core), self.own[i].at[offset], self.local.at[i * self.size + offset]
        )

    def across(self, i, offset):
        at = i * self.size + offset
        give = self.own[i].at[0, offset] if self.grads[i] is None else self.block(i, offset, 1 - self.core)
        return pltpu.make_async_remote_copy(
            src_ref=give,
            dst_ref=self.came[i].at[offset],
            send_sem=self.pair_send.at[at],
            recv_sem=self.pair_recv.at[at],
            device_id={"ctx": 1 - self.core},
            device_id_type=BY_AXIS,
        )

    def offset(self, way, step):
        return (-(step + 1) if way == 0 else step + 1) % self.size

    def ring(self, i, way, step):
        half = self.outs[i].shape[0] // 2
        at = (i * 2 + way) * (self.size - 1) + step
        return pltpu.make_async_remote_copy(
            src_ref=self.came[i].at[self.offset(way, step), pl.ds(way * half, half), :],
            dst_ref=self.passed[i].at[way, step],
            send_sem=self.ring_send.at[at],
            recv_sem=self.ring_recv.at[at],
            device_id={"fsdp": self.device(self.place + 1 - 2 * way)},
            device_id_type=BY_AXIS,
        )

    def order(self):
        used = []
        for step in range(self.size):
            for way in range(2):
                if self.offset(way, step) not in used:
                    used.append(self.offset(way, step))
        return used

    def start(self):
        for offset in self.order():
            for i in range(len(self.grads)):
                self.across(i, offset).start()
                self.local_copy(i, offset).start()

    def advance(self, step):
        before = {self.offset(way, s) for s in range(step) for way in range(2)}
        fresh = {self.offset(way, step) for way in range(2)} - before
        for i in range(len(self.grads)):
            for offset in sorted(fresh):
                self.across(i, offset).wait_recv()
                if self.grads[i] is not None:
                    self.local_copy(i, offset).wait()
            for way in range(2):
                if step > 0:
                    self.ring(i, way, step - 1).wait_recv()
                self.add(i, way, step)
                if step < self.size - 1:
                    self.ring(i, way, step).start()
                else:
                    self.save(i, way).start()

    def save(self, i, way):
        half = self.outs[i].shape[0] // 2
        rows = pl.ds(way * half, half)
        return pltpu.make_async_copy(
            self.outs[i].at[rows, :], self.results[i].at[rows, :], self.saved.at[2 * i + way]
        )

    def add(self, i, way, step):
        half = self.outs[i].shape[0] // 2
        offset = self.offset(way, step)
        own, came, passed, out = self.own[i], self.came[i], self.passed[i], self.outs[i]

        @pl.loop(0, half // 16)
        def _(r):
            rows = pl.ds(pl.multiple_of(way * half + r * 16, 16), 16)
            kept = own[offset, rows, :] if self.grads[i] is not None else own[1, offset, rows, :]
            total = kept.astype(F32) + came[offset, rows, :].astype(F32)
            if step > 0:
                total += passed[way, step - 1, pl.ds(pl.multiple_of(r * 16, 16), 16), :].astype(F32)
            if step < self.size - 1:
                came[offset, rows, :] = total.astype(BF16)
            else:
                out[rows, :] = total

    def finish(self):
        for i in range(len(self.grads)):
            for offset in range(self.size):
                self.across(i, offset).wait_send()
            for way in range(2):
                self.save(i, way).wait()
                for step in range(self.size - 1):
                    self.ring(i, way, step).wait_send()

    @staticmethod
    def out_shape(grad, dim, size):
        deep, wide = grad.shape
        return (deep // (2 * size), wide) if dim == 0 else (deep, wide // (2 * size))

    @staticmethod
    def buffers(shapes, size):
        full = [pltpu.VMEM((size,) + s, BF16) for s in shapes]
        passed = [pltpu.VMEM((2, size - 1, s[0] // 2, s[1]), BF16) for s in shapes]
        return full + full + passed + [pltpu.VMEM(s, F32) for s in shapes]

    @staticmethod
    def scratch(count, size):
        return [pltpu.SemaphoreType.DMA((count * size,)) for _ in range(3)] + [
            pltpu.SemaphoreType.DMA((count * 2 * (size - 1),)) for _ in range(2)
        ] + [pltpu.SemaphoreType.DMA((2 * count,))]


def meet(peers):
    barrier = pltpu.get_barrier_semaphore()
    total = 0
    for condition, peer in peers:
        if condition is None:
            pl.semaphore_signal(barrier, inc=1, device_id=peer, device_id_type=BY_AXIS)
            total = total + 1
        else:

            @pl.when(condition)
            def _():
                pl.semaphore_signal(barrier, inc=1, device_id=peer, device_id_type=BY_AXIS)

            total = total + condition.astype(jnp.int32)
    pl.semaphore_wait(barrier, total)


def project(x, cotangent, gain, valid, shards, w_out_shard, collective_id):
    size = lax.axis_size("fsdp")
    rows, width = x.shape
    deep, local = shards[0].shape
    count = len(shards)
    total = count * local
    half = deep // 2
    tile = min(512, total)
    step_rows = min(64, rows)
    row_tile = min(512, rows)
    copies = 1 + 2 * (size - 1)

    def kernel(
        valid_ref, gain_ref, x_ref, cot_ref, *refs
    ):
        shard_refs, refs = refs[: count + 1], refs[count + 1 :]
        pre_ref, normed_ref, grad_ref, four_ref, out_ref = refs[:5]
        x_here, grad_here, normed, acc, four, in_sem, save_sem, four_sem, pre_sem = refs[5:14]
        where = [(0, 0, i * local) for i in range(count)] + [(1, 1, 0)]
        job = RingGather(shard_refs, [four, out_ref], where, refs[14:], size, size == 4)
        loads = [
            pltpu.make_async_copy(x_ref, x_here, in_sem.at[0]),
            pltpu.make_async_copy(cot_ref, grad_here, in_sem.at[1]),
        ]
        for load in loads:
            load.start()
        meet([(None, peer) for peer in job.peers()])
        job.start()
        loads[0].wait()

        @pl.loop(0, rows // step_rows)
        def _(r):
            at = pl.ds(pl.multiple_of(r * step_rows, step_rows), step_rows)
            wide = x_here[at, :].astype(F32)
            normed[at, :] = (wide * rms(wide) * gain_ref[...]).astype(BF16)

        saves = [
            pltpu.make_async_copy(normed, normed_ref, save_sem.at[0]),
            pltpu.make_async_copy(grad_here, grad_ref, save_sem.at[1]),
        ]
        saves[0].start()

        def save_four(start, length, number):
            at = pl.ds(start, length)
            return pltpu.make_async_copy(four.at[at, :], four_ref.at[at, :], four_sem.at[number])

        def save_pre(n):
            at = pl.ds(pl.multiple_of(n * tile, tile), tile)
            return pltpu.make_async_copy(acc.at[:, at], pre_ref.at[:, at], pre_sem.at[n])

        def multiply(start, length, first, last):
            @pl.loop(0, total // tile)
            def _(n):
                cols = pl.ds(pl.multiple_of(n * tile, tile), tile)
                deep_at = pl.ds(start, length)

                @pl.loop(0, rows // row_tile)
                def _(r):
                    at = pl.ds(pl.multiple_of(r * row_tile, row_tile), row_tile)
                    term = dot(normed[at, deep_at], four[deep_at, cols])
                    acc[at, cols] = term if first else acc[at, cols] + term

                if last:
                    save_pre(n).start()

        for i in range(count):
            job.local_copy(i).wait()
        own = pl.multiple_of(job.device(job.place) * deep, deep)
        save_four(own, deep, 0).start()
        multiply(own, deep, True, False)
        loads[1].wait()

        @pl.loop(0, rows // step_rows)
        def _(r):
            at = pl.ds(pl.multiple_of(r * step_rows, step_rows), step_rows)
            row = lax.broadcasted_iota(jnp.int32, (step_rows, width), 0) + r * step_rows
            wide = grad_here[at, :].astype(F32)
            grad_here[at, :] = jnp.where(row < valid_ref[0], wide, 0.0).astype(BF16)

        saves[1].start()
        for step in range(size - 1):
            job.advance(step)
            job.wait_across(range(count), step)
            for way in range(2):
                block = job.device(job.place - (1 - 2 * way) * (step + 1))
                start = pl.multiple_of(block * deep + way * half, half)
                save_four(start, half, 1 + 2 * step + way).start()
                multiply(start, half, False, step == size - 2 and way == 1)
        job.finish(range(count))
        for save in saves:
            save.wait()
        save_four(own, deep, 0).wait()
        for step in range(size - 1):
            for way in range(2):
                save_four(0, half, 1 + 2 * step + way).wait()
        for n in range(total // tile):
            save_pre(n).wait()

    return pl.pallas_call(
        kernel,
        out_shape=[
            jax.ShapeDtypeStruct((rows, total), F32),
            jax.ShapeDtypeStruct((rows, width), BF16),
            jax.ShapeDtypeStruct((rows, width), BF16),
            jax.ShapeDtypeStruct((width, total), BF16),
            jax.ShapeDtypeStruct((w_out_shard.shape[0], width), BF16),
        ],
        in_specs=[pl.BlockSpec(memory_space=pltpu.SMEM), WHOLE, ANY, ANY] + [ANY] * count + [WHOLE],
        out_specs=[ANY] * 5,
        scratch_shapes=[
            pltpu.VMEM((rows, width), BF16),
            pltpu.VMEM((rows, width), BF16),
            pltpu.VMEM((rows, width), BF16),
            pltpu.VMEM((rows, total), F32),
            pltpu.VMEM((width, total), BF16),
            pltpu.SemaphoreType.DMA((2,)),
            pltpu.SemaphoreType.DMA((2,)),
            pltpu.SemaphoreType.DMA((copies,)),
            pltpu.SemaphoreType.DMA((total // tile,)),
        ]
        + RingGather.scratch(count + 1, size),
        compiler_params=pltpu.CompilerParams(
            collective_id=collective_id, has_side_effects=True, vmem_limit_bytes=VMEM_BYTES
        ),
        name="project",
    )(valid, gain, x, cotangent, *shards, w_out_shard)


class Job:
    first = 0

    def tasks(self):
        return []

    def follow(self, step, ways):
        pass


class ForwardJob(Job):
    def __init__(self, shards, grad_low, rows_in_group, first):
        self.size = lax.axis_size("fsdp")
        self.rows, self.width = grad_low.shape
        self.ff = shards[0].shape[1]
        self.group, self.first = rows_in_group, first
        self.inputs, self.in_specs = [*shards, grad_low], [ANY] * 4
        self.out_shape = [
            jax.ShapeDtypeStruct((self.width, 2 * self.ff), BF16),
            jax.ShapeDtypeStruct((self.ff, self.width), BF16),
            *[jax.ShapeDtypeStruct((self.rows, self.ff), BF16)] * 3,
        ]
        self.out_specs = [ANY] * 5
        self.scratch = [
            pltpu.VMEM((self.width, 2 * self.ff), BF16),
            pltpu.VMEM((self.ff, self.width), BF16),
            pltpu.VMEM((self.rows, self.width), BF16),
            pltpu.VMEM((2, self.group, 2 * self.ff), F32),
            pltpu.VMEM((2, 3, self.group, self.ff), BF16),
            pltpu.SemaphoreType.DMA((3,)),
            pltpu.SemaphoreType.DMA((2, 3)),
            *RingGather.scratch(2, self.size),
            *RingGather.scratch(1, self.size),
        ]

    def bind(self, ins, outs, scratch):
        self.grad_low = ins[3]
        self.both_out, self.back_out, *self.outs = outs
        self.both, self.back, self.grad_here, self.products, self.stage, self.sem, self.stage_sem = scratch[:7]
        size = self.size
        self.inward = RingGather(ins[:2], [self.both], [(0, 0, 0), (0, 0, self.ff)], scratch[7:12], size, size == 4)
        self.outward = RingGather(ins[2:3], [self.back], [(0, 1, 0)], scratch[12:], size, size == 4)

    def peers(self):
        return self.inward.peers()

    def cuts(self, steps):
        ring = self.size - 1
        ahead = [((16 * (i + 1)) // ring * steps) // 20 for i in range(ring)]
        return ahead + [((16 + (9 * (i + 1)) // ring) * steps) // 20 for i in range(ring)]

    def load(self):
        return pltpu.make_async_copy(self.grad_low, self.grad_here, self.sem.at[0])

    def keep(self):
        return [
            pltpu.make_async_copy(self.both, self.both_out, self.sem.at[1]),
            pltpu.make_async_copy(self.back, self.back_out, self.sem.at[2]),
        ]

    def start(self):
        self.inward.start()
        self.load().start()

    def advance(self, number):
        ring = self.size - 1
        if number < ring:
            self.inward.advance(number)
            if number == max(0, ring - 2):
                self.outward.start()
            return
        self.outward.advance(number - ring)
        if number == 2 * ring - 1:
            for step in range(ring):
                self.inward.wait_across(range(2), step)
                self.outward.wait_across(range(1), step)
            for i in range(2):
                self.inward.local_copy(i).wait()
            self.outward.local_copy(0).wait()
            self.load().wait()
            for copy in self.keep():
                copy.start()

    def save(self, way, k, at):
        return pltpu.make_async_copy(self.stage.at[way, k], self.outs[k].at[at, :], self.stage_sem.at[way, k])

    def follow(self, step, ways):
        normed, begins, periods, groups, bases = ways

        @pl.loop(0, 2)
        def _(way):
            begin, period, base = (jnp.where(way == 0, pair[0], pair[1]) for pair in (begins, periods, bases))
            k = step - begin
            g = lax.div(k, period)
            part = lax.rem(k, period)
            busy = jnp.logical_and(k >= 0, g < groups)
            at = pl.ds(pl.multiple_of(base + g * self.group, self.group), self.group)

            @pl.when(jnp.logical_and(busy, part == 0))
            def _():
                product_tile(normed, self.both, NN, at, self.products.at[way])

            @pl.when(jnp.logical_and(busy, part == 1))
            def _():
                @pl.when(g > 0)
                def _():
                    for n in range(3):
                        self.save(way, n, at).wait()

                grad_rows = self.grad_here[at, :]
                products, stage, ff = self.products.at[way], self.stage.at[way], self.ff
                wide = min(512, ff)
                for start in range(0, ff, wide):
                    length = min(wide, ff - start)
                    cols = slice(start, start + length)
                    gate, up = products[:, cols], products[:, ff + start : ff + start + length]
                    grad = dot(grad_rows, self.back[cols, :], NT)
                    sig = sigmoid(gate)
                    value = gate * sig
                    stage[0, :, cols] = (value * up).astype(BF16)
                    stage[1, :, cols] = (grad * up * slope(gate, sig)).astype(BF16)
                    stage[2, :, cols] = (grad * value).astype(BF16)
                for n in range(3):
                    self.save(way, n, at).start()

    def finish(self):
        for way in range(2):
            for n in range(3):
                self.save(way, n, pl.ds(0, self.group)).wait()
        for copy in self.keep():
            copy.wait()
        self.inward.finish(range(2))
        self.outward.finish(range(1))


class ScatterJob(Job):
    def __init__(self, grads, dims):
        self.size = lax.axis_size("fsdp")
        self.dims = dims
        shapes = [RingScatter.out_shape(g, d, self.size) for g, d in zip(grads, dims)]
        self.inputs, self.in_specs = grads, [ANY] * len(grads)
        self.out_shape = [jax.ShapeDtypeStruct(s, F32) for s in shapes]
        self.out_specs = [ANY] * len(grads)
        self.scratch = RingScatter.buffers(shapes, self.size) + RingScatter.scratch(len(grads), self.size)

    def bind(self, ins, outs, scratch):
        self.job = RingScatter(
            ins, outs, self.dims, scratch[:-6], scratch[-6:], self.size, self.size == 4
        )

    def peers(self):
        return self.job.peers()

    def start(self):
        self.job.start()

    def advance(self, number):
        self.job.advance(number)

    def finish(self):
        self.job.finish()

    def cuts(self, steps):
        first, last = (2 * steps) // 5, 2 * steps - 2
        return [first + ((last - first) * i) // (self.size - 1) for i in range(self.size)]


class ProductJob(Job):
    def __init__(self, left_at, right_at, dims, shape, tile):
        self.left_at, self.right_at, self.dims, self.shape, self.tile = left_at, right_at, dims, shape, tile
        self.inputs, self.in_specs = [], []
        self.out_shape, self.out_specs = [jax.ShapeDtypeStruct(shape, BF16)], [ANY]
        self.scratch = [pltpu.VMEM((2, tile, shape[1]), BF16), pltpu.SemaphoreType.DMA((2,))]

    def bind(self, ins, outs, scratch):
        (self.out,) = outs
        self.stage, self.sem = scratch

    def peers(self):
        return []

    def cuts(self, steps):
        return []

    def start(self):
        pass

    def tasks(self):
        return [(self.shape[0] // self.tile, self.act, (self.left_at, self.right_at))]

    def copy(self, i):
        where = pl.ds(pl.multiple_of(i * self.tile, self.tile), self.tile)
        return pltpu.make_async_copy(self.stage.at[i % 2], self.out.at[where, :], self.sem.at[i % 2])

    def act(self, i):
        @pl.when(i >= 2)
        def _():
            self.copy(i - 2).wait()

        where = pl.ds(pl.multiple_of(i * self.tile, self.tile), self.tile)
        product_tile(self.operands[self.left_at], self.operands[self.right_at], self.dims, where, self.stage.at[i % 2])
        self.copy(i).start()

    def finish(self):
        tiles = self.shape[0] // self.tile
        for i in range(max(0, tiles - 2), tiles):
            self.copy(i).wait()


def product_tile(left, right, dims, where, out):
    rows = left[:, where].T if dims == TN else left[where, :]

    def act(cols):
        if dims == NT:
            out[:, cols] = dot(rows, right[cols, :], NT).astype(out.dtype)
        else:
            out[:, cols] = dot(rows, right[:, cols]).astype(out.dtype)

    by_columns(out.shape[-1], act)


def by_columns(width, act):
    step = min(512, width)

    @pl.loop(0, width // step)
    def _(n):
        act(pl.ds(pl.multiple_of(n * step, step), step))

    if width % step:
        act(pl.ds(width - width % step, width % step))


class ProductScatterJob(ScatterJob):
    def __init__(self, pairs, shapes, dims):
        self.size = lax.axis_size("fsdp")
        self.pairs, self.dims = pairs, dims
        shapes = [RingScatter.out_shape(jax.ShapeDtypeStruct(s, BF16), d, self.size) for s, d in zip(shapes, dims)]
        self.inputs, self.in_specs = [], []
        self.out_shape = [jax.ShapeDtypeStruct(s, F32) for s in shapes]
        self.out_specs = [ANY] * len(shapes)
        self.scratch = [pltpu.VMEM((2, self.size) + s, BF16) for s in shapes]
        self.scratch += [pltpu.VMEM((self.size,) + s, BF16) for s in shapes]
        self.scratch += [pltpu.VMEM((2, self.size - 1, s[0] // 2, s[1]), BF16) for s in shapes]
        self.scratch += [pltpu.VMEM(s, F32) for s in shapes]
        self.scratch += RingScatter.scratch(len(shapes), self.size)

    def bind(self, ins, outs, scratch):
        self.job = RingScatter(
            [None] * len(outs), outs, self.dims, scratch[:-6], scratch[-6:], self.size, self.size == 4
        )

    def cuts(self, steps):
        first, last = min(self.ready_at + 2, 2 * steps - 8), 2 * steps - 3
        return [first + ((last - first) * i) // (self.size - 1) for i in range(self.size)]

    def start(self):
        pass

    def tasks(self):
        made = []
        for i in sorted(range(len(self.pairs)), key=lambda i: -self.dims[i]):
            tiles = 2 * self.size if self.dims[i] == 0 else self.size
            made.append((tiles, functools.partial(self.act, i), self.pairs[i]))
        return made

    def act(self, i, t):
        job = self.job
        left, right = (self.operands[p] for p in self.pairs[i])
        if self.dims[i] == 0:
            offset, mine = lax.rem(t // 2 + 1, self.size), t % 2
            core = mine * job.core + (1 - mine) * (1 - job.core)
            extent = job.outs[i].shape[0]
            index = job.device(job.place + offset) * 2 + core
            where = pl.ds(pl.multiple_of(index * extent, extent), extent)
            product_tile(left, right, TN, where, job.own[i].at[mine, offset])

            @pl.when(mine == 0)
            def _():
                job.across(i, offset).start()
        else:
            offset = lax.rem(t + 1, self.size)
            extent = job.outs[i].shape[1]
            start = pl.multiple_of(job.device(job.place + offset) * 2 * extent, 2 * extent)
            tile = dot(left[...].T, right[:, pl.ds(start, 2 * extent)]).astype(BF16)
            for core in range(2):
                mine = 1 - core + (2 * core - 1) * job.core
                job.own[i][mine, offset] = tile[:, core * extent : (core + 1) * extent]
            job.across(i, offset).start()


class MixBackJob(Job):
    def __init__(self, valid, grad_branch, w_out, mixed, pre, states, gap, gain, state_end):
        self.rows, self.width = grad_branch.shape
        self.local = w_out.shape[0]
        self.chunks, self.heads = states.shape[:2]
        self.length = self.rows // self.chunks
        self.inputs = [valid, grad_branch, w_out, mixed, pre, states, gap, gain, state_end]
        self.in_specs = [pl.BlockSpec(memory_space=pltpu.SMEM)] + [ANY] * 5 + [WHOLE] * 3
        self.out_shape = [jax.ShapeDtypeStruct((self.rows, self.local), BF16)] * 4 + [
            jax.ShapeDtypeStruct((1, self.local), F32),
            jax.ShapeDtypeStruct((1, HEAD_DIM), F32),
        ]
        self.out_specs = [ANY] * 4 + [WHOLE] * 2
        state = states.shape[1:]
        self.scratch = [
            pltpu.VMEM(w_out.shape, BF16),
            pltpu.VMEM((2, self.length, self.width), BF16),
            pltpu.VMEM((2, self.length, self.local), F32),
            pltpu.VMEM((2, self.length, 4 * self.local), F32),
            pltpu.VMEM((2,) + state, F32),
            pltpu.VMEM((self.length, self.local), F32),
            pltpu.VMEM((self.rows, self.local), BF16),
            *[pltpu.VMEM(state, F32)] * 4,
            pltpu.VMEM((2, 4, self.length, self.local), BF16),
            pltpu.SemaphoreType.DMA((2, 4)),
            pltpu.SemaphoreType.DMA((2, 4)),
            pltpu.SemaphoreType.DMA((3,)),
        ]

    def bind(self, ins, outs, scratch):
        self.valid, self.grad_branch, self.w_out, self.mixed, self.pre, self.states, self.gap, self.gain, self.last = ins
        self.outs, (self.gap_part, self.gain_part) = outs[:4], outs[4:]
        self.w_here, self.grad_here, self.mixed_here, self.pre_here, self.states_here = scratch[:5]
        self.gated, self.grad_mixed, self.begin, self.came, self.flow, self.after = scratch[5:11]
        self.stage, self.in_sem, self.out_sem, self.sem = scratch[11:]
        self.core = lax.axis_index("ctx")

    def peers(self):
        return [{"ctx": 1 - self.core}]

    def cuts(self, steps):
        return []

    def w_copy(self):
        return pltpu.make_async_copy(self.w_out, self.w_here, self.sem.at[0])

    def across(self):
        return pltpu.make_async_remote_copy(
            src_ref=self.begin,
            dst_ref=self.came,
            send_sem=self.sem.at[1],
            recv_sem=self.sem.at[2],
            device_id={"ctx": 1 - self.core},
            device_id_type=BY_AXIS,
        )

    def where(self, i):
        return pl.ds(pl.multiple_of((self.chunks - 1 - i) * self.length, self.length), self.length)

    def loads(self, phase, i):
        slot = i % 2
        copies = [pltpu.make_async_copy(self.pre.at[self.where(i), :], self.pre_here.at[slot], self.in_sem.at[slot, 0])]
        if phase == 0:
            whole = (self.grad_branch, self.grad_here, 1), (self.mixed, self.mixed_here, 2)
            for source, here, n in whole:
                copies.append(
                    pltpu.make_async_copy(source.at[self.where(i), :], here.at[slot], self.in_sem.at[slot, n])
                )
        else:
            copies.append(
                pltpu.make_async_copy(
                    self.states.at[self.chunks - 1 - i], self.states_here.at[slot], self.in_sem.at[slot, 3]
                )
            )
        return copies

    def begin_loads(self, phase, i):
        for copy in self.loads(phase, i):
            copy.start()

    def end_loads(self, phase, i):
        for copy in self.loads(phase, i):
            copy.wait()

    def save(self, k, i):
        slot = i % 2
        return pltpu.make_async_copy(
            self.stage.at[slot, k], self.outs[k].at[self.where(i), :], self.out_sem.at[slot, k]
        )

    def start(self):
        self.w_copy().start()
        for i in range(2):
            self.begin_loads(0, i)

    def tasks(self):
        return [(self.chunks, self.act_begin, ()), (1, lambda i: None, ()), (2 * self.chunks, self.act_back, ())]

    def column(self, slot, k, start=0, wide=None):
        return self.pre_here.at[slot, :, pl.ds(k * self.local + start, wide or self.local)]

    def act_begin(self, i):
        slot = i % 2

        @pl.when(i == 0)
        def _():
            self.w_copy().wait()

        self.end_loads(0, i)

        @pl.when(i >= 2)
        def _():
            self.save(3, i - 2).wait()

        self.gated[...] = dot(self.grad_here[slot], self.w_here[...], NT)
        span_begin_chunk(
            self.heads, self.length, i, self.chunks, self.valid, self.gated, self.mixed_here.at[slot],
            self.column(slot, 0), self.column(slot, 1), self.column(slot, 3), self.gap, self.gain,
            self.stage.at[slot, 3], self.grad_mixed.at[self.where(i), :], self.gain_part, self.begin,
        )
        self.save(3, i).start()

        @pl.when(i + 2 < self.chunks)
        def _():
            self.begin_loads(0, i + 2)

        @pl.when(i + 2 >= self.chunks)
        def _():
            self.begin_loads(1, i + 2 - self.chunks)

        @pl.when(i == self.chunks - 1)
        def _():
            self.across().start()

    def act_back(self, t):
        i, part = t // 2, t % 2
        slot = i % 2

        @pl.when(t == 0)
        def _():
            self.across().wait_recv()
            self.came[...] = jnp.where(self.core == 0, self.came[...], 0.0)

        @pl.when(part == 0)
        def _():
            self.end_loads(1, i)

            @pl.when(i >= 2)
            def _():
                for k in range(3):
                    self.save(k, i - 2).wait()

        heads, wide = self.heads // 2, self.local // 2
        start = pl.multiple_of(part * wide, HEAD_DIM)
        cols, some = pl.ds(start, wide), pl.ds(part * heads, heads)
        mix_back_chunk(
            heads, self.length, i, self.chunks, self.valid, self.grad_mixed.at[self.where(i), cols],
            *[self.column(slot, k, start, wide) for k in range(3)], self.gap.at[:, cols],
            self.states_here.at[pl.ds(slot, 1), some], self.last.at[some], self.came.at[some],
            *[self.stage.at[slot, k, :, cols] for k in range(3)],
            self.gap_part.at[:, cols], self.flow.at[some], self.after.at[some],
        )

        @pl.when(part == 1)
        def _():
            for k in range(3):
                self.save(k, i).start()

            @pl.when(i + 2 < self.chunks)
            def _():
                self.begin_loads(1, i + 2)

    def finish(self):
        for i in range(self.chunks - 2, self.chunks):
            for k in range(4):
                self.save(k, i).wait()
        self.across().wait_send()


class VectorJob(Job):
    def __init__(self, full, short, split):
        self.axes = [(axis, lax.axis_size(axis)) for axis in ("ctx", "fsdp", "tp")]
        self.inputs, self.in_specs = [full, short, split], [WHOLE] * 3
        self.out_shape, self.out_specs = [jax.ShapeDtypeStruct(full.shape, F32)], [WHOLE]
        self.scratch = [pltpu.VMEM((size,) + full.shape, F32) for _, size in self.axes] + [
            pltpu.SemaphoreType.DMA((size - 1,)) for _, size in self.axes
        ] * 2

    def bind(self, ins, outs, scratch):
        self.full, self.short, self.split = ins
        (self.out,) = outs
        self.slots, self.sends, self.recvs = scratch[:3], scratch[3:6], scratch[6:]

    def peers(self):
        return [
            {axis: lax.rem(lax.axis_index(axis) + step, size)} for axis, size in self.axes for step in range(1, size)
        ]

    def cuts(self, steps):
        return [steps + (steps * (i + 1)) // 6 for i in range(len(self.axes) + 1)]

    def tasks(self):
        return []

    def start(self):
        pass

    def copies(self, number):
        axis, size = self.axes[number]
        mine = lax.axis_index(axis)
        return [
            pltpu.make_async_remote_copy(
                src_ref=self.slots[number].at[mine],
                dst_ref=self.slots[number].at[mine],
                send_sem=self.sends[number].at[step - 1],
                recv_sem=self.recvs[number].at[step - 1],
                device_id={axis: lax.rem(mine + step, size)},
                device_id_type=BY_AXIS,
            )
            for step in range(1, size)
        ]

    def advance(self, number):
        if number == 0:
            mine = lax.axis_index(self.axes[0][0])
            slot, local = self.slots[0], self.split.shape[1]
            slot[mine] = self.extra()
            slot[mine, 1:2, :] = self.full[0:1, :]
            slot[mine, 2:3, : self.short.shape[1]] = self.short[...]
            slot[mine, 3:4, pl.ds(pl.multiple_of(lax.axis_index("tp") * local, local), local)] = self.split[...]
        else:
            for copy in self.copies(number - 1):
                copy.wait_recv()
            slot = self.slots[number - 1]
            total = slot[0]
            for k in range(1, self.axes[number - 1][1]):
                total = total + slot[k]
        if number == len(self.axes):
            self.out[...] = total
            return
        if number > 0:
            self.slots[number][lax.axis_index(self.axes[number][0])] = total
        for copy in self.copies(number):
            copy.start()

    def finish(self):
        for number in range(len(self.axes)):
            for copy in self.copies(number):
                copy.wait_send()


def line_sum(
    name, part, halves, gain, n_out, epilogue, collective_id, jobs=(), operands=(), chunk=32, skew=2
):
    size = lax.axis_size("tp")
    product = isinstance(part, tuple)
    operands = [o if isinstance(o, tuple) else (o,) for o in operands]
    operand_shapes = [(o[0].shape[0], sum(p.shape[1] for p in o)) for o in operands]
    pieces = [p for o in operands for p in o]
    if product:
        left_at, right_at, part_dims = part
        rows = operand_shapes[left_at][0]
        width = operand_shapes[right_at][1 - part_dims[1][0]]
    else:
        rows, width = part.shape
    half = rows // 2
    chunk = min(chunk, half)
    count = half // chunk
    group = min(128, half)
    groups = half // group
    per_group = group // chunk
    vector = [job for job in jobs if isinstance(job, VectorJob)]

    def kernel(*refs):
        refs = list(refs)

        def take(n):
            taken = refs[:n]
            del refs[:n]
            return taken

        part_refs, (gain_ref,) = take(0 if product else 1), take(1)
        half_refs = take(len(halves))
        operand_refs = take(len(pieces))
        job_ins = [take(len(job.inputs)) for job in jobs]
        (result_ref,) = take(1)
        own_refs = take(n_out)
        (gain_part_ref,) = take(1)
        job_outs = [take(len(job.out_shape)) for job in jobs]
        part_here, came, sum_send, sum_recv, back_send, back_recv, operand_sem, half_sem, own_sem, part_sem = take(10)
        out_ref, out_sem = take(2)
        half_here = take(len(halves))
        operand_here = take(len(operands))
        own_here = take(n_out)
        job_scratch = [take(len(job.scratch)) for job in jobs]
        place = lax.axis_index("tp")
        first, last = place == 0, place == size - 1
        source = (first, last)
        owner = (last, first)
        ahead = (place + 1, place - 1)
        behind = (place - 1, place + 1)
        base = (half, 0)

        loaded = set()

        def operand_copies(i):
            first, column = sum(len(o) for o in operands[:i]), 0
            for n, piece in enumerate(operands[i], first):
                where = operand_here[i].at[:, pl.ds(column, piece.shape[1])]
                yield pltpu.make_async_copy(operand_refs[n], where, operand_sem.at[n])
                column += piece.shape[1]

        def need(places):
            for i in places:
                if i not in loaded:
                    for copy in operand_copies(i):
                        copy.wait()
                    loaded.add(i)

        def half_copy(way, i):
            start = base[way] if half_refs[i].shape[0] == rows else 0
            return pltpu.make_async_copy(half_refs[i].at[pl.ds(start, half), :], half_here[i], half_sem.at[i])

        def part_copy(way, g):
            where = pl.ds(pl.multiple_of(base[way] + g * group, group), group)
            return pltpu.make_async_copy(part_refs[0].at[where, :], part_here.at[where, :], part_sem.at[way, g])

        if not product:
            for g in range(groups):
                for way in range(2):

                    @pl.when(jnp.logical_not(source[way]))
                    def _():
                        part_copy(way, g).start()

        def load(places):
            for i in places:
                for copy in operand_copies(i):
                    copy.start()

        early = (left_at, right_at) if product else ()
        load(early)
        for ins, outs, scratch, job in zip(job_ins, job_outs, job_scratch, jobs):
            job.operands = operand_here
            job.bind(ins, outs, scratch)
        peers = [(jnp.logical_not(first), {"tp": place - 1}), (jnp.logical_not(last), {"tp": place + 1})]
        meet(peers + [(None, peer) for job in jobs for peer in job.peers()])

        def at(way, k):
            return pl.ds(pl.multiple_of(k * chunk + base[way], chunk), chunk)

        def onward(way, k, from_part):
            return pltpu.make_async_remote_copy(
                src_ref=(part_here if product else part_refs[0]).at[at(way, k), :] if from_part else came.at[way, k],
                dst_ref=came.at[way, k],
                send_sem=sum_send.at[way, k],
                recv_sem=sum_recv.at[way, k],
                device_id={"tp": ahead[way]},
                device_id_type=BY_AXIS,
            )

        def back(way, k):
            piece = out_ref.at[at(way, k), :]
            return pltpu.make_async_remote_copy(
                src_ref=piece,
                dst_ref=piece,
                send_sem=back_send.at[way, k],
                recv_sem=back_recv.at[way, k],
                device_id={"tp": behind[way]},
                device_id_type=BY_AXIS,
            )

        def save(way, k):
            return pltpu.make_async_copy(out_ref.at[at(way, k), :], result_ref.at[at(way, k), :], out_sem.at[way, k])

        def own_copy(k):
            where = pl.ds(pl.multiple_of(k * chunk, chunk), chunk)
            return pltpu.make_async_copy(own_here[0].at[where, :], own_refs[0].at[where, :], own_sem.at[k])

        def part_rows(j):
            way, g = lax.rem(j + jnp.where(place < size // 2, 0, 1), 2), j // 2
            where = pl.ds(pl.multiple_of((1 - way) * half + g * group, group), group)
            left = operand_here[left_at][where, :]
            for start in range(0, width, 512):
                cols = slice(start, min(start + 512, width))
                right = operand_here[right_at]
                right = right[:, cols] if part_dims == NN else right[cols, :]
                part_here[where, cols] = dot(left, right, part_dims).astype(BF16)
            for w in range(2):

                @pl.when(jnp.logical_and(source[w], way == w))
                def _():
                    @pl.loop(0, per_group)
                    def _(k):
                        onward(w, g * per_group + k, True).start()

        tasks, at_step = [], 0
        need(early)
        load([i for i in range(len(operands)) if i not in early])
        for way in range(2):

            @pl.when(owner[way])
            def _():
                for i in range(len(halves)):
                    half_copy(way, i).start()

        if product:
            tasks, at_step = [(-2, 2 * groups, part_rows, ())], 2 * groups - 2
        else:
            for way in range(2):

                @pl.when(source[way])
                def _():
                    @pl.loop(0, count)
                    def _(k):
                        onward(way, k, True).start()

        for job in jobs:
            job.start()
        gain_part_ref[...] = jnp.zeros_like(gain_part_ref)

        away = (place - 1, size - 2 - place)

        def each_way(step, lead, act):
            for way in range(2):
                k = step - skew * lead[way]

                @pl.when(jnp.logical_and(k >= 0, k < count))
                def _():
                    act(way, k)

        def add(way, k):
            @pl.when(jnp.logical_not(source[way]))
            def _():
                if not product:

                    @pl.when(k % per_group == 0)
                    def _():
                        part_copy(way, k // per_group).wait()

                onward(way, k, False).wait_recv()
                total = came[way, k].astype(F32) + part_here[at(way, k), :].astype(F32)

                @pl.when(owner[way])
                def _():
                    @pl.when(k == 0)
                    def _():
                        for i in range(len(halves)):
                            half_copy(way, i).wait()

                    own = pl.ds(pl.multiple_of(k * chunk, chunk), chunk)
                    out_ref[at(way, k), :] = epilogue(
                        half_here, gain_ref[...], own_here[0] if n_out else None, gain_part_ref, own, total
                    )
                    back(way, k).start()
                    save(way, k).start()
                    if n_out:
                        own_copy(k).start()

                @pl.when(jnp.logical_not(owner[way]))
                def _():
                    came[way, k] = total.astype(BF16)
                    onward(way, k, False).start()

        def spread(way, k):
            @pl.when(jnp.logical_not(owner[way]))
            def _():
                back(way, k).wait_recv()

                @pl.when(jnp.logical_not(source[way]))
                def _():
                    back(way, k).start()

                save(way, k).start()

        steps = count + skew * (size - 2)
        extra, followed = 0, None
        for job in jobs:
            if isinstance(job, ForwardJob):
                slowest = max(job.first, per_group + skew * (size - 2))
                extra = max(0, slowest + (groups - 1) * per_group + 2 - steps, job.first + 2 * groups - steps)
                arrivals = [jnp.maximum(job.first, per_group + skew * away[1 - way]) for way in range(2)]
                begins = [jnp.where(owner[way], job.first, arrivals[way]) for way in range(2)]
                followed = out_ref, begins, [jnp.where(o, 2, per_group) for o in owner], groups, base
        for job in vector:
            job.extra = lambda: jnp.where(
                lax.broadcasted_iota(jnp.int32, (8, width), 0) == 0, gain_part_ref[...], 0.0
            )
        for job in jobs:
            for tiles, act, needs in job.tasks():
                tasks.append((at_step, tiles, act, needs))
                at_step += tiles
            job.ready_at = at_step
        acts = sorted((cut, n, i) for n, job in enumerate(jobs) for i, cut in enumerate(job.cuts(steps)))
        bounds = {t[0] for t in tasks} | {t[0] + t[1] for t in tasks}
        for number, (act, lead) in enumerate([(add, away), (spread, (away[1], away[0]))]):
            base_step, high = number * steps, (number + 1) * steps + (extra if number else 0)
            low = min([base_step] + [t[0] for t in tasks if number == 0])
            here = [a for a in acts if low <= a[0] < high]
            edges = sorted({low, high} | {a[0] for a in here} | {e for e in bounds if low < e < high})
            for left, right in zip(edges[:-1], edges[1:]):
                for cut, n, i in here:
                    if cut == left:
                        jobs[n].advance(i)
                active = [t for t in tasks if t[0] <= left and right <= t[0] + t[1]]
                for t in active:
                    need(t[3])

                @pl.loop(left - base_step, right - base_step)
                def _(step):
                    each_way(step, lead, act)
                    for t in active:
                        t[2](step + base_step - t[0])
                    for job in jobs:
                        if number and right - base_step > job.first:
                            job.follow(step, followed)

        for first_step, tiles, act, needs in tasks:
            done = min(max(2 * steps - first_step, 0), tiles)
            if done < tiles:
                need(needs)

                @pl.loop(done, tiles)
                def _(i):
                    act(i)

        need(range(len(operands)))
        for job in jobs:
            job.finish()

        for way in range(2):

            @pl.loop(0, count)
            def _(k):
                save(way, k).wait()

            @pl.when(jnp.logical_not(owner[way]))
            def _():
                @pl.loop(0, count)
                def _(k):
                    onward(way, k, False).wait_send()

            @pl.when(jnp.logical_not(source[way]))
            def _():
                @pl.loop(0, count)
                def _(k):
                    back(way, k).wait_send()

            if n_out:

                @pl.when(owner[way])
                def _():
                    @pl.loop(0, count)
                    def _(k):
                        own_copy(k).wait()

    scratch = [
        pltpu.VMEM((rows, width), BF16),
        pltpu.VMEM((2, count, chunk, width), BF16),
        *[pltpu.SemaphoreType.DMA((2, count)) for _ in range(4)],
        pltpu.SemaphoreType.DMA((max(1, len(pieces)),)),
        pltpu.SemaphoreType.DMA((max(1, len(halves)),)),
        pltpu.SemaphoreType.DMA((count,)),
        pltpu.SemaphoreType.DMA((2, groups)),
        pltpu.VMEM((rows, width), BF16),
        pltpu.SemaphoreType.DMA((2, count)),
        *[pltpu.VMEM((half, width), h.dtype) for h in halves],
        *[pltpu.VMEM(shape, o[0].dtype) for shape, o in zip(operand_shapes, operands)],
        *[pltpu.VMEM((half, width), F32)] * n_out,
    ]
    return pl.pallas_call(
        kernel,
        out_shape=[jax.ShapeDtypeStruct((rows, width), BF16)]
        + [jax.ShapeDtypeStruct((half, width), F32)] * n_out
        + [jax.ShapeDtypeStruct((8, width), F32)]
        + [shape for job in jobs for shape in job.out_shape],
        in_specs=[ANY] * (not product) + [WHOLE] + [ANY] * (len(halves) + len(pieces)) + [spec for job in jobs for spec in job.in_specs],
        out_specs=[ANY] + [ANY] * n_out + [WHOLE] + [spec for job in jobs for spec in job.out_specs],
        scratch_shapes=scratch + [shape for job in jobs for shape in job.scratch],
        compiler_params=pltpu.CompilerParams(
            collective_id=collective_id, has_side_effects=True, vmem_limit_bytes=VMEM_BYTES
        ),
        name=name,
    )(*([] if product else [part]), gain, *halves, *pieces, *[array for job in jobs for array in job.inputs])


def rms(value):
    return lax.rsqrt(jnp.mean(value * value, axis=-1, keepdims=True) + EPSILON)


def middle_rows(halves, gain, own_ref, gain_part_ref, own, total):
    middle = halves[0][own, :].astype(F32) + total
    own_ref[own, :] = middle
    return (middle * rms(middle) * gain).astype(BF16)


def output_rows(halves, gain, own_ref, gain_part_ref, own, total):
    return (halves[0][own, :] + total).astype(BF16)


def norm_back(grad, value, gain, gain_part_ref):
    inverse = rms(value)
    scaled = value * inverse
    weighted = grad * gain
    gain_part_ref[0:1, :] += jnp.sum(grad * scaled, axis=0, keepdims=True)
    return inverse * (weighted - scaled * jnp.mean(weighted * scaled, axis=-1, keepdims=True))


def grad_middle_rows(halves, gain, own_ref, gain_part_ref, own, total):
    back = norm_back(total, halves[0][own, :], gain, gain_part_ref)
    grad_middle = halves[1][own, :].astype(F32) + back
    own_ref[own, :] = grad_middle
    return grad_middle.astype(BF16)


def input_grad_rows(halves, gain, own_ref, gain_part_ref, own, total):
    back = norm_back(total, halves[0][own, :].astype(F32), gain, gain_part_ref)
    return (halves[1][own, :] + back).astype(BF16)


def lower_ones(length):
    at = lax.broadcasted_iota(jnp.int32, (length, length), 0)
    before = lax.broadcasted_iota(jnp.int32, (length, length), 1)
    return at >= before


def chunk_decay(forget, gap, live, lower):
    closing = sigmoid(-forget)
    opened = gap * closing
    remain = 1.0 - opened
    decay = jnp.where(live, jnp.log(remain), 0.0)
    keys = jnp.where(live, opened, 0.0)
    return closing, remain, keys, ones_times(lower, decay)


def rows_live(valid_ref, chunk_index, length):
    at = lax.broadcasted_iota(jnp.int32, (length, HEAD_DIM), 0) + chunk_index * length
    return at < valid_ref[0]


def span_end_kernel(heads, length, valid_ref, forget_ref, value_ref, gap_ref, end_ref):
    index = pl.program_id(0)

    @pl.when(index == 0)
    def _():
        end_ref[...] = jnp.zeros_like(end_ref)

    live = rows_live(valid_ref, index, length)
    lower = lower_ones(length).astype(BF16)
    for h in range(heads):
        cols = slice(h * HEAD_DIM, (h + 1) * HEAD_DIM)
        _, _, keys, cumulative = chunk_decay(forget_ref[:, cols], gap_ref[:, cols], live, lower)
        total = cumulative[length - 1 :, :]
        tail = (keys * jnp.exp(total - cumulative)).astype(BF16)
        end_ref[h] = jnp.exp(total) * end_ref[h] + dot(value_ref[:, cols].astype(BF16), tail, TN)


def mix_kernel(
    heads, length, valid_ref, query_ref, forget_ref, value_ref, gate_ref, gap_ref, gain_ref, start_ref,
    gated_ref, mixed_ref, states_ref, end_ref, state_ref,
):
    index = pl.program_id(0)

    @pl.when(index == 0)
    def _():
        state_ref[...] = start_ref[...]

    live = rows_live(valid_ref, index, length)
    mask = lower_ones(length)
    lower = mask.astype(BF16)
    for h in range(heads):
        cols = slice(h * HEAD_DIM, (h + 1) * HEAD_DIM)
        _, _, keys, cumulative = chunk_decay(forget_ref[:, cols], gap_ref[:, cols], live, lower)
        pre = query_ref[:, cols]
        queries = (pre * sigmoid(pre) * jnp.exp(cumulative)).astype(BF16)
        shrunk = keys * jnp.exp(-cumulative)
        values = value_ref[:, cols].astype(BF16)
        state = state_ref[h]
        states_ref[0, h] = state
        scores = jnp.where(mask, dot(queries, shrunk.astype(BF16), NT), 0.0).astype(BF16)
        mixed = dot(scores, values) + dot(queries, state.astype(BF16), NT)
        mixed_ref[:, cols] = mixed
        growth = jnp.exp(cumulative[length - 1 :, :])
        state_ref[h] = growth * state + dot(values, (shrunk * growth).astype(BF16), TN)
        gate = gate_ref[:, cols]
        gated_ref[:, cols] = (mixed * rms(mixed) * gain_ref[...] * (gate * sigmoid(gate))).astype(BF16)

    @pl.when(index == pl.num_programs(0) - 1)
    def _():
        end_ref[...] = state_ref[...]


def span_begin_kernel(heads, length, *refs):
    span_begin_chunk(heads, length, pl.program_id(0), pl.num_programs(0), *refs)


def span_begin_chunk(
    heads, length, step, steps, valid_ref, grad_ref, mixed_ref, query_ref, forget_ref, gate_ref, gap_ref, gain_ref,
    grad_gate_ref, grad_mixed_ref, gain_part_ref, begin_ref,
):
    index = steps - 1 - step

    @pl.when(step == 0)
    def _():
        begin_ref[...] = jnp.zeros_like(begin_ref)
        gain_part_ref[...] = jnp.zeros_like(gain_part_ref)

    live = rows_live(valid_ref, index, length)
    lower = lower_ones(length).astype(BF16)
    gain = gain_ref[...]
    for h in range(heads):
        cols = slice(h * HEAD_DIM, (h + 1) * HEAD_DIM)
        mixed = mixed_ref[:, cols]
        inverse = rms(mixed)
        scaled = mixed * inverse
        gate = gate_ref[:, cols]
        sig = sigmoid(gate)
        grad = grad_ref[:, cols].astype(F32)
        grad_gate_ref[:, cols] = (grad * scaled * gain * slope(gate, sig)).astype(BF16)
        grad_scaled = grad * (gate * sig)
        gain_part_ref[...] += jnp.sum(grad_scaled * scaled, axis=0, keepdims=True)
        weighted = grad_scaled * gain
        grad_mixed = inverse * (weighted - scaled * jnp.mean(weighted * scaled, axis=-1, keepdims=True))
        grad_mixed = grad_mixed.astype(BF16)
        grad_mixed_ref[:, cols] = grad_mixed
        _, _, _, cumulative = chunk_decay(forget_ref[:, cols], gap_ref[:, cols], live, lower)
        pre = query_ref[:, cols]
        queries = (pre * sigmoid(pre) * jnp.exp(cumulative)).astype(BF16)
        growth = jnp.exp(cumulative[length - 1 :, :])
        begin_ref[h] = growth * begin_ref[h] + dot(grad_mixed, queries, TN)


def mix_back_kernel(heads, length, *refs):
    mix_back_chunk(heads, length, pl.program_id(0), pl.num_programs(0), *refs)


def mix_back_chunk(
    heads, length, step, steps, valid_ref, grad_ref, query_ref, forget_ref, value_ref, gap_ref, states_ref, last_ref,
    end_ref, grad_query_ref, grad_forget_ref, grad_value_ref, gap_part_ref, flow_ref, after_ref,
):
    index = steps - 1 - step

    @pl.when(step == 0)
    def _():
        flow_ref[...] = end_ref[...]
        after_ref[...] = last_ref[...]
        gap_part_ref[...] = jnp.zeros_like(gap_part_ref)

    live = rows_live(valid_ref, index, length)
    mask = lower_ones(length)
    lower = mask.astype(BF16)
    for h in range(heads):
        cols = slice(h * HEAD_DIM, (h + 1) * HEAD_DIM)
        gap = gap_ref[:, cols]
        closing, remain, keys, cumulative = chunk_decay(forget_ref[:, cols], gap, live, lower)
        pre = query_ref[:, cols]
        sig = sigmoid(pre)
        growth = jnp.exp(cumulative)
        shrink = jnp.exp(-cumulative)
        end_growth = growth[length - 1 :, :]
        queries = (pre * sig * growth).astype(BF16)
        shrunk_wide = keys * shrink
        shrunk = shrunk_wide.astype(BF16)
        tail = (shrunk_wide * end_growth).astype(BF16)
        values = value_ref[:, cols].astype(BF16)
        grad = grad_ref[:, cols]
        state = states_ref[0, h]
        flow = flow_ref[h]
        low_flow = flow.astype(BF16)
        scores = jnp.where(mask, dot(queries, shrunk, NT), 0.0).astype(BF16)
        grad_scores = jnp.where(mask, dot(grad, values, NT), 0.0).astype(BF16)
        to_queries = dot(grad, state.astype(BF16)) + dot(grad_scores, shrunk)
        to_keys = dot(grad_scores, queries, TN) + end_growth * dot(values, low_flow)
        grad_value_ref[:, cols] = (dot(scores, grad, TN) + dot(tail, low_flow, NT)).astype(BF16)
        grad_query_ref[:, cols] = (to_queries * growth * slope(pre, sig)).astype(BF16)
        terms = queries.astype(F32) * to_queries - shrunk.astype(F32) * to_keys
        high = terms.astype(BF16)
        rest = (terms - high.astype(F32)).astype(BF16)
        suffix = dot(lower, high, TN) + dot(lower, rest, TN)
        crossing = jnp.sum(flow * after_ref[h], axis=0, keepdims=True)
        pressure = jnp.where(live, to_keys * shrink - (suffix + crossing) / remain, 0.0)
        gap_part_ref[:, cols] += jnp.sum(closing * pressure, axis=0, keepdims=True)
        grad_forget_ref[:, cols] = (-closing * (1.0 - closing) * gap * pressure).astype(BF16)
        flow_ref[h] = end_growth * flow + dot(grad, queries, TN)
        after_ref[h] = state


def plain_call(kernel, name, grid, in_specs, out_specs, out_shape, scratch, flops, moved):
    return pl.pallas_call(
        kernel,
        grid_spec=pltpu.PrefetchScalarGridSpec(
            num_scalar_prefetch=1, grid=grid, in_specs=in_specs, out_specs=out_specs, scratch_shapes=scratch
        ),
        out_shape=out_shape,
        compiler_params=pltpu.CompilerParams(
            dimension_semantics=("arbitrary",), vmem_limit_bytes=VMEM_BYTES
        ),
        cost_estimate=pl.CostEstimate(flops=flops, bytes_accessed=moved, transcendentals=flops // 64),
        name=name,
    )


def combine(earlier, later):
    return (earlier[0] * later[0], later[0][:, None, :] * earlier[1] + later[1])


def from_earlier(state, decay, axis):
    size = lax.axis_size(axis)
    if size == 2:
        return lax.ppermute(state, axis, [(0, 1)])
    mine = lax.axis_index(axis)
    states, decays = lax.all_gather(state, axis), lax.all_gather(decay, axis)
    total = jnp.zeros_like(state)
    for k in range(size):
        new = decays[k][:, None, :] * total + states[k]
        total = jnp.where(k < mine, new, total)
    return total


def from_later(state, decay, axis):
    size = lax.axis_size(axis)
    if size == 2:
        return lax.ppermute(state, axis, [(1, 0)])
    mine = lax.axis_index(axis)
    states, decays = lax.all_gather(state, axis), lax.all_gather(decay, axis)
    total = jnp.zeros_like(state)
    for k in reversed(range(size)):
        new = decays[k][:, None, :] * total + states[k]
        total = jnp.where(k > mine, new, total)
    return total


def per_device(
    inputs, lengths, w_query, w_forget, w_input, w_outgate, w_output, w_gate, w_up, w_down,
    norm_gain, ffn_gain, head_gain, forget_gap, cotangent,
):
    groups, span, width = inputs.shape
    rows = groups * span
    fsdp, ctx, tp = lax.axis_size("fsdp"), lax.axis_size("ctx"), lax.axis_size("tp")
    local = forget_gap.shape[0]
    heads = local // HEAD_DIM
    ff = w_gate.shape[1]
    length = min(128, span)
    chunks = span // length
    place = lax.axis_index("tp")

    valid = jnp.clip(lengths - lax.axis_index("ctx") * span, 0, span).astype(jnp.int32)
    x = inputs.reshape(rows, width)
    gap = forget_gap.reshape(1, local)
    head_row = head_gain.reshape(1, HEAD_DIM)
    norm_row, ffn_row = norm_gain.reshape(1, width), ffn_gain.reshape(1, width)

    pre, normed, grad_low, w_four, w_out = project(
        x, cotangent.reshape(rows, width), norm_row, valid, [w_query, w_forget, w_input, w_outgate], w_output, 1
    )

    def column(j):
        return pl.BlockSpec((length, local), lambda i, *_: (i, j))

    def column_back(j):
        return pl.BlockSpec((length, local), lambda i, *_: (chunks - 1 - i, j))

    fixed = lambda shape: pl.BlockSpec(shape, lambda i, *_: (0,) * len(shape))
    state_shape = (heads, HEAD_DIM, HEAD_DIM)
    work = 2 * rows * local * HEAD_DIM
    moved = rows * local * 4

    local_end = plain_call(
        functools.partial(span_end_kernel, heads, length), "span_end", (chunks,),
        [column(1), column(2), fixed((1, local))], fixed(state_shape),
        jax.ShapeDtypeStruct(state_shape, F32), [], 3 * work, 2 * moved,
    )(valid, pre, pre, gap)
    span_decay = None
    if ctx > 2:
        keep = (jnp.arange(rows, dtype=jnp.int32) < valid[0])[:, None]
        closing = jax.nn.sigmoid(-pre[:, local : 2 * local])
        logs = jnp.where(keep, jnp.log(1.0 - gap * closing), 0.0)
        span_decay = jnp.exp(jnp.sum(logs, axis=0)).reshape(heads, HEAD_DIM)
    start = from_earlier(local_end, span_decay, "ctx")
    gated, mixed, states, state_end = plain_call(
        functools.partial(mix_kernel, heads, length), "mix", (chunks,),
        [column(0), column(1), column(2), column(3), fixed((1, local)), fixed((1, HEAD_DIM)), fixed(state_shape)],
        [column(0), column(0), pl.BlockSpec((1,) + state_shape, lambda i, *_: (i, 0, 0, 0)), fixed(state_shape)],
        [
            jax.ShapeDtypeStruct((rows, local), BF16),
            jax.ShapeDtypeStruct((rows, local), F32),
            jax.ShapeDtypeStruct((chunks,) + state_shape, F32),
            jax.ShapeDtypeStruct(state_shape, F32),
        ],
        [pltpu.VMEM(state_shape, F32)], 6 * work, 6 * moved,
    )(valid, pre, pre, pre, pre, gap, head_row, start)

    normed_two, middle, _, w_both, w_back, hidden, grad_gate, grad_up = line_sum(
        "sum_branch", (0, 1, NN), [x], ffn_row, 1, middle_rows, 2,
        [ForwardJob([w_gate, w_up, w_down], grad_low, min(128, rows // 2), 5)], [gated, w_out],
    )

    both_axes = ("fsdp", "ctx")

    def scattered(grads, dims):
        if ctx == 2:
            return [ScatterJob(grads, dims)], None
        return [], [
            lax.psum_scatter(g, both_axes, scatter_dimension=d, tiled=True).astype(F32) for g, d in zip(grads, dims)
        ]

    grad_branch, grad_middle, ffn_gain_part, grad_w_down, grad_w_both = line_sum(
        "sum_norm_two", (0, 1, NT), [middle, grad_low], ffn_row, 1, grad_middle_rows, 3,
        [ProductJob(2, 3, TN, (ff, width), 128), ProductJob(4, 0, TN, (width, 2 * ff), 128)],
        [(grad_gate, grad_up), w_both, hidden, grad_low, normed_two],
    )

    jobs, sums_ffn = scattered([grad_w_both, grad_w_down], [0, 1])
    if ctx == 2:
        jobs.append(MixBackJob(valid, grad_branch, w_out, mixed, pre, states, gap, head_row, state_end))
    result, _, *more = line_sum(
        "sum_feed", (0, 1, NN), [middle], ffn_row, 0, output_rows, 5, jobs, [hidden, w_back]
    )
    result = result.reshape(groups, span, width)
    if ctx == 2:
        out_both, out_down, grad_query, grad_forget, grad_value, grad_outgate, gap_part, head_part = more
    else:
        out_both, out_down = sums_ffn
        grad_gated = dot(grad_branch, w_out, NT)
        grad_outgate, grad_mixed, head_part, local_begin = plain_call(
            functools.partial(span_begin_kernel, heads, length), "span_begin", (chunks,),
            [column_back(0), column_back(0), column_back(0), column_back(1), column_back(3), fixed((1, local)),
             fixed((1, HEAD_DIM))],
            [column_back(0), column_back(0), fixed((1, HEAD_DIM)), fixed(state_shape)],
            [
                jax.ShapeDtypeStruct((rows, local), BF16),
                jax.ShapeDtypeStruct((rows, local), BF16),
                jax.ShapeDtypeStruct((1, HEAD_DIM), F32),
                jax.ShapeDtypeStruct(state_shape, F32),
            ],
            [], 3 * work, 6 * moved,
        )(valid, grad_gated, mixed, pre, pre, pre, gap, head_row)
        grad_end = from_later(local_begin, span_decay, "ctx")
        grad_query, grad_forget, grad_value, gap_part = plain_call(
            functools.partial(mix_back_kernel, heads, length), "mix_back", (chunks,),
            [column_back(0), column_back(0), column_back(1), column_back(2), fixed((1, local)),
             pl.BlockSpec((1,) + state_shape, lambda i, *_: (chunks - 1 - i, 0, 0, 0)), fixed(state_shape),
             fixed(state_shape)],
            [column_back(0), column_back(0), column_back(0), fixed((1, local))],
            [jax.ShapeDtypeStruct((rows, local), BF16)] * 3 + [jax.ShapeDtypeStruct((1, local), F32)],
            [pltpu.VMEM(state_shape, F32), pltpu.VMEM(state_shape, F32)], 12 * work, 6 * moved,
        )(valid, grad_mixed, pre, pre, pre, gap, states, state_end, grad_end)

    grad_four = (grad_query, grad_forget, grad_value, grad_outgate)
    jobs, operands, sums_mix = [VectorJob(ffn_gain_part, head_part, gap_part)], [grad_four, w_four], None
    if ctx == 2:
        shapes = [(width, 4 * local), (local, width)]
        jobs.append(ProductScatterJob([(2, 0), (3, 4)], shapes, [0, 1]))
        operands += [normed, gated, grad_branch]
    else:
        grads = [dot(normed, jnp.concatenate(grad_four, axis=1), TN).astype(BF16), dot(gated, grad_branch, TN).astype(BF16)]
        _, sums_mix = scattered(grads, [0, 1])
    input_grad, _, sums, *more = line_sum(
        "sum_norm_one", (0, 1, NT), [x, grad_middle], norm_row, 0, input_grad_rows, 4, jobs, operands
    )
    out_four, out_output = sums_mix or more
    input_grad = input_grad.reshape(groups, span, width)
    grad_norm_gain, grad_ffn_gain, grad_head_gain = sums[0], sums[1], sums[2, :HEAD_DIM]
    grad_gap = lax.dynamic_slice(sums[3], (place * local,), (local,))
    return (
        result,
        input_grad,
        out_four[:, :local],
        out_four[:, local : 2 * local],
        out_four[:, 2 * local : 3 * local],
        out_four[:, 3 * local :],
        out_output,
        out_both[:, :ff],
        out_both[:, ff:],
        out_down,
        grad_norm_gain,
        grad_ffn_gain,
        grad_head_gain,
        grad_gap,
    )


def solution(mesh):
    tokens = P("fsdp", "ctx", None)
    inward, outward = P("fsdp", "tp"), P("tp", "fsdp")
    grad_in, grad_back = P(("fsdp", "ctx"), "tp"), P("tp", ("fsdp", "ctx"))
    return jax.shard_map(
        per_device,
        mesh=mesh,
        in_specs=(tokens, P("fsdp")) + (inward,) * 4 + (outward, inward, inward, outward)
        + (P(), P(), P(), P("tp"), tokens),
        out_specs=(tokens, tokens) + (grad_in,) * 4 + (grad_back, grad_in, grad_in, grad_back)
        + (P(), P(), P(), P("tp")),
        check_vma=False,
    )
```

```python
import functools

import jax
import jax.numpy as jnp
from jax import lax
from jax.experimental import pallas as pl
from jax.experimental.pallas import tpu as pltpu
from jax.sharding import PartitionSpec as P

HEAD_DIM = 128
EPSILON = 1e-05
F32 = jnp.float32
BF16 = jnp.bfloat16
BY_AXIS = pl.DeviceIdType.MESH
VMEM_BYTES = 67043328
ANY = pl.BlockSpec(memory_space=pl.ANY)
WHOLE = pl.BlockSpec(memory_space=pltpu.VMEM)


def dot(left, right, dims=((1,), (0,))):
    return lax.dot_general(left, right, (dims, ((), ())), preferred_element_type=F32)


NN = ((1,), (0,))
NT = ((1,), (1,))
TN = ((0,), (0,))


def sigmoid(value):
    return 1.0 / (1.0 + jnp.exp(-value))


def slope(pre, sig):
    return sig * (1.0 + pre * (1.0 - sig))


def ones_times(ones, value):
    high = value.astype(BF16)
    rest = (value - high.astype(F32)).astype(BF16)
    return dot(ones, high) + dot(ones, rest)


def ring_place(index, size, folded):
    if folded:
        return index + (index // 2) * (1 - 2 * (index % 2))
    return index


class RingGather:
    def __init__(self, shards, outs, where, sems, size, folded):
        self.shards, self.outs, self.where, self.size = shards, outs, where, size
        self.ring_send, self.ring_recv, self.pair_send, self.pair_recv, self.local = sems
        self.place = ring_place(lax.axis_index("fsdp"), size, folded)
        self.folded = folded
        self.core = lax.axis_index("ctx") % 2
        self.pair = lax.axis_index("ctx") + 1 - 2 * self.core

    def device(self, place):
        return ring_place(lax.rem(place + 2 * self.size, self.size), self.size, self.folded)

    def peers(self):
        return [
            {"fsdp": self.device(self.place + 1)},
            {"fsdp": self.device(self.place - 1)},
            {"ctx": self.pair},
        ]

    def rows(self, i, core, way):
        quarter = self.shards[i].shape[0] // 4
        return pl.multiple_of((2 * way + core) * quarter, 16), quarter

    def in_shard(self, i, core, way):
        at, length = self.rows(i, core, way)
        return self.shards[i].at[pl.ds(at, length), :]

    def in_out(self, i, block, core, way):
        out, dim, column = self.where[i]
        at, length = self.rows(i, core, way)
        deep, wide = self.shards[i].shape
        if dim == 0:
            start = pl.multiple_of(block * deep + at, 16)
            return self.outs[out].at[pl.ds(start, length), pl.ds(column, wide)]
        start = pl.multiple_of(block * wide, 128)
        return self.outs[out].at[pl.ds(at, length), pl.ds(start, wide)]

    def own_block(self, i):
        out, dim, column = self.where[i]
        deep, wide = self.shards[i].shape
        block = self.device(self.place)
        if dim == 0:
            start = pl.multiple_of(block * deep, 16)
            return self.outs[out].at[pl.ds(start, deep), pl.ds(column, wide)]
        return self.outs[out].at[:, pl.ds(pl.multiple_of(block * wide, 128), wide)]

    def local_copy(self, i):
        return pltpu.make_async_copy(self.shards[i], self.own_block(i), self.local.at[i])

    def ring(self, i, way, step):
        sign = 1 - 2 * way
        block = self.device(self.place - sign * step)
        there = self.in_out(i, block, self.core, way)
        here = self.in_shard(i, self.core, way) if step == 0 else there
        at = (i * 2 + way) * (self.size - 1) + step
        return pltpu.make_async_remote_copy(
            src_ref=here,
            dst_ref=there,
            send_sem=self.ring_send.at[at],
            recv_sem=self.ring_recv.at[at],
            device_id={"fsdp": self.device(self.place + sign)},
            device_id_type=BY_AXIS,
        )

    def across(self, i, way, step, core):
        sign = 1 - 2 * way
        block = self.device(self.place - sign * (step + 1))
        piece = self.in_out(i, block, core, way)
        at = (i * 2 + way) * (self.size - 1) + step
        return pltpu.make_async_remote_copy(
            src_ref=piece,
            dst_ref=piece,
            send_sem=self.pair_send.at[at],
            recv_sem=self.pair_recv.at[at],
            device_id={"ctx": self.pair},
            device_id_type=BY_AXIS,
        )

    def each(self):
        return [(i, way) for i in range(len(self.shards)) for way in range(2)]

    def start(self):
        for i, way in self.each():
            self.ring(i, way, 0).start()
        for i in range(len(self.shards)):
            self.local_copy(i).start()

    def advance(self, step):
        for i, way in self.each():
            arrived = self.ring(i, way, step)
            arrived.wait_recv()
            if step + 1 < self.size - 1:
                self.ring(i, way, step + 1).start()
            self.across(i, way, step, self.core).start()

    def wait_across(self, arrays, step):
        for i in arrays:
            for way in range(2):
                self.across(i, way, step, 1 - self.core).wait_recv()

    def finish(self, waited=()):
        for i, way in self.each():
            for step in range(self.size - 1):
                self.ring(i, way, step).wait_send()
                self.across(i, way, step, self.core).wait_send()
                if i not in waited:
                    self.across(i, way, step, 1 - self.core).wait_recv()
        for i in range(len(self.shards)):
            if i not in waited:
                self.local_copy(i).wait()

    @staticmethod
    def scratch(count, size):
        copies = count * 2 * (size - 1)
        return [pltpu.SemaphoreType.DMA((copies,)) for _ in range(4)] + [
            pltpu.SemaphoreType.DMA((count,))
        ]


class RingScatter:
    def __init__(self, grads, results, dims, scratch, sems, size, folded):
        self.grads, self.results, self.dims, self.size, self.folded = grads, results, dims, size, folded
        count = len(grads)
        self.own, self.came, self.passed, self.outs = (scratch[n * count : (n + 1) * count] for n in range(4))
        self.pair_send, self.pair_recv, self.local, self.ring_send, self.ring_recv, self.saved = sems
        self.place = ring_place(lax.axis_index("fsdp"), size, folded)
        self.core = lax.axis_index("ctx")

    device = RingGather.device

    def peers(self):
        return [
            {"fsdp": self.device(self.place + 1)},
            {"fsdp": self.device(self.place - 1)},
            {"ctx": 1 - self.core},
        ]

    def block(self, i, offset, core):
        index = self.device(self.place + offset) * 2 + core
        extent = self.outs[i].shape[self.dims[i]]
        start = pl.multiple_of(index * extent, extent)
        if self.dims[i] == 0:
            return self.grads[i].at[pl.ds(start, extent), :]
        return self.grads[i].at[:, pl.ds(start, extent)]

    def local_copy(self, i, offset):
        return pltpu.make_async_copy(
            self.block(i, offset, self.core), self.own[i].at[offset], self.local.at[i * self.size + offset]
        )

    def across(self, i, offset):
        at = i * self.size + offset
        give = self.own[i].at[0, offset] if self.grads[i] is None else self.block(i, offset, 1 - self.core)
        return pltpu.make_async_remote_copy(
            src_ref=give,
            dst_ref=self.came[i].at[offset],
            send_sem=self.pair_send.at[at],
            recv_sem=self.pair_recv.at[at],
            device_id={"ctx": 1 - self.core},
            device_id_type=BY_AXIS,
        )

    def offset(self, way, step):
        return (-(step + 1) if way == 0 else step + 1) % self.size

    def ring(self, i, way, step):
        half = self.outs[i].shape[0] // 2
        at = (i * 2 + way) * (self.size - 1) + step
        return pltpu.make_async_remote_copy(
            src_ref=self.came[i].at[self.offset(way, step), pl.ds(way * half, half), :],
            dst_ref=self.passed[i].at[way, step],
            send_sem=self.ring_send.at[at],
            recv_sem=self.ring_recv.at[at],
            device_id={"fsdp": self.device(self.place + 1 - 2 * way)},
            device_id_type=BY_AXIS,
        )

    def order(self):
        used = []
        for step in range(self.size):
            for way in range(2):
                if self.offset(way, step) not in used:
                    used.append(self.offset(way, step))
        return used

    def start(self):
        for offset in self.order():
            for i in range(len(self.grads)):
                self.across(i, offset).start()
                self.local_copy(i, offset).start()

    def advance(self, step):
        before = {self.offset(way, s) for s in range(step) for way in range(2)}
        fresh = {self.offset(way, step) for way in range(2)} - before
        for i in range(len(self.grads)):
            for offset in sorted(fresh):
                self.across(i, offset).wait_recv()
                if self.grads[i] is not None:
                    self.local_copy(i, offset).wait()
            for way in range(2):
                if step > 0:
                    self.ring(i, way, step - 1).wait_recv()
                self.add(i, way, step)
                if step < self.size - 1:
                    self.ring(i, way, step).start()
                else:
                    self.save(i, way).start()

    def save(self, i, way):
        half = self.outs[i].shape[0] // 2
        rows = pl.ds(way * half, half)
        return pltpu.make_async_copy(
            self.outs[i].at[rows, :], self.results[i].at[rows, :], self.saved.at[2 * i + way]
        )

    def add(self, i, way, step):
        half = self.outs[i].shape[0] // 2
        offset = self.offset(way, step)
        own, came, passed, out = self.own[i], self.came[i], self.passed[i], self.outs[i]

        @pl.loop(0, half // 16)
        def _(r):
            rows = pl.ds(pl.multiple_of(way * half + r * 16, 16), 16)
            kept = own[offset, rows, :] if self.grads[i] is not None else own[1, offset, rows, :]
            total = kept.astype(F32) + came[offset, rows, :].astype(F32)
            if step > 0:
                total += passed[way, step - 1, pl.ds(pl.multiple_of(r * 16, 16), 16), :].astype(F32)
            if step < self.size - 1:
                came[offset, rows, :] = total.astype(BF16)
            else:
                out[rows, :] = total

    def finish(self):
        for i in range(len(self.grads)):
            for offset in range(self.size):
                self.across(i, offset).wait_send()
            for way in range(2):
                self.save(i, way).wait()
                for step in range(self.size - 1):
                    self.ring(i, way, step).wait_send()

    @staticmethod
    def out_shape(grad, dim, size):
        deep, wide = grad.shape
        return (deep // (2 * size), wide) if dim == 0 else (deep, wide // (2 * size))

    @staticmethod
    def buffers(shapes, size):
        full = [pltpu.VMEM((size,) + s, BF16) for s in shapes]
        passed = [pltpu.VMEM((2, size - 1, s[0] // 2, s[1]), BF16) for s in shapes]
        return full + full + passed + [pltpu.VMEM(s, F32) for s in shapes]

    @staticmethod
    def scratch(count, size):
        return [pltpu.SemaphoreType.DMA((count * size,)) for _ in range(3)] + [
            pltpu.SemaphoreType.DMA((count * 2 * (size - 1),)) for _ in range(2)
        ] + [pltpu.SemaphoreType.DMA((2 * count,))]


def meet(peers):
    barrier = pltpu.get_barrier_semaphore()
    total = 0
    for condition, peer in peers:
        if condition is None:
            pl.semaphore_signal(barrier, inc=1, device_id=peer, device_id_type=BY_AXIS)
            total = total + 1
        else:

            @pl.when(condition)
            def _():
                pl.semaphore_signal(barrier, inc=1, device_id=peer, device_id_type=BY_AXIS)

            total = total + condition.astype(jnp.int32)
    pl.semaphore_wait(barrier, total)


def project(x, cotangent, gain, valid, shards, w_out_shard, collective_id):
    size = lax.axis_size("fsdp")
    rows, width = x.shape
    deep, local = shards[0].shape
    count = len(shards)
    total = count * local
    half = deep // 2
    tile = min(512, total)
    step_rows = min(64, rows)
    row_tile = min(512, rows)
    copies = 1 + 2 * (size - 1)

    def kernel(
        valid_ref, gain_ref, x_ref, cot_ref, *refs
    ):
        shard_refs, refs = refs[: count + 1], refs[count + 1 :]
        pre_ref, normed_ref, grad_ref, four_ref, out_ref = refs[:5]
        x_here, grad_here, normed, acc, four, in_sem, save_sem, four_sem, pre_sem = refs[5:14]
        where = [(0, 0, i * local) for i in range(count)] + [(1, 1, 0)]
        job = RingGather(shard_refs, [four, out_ref], where, refs[14:], size, size == 4)
        loads = [
            pltpu.make_async_copy(x_ref, x_here, in_sem.at[0]),
            pltpu.make_async_copy(cot_ref, grad_here, in_sem.at[1]),
        ]
        for load in loads:
            load.start()
        meet([(None, peer) for peer in job.peers()])
        job.start()
        loads[0].wait()

        @pl.loop(0, rows // step_rows)
        def _(r):
            at = pl.ds(pl.multiple_of(r * step_rows, step_rows), step_rows)
            wide = x_here[at, :].astype(F32)
            normed[at, :] = (wide * rms(wide) * gain_ref[...]).astype(BF16)

        saves = [
            pltpu.make_async_copy(normed, normed_ref, save_sem.at[0]),
            pltpu.make_async_copy(grad_here, grad_ref, save_sem.at[1]),
        ]
        saves[0].start()

        def save_four(start, length, number):
            at = pl.ds(start, length)
            return pltpu.make_async_copy(four.at[at, :], four_ref.at[at, :], four_sem.at[number])

        def save_pre(n):
            at = pl.ds(pl.multiple_of(n * tile, tile), tile)
            return pltpu.make_async_copy(acc.at[:, at], pre_ref.at[:, at], pre_sem.at[n])

        def multiply(start, length, first, last):
            @pl.loop(0, total // tile)
            def _(n):
                cols = pl.ds(pl.multiple_of(n * tile, tile), tile)
                deep_at = pl.ds(start, length)

                @pl.loop(0, rows // row_tile)
                def _(r):
                    at = pl.ds(pl.multiple_of(r * row_tile, row_tile), row_tile)
                    term = dot(normed[at, deep_at], four[deep_at, cols])
                    acc[at, cols] = term if first else acc[at, cols] + term

                if last:
                    save_pre(n).start()

        for i in range(count):
            job.local_copy(i).wait()
        own = pl.multiple_of(job.device(job.place) * deep, deep)
        save_four(own, deep, 0).start()
        multiply(own, deep, True, False)
        loads[1].wait()

        @pl.loop(0, rows // step_rows)
        def _(r):
            at = pl.ds(pl.multiple_of(r * step_rows, step_rows), step_rows)
            row = lax.broadcasted_iota(jnp.int32, (step_rows, width), 0) + r * step_rows
            wide = grad_here[at, :].astype(F32)
            grad_here[at, :] = jnp.where(row < valid_ref[0], wide, 0.0).astype(BF16)

        saves[1].start()
        for step in range(size - 1):
            job.advance(step)
            job.wait_across(range(count), step)
            for way in range(2):
                block = job.device(job.place - (1 - 2 * way) * (step + 1))
                start = pl.multiple_of(block * deep + way * half, half)
                save_four(start, half, 1 + 2 * step + way).start()
                multiply(start, half, False, step == size - 2 and way == 1)
        job.finish(range(count))
        for save in saves:
            save.wait()
        save_four(own, deep, 0).wait()
        for step in range(size - 1):
            for way in range(2):
                save_four(0, half, 1 + 2 * step + way).wait()
        for n in range(total // tile):
            save_pre(n).wait()

    return pl.pallas_call(
        kernel,
        out_shape=[
            jax.ShapeDtypeStruct((rows, total), F32),
            jax.ShapeDtypeStruct((rows, width), BF16),
            jax.ShapeDtypeStruct((rows, width), BF16),
            jax.ShapeDtypeStruct((width, total), BF16),
            jax.ShapeDtypeStruct((w_out_shard.shape[0], width), BF16),
        ],
        in_specs=[pl.BlockSpec(memory_space=pltpu.SMEM), WHOLE, ANY, ANY] + [ANY] * count + [WHOLE],
        out_specs=[ANY] * 5,
        scratch_shapes=[
            pltpu.VMEM((rows, width), BF16),
            pltpu.VMEM((rows, width), BF16),
            pltpu.VMEM((rows, width), BF16),
            pltpu.VMEM((rows, total), F32),
            pltpu.VMEM((width, total), BF16),
            pltpu.SemaphoreType.DMA((2,)),
            pltpu.SemaphoreType.DMA((2,)),
            pltpu.SemaphoreType.DMA((copies,)),
            pltpu.SemaphoreType.DMA((total // tile,)),
        ]
        + RingGather.scratch(count + 1, size),
        compiler_params=pltpu.CompilerParams(
            collective_id=collective_id, has_side_effects=True, vmem_limit_bytes=VMEM_BYTES
        ),
        name="project",
    )(valid, gain, x, cotangent, *shards, w_out_shard)


class Job:
    first = 0

    def tasks(self):
        return []

    def follow(self, step, ways):
        pass


class ForwardJob(Job):
    def __init__(self, shards, grad_low, rows_in_group, first):
        self.size = lax.axis_size("fsdp")
        self.rows, self.width = grad_low.shape
        self.ff = shards[0].shape[1]
        self.group, self.first = rows_in_group, first
        self.inputs, self.in_specs = [*shards, grad_low], [ANY] * 4
        self.out_shape = [
            jax.ShapeDtypeStruct((self.width, 2 * self.ff), BF16),
            jax.ShapeDtypeStruct((self.ff, self.width), BF16),
            *[jax.ShapeDtypeStruct((self.rows, self.ff), BF16)] * 3,
        ]
        self.out_specs = [ANY] * 5
        self.scratch = [
            pltpu.VMEM((self.width, 2 * self.ff), BF16),
            pltpu.VMEM((self.ff, self.width), BF16),
            pltpu.VMEM((self.rows, self.width), BF16),
            pltpu.VMEM((2, self.group, 2 * self.ff), F32),
            pltpu.VMEM((2, 3, self.group, self.ff), BF16),
            pltpu.SemaphoreType.DMA((3,)),
            pltpu.SemaphoreType.DMA((2, 3)),
            *RingGather.scratch(2, self.size),
            *RingGather.scratch(1, self.size),
        ]

    def bind(self, ins, outs, scratch):
        self.grad_low = ins[3]
        self.both_out, self.back_out, *self.outs = outs
        self.both, self.back, self.grad_here, self.products, self.stage, self.sem, self.stage_sem = scratch[:7]
        size = self.size
        self.inward = RingGather(ins[:2], [self.both], [(0, 0, 0), (0, 0, self.ff)], scratch[7:12], size, size == 4)
        self.outward = RingGather(ins[2:3], [self.back], [(0, 1, 0)], scratch[12:], size, size == 4)

    def peers(self):
        return self.inward.peers()

    def cuts(self, steps):
        ring = self.size - 1
        ahead = [((16 * (i + 1)) // ring * steps) // 20 for i in range(ring)]
        return ahead + [((16 + (9 * (i + 1)) // ring) * steps) // 20 for i in range(ring)]

    def load(self):
        return pltpu.make_async_copy(self.grad_low, self.grad_here, self.sem.at[0])

    def keep(self):
        return [
            pltpu.make_async_copy(self.both, self.both_out, self.sem.at[1]),
            pltpu.make_async_copy(self.back, self.back_out, self.sem.at[2]),
        ]

    def start(self):
        self.inward.start()
        self.load().start()

    def advance(self, number):
        ring = self.size - 1
        if number < ring:
            self.inward.advance(number)
            if number == max(0, ring - 2):
                self.outward.start()
            return
        self.outward.advance(number - ring)
        if number == 2 * ring - 1:
            for step in range(ring):
                self.inward.wait_across(range(2), step)
                self.outward.wait_across(range(1), step)
            for i in range(2):
                self.inward.local_copy(i).wait()
            self.outward.local_copy(0).wait()
            self.load().wait()
            for copy in self.keep():
                copy.start()

    def save(self, way, k, at):
        return pltpu.make_async_copy(self.stage.at[way, k], self.outs[k].at[at, :], self.stage_sem.at[way, k])

    def follow(self, step, ways):
        normed, begins, periods, groups, bases = ways

        @pl.loop(0, 2)
        def _(way):
            begin, period, base = (jnp.where(way == 0, pair[0], pair[1]) for pair in (begins, periods, bases))
            k = step - begin
            g = lax.div(k, period)
            part = lax.rem(k, period)
            busy = jnp.logical_and(k >= 0, g < groups)
            at = pl.ds(pl.multiple_of(base + g * self.group, self.group), self.group)

            @pl.when(jnp.logical_and(busy, part == 0))
            def _():
                product_tile(normed, self.both, NN, at, self.products.at[way])

            @pl.when(jnp.logical_and(busy, part == 1))
            def _():
                @pl.when(g > 0)
                def _():
                    for n in range(3):
                        self.save(way, n, at).wait()

                grad_rows = self.grad_here[at, :]
                products, stage, ff = self.products.at[way], self.stage.at[way], self.ff
                wide = min(512, ff)
                for start in range(0, ff, wide):
                    length = min(wide, ff - start)
                    cols = slice(start, start + length)
                    gate, up = products[:, cols], products[:, ff + start : ff + start + length]
                    grad = dot(grad_rows, self.back[cols, :], NT)
                    sig = sigmoid(gate)
                    value = gate * sig
                    stage[0, :, cols] = (value * up).astype(BF16)
                    stage[1, :, cols] = (grad * up * slope(gate, sig)).astype(BF16)
                    stage[2, :, cols] = (grad * value).astype(BF16)
                for n in range(3):
                    self.save(way, n, at).start()

    def finish(self):
        for way in range(2):
            for n in range(3):
                self.save(way, n, pl.ds(0, self.group)).wait()
        for copy in self.keep():
            copy.wait()
        self.inward.finish(range(2))
        self.outward.finish(range(1))


class ScatterJob(Job):
    def __init__(self, grads, dims):
        self.size = lax.axis_size("fsdp")
        self.dims = dims
        shapes = [RingScatter.out_shape(g, d, self.size) for g, d in zip(grads, dims)]
        self.inputs, self.in_specs = grads, [ANY] * len(grads)
        self.out_shape = [jax.ShapeDtypeStruct(s, F32) for s in shapes]
        self.out_specs = [ANY] * len(grads)
        self.scratch = RingScatter.buffers(shapes, self.size) + RingScatter.scratch(len(grads), self.size)

    def bind(self, ins, outs, scratch):
        self.job = RingScatter(
            ins, outs, self.dims, scratch[:-6], scratch[-6:], self.size, self.size == 4
        )

    def peers(self):
        return self.job.peers()

    def start(self):
        self.job.start()

    def advance(self, number):
        self.job.advance(number)

    def finish(self):
        self.job.finish()

    def cuts(self, steps):
        first, last = (2 * steps) // 5, 2 * steps - 2
        return [first + ((last - first) * i) // (self.size - 1) for i in range(self.size)]


class ProductJob(Job):
    def __init__(self, left_at, right_at, dims, shape, tile):
        self.left_at, self.right_at, self.dims, self.shape, self.tile = left_at, right_at, dims, shape, tile
        self.inputs, self.in_specs = [], []
        self.out_shape, self.out_specs = [jax.ShapeDtypeStruct(shape, BF16)], [ANY]
        self.scratch = [pltpu.VMEM((2, tile, shape[1]), BF16), pltpu.SemaphoreType.DMA((2,))]

    def bind(self, ins, outs, scratch):
        (self.out,) = outs
        self.stage, self.sem = scratch

    def peers(self):
        return []

    def cuts(self, steps):
        return []

    def start(self):
        pass

    def tasks(self):
        return [(self.shape[0] // self.tile, self.act, (self.left_at, self.right_at))]

    def copy(self, i):
        where = pl.ds(pl.multiple_of(i * self.tile, self.tile), self.tile)
        return pltpu.make_async_copy(self.stage.at[i % 2], self.out.at[where, :], self.sem.at[i % 2])

    def act(self, i):
        @pl.when(i >= 2)
        def _():
            self.copy(i - 2).wait()

        where = pl.ds(pl.multiple_of(i * self.tile, self.tile), self.tile)
        product_tile(self.operands[self.left_at], self.operands[self.right_at], self.dims, where, self.stage.at[i % 2])
        self.copy(i).start()

    def finish(self):
        tiles = self.shape[0] // self.tile
        for i in range(max(0, tiles - 2), tiles):
            self.copy(i).wait()


def product_tile(left, right, dims, where, out):
    rows = left[:, where].T if dims == TN else left[where, :]

    def act(cols):
        if dims == NT:
            out[:, cols] = dot(rows, right[cols, :], NT).astype(out.dtype)
        else:
            out[:, cols] = dot(rows, right[:, cols]).astype(out.dtype)

    by_columns(out.shape[-1], act)


def by_columns(width, act):
    step = min(512, width)

    @pl.loop(0, width // step)
    def _(n):
        act(pl.ds(pl.multiple_of(n * step, step), step))

    if width % step:
        act(pl.ds(width - width % step, width % step))


class ProductScatterJob(ScatterJob):
    def __init__(self, pairs, shapes, dims):
        self.size = lax.axis_size("fsdp")
        self.pairs, self.dims = pairs, dims
        shapes = [RingScatter.out_shape(jax.ShapeDtypeStruct(s, BF16), d, self.size) for s, d in zip(shapes, dims)]
        self.inputs, self.in_specs = [], []
        self.out_shape = [jax.ShapeDtypeStruct(s, F32) for s in shapes]
        self.out_specs = [ANY] * len(shapes)
        self.scratch = [pltpu.VMEM((2, self.size) + s, BF16) for s in shapes]
        self.scratch += [pltpu.VMEM((self.size,) + s, BF16) for s in shapes]
        self.scratch += [pltpu.VMEM((2, self.size - 1, s[0] // 2, s[1]), BF16) for s in shapes]
        self.scratch += [pltpu.VMEM(s, F32) for s in shapes]
        self.scratch += RingScatter.scratch(len(shapes), self.size)

    def bind(self, ins, outs, scratch):
        self.job = RingScatter(
            [None] * len(outs), outs, self.dims, scratch[:-6], scratch[-6:], self.size, self.size == 4
        )

    def cuts(self, steps):
        first, last = min(self.ready_at + 2, 2 * steps - 8), 2 * steps - 3
        return [first + ((last - first) * i) // (self.size - 1) for i in range(self.size)]

    def start(self):
        pass

    def tasks(self):
        made = []
        for i in sorted(range(len(self.pairs)), key=lambda i: -self.dims[i]):
            tiles = 2 * self.size if self.dims[i] == 0 else self.size
            made.append((tiles, functools.partial(self.act, i), self.pairs[i]))
        return made

    def act(self, i, t):
        job = self.job
        left, right = (self.operands[p] for p in self.pairs[i])
        if self.dims[i] == 0:
            offset, mine = lax.rem(t // 2 + 1, self.size), t % 2
            core = mine * job.core + (1 - mine) * (1 - job.core)
            extent = job.outs[i].shape[0]
            index = job.device(job.place + offset) * 2 + core
            where = pl.ds(pl.multiple_of(index * extent, extent), extent)
            product_tile(left, right, TN, where, job.own[i].at[mine, offset])

            @pl.when(mine == 0)
            def _():
                job.across(i, offset).start()
        else:
            offset = lax.rem(t + 1, self.size)
            extent = job.outs[i].shape[1]
            start = pl.multiple_of(job.device(job.place + offset) * 2 * extent, 2 * extent)
            tile = dot(left[...].T, right[:, pl.ds(start, 2 * extent)]).astype(BF16)
            for core in range(2):
                mine = 1 - core + (2 * core - 1) * job.core
                job.own[i][mine, offset] = tile[:, core * extent : (core + 1) * extent]
            job.across(i, offset).start()


class MixBackJob(Job):
    def __init__(self, valid, grad_branch, w_out, mixed, pre, states, gap, gain, state_end):
        self.rows, self.width = grad_branch.shape
        self.local = w_out.shape[0]
        self.chunks, self.heads = states.shape[:2]
        self.length = self.rows // self.chunks
        self.inputs = [valid, grad_branch, w_out, mixed, pre, states, gap, gain, state_end]
        self.in_specs = [pl.BlockSpec(memory_space=pltpu.SMEM)] + [ANY] * 5 + [WHOLE] * 3
        self.out_shape = [jax.ShapeDtypeStruct((self.rows, self.local), BF16)] * 4 + [
            jax.ShapeDtypeStruct((1, self.local), F32),
            jax.ShapeDtypeStruct((1, HEAD_DIM), F32),
        ]
        self.out_specs = [ANY] * 4 + [WHOLE] * 2
        state = states.shape[1:]
        self.scratch = [
            pltpu.VMEM(w_out.shape, BF16),
            pltpu.VMEM((2, self.length, self.width), BF16),
            pltpu.VMEM((2, self.length, self.local), F32),
            pltpu.VMEM((2, self.length, 4 * self.local), F32),
            pltpu.VMEM((2,) + state, F32),
            pltpu.VMEM((self.length, self.local), F32),
            pltpu.VMEM((self.rows, self.local), BF16),
            *[pltpu.VMEM(state, F32)] * 4,
            pltpu.VMEM((2, 4, self.length, self.local), BF16),
            pltpu.SemaphoreType.DMA((2, 4)),
            pltpu.SemaphoreType.DMA((2, 4)),
            pltpu.SemaphoreType.DMA((3,)),
        ]

    def bind(self, ins, outs, scratch):
        self.valid, self.grad_branch, self.w_out, self.mixed, self.pre, self.states, self.gap, self.gain, self.last = ins
        self.outs, (self.gap_part, self.gain_part) = outs[:4], outs[4:]
        self.w_here, self.grad_here, self.mixed_here, self.pre_here, self.states_here = scratch[:5]
        self.gated, self.grad_mixed, self.begin, self.came, self.flow, self.after = scratch[5:11]
        self.stage, self.in_sem, self.out_sem, self.sem = scratch[11:]
        self.core = lax.axis_index("ctx")

    def peers(self):
        return [{"ctx": 1 - self.core}]

    def cuts(self, steps):
        return []

    def w_copy(self):
        return pltpu.make_async_copy(self.w_out, self.w_here, self.sem.at[0])

    def across(self):
        return pltpu.make_async_remote_copy(
            src_ref=self.begin,
            dst_ref=self.came,
            send_sem=self.sem.at[1],
            recv_sem=self.sem.at[2],
            device_id={"ctx": 1 - self.core},
            device_id_type=BY_AXIS,
        )

    def where(self, i):
        return pl.ds(pl.multiple_of((self.chunks - 1 - i) * self.length, self.length), self.length)

    def loads(self, phase, i):
        slot = i % 2
        copies = [pltpu.make_async_copy(self.pre.at[self.where(i), :], self.pre_here.at[slot], self.in_sem.at[slot, 0])]
        if phase == 0:
            whole = (self.grad_branch, self.grad_here, 1), (self.mixed, self.mixed_here, 2)
            for source, here, n in whole:
                copies.append(
                    pltpu.make_async_copy(source.at[self.where(i), :], here.at[slot], self.in_sem.at[slot, n])
                )
        else:
            copies.append(
                pltpu.make_async_copy(
                    self.states.at[self.chunks - 1 - i], self.states_here.at[slot], self.in_sem.at[slot, 3]
                )
            )
        return copies

    def begin_loads(self, phase, i):
        for copy in self.loads(phase, i):
            copy.start()

    def end_loads(self, phase, i):
        for copy in self.loads(phase, i):
            copy.wait()

    def save(self, k, i):
        slot = i % 2
        return pltpu.make_async_copy(
            self.stage.at[slot, k], self.outs[k].at[self.where(i), :], self.out_sem.at[slot, k]
        )

    def start(self):
        self.w_copy().start()
        for i in range(2):
            self.begin_loads(0, i)

    def tasks(self):
        return [(self.chunks, self.act_begin, ()), (1, lambda i: None, ()), (2 * self.chunks, self.act_back, ())]

    def column(self, slot, k, start=0, wide=None):
        return self.pre_here.at[slot, :, pl.ds(k * self.local + start, wide or self.local)]

    def act_begin(self, i):
        slot = i % 2

        @pl.when(i == 0)
        def _():
            self.w_copy().wait()

        self.end_loads(0, i)

        @pl.when(i >= 2)
        def _():
            self.save(3, i - 2).wait()

        self.gated[...] = dot(self.grad_here[slot], self.w_here[...], NT)
        span_begin_chunk(
            self.heads, self.length, i, self.chunks, self.valid, self.gated, self.mixed_here.at[slot],
            self.column(slot, 0), self.column(slot, 1), self.column(slot, 3), self.gap, self.gain,
            self.stage.at[slot, 3], self.grad_mixed.at[self.where(i), :], self.gain_part, self.begin,
        )
        self.save(3, i).start()

        @pl.when(i + 2 < self.chunks)
        def _():
            self.begin_loads(0, i + 2)

        @pl.when(i + 2 >= self.chunks)
        def _():
            self.begin_loads(1, i + 2 - self.chunks)

        @pl.when(i == self.chunks - 1)
        def _():
            self.across().start()

    def act_back(self, t):
        i, part = t // 2, t % 2
        slot = i % 2

        @pl.when(t == 0)
        def _():
            self.across().wait_recv()
            self.came[...] = jnp.where(self.core == 0, self.came[...], 0.0)

        @pl.when(part == 0)
        def _():
            self.end_loads(1, i)

            @pl.when(i >= 2)
            def _():
                for k in range(3):
                    self.save(k, i - 2).wait()

        heads, wide = self.heads // 2, self.local // 2
        start = pl.multiple_of(part * wide, HEAD_DIM)
        cols, some = pl.ds(start, wide), pl.ds(part * heads, heads)
        mix_back_chunk(
            heads, self.length, i, self.chunks, self.valid, self.grad_mixed.at[self.where(i), cols],
            *[self.column(slot, k, start, wide) for k in range(3)], self.gap.at[:, cols],
            self.states_here.at[pl.ds(slot, 1), some], self.last.at[some], self.came.at[some],
            *[self.stage.at[slot, k, :, cols] for k in range(3)],
            self.gap_part.at[:, cols], self.flow.at[some], self.after.at[some],
        )

        @pl.when(part == 1)
        def _():
            for k in range(3):
                self.save(k, i).start()

            @pl.when(i + 2 < self.chunks)
            def _():
                self.begin_loads(1, i + 2)

    def finish(self):
        for i in range(self.chunks - 2, self.chunks):
            for k in range(4):
                self.save(k, i).wait()
        self.across().wait_send()


class VectorJob(Job):
    def __init__(self, full, short, split):
        self.axes = [(axis, lax.axis_size(axis)) for axis in ("ctx", "fsdp", "tp")]
        self.inputs, self.in_specs = [full, short, split], [WHOLE] * 3
        self.out_shape, self.out_specs = [jax.ShapeDtypeStruct(full.shape, F32)], [WHOLE]
        self.scratch = [pltpu.VMEM((size,) + full.shape, F32) for _, size in self.axes] + [
            pltpu.SemaphoreType.DMA((size - 1,)) for _, size in self.axes
        ] * 2

    def bind(self, ins, outs, scratch):
        self.full, self.short, self.split = ins
        (self.out,) = outs
        self.slots, self.sends, self.recvs = scratch[:3], scratch[3:6], scratch[6:]

    def peers(self):
        return [
            {axis: lax.rem(lax.axis_index(axis) + step, size)} for axis, size in self.axes for step in range(1, size)
        ]

    def cuts(self, steps):
        return [steps + (steps * (i + 1)) // 6 for i in range(len(self.axes) + 1)]

    def tasks(self):
        return []

    def start(self):
        pass

    def copies(self, number):
        axis, size = self.axes[number]
        mine = lax.axis_index(axis)
        return [
            pltpu.make_async_remote_copy(
                src_ref=self.slots[number].at[mine],
                dst_ref=self.slots[number].at[mine],
                send_sem=self.sends[number].at[step - 1],
                recv_sem=self.recvs[number].at[step - 1],
                device_id={axis: lax.rem(mine + step, size)},
                device_id_type=BY_AXIS,
            )
            for step in range(1, size)
        ]

    def advance(self, number):
        if number == 0:
            mine = lax.axis_index(self.axes[0][0])
            slot, local = self.slots[0], self.split.shape[1]
            slot[mine] = self.extra()
            slot[mine, 1:2, :] = self.full[0:1, :]
            slot[mine, 2:3, : self.short.shape[1]] = self.short[...]
            slot[mine, 3:4, pl.ds(pl.multiple_of(lax.axis_index("tp") * local, local), local)] = self.split[...]
        else:
            for copy in self.copies(number - 1):
                copy.wait_recv()
            slot = self.slots[number - 1]
            total = slot[0]
            for k in range(1, self.axes[number - 1][1]):
                total = total + slot[k]
        if number == len(self.axes):
            self.out[...] = total
            return
        if number > 0:
            self.slots[number][lax.axis_index(self.axes[number][0])] = total
        for copy in self.copies(number):
            copy.start()

    def finish(self):
        for number in range(len(self.axes)):
            for copy in self.copies(number):
                copy.wait_send()


def line_sum(
    name, part, halves, gain, n_out, epilogue, collective_id, jobs=(), operands=(), chunk=32, skew=2, group=128
):
    size = lax.axis_size("tp")
    product = isinstance(part, tuple)
    operands = [o if isinstance(o, tuple) else (o,) for o in operands]
    operand_shapes = [(o[0].shape[0], sum(p.shape[1] for p in o)) for o in operands]
    pieces = [p for o in operands for p in o]
    if product:
        left_at, right_at, part_dims = part
        rows = operand_shapes[left_at][0]
        width = operand_shapes[right_at][1 - part_dims[1][0]]
    else:
        rows, width = part.shape
    half = rows // 2
    chunk = min(chunk, half)
    count = half // chunk
    group = min(group, half)
    groups = half // group
    per_group = group // chunk
    vector = [job for job in jobs if isinstance(job, VectorJob)]

    def kernel(*refs):
        refs = list(refs)

        def take(n):
            taken = refs[:n]
            del refs[:n]
            return taken

        part_refs, (gain_ref,) = take(0 if product else 1), take(1)
        half_refs = take(len(halves))
        operand_refs = take(len(pieces))
        job_ins = [take(len(job.inputs)) for job in jobs]
        (result_ref,) = take(1)
        own_refs = take(n_out)
        (gain_part_ref,) = take(1)
        job_outs = [take(len(job.out_shape)) for job in jobs]
        part_here, came, sum_send, sum_recv, back_send, back_recv, operand_sem, half_sem, own_sem, part_sem = take(10)
        out_ref, out_sem = take(2)
        half_here = take(len(halves))
        operand_here = take(len(operands))
        own_here = take(n_out)
        job_scratch = [take(len(job.scratch)) for job in jobs]
        place = lax.axis_index("tp")
        first, last = place == 0, place == size - 1
        source = (first, last)
        owner = (last, first)
        ahead = (place + 1, place - 1)
        behind = (place - 1, place + 1)
        base = (half, 0)

        loaded = set()

        def operand_copies(i):
            first, column = sum(len(o) for o in operands[:i]), 0
            for n, piece in enumerate(operands[i], first):
                where = operand_here[i].at[:, pl.ds(column, piece.shape[1])]
                yield pltpu.make_async_copy(operand_refs[n], where, operand_sem.at[n])
                column += piece.shape[1]

        def need(places):
            for i in places:
                if i not in loaded:
                    for copy in operand_copies(i):
                        copy.wait()
                    loaded.add(i)

        def half_copy(way, i):
            start = base[way] if half_refs[i].shape[0] == rows else 0
            return pltpu.make_async_copy(half_refs[i].at[pl.ds(start, half), :], half_here[i], half_sem.at[i])

        def part_copy(way, g):
            where = pl.ds(pl.multiple_of(base[way] + g * group, group), group)
            return pltpu.make_async_copy(part_refs[0].at[where, :], part_here.at[where, :], part_sem.at[way, g])

        if not product:
            for g in range(groups):
                for way in range(2):

                    @pl.when(jnp.logical_not(source[way]))
                    def _():
                        part_copy(way, g).start()

        def load(places):
            for i in places:
                for copy in operand_copies(i):
                    copy.start()

        early = (left_at, right_at) if product else ()
        load(early)
        for ins, outs, scratch, job in zip(job_ins, job_outs, job_scratch, jobs):
            job.operands = operand_here
            job.bind(ins, outs, scratch)
        peers = [(jnp.logical_not(first), {"tp": place - 1}), (jnp.logical_not(last), {"tp": place + 1})]
        meet(peers + [(None, peer) for job in jobs for peer in job.peers()])

        def at(way, k):
            return pl.ds(pl.multiple_of(k * chunk + base[way], chunk), chunk)

        def onward(way, k, from_part):
            return pltpu.make_async_remote_copy(
                src_ref=(part_here if product else part_refs[0]).at[at(way, k), :] if from_part else came.at[way, k],
                dst_ref=came.at[way, k],
                send_sem=sum_send.at[way, k],
                recv_sem=sum_recv.at[way, k],
                device_id={"tp": ahead[way]},
                device_id_type=BY_AXIS,
            )

        def back(way, k):
            piece = out_ref.at[at(way, k), :]
            return pltpu.make_async_remote_copy(
                src_ref=piece,
                dst_ref=piece,
                send_sem=back_send.at[way, k],
                recv_sem=back_recv.at[way, k],
                device_id={"tp": behind[way]},
                device_id_type=BY_AXIS,
            )

        def save(way, k):
            return pltpu.make_async_copy(out_ref.at[at(way, k), :], result_ref.at[at(way, k), :], out_sem.at[way, k])

        def own_copy(k):
            where = pl.ds(pl.multiple_of(k * chunk, chunk), chunk)
            return pltpu.make_async_copy(own_here[0].at[where, :], own_refs[0].at[where, :], own_sem.at[k])

        def part_rows(j):
            way, g = lax.rem(j + jnp.where(place < size // 2, 0, 1), 2), j // 2
            where = pl.ds(pl.multiple_of((1 - way) * half + g * group, group), group)
            left = operand_here[left_at][where, :]
            for start in range(0, width, 512):
                cols = slice(start, min(start + 512, width))
                right = operand_here[right_at]
                right = right[:, cols] if part_dims == NN else right[cols, :]
                part_here[where, cols] = dot(left, right, part_dims).astype(BF16)
            for w in range(2):

                @pl.when(jnp.logical_and(source[w], way == w))
                def _():
                    @pl.loop(0, per_group)
                    def _(k):
                        onward(w, g * per_group + k, True).start()

        tasks, at_step = [], 0
        need(early)
        load([i for i in range(len(operands)) if i not in early])
        for way in range(2):

            @pl.when(owner[way])
            def _():
                for i in range(len(halves)):
                    half_copy(way, i).start()

        if product:
            tasks, at_step = [(-2, 2 * groups, part_rows, ())], 2 * groups - 2
        else:
            for way in range(2):

                @pl.when(source[way])
                def _():
                    @pl.loop(0, count)
                    def _(k):
                        onward(way, k, True).start()

        for job in jobs:
            job.start()
        gain_part_ref[...] = jnp.zeros_like(gain_part_ref)

        away = (place - 1, size - 2 - place)

        def each_way(step, lead, act):
            for way in range(2):
                k = step - skew * lead[way]

                @pl.when(jnp.logical_and(k >= 0, k < count))
                def _():
                    act(way, k)

        def add(way, k):
            @pl.when(jnp.logical_not(source[way]))
            def _():
                if not product:

                    @pl.when(k % per_group == 0)
                    def _():
                        part_copy(way, k // per_group).wait()

                onward(way, k, False).wait_recv()
                total = came[way, k].astype(F32) + part_here[at(way, k), :].astype(F32)

                @pl.when(owner[way])
                def _():
                    @pl.when(k == 0)
                    def _():
                        for i in range(len(halves)):
                            half_copy(way, i).wait()

                    own = pl.ds(pl.multiple_of(k * chunk, chunk), chunk)
                    out_ref[at(way, k), :] = epilogue(
                        half_here, gain_ref[...], own_here[0] if n_out else None, gain_part_ref, own, total
                    )
                    back(way, k).start()
                    save(way, k).start()
                    if n_out:
                        own_copy(k).start()

                @pl.when(jnp.logical_not(owner[way]))
                def _():
                    came[way, k] = total.astype(BF16)
                    onward(way, k, False).start()

        def spread(way, k):
            @pl.when(jnp.logical_not(owner[way]))
            def _():
                back(way, k).wait_recv()

                @pl.when(jnp.logical_not(source[way]))
                def _():
                    back(way, k).start()

                save(way, k).start()

        steps = count + skew * (size - 2)
        extra, followed = 0, None
        for job in jobs:
            if isinstance(job, ForwardJob):
                slowest = max(job.first, per_group + skew * (size - 2))
                extra = max(0, slowest + (groups - 1) * per_group + 2 - steps, job.first + 2 * groups - steps)
                arrivals = [jnp.maximum(job.first, per_group + skew * away[1 - way]) for way in range(2)]
                begins = [jnp.where(owner[way], job.first, arrivals[way]) for way in range(2)]
                followed = out_ref, begins, [jnp.where(o, 2, per_group) for o in owner], groups, base
        for job in vector:
            job.extra = lambda: jnp.where(
                lax.broadcasted_iota(jnp.int32, (8, width), 0) == 0, gain_part_ref[...], 0.0
            )
        for job in jobs:
            for tiles, act, needs in job.tasks():
                tasks.append((at_step, tiles, act, needs))
                at_step += tiles
            job.ready_at = at_step
        acts = sorted((cut, n, i) for n, job in enumerate(jobs) for i, cut in enumerate(job.cuts(steps)))
        bounds = {t[0] for t in tasks} | {t[0] + t[1] for t in tasks}
        for number, (act, lead) in enumerate([(add, away), (spread, (away[1], away[0]))]):
            base_step, high = number * steps, (number + 1) * steps + (extra if number else 0)
            low = min([base_step] + [t[0] for t in tasks if number == 0])
            here = [a for a in acts if low <= a[0] < high]
            edges = sorted({low, high} | {a[0] for a in here} | {e for e in bounds if low < e < high})
            for left, right in zip(edges[:-1], edges[1:]):
                for cut, n, i in here:
                    if cut == left:
                        jobs[n].advance(i)
                active = [t for t in tasks if t[0] <= left and right <= t[0] + t[1]]
                for t in active:
                    need(t[3])

                @pl.loop(left - base_step, right - base_step)
                def _(step):
                    each_way(step, lead, act)
                    for t in active:
                        t[2](step + base_step - t[0])
                    for job in jobs:
                        if number and right - base_step > job.first:
                            job.follow(step, followed)

        for first_step, tiles, act, needs in tasks:
            done = min(max(2 * steps - first_step, 0), tiles)
            if done < tiles:
                need(needs)

                @pl.loop(done, tiles)
                def _(i):
                    act(i)

        need(range(len(operands)))
        for job in jobs:
            job.finish()

        for way in range(2):

            @pl.loop(0, count)
            def _(k):
                save(way, k).wait()

            @pl.when(jnp.logical_not(owner[way]))
            def _():
                @pl.loop(0, count)
                def _(k):
                    onward(way, k, False).wait_send()

            @pl.when(jnp.logical_not(source[way]))
            def _():
                @pl.loop(0, count)
                def _(k):
                    back(way, k).wait_send()

            if n_out:

                @pl.when(owner[way])
                def _():
                    @pl.loop(0, count)
                    def _(k):
                        own_copy(k).wait()

    scratch = [
        pltpu.VMEM((rows, width), BF16),
        pltpu.VMEM((2, count, chunk, width), BF16),
        *[pltpu.SemaphoreType.DMA((2, count)) for _ in range(4)],
        pltpu.SemaphoreType.DMA((max(1, len(pieces)),)),
        pltpu.SemaphoreType.DMA((max(1, len(halves)),)),
        pltpu.SemaphoreType.DMA((count,)),
        pltpu.SemaphoreType.DMA((2, groups)),
        pltpu.VMEM((rows, width), BF16),
        pltpu.SemaphoreType.DMA((2, count)),
        *[pltpu.VMEM((half, width), h.dtype) for h in halves],
        *[pltpu.VMEM(shape, o[0].dtype) for shape, o in zip(operand_shapes, operands)],
        *[pltpu.VMEM((half, width), F32)] * n_out,
    ]
    return pl.pallas_call(
        kernel,
        out_shape=[jax.ShapeDtypeStruct((rows, width), BF16)]
        + [jax.ShapeDtypeStruct((half, width), F32)] * n_out
        + [jax.ShapeDtypeStruct((8, width), F32)]
        + [shape for job in jobs for shape in job.out_shape],
        in_specs=[ANY] * (not product) + [WHOLE] + [ANY] * (len(halves) + len(pieces)) + [spec for job in jobs for spec in job.in_specs],
        out_specs=[ANY] + [ANY] * n_out + [WHOLE] + [spec for job in jobs for spec in job.out_specs],
        scratch_shapes=scratch + [shape for job in jobs for shape in job.scratch],
        compiler_params=pltpu.CompilerParams(
            collective_id=collective_id, has_side_effects=True, vmem_limit_bytes=VMEM_BYTES
        ),
        name=name,
    )(*([] if product else [part]), gain, *halves, *pieces, *[array for job in jobs for array in job.inputs])


def rms(value):
    return lax.rsqrt(jnp.mean(value * value, axis=-1, keepdims=True) + EPSILON)


def middle_rows(halves, gain, own_ref, gain_part_ref, own, total):
    middle = halves[0][own, :].astype(F32) + total
    own_ref[own, :] = middle
    return (middle * rms(middle) * gain).astype(BF16)


def output_rows(halves, gain, own_ref, gain_part_ref, own, total):
    return (halves[0][own, :] + total).astype(BF16)


def norm_back(grad, value, gain, gain_part_ref):
    inverse = rms(value)
    scaled = value * inverse
    weighted = grad * gain
    gain_part_ref[0:1, :] += jnp.sum(grad * scaled, axis=0, keepdims=True)
    return inverse * (weighted - scaled * jnp.mean(weighted * scaled, axis=-1, keepdims=True))


def grad_middle_rows(halves, gain, own_ref, gain_part_ref, own, total):
    back = norm_back(total, halves[0][own, :], gain, gain_part_ref)
    grad_middle = halves[1][own, :].astype(F32) + back
    own_ref[own, :] = grad_middle
    return grad_middle.astype(BF16)


def input_grad_rows(halves, gain, own_ref, gain_part_ref, own, total):
    back = norm_back(total, halves[0][own, :].astype(F32), gain, gain_part_ref)
    return (halves[1][own, :] + back).astype(BF16)


def lower_ones(length):
    at = lax.broadcasted_iota(jnp.int32, (length, length), 0)
    before = lax.broadcasted_iota(jnp.int32, (length, length), 1)
    return at >= before


def chunk_decay(forget, gap, live, lower):
    closing = sigmoid(-forget)
    opened = gap * closing
    remain = 1.0 - opened
    decay = jnp.where(live, jnp.log(remain), 0.0)
    keys = jnp.where(live, opened, 0.0)
    return closing, remain, keys, ones_times(lower, decay)


def rows_live(valid_ref, chunk_index, length):
    at = lax.broadcasted_iota(jnp.int32, (length, HEAD_DIM), 0) + chunk_index * length
    return at < valid_ref[0]


def span_end_kernel(heads, length, valid_ref, forget_ref, value_ref, gap_ref, end_ref):
    index = pl.program_id(0)

    @pl.when(index == 0)
    def _():
        end_ref[...] = jnp.zeros_like(end_ref)

    live = rows_live(valid_ref, index, length)
    lower = lower_ones(length).astype(BF16)
    for h in range(heads):
        cols = slice(h * HEAD_DIM, (h + 1) * HEAD_DIM)
        _, _, keys, cumulative = chunk_decay(forget_ref[:, cols], gap_ref[:, cols], live, lower)
        total = cumulative[length - 1 :, :]
        tail = (keys * jnp.exp(total - cumulative)).astype(BF16)
        end_ref[h] = jnp.exp(total) * end_ref[h] + dot(value_ref[:, cols].astype(BF16), tail, TN)


def mix_kernel(
    heads, length, valid_ref, query_ref, forget_ref, value_ref, gate_ref, gap_ref, gain_ref, start_ref,
    gated_ref, mixed_ref, states_ref, end_ref, state_ref,
):
    index = pl.program_id(0)

    @pl.when(index == 0)
    def _():
        state_ref[...] = start_ref[...]

    live = rows_live(valid_ref, index, length)
    mask = lower_ones(length)
    lower = mask.astype(BF16)
    for h in range(heads):
        cols = slice(h * HEAD_DIM, (h + 1) * HEAD_DIM)
        _, _, keys, cumulative = chunk_decay(forget_ref[:, cols], gap_ref[:, cols], live, lower)
        pre = query_ref[:, cols]
        queries = (pre * sigmoid(pre) * jnp.exp(cumulative)).astype(BF16)
        shrunk = keys * jnp.exp(-cumulative)
        values = value_ref[:, cols].astype(BF16)
        state = state_ref[h]
        states_ref[0, h] = state
        scores = jnp.where(mask, dot(queries, shrunk.astype(BF16), NT), 0.0).astype(BF16)
        mixed = dot(scores, values) + dot(queries, state.astype(BF16), NT)
        mixed_ref[:, cols] = mixed
        growth = jnp.exp(cumulative[length - 1 :, :])
        state_ref[h] = growth * state + dot(values, (shrunk * growth).astype(BF16), TN)
        gate = gate_ref[:, cols]
        gated_ref[:, cols] = (mixed * rms(mixed) * gain_ref[...] * (gate * sigmoid(gate))).astype(BF16)

    @pl.when(index == pl.num_programs(0) - 1)
    def _():
        end_ref[...] = state_ref[...]


def span_begin_kernel(heads, length, *refs):
    span_begin_chunk(heads, length, pl.program_id(0), pl.num_programs(0), *refs)


def span_begin_chunk(
    heads, length, step, steps, valid_ref, grad_ref, mixed_ref, query_ref, forget_ref, gate_ref, gap_ref, gain_ref,
    grad_gate_ref, grad_mixed_ref, gain_part_ref, begin_ref,
):
    index = steps - 1 - step

    @pl.when(step == 0)
    def _():
        begin_ref[...] = jnp.zeros_like(begin_ref)
        gain_part_ref[...] = jnp.zeros_like(gain_part_ref)

    live = rows_live(valid_ref, index, length)
    lower = lower_ones(length).astype(BF16)
    gain = gain_ref[...]
    for h in range(heads):
        cols = slice(h * HEAD_DIM, (h + 1) * HEAD_DIM)
        mixed = mixed_ref[:, cols]
        inverse = rms(mixed)
        scaled = mixed * inverse
        gate = gate_ref[:, cols]
        sig = sigmoid(gate)
        grad = grad_ref[:, cols].astype(F32)
        grad_gate_ref[:, cols] = (grad * scaled * gain * slope(gate, sig)).astype(BF16)
        grad_scaled = grad * (gate * sig)
        gain_part_ref[...] += jnp.sum(grad_scaled * scaled, axis=0, keepdims=True)
        weighted = grad_scaled * gain
        grad_mixed = inverse * (weighted - scaled * jnp.mean(weighted * scaled, axis=-1, keepdims=True))
        grad_mixed = grad_mixed.astype(BF16)
        grad_mixed_ref[:, cols] = grad_mixed
        _, _, _, cumulative = chunk_decay(forget_ref[:, cols], gap_ref[:, cols], live, lower)
        pre = query_ref[:, cols]
        queries = (pre * sigmoid(pre) * jnp.exp(cumulative)).astype(BF16)
        growth = jnp.exp(cumulative[length - 1 :, :])
        begin_ref[h] = growth * begin_ref[h] + dot(grad_mixed, queries, TN)


def mix_back_kernel(heads, length, *refs):
    mix_back_chunk(heads, length, pl.program_id(0), pl.num_programs(0), *refs)


def mix_back_chunk(
    heads, length, step, steps, valid_ref, grad_ref, query_ref, forget_ref, value_ref, gap_ref, states_ref, last_ref,
    end_ref, grad_query_ref, grad_forget_ref, grad_value_ref, gap_part_ref, flow_ref, after_ref,
):
    index = steps - 1 - step

    @pl.when(step == 0)
    def _():
        flow_ref[...] = end_ref[...]
        after_ref[...] = last_ref[...]
        gap_part_ref[...] = jnp.zeros_like(gap_part_ref)

    live = rows_live(valid_ref, index, length)
    mask = lower_ones(length)
    lower = mask.astype(BF16)
    for h in range(heads):
        cols = slice(h * HEAD_DIM, (h + 1) * HEAD_DIM)
        gap = gap_ref[:, cols]
        closing, remain, keys, cumulative = chunk_decay(forget_ref[:, cols], gap, live, lower)
        pre = query_ref[:, cols]
        sig = sigmoid(pre)
        growth = jnp.exp(cumulative)
        shrink = jnp.exp(-cumulative)
        end_growth = growth[length - 1 :, :]
        queries = (pre * sig * growth).astype(BF16)
        shrunk_wide = keys * shrink
        shrunk = shrunk_wide.astype(BF16)
        tail = (shrunk_wide * end_growth).astype(BF16)
        values = value_ref[:, cols].astype(BF16)
        grad = grad_ref[:, cols]
        state = states_ref[0, h]
        flow = flow_ref[h]
        low_flow = flow.astype(BF16)
        scores = jnp.where(mask, dot(queries, shrunk, NT), 0.0).astype(BF16)
        grad_scores = jnp.where(mask, dot(grad, values, NT), 0.0).astype(BF16)
        to_queries = dot(grad, state.astype(BF16)) + dot(grad_scores, shrunk)
        to_keys = dot(grad_scores, queries, TN) + end_growth * dot(values, low_flow)
        grad_value_ref[:, cols] = (dot(scores, grad, TN) + dot(tail, low_flow, NT)).astype(BF16)
        grad_query_ref[:, cols] = (to_queries * growth * slope(pre, sig)).astype(BF16)
        terms = queries.astype(F32) * to_queries - shrunk.astype(F32) * to_keys
        high = terms.astype(BF16)
        rest = (terms - high.astype(F32)).astype(BF16)
        suffix = dot(lower, high, TN) + dot(lower, rest, TN)
        crossing = jnp.sum(flow * after_ref[h], axis=0, keepdims=True)
        pressure = jnp.where(live, to_keys * shrink - (suffix + crossing) / remain, 0.0)
        gap_part_ref[:, cols] += jnp.sum(closing * pressure, axis=0, keepdims=True)
        grad_forget_ref[:, cols] = (-closing * (1.0 - closing) * gap * pressure).astype(BF16)
        flow_ref[h] = end_growth * flow + dot(grad, queries, TN)
        after_ref[h] = state


def plain_call(kernel, name, grid, in_specs, out_specs, out_shape, scratch, flops, moved):
    return pl.pallas_call(
        kernel,
        grid_spec=pltpu.PrefetchScalarGridSpec(
            num_scalar_prefetch=1, grid=grid, in_specs=in_specs, out_specs=out_specs, scratch_shapes=scratch
        ),
        out_shape=out_shape,
        compiler_params=pltpu.CompilerParams(
            dimension_semantics=("arbitrary",), vmem_limit_bytes=VMEM_BYTES
        ),
        cost_estimate=pl.CostEstimate(flops=flops, bytes_accessed=moved, transcendentals=flops // 64),
        name=name,
    )


def combine(earlier, later):
    return (earlier[0] * later[0], later[0][:, None, :] * earlier[1] + later[1])


def from_earlier(state, decay, axis):
    size = lax.axis_size(axis)
    if size == 2:
        return lax.ppermute(state, axis, [(0, 1)])
    mine = lax.axis_index(axis)
    states, decays = lax.all_gather(state, axis), lax.all_gather(decay, axis)
    total = jnp.zeros_like(state)
    for k in range(size):
        new = decays[k][:, None, :] * total + states[k]
        total = jnp.where(k < mine, new, total)
    return total


def from_later(state, decay, axis):
    size = lax.axis_size(axis)
    if size == 2:
        return lax.ppermute(state, axis, [(1, 0)])
    mine = lax.axis_index(axis)
    states, decays = lax.all_gather(state, axis), lax.all_gather(decay, axis)
    total = jnp.zeros_like(state)
    for k in reversed(range(size)):
        new = decays[k][:, None, :] * total + states[k]
        total = jnp.where(k > mine, new, total)
    return total


def per_device(
    inputs, lengths, w_query, w_forget, w_input, w_outgate, w_output, w_gate, w_up, w_down,
    norm_gain, ffn_gain, head_gain, forget_gap, cotangent,
):
    groups, span, width = inputs.shape
    rows = groups * span
    fsdp, ctx, tp = lax.axis_size("fsdp"), lax.axis_size("ctx"), lax.axis_size("tp")
    local = forget_gap.shape[0]
    heads = local // HEAD_DIM
    ff = w_gate.shape[1]
    length = min(128, span)
    chunks = span // length
    place = lax.axis_index("tp")

    valid = jnp.clip(lengths - lax.axis_index("ctx") * span, 0, span).astype(jnp.int32)
    x = inputs.reshape(rows, width)
    gap = forget_gap.reshape(1, local)
    head_row = head_gain.reshape(1, HEAD_DIM)
    norm_row, ffn_row = norm_gain.reshape(1, width), ffn_gain.reshape(1, width)

    pre, normed, grad_low, w_four, w_out = project(
        x, cotangent.reshape(rows, width), norm_row, valid, [w_query, w_forget, w_input, w_outgate], w_output, 1
    )

    def column(j):
        return pl.BlockSpec((length, local), lambda i, *_: (i, j))

    def column_back(j):
        return pl.BlockSpec((length, local), lambda i, *_: (chunks - 1 - i, j))

    fixed = lambda shape: pl.BlockSpec(shape, lambda i, *_: (0,) * len(shape))
    state_shape = (heads, HEAD_DIM, HEAD_DIM)
    work = 2 * rows * local * HEAD_DIM
    moved = rows * local * 4

    local_end = plain_call(
        functools.partial(span_end_kernel, heads, length), "span_end", (chunks,),
        [column(1), column(2), fixed((1, local))], fixed(state_shape),
        jax.ShapeDtypeStruct(state_shape, F32), [], 3 * work, 2 * moved,
    )(valid, pre, pre, gap)
    span_decay = None
    if ctx > 2:
        keep = (jnp.arange(rows, dtype=jnp.int32) < valid[0])[:, None]
        closing = jax.nn.sigmoid(-pre[:, local : 2 * local])
        logs = jnp.where(keep, jnp.log(1.0 - gap * closing), 0.0)
        span_decay = jnp.exp(jnp.sum(logs, axis=0)).reshape(heads, HEAD_DIM)
    start = from_earlier(local_end, span_decay, "ctx")
    gated, mixed, states, state_end = plain_call(
        functools.partial(mix_kernel, heads, length), "mix", (chunks,),
        [column(0), column(1), column(2), column(3), fixed((1, local)), fixed((1, HEAD_DIM)), fixed(state_shape)],
        [column(0), column(0), pl.BlockSpec((1,) + state_shape, lambda i, *_: (i, 0, 0, 0)), fixed(state_shape)],
        [
            jax.ShapeDtypeStruct((rows, local), BF16),
            jax.ShapeDtypeStruct((rows, local), F32),
            jax.ShapeDtypeStruct((chunks,) + state_shape, F32),
            jax.ShapeDtypeStruct(state_shape, F32),
        ],
        [pltpu.VMEM(state_shape, F32)], 6 * work, 6 * moved,
    )(valid, pre, pre, pre, pre, gap, head_row, start)

    normed_two, middle, _, w_both, w_back, hidden, grad_gate, grad_up = line_sum(
        "sum_branch", (0, 1, NN), [x], ffn_row, 1, middle_rows, 2,
        [ForwardJob([w_gate, w_up, w_down], grad_low, min(128, rows // 2), 5)], [gated, w_out],
    )

    both_axes = ("fsdp", "ctx")

    def scattered(grads, dims):
        if ctx == 2:
            return [ScatterJob(grads, dims)], None
        return [], [
            lax.psum_scatter(g, both_axes, scatter_dimension=d, tiled=True).astype(F32) for g, d in zip(grads, dims)
        ]

    grad_branch, grad_middle, ffn_gain_part, grad_w_down, grad_w_both = line_sum(
        "sum_norm_two", (0, 1, NT), [middle, grad_low], ffn_row, 1, grad_middle_rows, 3,
        [ProductJob(2, 3, TN, (ff, width), 128), ProductJob(4, 0, TN, (width, 2 * ff), 128)],
        [(grad_gate, grad_up), w_both, hidden, grad_low, normed_two], group=256,
    )

    jobs, sums_ffn = scattered([grad_w_both, grad_w_down], [0, 1])
    if ctx == 2:
        jobs.append(MixBackJob(valid, grad_branch, w_out, mixed, pre, states, gap, head_row, state_end))
    result, _, *more = line_sum(
        "sum_feed", (0, 1, NN), [middle], ffn_row, 0, output_rows, 5, jobs, [hidden, w_back]
    )
    result = result.reshape(groups, span, width)
    if ctx == 2:
        out_both, out_down, grad_query, grad_forget, grad_value, grad_outgate, gap_part, head_part = more
    else:
        out_both, out_down = sums_ffn
        grad_gated = dot(grad_branch, w_out, NT)
        grad_outgate, grad_mixed, head_part, local_begin = plain_call(
            functools.partial(span_begin_kernel, heads, length), "span_begin", (chunks,),
            [column_back(0), column_back(0), column_back(0), column_back(1), column_back(3), fixed((1, local)),
             fixed((1, HEAD_DIM))],
            [column_back(0), column_back(0), fixed((1, HEAD_DIM)), fixed(state_shape)],
            [
                jax.ShapeDtypeStruct((rows, local), BF16),
                jax.ShapeDtypeStruct((rows, local), BF16),
                jax.ShapeDtypeStruct((1, HEAD_DIM), F32),
                jax.ShapeDtypeStruct(state_shape, F32),
            ],
            [], 3 * work, 6 * moved,
        )(valid, grad_gated, mixed, pre, pre, pre, gap, head_row)
        grad_end = from_later(local_begin, span_decay, "ctx")
        grad_query, grad_forget, grad_value, gap_part = plain_call(
            functools.partial(mix_back_kernel, heads, length), "mix_back", (chunks,),
            [column_back(0), column_back(0), column_back(1), column_back(2), fixed((1, local)),
             pl.BlockSpec((1,) + state_shape, lambda i, *_: (chunks - 1 - i, 0, 0, 0)), fixed(state_shape),
             fixed(state_shape)],
            [column_back(0), column_back(0), column_back(0), fixed((1, local))],
            [jax.ShapeDtypeStruct((rows, local), BF16)] * 3 + [jax.ShapeDtypeStruct((1, local), F32)],
            [pltpu.VMEM(state_shape, F32), pltpu.VMEM(state_shape, F32)], 12 * work, 6 * moved,
        )(valid, grad_mixed, pre, pre, pre, gap, states, state_end, grad_end)

    grad_four = (grad_query, grad_forget, grad_value, grad_outgate)
    jobs, operands, sums_mix = [VectorJob(ffn_gain_part, head_part, gap_part)], [grad_four, w_four], None
    if ctx == 2:
        shapes = [(width, 4 * local), (local, width)]
        jobs.append(ProductScatterJob([(2, 0), (3, 4)], shapes, [0, 1]))
        operands += [normed, gated, grad_branch]
    else:
        grads = [dot(normed, jnp.concatenate(grad_four, axis=1), TN).astype(BF16), dot(gated, grad_branch, TN).astype(BF16)]
        _, sums_mix = scattered(grads, [0, 1])
    input_grad, _, sums, *more = line_sum(
        "sum_norm_one", (0, 1, NT), [x, grad_middle], norm_row, 0, input_grad_rows, 4, jobs, operands
    )
    out_four, out_output = sums_mix or more
    input_grad = input_grad.reshape(groups, span, width)
    grad_norm_gain, grad_ffn_gain, grad_head_gain = sums[0], sums[1], sums[2, :HEAD_DIM]
    grad_gap = lax.dynamic_slice(sums[3], (place * local,), (local,))
    return (
        result,
        input_grad,
        out_four[:, :local],
        out_four[:, local : 2 * local],
        out_four[:, 2 * local : 3 * local],
        out_four[:, 3 * local :],
        out_output,
        out_both[:, :ff],
        out_both[:, ff:],
        out_down,
        grad_norm_gain,
        grad_ffn_gain,
        grad_head_gain,
        grad_gap,
    )


def solution(mesh):
    tokens = P("fsdp", "ctx", None)
    inward, outward = P("fsdp", "tp"), P("tp", "fsdp")
    grad_in, grad_back = P(("fsdp", "ctx"), "tp"), P("tp", ("fsdp", "ctx"))
    return jax.shard_map(
        per_device,
        mesh=mesh,
        in_specs=(tokens, P("fsdp")) + (inward,) * 4 + (outward, inward, inward, outward)
        + (P(), P(), P(), P("tp"), tokens),
        out_specs=(tokens, tokens) + (grad_in,) * 4 + (grad_back, grad_in, grad_in, grad_back)
        + (P(), P(), P(), P("tp")),
        check_vma=False,
    )
```
